32 devices in a mesh: dp: 4 (over y, x), strip: 8 (over z, core).
Axes of the slice: x: 2, y: 2, z: 4, core: 2. Of those that a mesh axis runs over, the one named last changes fastest.
Arguments:
- latents: bfloat16 [2, 4, 64, 64, 768], P(None, 'dp', 'strip'), may hold values from -6 to 6
- timesteps: int32 [2, 4], P(None, 'dp'), may hold values from 0 to 999
- size_tags: int32 [2, 4], P(None, 'dp'), may hold values from 0 to 1
- w_ada: bfloat16 [768, 4608], P('dp'), may hold values from -0.625 to 0.625
- b_ada: bfloat16 [4608], P('dp'), may hold values from -3 to 3
- conv_attn: bfloat16 [9, 768], P(None, 'dp'), may hold values from -2 to 2
- w_qkv: bfloat16 [768, 2304], P('dp'), may hold values from -0.21875 to 0.21875
- w_proj: bfloat16 [768, 768], P('dp'), may hold values from -6 to 6
- w_fc1: bfloat16 [768, 3072], P('dp'), may hold values from -0.21875 to 0.21875
- b_fc1: bfloat16 [3072], P('dp'), may hold values from -3 to 3
- conv_ffn: bfloat16 [9, 3072], P(None, 'dp'), may hold values from -2 to 2
- w_fc2: bfloat16 [3072, 768], P('dp'), may hold values from -0.109375 to 0.109375
- cotangent: bfloat16 [2, 4, 64, 64, 768], P(None, 'dp', 'strip'), may hold values from -6 to 6
Outputs:
- mixed: bfloat16 [2, 4, 64, 64, 768], P(None, 'dp', 'strip')
- d_latents: float32 [2, 4, 64, 64, 768], P(None, 'dp', 'strip')
- g_w_ada: float32 [768, 4608], P(('dp', 'strip'))
- g_b_ada: float32 [4608], P(('dp', 'strip'))
- g_conv_attn: float32 [9, 768], P(None, ('dp', 'strip'))
- g_w_qkv: float32 [768, 2304], P(('dp', 'strip'))
- g_w_proj: float32 [768, 768], P(('dp', 'strip'))
- g_w_fc1: float32 [768, 3072], P(('dp', 'strip'))
- g_b_fc1: float32 [3072], P(('dp', 'strip'))
- g_conv_ffn: float32 [9, 3072], P(None, ('dp', 'strip'))
- g_w_fc2: float32 [3072, 768], P(('dp', 'strip'))
The draws below stay inside these ranges and needn't reach their ends.
Inputs may be any that keep to these rules, and one draw needn't show every extreme that they name: `size_tags`: 1 marks a latent of 64 x 64 tokens, 0 one of 32 x 32 tokens in the first rows and columns of its canvas, the other cells being padding.
All inputs are finite; a program needn't handle non-finite values.
Results may differ from the reference program's by a relative error of at most 0.024.
The reference program's roundings to bfloat16 on the way count: a program that leaves them out, or rounds other values in their place, can miss the bound.
Values may be sent and summed in bfloat16 or wider, within the bound.
No kernel may reach another device: no remote copies, remote signals or barrier semaphores. Data moves between devices by JAX's collectives and lax.ppermute only.
A program may use at most 320 MiB of HBM per device.

```python
import math
import jax
import jax.numpy as jnp
from jax import lax

D = 768
HEADS = 12
FF = 3072
SIDE = 64
MICRO = 2
BATCH = 4
KEYS = 1024


def place_ends(array, key, least, top_value):
    spot = [jax.random.randint(jax.random.fold_in(key, axis), (), 0, length) for axis, length in enumerate(array.shape)]
    longest = array.shape.index(max(array.shape))
    next_to = spot[:longest] + [(spot[longest] + 1) % array.shape[longest]] + spot[longest + 1:]
    return array.at[tuple(spot)].set(least).at[tuple(next_to)].set(top_value)


def level_of(key, extent, shards, least, largest):
    factor_of = 1.0
    for axis_at, parts in shards:
        steps = jax.random.uniform(jax.random.fold_in(jax.random.fold_in(key, 6), axis_at), (parts,), jnp.float32, least / len(shards), largest / len(shards))
        factor_of = factor_of * jnp.repeat(jnp.exp(steps), extent[axis_at] // parts).reshape((-1,) + (1,) * (len(extent) - 1 - axis_at))
    return factor_of


def scatter_about(stream_key, shape, spread, reach, cuts=(), kind=jnp.bfloat16):
    array = spread * jax.random.normal(stream_key, shape, jnp.float32)
    if cuts:
        array = array * level_of(stream_key, shape, cuts, -0.22, 0.18)
    return jnp.clip(array, -reach, reach).astype(kind)


def setup_inputs(seed: int = 0) -> dict:
    seeds = jax.random.split(jax.random.key(seed), 14)
    return {
        "latents": scatter_about(seeds[0], (MICRO, BATCH, SIDE, SIDE, D), 1.0, 6.0, ((1, 4), (2, 8))),
        "timesteps": place_ends(jax.random.randint(seeds[1], (MICRO, BATCH), 0, 1000), jax.random.fold_in(seeds[1], 1), 0, 999).astype(jnp.int32),
        "size_tags": place_ends(jax.random.randint(seeds[2], (MICRO, BATCH), 0, 2), jax.random.fold_in(seeds[2], 1), 0, 1).astype(jnp.int32),
        "w_ada": scatter_about(seeds[3], (D, 6 * D), (D // 8) ** -0.5, 0.625, ((0, 4),)),
        "b_ada": scatter_about(seeds[4], (6 * D,), 0.5, 3.0, ((0, 4),)),
        "conv_attn": scatter_about(seeds[5], (9, D), 9 ** -0.5, 2.0, ((1, 4),)),
        "w_qkv": scatter_about(seeds[6], (D, 3 * D), D ** -0.5, 0.21875, ((0, 4),)),
        "w_proj": scatter_about(seeds[7], (D, D), ((KEYS / (2.0 * D)) ** 0.5), 6.0, ((0, 4),)),
        "w_fc1": scatter_about(seeds[8], (D, FF), D ** -0.5, 0.21875, ((0, 4),)),
        "b_fc1": scatter_about(seeds[9], (FF,), 0.5, 3.0, ((0, 4),)),
        "conv_ffn": scatter_about(seeds[10], (9, FF), 9 ** -0.5, 2.0, ((1, 4),)),
        "w_fc2": scatter_about(seeds[11], (FF, D), FF ** -0.5, 0.109375, ((0, 4),)),
        "cotangent": scatter_about(seeds[12], (MICRO, BATCH, SIDE, SIDE, D), 1.0, 6.0, ((1, 4), (2, 8))),
    }


@jax.custom_vjp
def low(v):
    return lax.optimization_barrier(v.astype(jnp.bfloat16)).astype(jnp.float32)

@jax.custom_vjp
def low_back(v):
    return v

def low_keep(v):
    return (low(v), None)

def low_pass(kept, grad):
    return (grad,)

def back_keep(v):
    return (v, None)

def back_low(kept, grad):
    return (low(grad),)
low.defvjp(low_keep, low_pass)
low_back.defvjp(back_keep, back_low)
root_half = 0.7071067811865476

def normalize(values):
    centre = values - lax.optimization_barrier(jnp.mean(values, axis=-1, keepdims=True))
    inverse = lax.rsqrt(lax.optimization_barrier(jnp.mean(centre * centre, axis=-1, keepdims=True)) + 1e-06)
    return centre * inverse

def embed_time(time_stamp, features):
    half_count = features // 2
    frequency = jnp.exp(-math.log(10000.0) * jnp.arange(half_count, dtype=jnp.float32) / half_count)
    angles = time_stamp.astype(jnp.float32) * frequency
    return jnp.concatenate([jnp.cos(angles), jnp.sin(angles)])

def silu_of(values):
    return values / (1.0 + jnp.exp(-values))

def gelu_of(values):
    return 0.5 * values * (1.0 + lax.erf(values * root_half))

def depth_conv_full(values, conv_taps):
    padded = jnp.pad(values, ((1, 1), (1, 1), (0, 0)))
    summed = jnp.zeros(values.shape, jnp.float32)
    for tap_row in range(3):
        for tap_col in range(3):
            summed = summed + padded[tap_row:tap_row + SIDE, tap_col:tap_col + SIDE] * conv_taps[3 * tap_row + tap_col]
    return summed

def highest(left, right):
    return jnp.dot(left, right, precision=lax.Precision.HIGHEST)

def attention(queries, keys_in, values_in, live_side):
    head_size = D // HEADS
    score_scale = head_size ** (-0.5)
    half_side = SIDE // 2

    def to_maps(canvas):
        return canvas.reshape(half_side, 2, half_side, 2, D).transpose(1, 3, 0, 2, 4).reshape(4, KEYS, HEADS, head_size)
    key_index = jnp.arange(KEYS)
    live_keys = (key_index // half_side < live_side // 2) & (key_index % half_side < live_side // 2)

    def single_map(map_parts):
        query_map, key_map, value_map = map_parts
        scores = low_back(jnp.einsum('qhd,khd->hqk', query_map, key_map, precision=lax.Precision.HIGHEST) * score_scale)
        scores = jnp.where(live_keys[None, None, :], scores, -1e+30)
        row_max = lax.optimization_barrier(jnp.max(scores, axis=-1, keepdims=True))
        exponent = jnp.exp(scores - row_max)
        probability = low(exponent / lax.optimization_barrier(jnp.sum(exponent, axis=-1, keepdims=True)))
        return jnp.einsum('hqk,khd->qhd', probability, value_map, precision=lax.Precision.HIGHEST)
    outputs = lax.map(jax.checkpoint(single_map), (to_maps(queries), to_maps(keys_in), to_maps(values_in)))
    return outputs.reshape(2, 2, half_side, half_side, D).transpose(2, 0, 3, 1, 4).reshape(SIDE, SIDE, D)

def image_forward(inputs, time_stamp, size_tag, weight_set):
    w_ada, b_ada, conv_attn, w_qkv, w_proj, w_fc1, b_fc1, conv_ffn, w_fc2 = weight_set
    live_side = jnp.where(size_tag == 1, SIDE, SIDE // 2)
    positions = jnp.arange(SIDE)
    live_cells = ((positions[:, None] < live_side) & (positions[None, :] < live_side)).astype(jnp.float32)[:, :, None]
    modulation = highest(silu_of(embed_time(time_stamp, D))[None, :], w_ada)[0] + b_ada
    shift_one, scale_one, gate_one = (modulation[0:D], modulation[D:2 * D], modulation[2 * D:3 * D])
    shift_two, scale_two, gate_two = (modulation[3 * D:4 * D], modulation[4 * D:5 * D], modulation[5 * D:6 * D])
    first = low(normalize(inputs) * (1.0 + scale_one) + shift_one) * live_cells
    mixed_one = low_back(low(depth_conv_full(first, conv_attn)))
    triple = highest(mixed_one.reshape(SIDE * SIDE, D), w_qkv).reshape(SIDE, SIDE, 3 * D)
    queries = low_back(low(triple[:, :, 0:D]))
    keys_in = low_back(low(triple[:, :, D:2 * D]))
    values_in = low_back(low(triple[:, :, 2 * D:3 * D]))
    attended = low_back(low(attention(queries, keys_in, values_in, live_side)))
    branch_one = low_back(highest(attended.reshape(SIDE * SIDE, D), w_proj).reshape(SIDE, SIDE, D))
    middle = inputs + gate_one * branch_one
    second = low(normalize(middle) * (1.0 + scale_two) + shift_two)
    expanded = (highest(second.reshape(SIDE * SIDE, D), w_fc1) + b_fc1).reshape(SIDE, SIDE, FF)
    expanded = low_back(low(expanded * live_cells))
    conv_out = low_back(depth_conv_full(expanded, conv_ffn))
    activated = low(gelu_of(conv_out))
    branch_two = low_back(highest(activated.reshape(SIDE * SIDE, FF), w_fc2).reshape(SIDE, SIDE, D))
    return (middle + gate_two * branch_two) * live_cells

def reference(latents, timesteps, size_tags, w_ada, b_ada, conv_attn, w_qkv, w_proj, w_fc1, b_fc1, conv_ffn, w_fc2, cotangent):
    image_count = MICRO * BATCH
    weight_set = tuple((weight_item.astype(jnp.float32) for weight_item in (w_ada, b_ada, conv_attn, w_qkv, w_proj, w_fc1, b_fc1, conv_ffn, w_fc2)))
    inputs = latents.astype(jnp.float32).reshape(image_count, SIDE, SIDE, D)
    stamps = timesteps.reshape(image_count)
    size_list = size_tags.reshape(image_count)

    def forward(inputs_all, weights_all):

        def one_image(image_parts):
            return image_forward(image_parts[0], image_parts[1], image_parts[2], weights_all)
        return lax.map(jax.checkpoint(one_image), (inputs_all, stamps, size_list))
    result, pullback = jax.vjp(forward, inputs, weight_set)
    grad_inputs, grad_weights = pullback(cotangent.astype(jnp.float32).reshape(image_count, SIDE, SIDE, D))
    mixed = result.astype(jnp.bfloat16).reshape(MICRO, BATCH, SIDE, SIDE, D)
    d_latents = grad_inputs.reshape(MICRO, BATCH, SIDE, SIDE, D)
    return (mixed, d_latents, grad_weights[0], grad_weights[1], grad_weights[2], grad_weights[3], grad_weights[4], grad_weights[5], grad_weights[6], grad_weights[7], grad_weights[8])
```

```python
import math

import jax
import jax.numpy as jnp
from jax import lax
from jax.sharding import PartitionSpec as P

HEADS = 12


root_half = 0.7071067811865476
inverse_root_tau = 0.3989422804014327


def permute_xor(x, axis, step):
    size = lax.axis_size(axis)
    return lax.ppermute(x, axis, [(i, i ^ step) for i in range(size)])


def pick(x, at, axis=0):
    return lax.dynamic_index_in_dim(x, at, axis, keepdims=False)


def halo_rows(x):
    size, length = (lax.axis_size("strip"), x.shape[0])
    up = [(i, i + 1) for i in range(size - 1)]
    down = [(i + 1, i) for i in range(size - 1)]
    before = lax.ppermute(x[length - 1 :], "strip", up)
    after = lax.ppermute(x[:1], "strip", down)
    return (before, after)


def place_blocks(blocks, me):
    stacked = jnp.stack(blocks)
    return jnp.stack([pick(stacked, me ^ at) for at in range(len(blocks))])


def gather_small(x):
    me = lax.axis_index("dp")
    blocks = [x] + [permute_xor(x, "dp", k) for k in range(1, lax.axis_size("dp"))]
    return place_blocks(blocks, me)


def gather_rows(w):
    rows, cols = w.shape
    size, me = (lax.axis_size("dp"), lax.axis_index("dp"))
    core = lax.axis_index("strip") & 1
    half = pick(w.reshape(2, rows // 2, cols), core)
    mine = jnp.stack([half] + [permute_xor(half, "dp", k) for k in range(1, size)])
    other = permute_xor(mine, "strip", 1)
    whole = jnp.zeros((size, 2, rows // 2, cols), w.dtype)
    for k in range(size):
        whole = lax.dynamic_update_slice(whole, mine[k][None, None], (me ^ k, core, 0, 0))
        whole = lax.dynamic_update_slice(whole, other[k][None, None], (me ^ k, 1 - core, 0, 0))
    return whole.reshape(size * rows, cols)


def gather_group(w, groups):
    rows, cols = w.shape
    width = cols // 3 // groups
    size, me = (lax.axis_size("dp"), lax.axis_index("dp"))
    group = lax.axis_index("strip") % groups
    mine = pick(w.reshape(rows, 3, groups, width), group, 2).reshape(rows, 3 * width)
    blocks = [mine] + [permute_xor(mine, "dp", k) for k in range(1, size)]
    whole = jnp.zeros((size, rows, 3 * width), w.dtype)
    for k in range(size):
        whole = lax.dynamic_update_slice(whole, blocks[k][None], (me ^ k, 0, 0))
    return whole.reshape(size * rows, 3 * width)


def exchange_sum(x, axis, me, step, wire):
    total = pick(x, me)
    parts = [
        permute_xor(pick(x, me ^ k).astype(wire), axis, k * step) for k in range(1, x.shape[0])
    ]
    for part in parts:
        total = total + part.astype(jnp.float32)
    return total


def scatter_rows(g, wire=jnp.bfloat16):
    rows, cols = g.shape
    dp, strips = (lax.axis_size("dp"), lax.axis_size("strip"))
    strip = lax.axis_index("strip")
    shaped = g.reshape(dp, strips // 2, 2, rows // dp // strips, cols)
    core = strip & 1
    sent = permute_xor(pick(shaped, 1 - core, 2).astype(wire), "strip", 1)
    kept = pick(shaped, core, 2) + sent.astype(jnp.float32)
    kept = exchange_sum(kept, "dp", lax.axis_index("dp"), 1, wire)
    return exchange_sum(kept, "strip", strip >> 1, 2, wire)


def scatter_group(g, groups, wire=jnp.bfloat16):
    rows, cols = g.shape
    dp, strips = (lax.axis_size("dp"), lax.axis_size("strip"))
    strip = lax.axis_index("strip")
    group = strip % groups
    row_block = rows // dp // strips
    kept = g.reshape(dp, strips // groups, groups, row_block, cols)
    kept = exchange_sum(kept, "dp", lax.axis_index("dp"), 1, wire)
    kept = exchange_sum(kept, "strip", strip // groups, groups, wire)
    blocks = [pick(kept, group)] + [
        permute_xor(pick(kept, group ^ k).astype(wire), "strip", k).astype(jnp.float32)
        for k in range(1, groups)
    ]
    whole = place_blocks(blocks, group).reshape(groups, row_block, 3, cols // 3)
    return whole.transpose(1, 2, 0, 3).reshape(row_block, groups * cols)


def to_maps(canvas):
    rows, cols, width = canvas.shape
    shaped = canvas.reshape(rows // 2, 2, cols // 2, 2, width).transpose(1, 3, 0, 2, 4)
    return shaped.reshape(4, rows * cols // 4, width)


def to_canvas(maps, rows, cols):
    width = maps.shape[-1]
    shaped = maps.reshape(2, 2, rows // 2, cols // 2, width).transpose(2, 0, 3, 1, 4)
    return shaped.reshape(rows, cols, width)


def map_exchange(maps, groups):
    me = lax.axis_index("strip") // groups
    return jnp.stack(
        [pick(maps, me)]
        + [permute_xor(pick(maps, me ^ k), "strip", k * groups) for k in range(1, 4)]
    )


def map_return(blocks, groups):
    me = lax.axis_index("strip") // groups
    return place_blocks(
        [blocks[0]] + [permute_xor(blocks[k], "strip", k * groups) for k in range(1, 4)], me
    )


def group_gather(x, groups):
    return jnp.stack([x] + [permute_xor(x, "strip", k) for k in range(1, groups)])


def group_swap(x, groups):
    return [x[0]] + [permute_xor(x[k], "strip", k) for k in range(1, groups)]


def silu_of(values):
    return values / (1.0 + jnp.exp(-values))


def embed_times(stamps, features):
    half_count = features // 2
    frequency = jnp.exp(-math.log(10000.0) * jnp.arange(half_count, dtype=jnp.float32) / half_count)
    angles = stamps[:, None] * frequency[None, :]
    return jnp.concatenate([jnp.cos(angles), jnp.sin(angles)], axis=1)

def normalize(values):
    centre = values - jnp.mean(values, axis=-1, keepdims=True)
    inverse = lax.rsqrt(jnp.mean(centre * centre, axis=-1, keepdims=True) + 1e-06)
    return (centre * inverse, inverse)


def norm_back(normed, inverse, upstream):
    return inverse * (
        upstream
        - jnp.mean(upstream, axis=-1, keepdims=True)
        - normed * jnp.mean(upstream * normed, axis=-1, keepdims=True)
    )


def gelu_of(values):
    return 0.5 * values * (1.0 + lax.erf(values * root_half))


def gelu_slope(values):
    return (
        0.5 * (1.0 + lax.erf(values * root_half))
        + values * jnp.exp(-0.5 * values * values) * inverse_root_tau
    )


def pad_columns(values):
    return jnp.pad(values, ((0, 0), (1, 1), (0, 0)))


def depth_conv(padded, conv_taps):
    row_count = padded.shape[0] - 2
    col_count = padded.shape[1] - 2
    summed = jnp.zeros((row_count, col_count, padded.shape[2]), jnp.float32)
    for tap_row in range(3):
        for tap_col in range(3):
            window = padded[tap_row : tap_row + row_count, tap_col : tap_col + col_count]
            summed = summed + window.astype(jnp.float32) * conv_taps[3 * tap_row + tap_col].astype(
                jnp.float32
            )
    return summed


def depth_conv_back(padded, conv_taps):
    row_count = padded.shape[0] - 2
    col_count = padded.shape[1] - 2
    summed = jnp.zeros((row_count, col_count, padded.shape[2]), jnp.float32)
    for tap_row in range(3):
        for tap_col in range(3):
            window = padded[
                2 - tap_row : 2 - tap_row + row_count, 2 - tap_col : 2 - tap_col + col_count
            ]
            summed = summed + window.astype(jnp.float32) * conv_taps[3 * tap_row + tap_col].astype(
                jnp.float32
            )
    return summed


def tap_grads(padded, upstream):
    row_count = upstream.shape[0]
    col_count = upstream.shape[1]
    return jnp.stack(
        [
            jnp.einsum(
                "rsc,rsc->c",
                padded[tap_row : tap_row + row_count, tap_col : tap_col + col_count],
                upstream,
                preferred_element_type=jnp.float32,
            )
            for tap_row in range(3)
            for tap_col in range(3)
        ]
    )


def matmul(left, right):
    return jnp.dot(left, right, preferred_element_type=jnp.float32)


def transposed_left(left, right):
    return lax.dot_general(
        left, right, (((0,), (0,)), ((), ())), preferred_element_type=jnp.float32
    )


def transposed_right(left, right):
    return lax.dot_general(
        left, right, (((1,), (1,)), ((), ())), preferred_element_type=jnp.float32
    )


def attend(u_all, qkv_group, live_keys, heads, score_scale):
    width = qkv_group.shape[1] // 3
    tokens = u_all.shape[0]
    triple = matmul(u_all, qkv_group).astype(jnp.bfloat16)
    shape = (tokens, heads, width // heads)
    q = triple[:, :width].reshape(shape)
    k = triple[:, width : 2 * width].reshape(shape)
    v = triple[:, 2 * width :].reshape(shape)
    s = jnp.einsum("qhd,khd->hqk", q, k, preferred_element_type=jnp.float32) * score_scale
    s = jnp.where(live_keys[None, None, :], s, -1e30)
    row_max = jnp.max(s, axis=-1, keepdims=True)
    log_total = row_max + jnp.log(jnp.sum(jnp.exp(s - row_max), axis=-1, keepdims=True))
    p = jnp.exp(s - log_total).astype(jnp.bfloat16)
    o = jnp.einsum("hqk,khd->qhd", p, v, preferred_element_type=jnp.float32)
    return (triple, o.reshape(tokens, width).astype(jnp.bfloat16), log_total)


def attend_back(triple, d_o, log_total, live_keys, heads, score_scale):
    width = triple.shape[1] // 3
    tokens = triple.shape[0]
    shape = (tokens, heads, width // heads)
    q = triple[:, :width].reshape(shape)
    k = triple[:, width : 2 * width].reshape(shape)
    v = triple[:, 2 * width :].reshape(shape)
    d_o = d_o.reshape(shape)
    s = jnp.einsum("qhd,khd->hqk", q, k, preferred_element_type=jnp.float32) * score_scale
    s = jnp.where(live_keys[None, None, :], s, -1e30)
    p = jnp.exp(s - log_total)
    d_p = jnp.einsum("qhd,khd->hqk", d_o, v, preferred_element_type=jnp.float32)
    d_s = (p * (d_p - jnp.sum(p * d_p, axis=-1, keepdims=True))).astype(jnp.bfloat16)
    d_q = jnp.einsum("hqk,khd->qhd", d_s, k, preferred_element_type=jnp.float32) * score_scale
    d_k = jnp.einsum("hqk,qhd->khd", d_s, q, preferred_element_type=jnp.float32) * score_scale
    d_v = jnp.einsum(
        "hqk,qhd->khd", p.astype(jnp.bfloat16), d_o, preferred_element_type=jnp.float32
    )
    parts = [part.reshape(tokens, width).astype(jnp.bfloat16) for part in (d_q, d_k, d_v)]
    return jnp.concatenate(parts, axis=1)


def with_halo(x, halo):
    return jnp.pad(jnp.concatenate([halo[0], x, halo[1]], axis=0), ((0, 0), (1, 1), (0, 0)))


def shards(
    latents,
    timesteps,
    size_tags,
    w_ada,
    b_ada,
    conv_attn,
    w_qkv,
    w_proj,
    w_fc1,
    b_fc1,
    conv_ffn,
    w_fc2,
    cotangent,
):
    micro_count, _, row_count, side_count, features = latents.shape
    dp, strips = (lax.axis_size("dp"), lax.axis_size("strip"))
    dp_at, strip_at = (lax.axis_index("dp"), lax.axis_index("strip"))
    hidden = conv_ffn.shape[1] * dp
    groups = strips // 4
    heads = HEADS // groups
    group_at, map_at = (strip_at % groups, strip_at // groups)
    score_scale = (features // HEADS) ** (-0.5)
    tokens = row_count * side_count
    quarter = tokens // 4
    half_side = side_count // 2
    width = features // groups

    stamps = timesteps[:, 0].astype(jnp.float32)
    all_stamps = [stamps] + [permute_xor(stamps, "dp", k) for k in range(1, dp)]
    conds = [silu_of(embed_times(each, features)) for each in all_stamps]
    ada_rows = features // dp
    ada_wide = w_ada.astype(jnp.float32)
    partial_mods = jnp.dot(
        lax.dynamic_slice_in_dim(jnp.concatenate(conds), dp_at * ada_rows, ada_rows, 1),
        ada_wide,
        precision=lax.Precision.HIGHEST,
    )
    bias_here = lax.dynamic_update_slice_in_dim(
        jnp.zeros((6 * features,), jnp.float32),
        b_ada.astype(jnp.float32),
        dp_at * b_ada.shape[0],
        0,
    )
    partial_mods = (partial_mods + bias_here[None, :]).reshape(dp, micro_count, 6 * features)
    modulation = partial_mods[0]
    for k in range(1, dp):
        modulation = modulation + permute_xor(partial_mods[k], "dp", k)

    small = jnp.concatenate([conv_attn.reshape(-1), conv_ffn.reshape(-1), b_fc1])
    small = gather_small(small)
    n_one, n_two = (conv_attn.size, conv_attn.size + conv_ffn.size)
    conv_one = small[:, :n_one].reshape(dp, 9, -1).transpose(1, 0, 2).reshape(9, features)
    conv_two = small[:, n_one:n_two].reshape(dp, 9, -1).transpose(1, 0, 2).reshape(9, hidden)
    fc1_bias = small[:, n_two:].reshape(hidden)
    qkv_group = gather_group(w_qkv, groups)
    proj_full = gather_rows(w_proj)
    fc1_full = gather_rows(w_fc1)
    fc2_full = gather_rows(w_fc2)

    row_ids = strip_at * row_count + jnp.arange(row_count, dtype=jnp.int32)
    col_ids = jnp.arange(side_count, dtype=jnp.int32)
    token_strip = (
        (map_at ^ jnp.arange(4, dtype=jnp.int32))[None, :] * groups
        + (group_at ^ jnp.arange(groups, dtype=jnp.int32))[:, None]
    ).reshape(-1)
    in_strip = jnp.arange(quarter, dtype=jnp.int32)
    key_row = (token_strip[:, None] * (row_count // 2) + (in_strip // half_side)[None, :]).reshape(-1)
    key_col = jnp.tile(in_strip % half_side, token_strip.shape[0])

    mixed_list = []
    grad_list = []
    mod_grads = []
    sums = None
    for at in range(micro_count):
        live_side = jnp.where(size_tags[at, 0] == 1, side_count, side_count // 2)
        live_cells = ((row_ids[:, None] < live_side) & (col_ids[None, :] < live_side)).astype(
            jnp.float32
        )[:, :, None]
        live_low = live_cells.astype(jnp.bfloat16)
        live_keys = (key_row < live_side // 2) & (key_col < live_side // 2)
        shift_one, scale_one, gate_one, shift_two, scale_two, gate_two = [
            modulation[at, i * features : (i + 1) * features] for i in range(6)
        ]
        inputs = latents[at, 0].astype(jnp.float32)
        normed_one, inverse_one = normalize(inputs)
        first_mod = (normed_one * (1.0 + scale_one) + shift_one).astype(jnp.bfloat16) * live_low
        first_rim = with_halo(first_mod, halo_rows(first_mod))
        mixed_one = depth_conv(first_rim, conv_one).astype(jnp.bfloat16)

        u_mine = map_exchange(to_maps(mixed_one), groups).reshape(tokens, features)
        u_all = group_gather(u_mine, groups).reshape(groups * tokens, features)
        triple, o_group, log_total = attend(u_all, qkv_group, live_keys, heads, score_scale)
        o_parts = group_swap(o_group.reshape(groups, tokens, width), groups)
        o_mine = place_blocks(o_parts, group_at).transpose(1, 0, 2).reshape(4, quarter, features)
        attended_low = to_canvas(map_return(o_mine, groups), row_count, side_count)
        attended_low = attended_low.reshape(tokens, features)

        branch_one = matmul(attended_low, proj_full).reshape(row_count, side_count, features)
        middle = inputs + gate_one * branch_one
        normed_two, inverse_two = normalize(middle)
        second_mod = (
            (normed_two * (1.0 + scale_two) + shift_two)
            .astype(jnp.bfloat16)
            .reshape(tokens, features)
        )
        expanded = (matmul(second_mod, fc1_full) + fc1_bias.astype(jnp.float32)).reshape(
            row_count, side_count, hidden
        )
        expanded = (expanded * live_cells).astype(jnp.bfloat16)
        expand_rim = with_halo(expanded, halo_rows(expanded))
        conv_out = depth_conv(expand_rim, conv_two)
        activated = gelu_of(conv_out).astype(jnp.bfloat16).reshape(tokens, hidden)
        branch_two = matmul(activated, fc2_full).reshape(row_count, side_count, features)
        summed_out = middle + gate_two * branch_two
        mixed_list.append((summed_out * live_cells).astype(jnp.bfloat16))

        upstream = cotangent[at, 0].astype(jnp.float32) * live_cells
        grad_gate_two = jnp.sum(upstream * branch_two, axis=(0, 1))
        grad_branch_two = (upstream * gate_two).astype(jnp.bfloat16).reshape(tokens, features)
        term_fc2 = transposed_left(activated, grad_branch_two)
        grad_conv_out = (
            transposed_right(grad_branch_two, fc2_full).reshape(row_count, side_count, hidden)
            * gelu_slope(conv_out)
        ).astype(jnp.bfloat16)
        grad_conv_rim = with_halo(grad_conv_out, halo_rows(grad_conv_out))
        term_conv_two = tap_grads(expand_rim, grad_conv_out)
        grad_expanded = (
            depth_conv_back(grad_conv_rim, conv_two).astype(jnp.bfloat16) * live_low
        ).reshape(tokens, hidden)
        term_fc1_bias = jnp.sum(grad_expanded.astype(jnp.float32), axis=0)
        term_fc1 = transposed_left(second_mod, grad_expanded)
        grad_second = transposed_right(grad_expanded, fc1_full).reshape(
            row_count, side_count, features
        )
        grad_scale_two = jnp.sum(grad_second * normed_two, axis=(0, 1))
        grad_shift_two = jnp.sum(grad_second, axis=(0, 1))
        grad_middle = upstream + norm_back(normed_two, inverse_two, grad_second * (1.0 + scale_two))
        grad_gate_one = jnp.sum(grad_middle * branch_one, axis=(0, 1))
        grad_branch_one = (grad_middle * gate_one).astype(jnp.bfloat16).reshape(tokens, features)
        term_proj = transposed_left(attended_low, grad_branch_one)
        grad_attended = (
            transposed_right(grad_branch_one, proj_full)
            .astype(jnp.bfloat16)
            .reshape(row_count, side_count, features)
        )

        d_o_mine = map_exchange(to_maps(grad_attended), groups).reshape(tokens, groups, width)
        d_o_parts = group_swap(
            [pick(d_o_mine, group_at ^ k, 1) for k in range(groups)], groups
        )
        grad_triple = attend_back(
            triple, jnp.concatenate(d_o_parts), log_total, live_keys, heads, score_scale
        )
        term_qkv = transposed_left(u_all, grad_triple)
        d_u_parts = transposed_right(grad_triple, qkv_group).reshape(groups, tokens, features)
        d_u_parts = group_swap(d_u_parts, groups)
        d_u = d_u_parts[0]
        for k in range(1, groups):
            d_u = d_u + d_u_parts[k]
        d_u = d_u.astype(jnp.bfloat16).reshape(4, quarter, features)
        grad_mixed = to_canvas(map_return(d_u, groups), row_count, side_count)

        grad_mixed_rim = with_halo(grad_mixed, halo_rows(grad_mixed))
        term_conv_one = tap_grads(first_rim, grad_mixed)
        grad_first = depth_conv_back(grad_mixed_rim, conv_one) * live_cells
        grad_scale_one = jnp.sum(grad_first * normed_one, axis=(0, 1))
        grad_shift_one = jnp.sum(grad_first, axis=(0, 1))
        grad_list.append(
            grad_middle + norm_back(normed_one, inverse_one, grad_first * (1.0 + scale_one))
        )
        mod_grads.append(
            jnp.concatenate(
                [
                    grad_shift_one,
                    grad_scale_one,
                    grad_gate_one,
                    grad_shift_two,
                    grad_scale_two,
                    grad_gate_two,
                ]
            )
        )
        terms = (
            term_conv_one,
            term_qkv,
            term_proj,
            term_fc1,
            term_fc1_bias,
            term_conv_two,
            term_fc2,
        )
        if sums is None:
            sums = terms
        else:
            sums = tuple(earlier + latest for earlier, latest in zip(sums, terms))

    g_fc2 = scatter_rows(sums[6])
    g_fc1 = scatter_rows(sums[3])
    g_proj = scatter_rows(sums[2])
    g_qkv = scatter_group(sums[1], groups)
    blocks = dp * strips
    packed = jnp.concatenate(
        [
            sums[5].reshape(9, blocks, -1).transpose(1, 0, 2).reshape(blocks, -1),
            sums[4].reshape(blocks, -1),
            sums[0].reshape(9, blocks, -1).transpose(1, 0, 2).reshape(blocks, -1),
        ],
        axis=1,
    )
    packed = scatter_rows(packed, jnp.float32)[0]
    wide, narrow = (hidden // blocks, features // blocks)
    g_conv_two = packed[: 9 * wide].reshape(9, wide)
    g_fc1_bias = packed[9 * wide : 10 * wide]
    g_conv_one = packed[10 * wide :].reshape(9, narrow)

    grad_mod = jnp.stack(mod_grads)
    step = 1
    while step < strips:
        grad_mod = grad_mod + permute_xor(grad_mod, "strip", step)
        step *= 2
    all_mods = jnp.concatenate([grad_mod] + [permute_xor(grad_mod, "dp", k) for k in range(1, dp)])
    block_at = dp_at * strips + strip_at
    conds_here = lax.dynamic_slice_in_dim(
        jnp.concatenate(conds), block_at * narrow, narrow, 1
    )
    g_ada = lax.dot_general(
        conds_here, all_mods, (((0,), (0,)), ((), ())), precision=lax.Precision.HIGHEST
    )
    ada_wide_block = 6 * features // blocks
    g_ada_bias = lax.dynamic_slice_in_dim(
        jnp.sum(all_mods, axis=0), block_at * ada_wide_block, ada_wide_block, 0
    )
    return (
        jnp.stack(mixed_list)[:, None],
        jnp.stack(grad_list)[:, None],
        g_ada,
        g_ada_bias,
        g_conv_one,
        g_qkv,
        g_proj,
        g_fc1,
        g_fc1_bias,
        g_conv_two,
        g_fc2,
    )


def solution(mesh):
    return jax.shard_map(
        shards,
        mesh=mesh,
        in_specs=(
            P(None, "dp", "strip", None, None),
            P(None, "dp"),
            P(None, "dp"),
            P("dp", None),
            P("dp"),
            P(None, "dp"),
            P("dp", None),
            P("dp", None),
            P("dp", None),
            P("dp"),
            P(None, "dp"),
            P("dp", None),
            P(None, "dp", "strip", None, None),
        ),
        out_specs=(
            P(None, "dp", "strip", None, None),
            P(None, "dp", "strip", None, None),
            P(("dp", "strip"), None),
            P(("dp", "strip")),
            P(None, ("dp", "strip")),
            P(("dp", "strip"), None),
            P(("dp", "strip"), None),
            P(("dp", "strip"), None),
            P(("dp", "strip")),
            P(None, ("dp", "strip")),
            P(("dp", "strip"), None),
        ),
        check_vma=False,
    )
```

```python
import functools
import math

import jax
import jax.numpy as jnp
from jax import lax
from jax.experimental import pallas as pl
from jax.experimental.pallas import tpu as pltpu
from jax.sharding import PartitionSpec as P

HEADS = 12


root_half = 0.7071067811865476
inverse_root_tau = 0.3989422804014327


def permute_xor(x, axis, step):
    size = lax.axis_size(axis)
    return lax.ppermute(x, axis, [(i, i ^ step) for i in range(size)])


def pick(x, at, axis=0):
    return lax.dynamic_index_in_dim(x, at, axis, keepdims=False)


def halo_rows(x):
    size, length = (lax.axis_size("strip"), x.shape[0])
    up = [(i, i + 1) for i in range(size - 1)]
    down = [(i + 1, i) for i in range(size - 1)]
    before = lax.ppermute(x[length - 1 :], "strip", up)
    after = lax.ppermute(x[:1], "strip", down)
    return (before, after)


def place_blocks(blocks, me):
    stacked = jnp.stack(blocks)
    return jnp.stack([pick(stacked, me ^ at) for at in range(len(blocks))])


def gather_small(x):
    me = lax.axis_index("dp")
    blocks = [x] + [permute_xor(x, "dp", k) for k in range(1, lax.axis_size("dp"))]
    return place_blocks(blocks, me)


def after(x, *done):
    return lax.optimization_barrier((x, done))[0]


def assemble_kernel(plan, at_ref, *refs):
    pieces, whole, sem = (refs[:-2], refs[-2], refs[-1])
    copies = []
    for i, (axis, size) in enumerate(plan):
        start = pl.multiple_of(at_ref[i], 16)
        target = whole.at[:, pl.ds(start, size), :] if axis else whole.at[pl.ds(start, size), :]
        copies.append(pltpu.make_async_copy(pieces[i], target, sem.at[i]))
    for copy in copies:
        copy.start()
    for copy in copies:
        copy.wait()


def assemble(pieces, starts, shape, axis):
    plan = tuple((axis, piece.shape[axis]) for piece in pieces)
    hbm = pl.BlockSpec(memory_space=pl.ANY)
    return pl.pallas_call(
        functools.partial(assemble_kernel, plan),
        grid_spec=pltpu.PrefetchScalarGridSpec(
            num_scalar_prefetch=1,
            grid=(1,),
            in_specs=[hbm] * len(pieces),
            out_specs=pl.BlockSpec(shape, lambda j, s: (0,) * len(shape)),
            scratch_shapes=[pltpu.SemaphoreType.DMA((len(pieces),))],
        ),
        out_shape=jax.ShapeDtypeStruct(shape, pieces[0].dtype),
        cost_estimate=pl.CostEstimate(
            flops=0, transcendentals=0, bytes_accessed=4 * math.prod(shape)
        ),
        name="assemble",
    )(jnp.stack(starts).astype(jnp.int32), *pieces)


def fetch_rows(w):
    rows, cols = w.shape
    core = lax.axis_index("strip") & 1
    half = pick(w.reshape(2, rows // 2, cols), core)
    return [permute_xor(half, "dp", k) for k in range(1, lax.axis_size("dp"))]


def gather_rows(w, fetched):
    rows, cols = w.shape
    me, core = (lax.axis_index("dp"), lax.axis_index("strip") & 1)
    pieces, starts = ([w], [me * rows])
    for k, mine in enumerate(fetched, 1):
        pieces += [mine, permute_xor(mine, "strip", 1)]
        base = (me ^ k) * rows
        starts += [base + core * (rows // 2), base + (1 - core) * (rows // 2)]
    return assemble(pieces, starts, (lax.axis_size("dp") * rows, cols), 0)


def fetch_group(w, groups):
    rows, cols = w.shape
    width = cols // 3 // groups
    group = lax.axis_index("strip") % groups
    mine = pick(w.reshape(rows, 3, groups, width), group, 2).transpose(1, 0, 2)
    mine = jnp.pad(mine, ((0, 0), (0, 0), (0, -width % 128)))
    return [mine] + [permute_xor(mine, "dp", k) for k in range(1, lax.axis_size("dp"))]


def gather_group(pieces):
    me, rows = (lax.axis_index("dp"), pieces[0].shape[1])
    starts = [(me ^ k) * rows for k in range(len(pieces))]
    return assemble(pieces, starts, (3, len(pieces) * rows, pieces[0].shape[2]), 1)


def exchange_sum(x, axis, me, step, wire):
    total = pick(x, me).astype(jnp.float32)
    parts = [
        permute_xor(pick(x, me ^ k).astype(wire), axis, k * step) for k in range(1, x.shape[0])
    ]
    for part in parts:
        total = total + part.astype(jnp.float32)
    return total


def scatter_rows(g, wire=jnp.bfloat16):
    rows, cols = g.shape
    dp, strips = (lax.axis_size("dp"), lax.axis_size("strip"))
    strip = lax.axis_index("strip")
    shaped = g.reshape(dp, strips // 2, 2, rows // dp // strips, cols)
    core = strip & 1
    sent = permute_xor(pick(shaped, 1 - core, 2).astype(wire), "strip", 1)
    kept = pick(shaped, core, 2).astype(jnp.float32) + sent.astype(jnp.float32)
    kept = exchange_sum(kept, "dp", lax.axis_index("dp"), 1, wire)
    return exchange_sum(kept, "strip", strip >> 1, 2, wire)


def scatter_group(g, groups, width, wire=jnp.bfloat16):
    rows = g.shape[1]
    dp, strips = (lax.axis_size("dp"), lax.axis_size("strip"))
    strip = lax.axis_index("strip")
    group = strip % groups
    row_block = rows // dp // strips
    kept = g[:, :, :width].reshape(3, dp, strips // groups, groups, row_block, width)
    kept = kept.transpose(1, 2, 3, 4, 0, 5).reshape(dp, strips // groups, groups, row_block, 3 * width)
    kept = exchange_sum(kept, "dp", lax.axis_index("dp"), 1, wire)
    kept = exchange_sum(kept, "strip", strip // groups, groups, wire)
    blocks = [pick(kept, group)] + [
        permute_xor(pick(kept, group ^ k).astype(wire), "strip", k).astype(jnp.float32)
        for k in range(1, groups)
    ]
    whole = place_blocks(blocks, group).reshape(groups, row_block, 3, width)
    return whole.transpose(1, 2, 0, 3).reshape(row_block, groups * 3 * width)


def map_exchange(pieces, groups):
    return [pieces[0]] + [permute_xor(pieces[k], "strip", k * groups) for k in range(1, 4)]


def group_exchange(pieces, groups):
    return list(pieces) + [
        permute_xor(piece, "strip", k) for k in range(1, groups) for piece in pieces
    ]


def silu_of(values):
    return values / (1.0 + jnp.exp(-values))


def embed_times(stamps, features):
    half_count = features // 2
    frequency = jnp.exp(-math.log(10000.0) * jnp.arange(half_count, dtype=jnp.float32) / half_count)
    angles = stamps[:, None] * frequency[None, :]
    return jnp.concatenate([jnp.cos(angles), jnp.sin(angles)], axis=1)

def normalize(values):
    centre = values - jnp.mean(values, axis=-1, keepdims=True)
    inverse = lax.rsqrt(jnp.mean(centre * centre, axis=-1, keepdims=True) + 1e-06)
    return (centre * inverse, inverse)


def norm_back(normed, inverse, upstream):
    return inverse * (
        upstream
        - jnp.mean(upstream, axis=-1, keepdims=True)
        - normed * jnp.mean(upstream * normed, axis=-1, keepdims=True)
    )


def dot_nn(a, b):
    return lax.dot_general(a, b, (((1,), (0,)), ((), ())), preferred_element_type=jnp.float32)


def dot_nt(a, b):
    return lax.dot_general(a, b, (((1,), (1,)), ((), ())), preferred_element_type=jnp.float32)


def dot_tn(a, b):
    return lax.dot_general(a, b, (((0,), (0,)), ((), ())), preferred_element_type=jnp.float32)


def key_mask(s_ref, groups, tokens, cols):
    block = tokens // groups // 4
    token = lax.broadcasted_iota(jnp.int32, (tokens, 128), 0)
    piece, within = (token // block, token % block)
    strip = ((s_ref[2] ^ (piece % 4)) * groups) + (s_ref[3] ^ (piece // 4))
    row = strip * (block // (cols // 2)) + within // (cols // 2)
    half = s_ref[0] // 2
    return jnp.where((row < half) & (within % (cols // 2) < half), 0.0, -1e30)


def store_sum(ref, part):
    @pl.when(pl.program_id(0) == 0)
    def _():
        ref[...] = part

    @pl.when(pl.program_id(0) > 0)
    def _():
        ref[...] += part


def attend_kernel(chunk, scale, groups, cols, s_ref, *refs):
    pieces, w_ref, t_ref = (refs[: 4 * groups], refs[4 * groups], refs[4 * groups + 1])
    o_refs = refs[4 * groups + 2 : 5 * groups + 2]
    l_ref, u_sc, b_sc, q_sc, k_sc, v_sc, o_sc, l_sc = refs[5 * groups + 2 :]
    tokens = u_sc.shape[0]

    @pl.when(pl.program_id(0) == 0)
    def _():
        size = pieces[0].shape[0]
        for i, piece in enumerate(pieces):
            u_sc[i * size : (i + 1) * size, :] = piece[...]
        b_sc[...] = key_mask(s_ref, groups, tokens, cols)

    u = u_sc[...]
    for part in range(3):
        t_ref[part] = dot_nn(u, w_ref[part]).astype(jnp.bfloat16)
    q, k, v = (t_ref[0].astype(jnp.float32), t_ref[1].astype(jnp.float32), t_ref[2].astype(jnp.float32))
    lane = lax.broadcasted_iota(jnp.int32, (tokens, 128), 1)
    bias = b_sc[...]
    for head in range(2):
        here = (lane < 64) if head == 0 else (lane >= 64)
        spare = lane == (64 if head == 0 else 0)
        q_sc[head] = jnp.where(here, q * scale, jnp.where(spare, 1.0, 0.0)).astype(jnp.bfloat16)
        k_sc[head] = jnp.where(here, k, jnp.where(spare, bias, 0.0)).astype(jnp.bfloat16)
        v_sc[head] = jnp.where(here, v, 0.0).astype(jnp.bfloat16)

    def body(i, carry):
        at = pl.ds(pl.multiple_of(i * chunk, chunk), chunk)
        outs, logs = ([], [])
        for head in range(2):
            s = dot_nt(q_sc[head, at, :], k_sc[head])
            top = jnp.max(s, axis=1, keepdims=True)
            p = jnp.exp(s - top)
            total = jnp.sum(p, axis=1, keepdims=True)
            outs.append(dot_nn(p.astype(jnp.bfloat16), v_sc[head]) * (1.0 / total))
            logs.append(top + jnp.log(total))
        o_sc[at, :] = (outs[0] + outs[1]).astype(jnp.bfloat16)
        l_sc[at, :] = jnp.where(
            lax.broadcasted_iota(jnp.int32, (chunk, 128), 1) < 64, logs[0], logs[1]
        )
        return carry

    lax.fori_loop(0, tokens // chunk, body, 0, unroll=True)
    size = tokens // groups
    for i, o_ref in enumerate(o_refs):
        o_ref[...] = o_sc[i * size : (i + 1) * size, :]
    logs = l_sc[...].T
    l_ref[...] = jnp.concatenate(
        [logs[0:1], logs[64:65], jnp.zeros((6, tokens), jnp.float32)], axis=0
    )[None]


def attend(scalars, pieces, w, score_scale, cols):
    groups = len(pieces) // 4
    features, width = w.shape[1:]
    tokens = 4 * groups * pieces[0].shape[0]
    chunk = min(512, tokens)
    piece_spec = pl.BlockSpec(pieces[0].shape, lambda j, s: (0, 0))
    return pl.pallas_call(
        functools.partial(attend_kernel, chunk, score_scale, groups, cols),
        grid_spec=pltpu.PrefetchScalarGridSpec(
            num_scalar_prefetch=1,
            grid=(width // 128,),
            in_specs=[piece_spec] * len(pieces)
            + [pl.BlockSpec((3, features, 128), lambda j, s: (0, 0, j))],
            out_specs=[pl.BlockSpec((3, tokens, 128), lambda j, s: (0, 0, j))]
            + [pl.BlockSpec((tokens // groups, 128), lambda j, s: (0, j))] * groups
            + [pl.BlockSpec((1, 8, tokens), lambda j, s: (j, 0, 0))],
            scratch_shapes=[
                pltpu.VMEM((tokens, features), jnp.bfloat16),
                pltpu.VMEM((tokens, 128), jnp.float32),
            ]
            + [pltpu.VMEM((2, tokens, 128), jnp.bfloat16)] * 3
            + [pltpu.VMEM((tokens, 128), jnp.bfloat16), pltpu.VMEM((tokens, 128), jnp.float32)],
        ),
        out_shape=[jax.ShapeDtypeStruct((3, tokens, width), jnp.bfloat16)]
        + [jax.ShapeDtypeStruct((tokens // groups, width), jnp.bfloat16)] * groups
        + [jax.ShapeDtypeStruct((width // 128, 8, tokens), jnp.float32)],
        cost_estimate=pl.CostEstimate(
            flops=2 * tokens * width * (3 * features + 8 * tokens),
            transcendentals=tokens * tokens * width // 64,
            bytes_accessed=2 * tokens * (features + 4 * width) + 6 * features * width,
        ),
        name="attend_forward",
    )(scalars, *pieces, w)


def attend_back_kernel(chunk, scale, groups, cols, first, s_ref, *refs):
    count = 4 * groups
    pieces, do_pieces, o_refs = (refs[:count], refs[count : 2 * count], refs[2 * count : 2 * count + groups])
    w_ref, t_ref, l_ref = refs[2 * count + groups : 2 * count + groups + 3]
    rest = refs[2 * count + groups + 3 :]
    if not first:
        prev_ref, rest = (rest[0], rest[1:])
    du_refs, g_ref = (rest[:groups], rest[groups])
    u_sc, b_sc, o_sc, din_sc, q_sc, k_sc, do_sc, dq_sc, dt_sc, d_sc = rest[groups + 1 :]
    tokens = u_sc.shape[0]
    size = pieces[0].shape[0]

    @pl.when(pl.program_id(0) == 0)
    def _():
        for i, piece in enumerate(pieces):
            u_sc[i * size : (i + 1) * size, :] = piece[...]
        b_sc[...] = key_mask(s_ref, groups, tokens, cols)

    for i, piece in enumerate(do_pieces):
        din_sc[i * size : (i + 1) * size, :] = piece[...]
    for i, piece in enumerate(o_refs):
        o_sc[i * 4 * size : (i + 1) * 4 * size, :] = piece[...]
    q, k, do = (t_ref[0].astype(jnp.float32), t_ref[1].astype(jnp.float32), din_sc[...])
    lane = lax.broadcasted_iota(jnp.int32, (tokens, 128), 1)
    bias = b_sc[...]
    do = do.astype(jnp.float32)
    inner = (do * o_sc[...].astype(jnp.float32)).T
    for head in range(2):
        here = (lane < 64) if head == 0 else (lane >= 64)
        spare = lane == (64 if head == 0 else 0)
        q_sc[head] = jnp.where(here, q * scale, jnp.where(spare, 1.0, 0.0)).astype(jnp.bfloat16)
        k_sc[head] = jnp.where(here, k, jnp.where(spare, bias, 0.0)).astype(jnp.bfloat16)
        do_sc[head] = jnp.where(here, do, 0.0).astype(jnp.bfloat16)
        d_sc[head : head + 1, :] = jnp.sum(
            inner[64 * head : 64 * head + 64], axis=0, keepdims=True
        )
    dq_sc[...] = jnp.zeros_like(dq_sc)

    def body(i, carry):
        at = pl.ds(pl.multiple_of(i * chunk, chunk), chunk)
        lanes = lax.broadcasted_iota(jnp.int32, (chunk, 128), 1)
        d_k, d_v, d_q = ([], [], [])
        for head in range(2):
            here = (lanes < 64) if head == 0 else (lanes >= 64)
            s = dot_nt(k_sc[head, at, :], q_sc[head])
            p = jnp.exp(s - l_ref[0, head : head + 1, :])
            d_p = dot_nt(t_ref[2, at, :], do_sc[head])
            d_s = (p * (d_p - d_sc[head : head + 1, :])).astype(jnp.bfloat16)
            d_v.append(dot_nn(p.astype(jnp.bfloat16), do_sc[head]))
            d_k.append(dot_nn(d_s, q_sc[head]))
            keys = jnp.where(here, t_ref[1, at, :].astype(jnp.float32), 0.0).astype(jnp.bfloat16)
            d_q.append(dot_tn(d_s, keys))
        dq_sc[...] += d_q[0] + d_q[1]
        dt_sc[at, 128:256] = jnp.where(lanes < 64, d_k[0], d_k[1]).astype(jnp.bfloat16)
        dt_sc[at, 256:384] = (d_v[0] + d_v[1]).astype(jnp.bfloat16)
        return carry

    lax.fori_loop(0, tokens // chunk, body, 0, unroll=True)
    dt_sc[:, 0:128] = (dq_sc[...] * scale).astype(jnp.bfloat16)
    for i, du_ref in enumerate(du_refs):
        at = slice(i * 4 * size, (i + 1) * 4 * size)
        part = dot_nt(dt_sc[at, 0:128], w_ref[0])
        part = part + dot_nt(dt_sc[at, 128:256], w_ref[1])
        part = part + dot_nt(dt_sc[at, 256:384], w_ref[2])
        store_sum(du_ref, part)
    grad = dot_tn(u_sc[...], dt_sc[...])
    for at in range(3):
        piece = grad[:, 128 * at : 128 * at + 128]
        if not first:
            piece = piece + prev_ref[at]
        g_ref[at] = piece.astype(g_ref.dtype)


def attend_back(scalars, pieces, d_pieces, outs, w, t, logs, score_scale, cols, prev, grad_type):
    groups = len(outs)
    features, width = w.shape[1:]
    tokens = t.shape[1]
    chunk = min(256, tokens)
    size = pieces[0].shape[0]
    blocks = width // 128
    weight_spec = pl.BlockSpec((3, features, 128), lambda j, s: (0, 0, j))
    offset = 0 if d_pieces[0].shape[1] == width else blocks
    args = list(pieces) + list(d_pieces) + list(outs) + [w, t, logs]
    args += [] if prev is None else [prev]
    return pl.pallas_call(
        functools.partial(attend_back_kernel, chunk, score_scale, groups, cols, prev is None),
        grid_spec=pltpu.PrefetchScalarGridSpec(
            num_scalar_prefetch=1,
            grid=(blocks,),
            in_specs=[pl.BlockSpec((size, features), lambda j, s: (0, 0))] * len(pieces)
            + [pl.BlockSpec((size, 128), lambda j, s: (0, s[3] * offset + j))] * len(d_pieces)
            + [pl.BlockSpec((4 * size, 128), lambda j, s: (0, j))] * groups
            + [
                weight_spec,
                pl.BlockSpec((3, tokens, 128), lambda j, s: (0, 0, j)),
                pl.BlockSpec((1, 8, tokens), lambda j, s: (j, 0, 0)),
            ]
            + ([] if prev is None else [weight_spec]),
            out_specs=[pl.BlockSpec((4 * size, features), lambda j, s: (0, 0))] * groups
            + [weight_spec],
            scratch_shapes=[
                pltpu.VMEM((tokens, features), jnp.bfloat16),
                pltpu.VMEM((tokens, 128), jnp.float32),
                pltpu.VMEM((tokens, 128), jnp.bfloat16),
                pltpu.VMEM((tokens, 128), jnp.bfloat16),
            ]
            + [pltpu.VMEM((2, tokens, 128), jnp.bfloat16)] * 3
            + [
                pltpu.VMEM((tokens, 128), jnp.float32),
                pltpu.VMEM((tokens, 384), jnp.bfloat16),
                pltpu.VMEM((8, tokens), jnp.float32),
            ],
        ),
        out_shape=[jax.ShapeDtypeStruct((4 * size, features), jnp.float32)] * groups
        + [jax.ShapeDtypeStruct(w.shape, grad_type)],
        cost_estimate=pl.CostEstimate(
            flops=2 * tokens * width * (6 * features + 20 * tokens),
            transcendentals=tokens * tokens * width // 64,
            bytes_accessed=6 * tokens * features + 10 * tokens * width + 18 * features * width,
        ),
        name="attend_backward",
    )(scalars, *args)


def shift_cols(x, by, col):
    size = x.shape[0]
    rolled = pltpu.roll(x, (-by) % size, 0)
    return jnp.where(col == (size - 1 if by > 0 else 0), 0.0, rolled)


def wide_taps(c_ref, lanes, cols):
    return [
        jnp.broadcast_to(c_ref[k : k + 1, lanes].astype(jnp.float32), (cols, 128)) for k in range(9)
    ]


def sublane_sum(x):
    return jnp.sum(x.reshape(x.shape[0] // 8, 8, 128), axis=0)


def modulate(x, m_ref, shift_at, col, row, side):
    normed, _ = normalize(x.astype(jnp.float32))
    value = normed * (1.0 + m_ref[shift_at + 1 : shift_at + 2, :]) + m_ref[shift_at : shift_at + 1, :]
    live = (col < side) & (row >= 0) & (row < side)
    return jnp.where(live, value, 0.0).astype(jnp.bfloat16)


def modulated_rows(a_sc, s_ref, x_ref, top_ref, end_ref, m_ref):
    rows, cols, features = x_ref.shape
    side, row_zero = (s_ref[0], s_ref[1])
    col = lax.broadcasted_iota(jnp.int32, (cols, features), 0)
    a_sc[0] = modulate(top_ref[...], m_ref, 0, col, row_zero - 1, side)
    a_sc[rows + 1] = modulate(end_ref[...], m_ref, 0, col, row_zero + rows, side)

    def body(r, carry):
        a_sc[r + 1] = modulate(x_ref[r], m_ref, 0, col, row_zero + r, side)
        return carry

    lax.fori_loop(0, rows, body, 0)


def to_pieces(s_ref, canvas, u_sc, piece_refs):
    blocks, rows, cols, _ = canvas.shape
    half = cols // 2

    def body(r, carry):
        at = pl.ds(pl.multiple_of(r * half, half), half)
        for m in range(4):
            for b in range(blocks):
                part = canvas[b, 2 * r + m // 2, pl.ds(m % 2, half, stride=2), :]
                u_sc[m, at, 128 * b : 128 * b + 128] = part.astype(jnp.bfloat16)
        return carry

    lax.fori_loop(0, rows // 2, body, 0)
    for k, piece_ref in enumerate(piece_refs):
        piece_ref[...] = u_sc[s_ref[2] ^ k]


def from_pieces(s_ref, piece_refs, u_sc, canvas, row_offset):
    half = canvas.shape[2] // 2
    rows = piece_refs[0].shape[0] // half * 2
    for k, piece_ref in enumerate(piece_refs):
        u_sc[k] = piece_ref[...]

    def body(r, carry):
        at = pl.ds(pl.multiple_of(r * half, half), half)
        for m in range(4):
            for b in range(canvas.shape[0]):
                part = u_sc[s_ref[2] ^ m, at, 128 * b : 128 * b + 128].astype(jnp.float32)
                canvas[b, row_offset + 2 * r + m // 2, pl.ds(m % 2, half, stride=2), :] = part
        return carry

    lax.fori_loop(0, rows // 2, body, 0)


def before_kernel(s_ref, x_ref, top_ref, end_ref, m_ref, c_ref, *refs):
    piece_refs, (a_sc, t_sc, u_sc) = (refs[:4], refs[4:])
    rows, cols, features = x_ref.shape
    modulated_rows(a_sc, s_ref, x_ref, top_ref, end_ref, m_ref)
    col = lax.broadcasted_iota(jnp.int32, (cols, 128), 0)
    for first in range(0, features, 128):
        lanes = slice(first, first + 128)
        taps = wide_taps(c_ref, lanes, cols)

        def body(r, carry):
            x = [a_sc[r + i, :, lanes].astype(jnp.float32) for i in range(3)]
            a = [x[0] * taps[j] + x[1] * taps[3 + j] + x[2] * taps[6 + j] for j in range(3)]
            t_sc[first // 128, r] = a[1] + shift_cols(a[0], -1, col) + shift_cols(a[2], 1, col)
            return carry

        lax.fori_loop(0, rows, body, 0)
    to_pieces(s_ref, t_sc, u_sc, piece_refs)


def canvas_specs(latents, at):
    rows, cols, features = latents.shape[2:]
    return [
        pl.BlockSpec((None, None, rows, cols, features), lambda j, s: (at, 0, 0, 0, 0)),
        pl.BlockSpec((None, cols, features), lambda j, s: (at, 0, 0)),
        pl.BlockSpec((None, cols, features), lambda j, s: (at, 0, 0)),
        pl.BlockSpec((None, 6, features), lambda j, s: (at, 0, 0)),
    ]


def whole_spec(shape):
    return pl.BlockSpec(shape, lambda j, s: (0,) * len(shape))


def before_attention(at, scalars, latents, top, end, mods, taps):
    rows, cols, features = latents.shape[2:]
    piece = (rows * cols // 4, features)
    return pl.pallas_call(
        before_kernel,
        grid_spec=pltpu.PrefetchScalarGridSpec(
            num_scalar_prefetch=1,
            grid=(1,),
            in_specs=canvas_specs(latents, at) + [whole_spec(taps.shape)],
            out_specs=[whole_spec(piece)] * 4,
            scratch_shapes=[
                pltpu.VMEM((rows + 2, cols, features), jnp.bfloat16),
                pltpu.VMEM((features // 128, rows, cols, 128), jnp.float32),
                pltpu.VMEM((4,) + piece, jnp.bfloat16),
            ],
        ),
        out_shape=[jax.ShapeDtypeStruct(piece, jnp.bfloat16)] * 4,
        cost_estimate=pl.CostEstimate(
            flops=40 * rows * cols * features,
            transcendentals=0,
            bytes_accessed=4 * rows * cols * features,
        ),
        name="before_attention",
    )(scalars, latents, top, end, mods, taps)


def join_kernel(s_ref, mine_ref, other_ref, *piece_refs):
    size, width = (piece_refs[0].shape[0], mine_ref.shape[1])

    def write(low_ref, high_ref):
        for k, piece_ref in enumerate(piece_refs):
            at = slice(k * size, (k + 1) * size)
            piece_ref[:, :width] = low_ref[at, :]
            piece_ref[:, width:] = high_ref[at, :]

    @pl.when(s_ref[3] == 0)
    def _():
        write(mine_ref, other_ref)

    @pl.when(s_ref[3] == 1)
    def _():
        write(other_ref, mine_ref)


def join_groups(scalars, parts, width):
    groups = len(parts)
    size = parts[0].shape[0] // 4
    if groups != 2 or parts[0].shape[1] != width:
        whole = place_blocks([part[:, :width] for part in parts], scalars[3])
        whole = whole.transpose(1, 0, 2).reshape(4, size, groups * width)
        return [whole[k] for k in range(4)]
    piece = (size, groups * width)
    return pl.pallas_call(
        join_kernel,
        grid_spec=pltpu.PrefetchScalarGridSpec(
            num_scalar_prefetch=1,
            grid=(1,),
            in_specs=[whole_spec(part.shape) for part in parts],
            out_specs=[whole_spec(piece)] * 4,
        ),
        out_shape=[jax.ShapeDtypeStruct(piece, parts[0].dtype)] * 4,
        name="join_groups",
    )(scalars, *parts)


def sum_kernel(count, *refs):
    size = refs[count].shape[0]
    for k, piece_ref in enumerate(refs[count:]):
        at = slice(k * size, (k + 1) * size)
        total = refs[0][at, :]
        for part in refs[1:count]:
            total = total + part[at, :]
        piece_ref[...] = total.astype(piece_ref.dtype)


def sum_groups(parts):
    size, features = (parts[0].shape[0] // 4, parts[0].shape[1])
    return pl.pallas_call(
        functools.partial(sum_kernel, len(parts)),
        out_shape=[jax.ShapeDtypeStruct((size, features), jnp.bfloat16)] * 4,
        name="sum_groups",
    )(*parts)


def edge_kernel(half, s_ref, *refs):
    pieces, first_ref, last_ref, u_sc = (refs[:4], refs[4], refs[5], refs[6])
    size = pieces[0].shape[0]
    for k, piece in enumerate(pieces):
        u_sc[k] = piece[...]
    for j in range(2):
        first_ref[j * half : (j + 1) * half, :] = u_sc[s_ref[2] ^ j, :half, :]
        last_ref[j * half : (j + 1) * half, :] = u_sc[s_ref[2] ^ (2 + j), size - half :, :]


def edge_rows(scalars, pieces, cols):
    size, features = pieces[0].shape
    row = (cols, features)
    return pl.pallas_call(
        functools.partial(edge_kernel, cols // 2),
        grid_spec=pltpu.PrefetchScalarGridSpec(
            num_scalar_prefetch=1,
            grid=(1,),
            in_specs=[whole_spec((size, features))] * 4,
            out_specs=[whole_spec(row)] * 2,
            scratch_shapes=[pltpu.VMEM((4, size, features), jnp.bfloat16)],
        ),
        out_shape=[jax.ShapeDtypeStruct(row, jnp.bfloat16)] * 2,
        name="edge_rows",
    )(scalars, *pieces)


def expand_kernel(s_ref, p0, p1, p2, p3, x_ref, m_ref, wp_ref, w_ref, b_ref, *refs):
    oc_ref, at_ref, x1_ref, a2_ref, f_ref, u_sc, t_sc = refs
    rows, cols, features = x_ref.shape
    side, row_zero = (s_ref[0], s_ref[1])

    @pl.when(pl.program_id(0) == 0)
    def _():
        from_pieces(s_ref, (p0, p1, p2, p3), u_sc, t_sc, 0)
        for b in range(features // 128):
            part = t_sc[b].reshape(rows * cols, 128)
            oc_ref[:, 128 * b : 128 * b + 128] = part.astype(jnp.bfloat16)
        at_ref[...] = dot_nn(oc_ref[...], wp_ref[...])

        def body(r, carry):
            here = pl.ds(pl.multiple_of(r * cols, cols), cols)
            x1 = x_ref[r].astype(jnp.float32) + m_ref[2:3, :] * at_ref[here, :]
            x1_ref[here, :] = x1
            normed, _ = normalize(x1)
            a2 = normed * (1.0 + m_ref[4:5, :]) + m_ref[3:4, :]
            a2_ref[here, :] = a2.astype(jnp.bfloat16)
            return carry

        lax.fori_loop(0, rows, body, 0)

    block = f_ref.shape[2]
    f = (dot_nn(a2_ref[...], w_ref[...]) + b_ref[...].astype(jnp.float32)).reshape(rows, cols, block)
    col = lax.broadcasted_iota(jnp.int32, (cols, block), 0)
    for r in range(rows):
        live = (col < side) & (row_zero + r < side)
        f_ref[r] = jnp.where(live, f[r], 0.0).astype(jnp.bfloat16)


def expand(at, scalars, pieces, latents, mods, w_proj, w_fc1, bias):
    rows, cols, features = latents.shape[2:]
    hidden = w_fc1.shape[1]
    tokens, block = (rows * cols, 512)
    flat = (tokens, features)
    specs = canvas_specs(latents, at)
    return pl.pallas_call(
        expand_kernel,
        grid_spec=pltpu.PrefetchScalarGridSpec(
            num_scalar_prefetch=1,
            grid=(hidden // block,),
            in_specs=[whole_spec(pieces[0].shape)] * 4
            + [
                specs[0],
                specs[3],
                whole_spec(w_proj.shape),
                pl.BlockSpec((features, block), lambda j, s: (0, j)),
                pl.BlockSpec((1, block), lambda j, s: (0, j)),
            ],
            out_specs=[whole_spec(flat)] * 4
            + [pl.BlockSpec((rows, cols, block), lambda j, s: (0, 0, j))],
            scratch_shapes=[
                pltpu.VMEM((4,) + pieces[0].shape, jnp.bfloat16),
                pltpu.VMEM((features // 128, rows, cols, 128), jnp.float32),
            ],
        ),
        out_shape=[
            jax.ShapeDtypeStruct(flat, jnp.bfloat16),
            jax.ShapeDtypeStruct(flat, jnp.float32),
            jax.ShapeDtypeStruct(flat, jnp.float32),
            jax.ShapeDtypeStruct(flat, jnp.bfloat16),
            jax.ShapeDtypeStruct((rows, cols, hidden), jnp.bfloat16),
        ],
        cost_estimate=pl.CostEstimate(
            flops=2 * tokens * features * (features + hidden),
            transcendentals=0,
            bytes_accessed=2 * hidden * (tokens + features) + 16 * tokens * features,
        ),
        name="expand",
    )(scalars, *pieces, latents, mods, w_proj, w_fc1, bias)


def middle_kernel(first, s_ref, f_ref, top_ref, end_ref, c_ref, w_ref, ct_ref, x1_ref, m_ref, *rest):
    if first:
        mixed_ref, dg_ref, dz_ref, g_ref, gc_ref = rest[:5]
    else:
        gp_ref, gcp_ref = rest[:2]
        mixed_ref, dg_ref, dz_ref, g_ref, gc_ref = rest[3:8]
    out_sc, d_sc, x_sc, t_sc, gz_sc, acc_sc = rest[-6:]
    rows, cols, block = f_ref.shape
    features = out_sc.shape[1]
    side, row_zero = (s_ref[0], s_ref[1])

    def upstream(r):
        col = lax.broadcasted_iota(jnp.int32, (cols, features), 0)
        live = (col < side) & (row_zero + r < side)
        return jnp.where(live, ct_ref[r].astype(jnp.float32), 0.0), live

    @pl.when(pl.program_id(0) == 0)
    def _():
        def body(r, carry):
            here = pl.ds(pl.multiple_of(r * cols, cols), cols)
            d_sc[here, :] = (upstream(r)[0] * m_ref[5:6, :]).astype(jnp.bfloat16)
            return carry

        lax.fori_loop(0, rows, body, 0)

    d = d_sc[...]
    t_sc[...] = dot_nt(d, w_ref[...]).reshape(rows, cols, block)
    x_sc[0:1] = top_ref[...]
    x_sc[1 : rows + 1] = f_ref[...]
    x_sc[rows + 1 : rows + 2] = end_ref[...]
    acc_sc[...] = jnp.zeros_like(acc_sc)
    col = lax.broadcasted_iota(jnp.int32, (cols, 128), 0)
    for at in range(block // 128):
        lanes = slice(128 * at, 128 * at + 128)
        taps = wide_taps(c_ref, lanes, cols)

        def body(r, carry):
            x = [x_sc[r + i, :, lanes].astype(jnp.float32) for i in range(3)]
            a = [x[0] * taps[j] + x[1] * taps[3 + j] + x[2] * taps[6 + j] for j in range(3)]
            z = a[1] + shift_cols(a[0], -1, col) + shift_cols(a[2], 1, col)
            half = 0.5 * (1.0 + lax.erf(z * root_half))
            gz_sc[r, :, lanes] = (z * half).astype(jnp.bfloat16)
            slope = half + z * jnp.exp(-0.5 * z * z) * inverse_root_tau
            d_z = (t_sc[r, :, lanes] * slope).astype(jnp.bfloat16)
            dz_ref[r, :, lanes] = d_z
            d_z = d_z.astype(jnp.float32)
            moved = [shift_cols(d_z, 1, col), d_z, shift_cols(d_z, -1, col)]
            for i in range(3):
                for j in range(3):
                    acc_sc[3 * i + j, :, lanes] += sublane_sum(x[i] * moved[j])
            return carry

        lax.fori_loop(0, rows, body, 0, unroll=2)
    gz = gz_sc[...].reshape(rows * cols, block)
    store_sum(out_sc, dot_nn(gz, w_ref[...]))
    grad = dot_tn(gz, d)
    taps_grad = jnp.concatenate(
        [jnp.sum(acc_sc[k], axis=0, keepdims=True) for k in range(9)], axis=0
    )
    if not first:
        grad = grad + gp_ref[...]
        taps_grad = taps_grad + gcp_ref[...]
    g_ref[...] = grad.astype(g_ref.dtype)
    gc_ref[...] = taps_grad

    @pl.when(pl.program_id(0) == pl.num_programs(0) - 1)
    def _():
        def body(r, total):
            here = pl.ds(pl.multiple_of(r * cols, cols), cols)
            value, live = upstream(r)
            out = out_sc[here, :]
            mixed = x1_ref[here, :] + m_ref[5:6, :] * out
            mixed_ref[r] = jnp.where(live, mixed, 0.0).astype(jnp.bfloat16)
            return total + sublane_sum(value * out)

        total = lax.fori_loop(0, rows, body, jnp.zeros((8, features), jnp.float32))
        dg_ref[...] = jnp.sum(total, axis=0, keepdims=True)


def sublane_sum(x):
    return jnp.sum(x.reshape(x.shape[0] // 8, 8, x.shape[1]), axis=0)


def ffn_middle(at, scalars, f, halo, taps, w, cotangent, x1, mods, prev, grad_type):
    rows, cols, hidden = f.shape
    features = w.shape[1]
    block = 512
    wide = lambda j, s: (0, 0, j)
    row_spec = pl.BlockSpec((1, cols, block), wide)
    weight_spec = pl.BlockSpec((block, features), lambda j, s: (j, 0))
    tap_spec = pl.BlockSpec((9, block), lambda j, s: (0, j))
    canvas_spec = pl.BlockSpec((rows, cols, block), wide)
    specs = canvas_specs(cotangent, at)
    args = [scalars, f, halo[0], halo[1], taps, w, cotangent, x1, mods]
    args += [] if prev is None else list(prev)
    return pl.pallas_call(
        functools.partial(middle_kernel, prev is None),
        grid_spec=pltpu.PrefetchScalarGridSpec(
            num_scalar_prefetch=1,
            grid=(hidden // block,),
            in_specs=[canvas_spec, row_spec, row_spec, tap_spec, weight_spec]
            + [specs[0], whole_spec(x1.shape), specs[3]]
            + ([] if prev is None else [weight_spec, tap_spec, pl.BlockSpec(memory_space=pl.ANY)]),
            out_specs=[specs[0], whole_spec((1, features)), canvas_spec, weight_spec, tap_spec],
            scratch_shapes=[
                pltpu.VMEM((rows * cols, features), jnp.float32),
                pltpu.VMEM((rows * cols, features), jnp.bfloat16),
                pltpu.VMEM((rows + 2, cols, block), jnp.bfloat16),
                pltpu.VMEM((rows, cols, block), jnp.float32),
                pltpu.VMEM((rows, cols, block), jnp.bfloat16),
                pltpu.VMEM((9, 8, block), jnp.float32),
            ],
        ),
        out_shape=[
            jax.ShapeDtypeStruct(cotangent.shape, jnp.bfloat16),
            jax.ShapeDtypeStruct((1, features), jnp.float32),
            jax.ShapeDtypeStruct(f.shape, jnp.bfloat16),
            jax.ShapeDtypeStruct((hidden, features), grad_type),
            jax.ShapeDtypeStruct((9, hidden), jnp.float32),
        ],
        input_output_aliases={} if prev is None else {11: 0},
        cost_estimate=pl.CostEstimate(
            flops=2 * rows * cols * hidden * (6 * features),
            transcendentals=2 * rows * cols * hidden,
            bytes_accessed=hidden * (4 * rows * cols + 8 * features) + 8 * rows * cols * features,
        ),
        name="ffn_middle",
    )(*args)


def ffn_back_kernel(first, s_ref, z_ref, top_ref, end_ref, c_ref, w_ref, a_ref, *rest):
    ct_ref, x1_ref, at_ref, oc_ref, wp_ref, m_ref = rest[:6]
    rest = rest[6:]
    if not first:
        gp_ref, gbp_ref, gpp_ref = rest[:3]
        rest = rest[3:]
    piece_refs = rest[:4]
    dx_ref, dm_ref, g_ref, gb_ref, gp_out = rest[4:9]
    da_sc, x_sc, df_sc, acc_sc, t_sc, dat_sc, u_sc = rest[9:]
    rows, cols, block = z_ref.shape
    features = da_sc.shape[1]
    x_sc[0:1] = top_ref[...]
    x_sc[1 : rows + 1] = z_ref[...]
    x_sc[rows + 1 : rows + 2] = end_ref[...]
    acc_sc[...] = jnp.zeros_like(acc_sc)
    col = lax.broadcasted_iota(jnp.int32, (cols, 128), 0)
    side, row_zero = (s_ref[0], s_ref[1])
    for at in range(block // 128):
        lanes = slice(128 * at, 128 * at + 128)
        taps = wide_taps(c_ref, lanes, cols)

        def body(r, carry):
            x = [x_sc[r + i, :, lanes].astype(jnp.float32) for i in range(3)]
            b = [x[2] * taps[j] + x[1] * taps[3 + j] + x[0] * taps[6 + j] for j in range(3)]
            d_f = b[1] + shift_cols(b[0], 1, col) + shift_cols(b[2], -1, col)
            live = (col < side) & (row_zero + r < side)
            d_f = jnp.where(live, d_f, 0.0).astype(jnp.bfloat16)
            df_sc[r, :, lanes] = d_f
            acc_sc[:, lanes] += sublane_sum(d_f.astype(jnp.float32))
            return carry

        lax.fori_loop(0, rows, body, 0, unroll=2)
    d_f = df_sc[...].reshape(rows * cols, block)
    store_sum(da_sc, dot_nt(d_f, w_ref[...]))
    grad = dot_tn(a_ref[...], d_f)
    bias_grad = jnp.sum(acc_sc[...], axis=0, keepdims=True)
    if not first:
        grad = grad + gp_ref[...]
        bias_grad = bias_grad + gbp_ref[...]
    g_ref[...] = grad.astype(g_ref.dtype)
    gb_ref[...] = bias_grad

    @pl.when(pl.program_id(0) == pl.num_programs(0) - 1)
    def _():
        wide_col = lax.broadcasted_iota(jnp.int32, (cols, features), 0)

        def body(r, totals):
            here = pl.ds(pl.multiple_of(r * cols, cols), cols)
            d_a = da_sc[here, :]
            normed, inverse = normalize(x1_ref[here, :])
            live = (wide_col < side) & (row_zero + r < side)
            d_x = jnp.where(live, ct_ref[r].astype(jnp.float32), 0.0)
            d_x = d_x + norm_back(normed, inverse, d_a * (1.0 + m_ref[4:5, :]))
            dx_ref[here, :] = d_x
            dat_sc[here, :] = (d_x * m_ref[2:3, :]).astype(jnp.bfloat16)
            return (
                totals[0] + sublane_sum(d_x * at_ref[here, :]),
                totals[1] + sublane_sum(d_a),
                totals[2] + sublane_sum(d_a * normed),
            )

        zero = jnp.zeros((8, features), jnp.float32)
        totals = lax.fori_loop(0, rows, body, (zero, zero, zero))
        for i in range(3):
            dm_ref[i : i + 1, :] = jnp.sum(totals[i], axis=0, keepdims=True)
        proj = dot_tn(oc_ref[...], dat_sc[...])
        if not first:
            proj = proj + gpp_ref[...]
        gp_out[...] = proj.astype(gp_out.dtype)
        d_o = dot_nt(dat_sc[...], wp_ref[...])
        for b in range(features // 128):
            t_sc[b] = d_o[:, 128 * b : 128 * b + 128].reshape(rows, cols, 128)
        to_pieces(s_ref, t_sc, u_sc, piece_refs)


def ffn_back(
    at, scalars, d_z, halo, taps, w, a, cotangent, x1, attn, oc, w_proj, mods, prev, grad_type
):
    rows, cols, hidden = d_z.shape
    features = a.shape[1]
    block = 512
    wide = lambda j, s: (0, 0, j)
    row_spec = pl.BlockSpec((1, cols, block), wide)
    weight_spec = pl.BlockSpec((features, block), lambda j, s: (0, j))
    bias_spec = pl.BlockSpec((1, block), lambda j, s: (0, j))
    flat_spec = whole_spec((rows * cols, features))
    proj_spec = whole_spec(w_proj.shape)
    piece = (rows * cols // 4, features)
    specs = canvas_specs(cotangent, at)
    args = [scalars, d_z, halo[0], halo[1], taps, w, a, cotangent, x1, attn, oc, w_proj, mods]
    args += [] if prev is None else list(prev)
    return pl.pallas_call(
        functools.partial(ffn_back_kernel, prev is None),
        grid_spec=pltpu.PrefetchScalarGridSpec(
            num_scalar_prefetch=1,
            grid=(hidden // block,),
            in_specs=[
                pl.BlockSpec((rows, cols, block), wide),
                row_spec,
                row_spec,
                pl.BlockSpec((9, block), lambda j, s: (0, j)),
                weight_spec,
                flat_spec,
                specs[0],
                flat_spec,
                flat_spec,
                flat_spec,
                proj_spec,
                specs[3],
            ]
            + ([] if prev is None else [weight_spec, bias_spec, proj_spec]),
            out_specs=[whole_spec(piece)] * 4
            + [flat_spec, whole_spec((3, features)), weight_spec, bias_spec, proj_spec],
            scratch_shapes=[
                pltpu.VMEM((rows * cols, features), jnp.float32),
                pltpu.VMEM((rows + 2, cols, block), jnp.bfloat16),
                pltpu.VMEM((rows, cols, block), jnp.bfloat16),
                pltpu.VMEM((8, block), jnp.float32),
                pltpu.VMEM((features // 128, rows, cols, 128), jnp.float32),
                pltpu.VMEM((rows * cols, features), jnp.bfloat16),
                pltpu.VMEM((4,) + piece, jnp.bfloat16),
            ],
        ),
        out_shape=[jax.ShapeDtypeStruct(piece, jnp.bfloat16)] * 4
        + [
            jax.ShapeDtypeStruct((rows * cols, features), jnp.float32),
            jax.ShapeDtypeStruct((3, features), jnp.float32),
            jax.ShapeDtypeStruct(w.shape, grad_type),
            jax.ShapeDtypeStruct((1, hidden), jnp.float32),
            jax.ShapeDtypeStruct(w_proj.shape, grad_type),
        ],
        cost_estimate=pl.CostEstimate(
            flops=2 * rows * cols * features * (4 * hidden + 2 * features),
            transcendentals=0,
            bytes_accessed=hidden * (2 * rows * cols + 8 * features) + 20 * rows * cols * features,
        ),
        name="ffn_backward",
    )(*args)


def last_kernel(first, s_ref, p0, p1, p2, p3, dtop_ref, dend_ref, *rest):
    x_ref, top_ref, end_ref, m_ref, c_ref, dx_ref = rest[:6]
    rest = rest[6:]
    if not first:
        gcp_ref = rest[0]
        rest = rest[2:]
    dl_ref, dm_ref, gc_ref, a_sc, t_sc, d_sc, u_sc, acc_sc = rest
    rows, cols, features = x_ref.shape
    half = cols // 2
    side, row_zero = (s_ref[0], s_ref[1])
    modulated_rows(a_sc, s_ref, x_ref, top_ref, end_ref, m_ref)
    from_pieces(s_ref, (p0, p1, p2, p3), u_sc, t_sc, 1)
    for at, ref in ((0, dtop_ref), (rows + 1, dend_ref)):
        for j in range(2):
            for start in range(0, features, 128):
                lanes = slice(start, start + 128)
                part = ref[j * half : (j + 1) * half, lanes].astype(jnp.float32)
                t_sc[start // 128, at, pl.ds(j, half, stride=2), :] = part
    acc_sc[...] = jnp.zeros_like(acc_sc)
    col = lax.broadcasted_iota(jnp.int32, (cols, 128), 0)
    for start in range(0, features, 128):
        lanes = slice(start, start + 128)
        taps = wide_taps(c_ref, lanes, cols)

        def conv_body(r, carry):
            d = [t_sc[start // 128, r + i] for i in range(3)]
            b = [d[2] * taps[j] + d[1] * taps[3 + j] + d[0] * taps[6 + j] for j in range(3)]
            d_a = b[1] + shift_cols(b[0], 1, col) + shift_cols(b[2], -1, col)
            live = (col < side) & (row_zero + r < side)
            d_sc[r, :, lanes] = jnp.where(live, d_a, 0.0)
            moved = [shift_cols(d[1], 1, col), d[1], shift_cols(d[1], -1, col)]
            for i in range(3):
                x = a_sc[r + i, :, lanes].astype(jnp.float32)
                for j in range(3):
                    acc_sc[3 * i + j, :, lanes] += sublane_sum(x * moved[j])
            return carry

        lax.fori_loop(0, rows, conv_body, 0, unroll=2)
    taps_grad = jnp.concatenate(
        [jnp.sum(acc_sc[k], axis=0, keepdims=True) for k in range(9)], axis=0
    )
    if not first:
        taps_grad = taps_grad + gcp_ref[...]
    gc_ref[...] = taps_grad

    def body(r, totals):
        here = pl.ds(pl.multiple_of(r * cols, cols), cols)
        normed, inverse = normalize(x_ref[r].astype(jnp.float32))
        d_a = d_sc[r]
        dl_ref[r] = dx_ref[here, :] + norm_back(normed, inverse, d_a * (1.0 + m_ref[1:2, :]))
        return (totals[0] + sublane_sum(d_a), totals[1] + sublane_sum(d_a * normed))

    zero = jnp.zeros((8, features), jnp.float32)
    totals = lax.fori_loop(0, rows, body, (zero, zero))
    for i in range(2):
        dm_ref[i : i + 1, :] = jnp.sum(totals[i], axis=0, keepdims=True)


def last_stage(at, scalars, pieces, d_halo, latents, top, end, mods, taps, d_x, prev):
    rows, cols, features = latents.shape[2:]
    specs = canvas_specs(latents, at)
    args = [scalars, *pieces, *d_halo, latents, top, end, mods, taps, d_x]
    args += [] if prev is None else list(prev)
    return pl.pallas_call(
        functools.partial(last_kernel, prev is None),
        grid_spec=pltpu.PrefetchScalarGridSpec(
            num_scalar_prefetch=1,
            grid=(1,),
            in_specs=[whole_spec(pieces[0].shape)] * 4
            + [whole_spec((cols, features))] * 2
            + specs
            + [whole_spec(taps.shape), whole_spec(d_x.shape)]
            + ([] if prev is None else [whole_spec(taps.shape), pl.BlockSpec(memory_space=pl.ANY)]),
            out_specs=[specs[0], whole_spec((2, features)), whole_spec(taps.shape)],
            scratch_shapes=[
                pltpu.VMEM((rows + 2, cols, features), jnp.bfloat16),
                pltpu.VMEM((features // 128, rows + 2, cols, 128), jnp.float32),
                pltpu.VMEM((rows, cols, features), jnp.float32),
                pltpu.VMEM((4,) + pieces[0].shape, jnp.bfloat16),
                pltpu.VMEM((9, 8, features), jnp.float32),
            ],
        ),
        out_shape=[
            jax.ShapeDtypeStruct(latents.shape, jnp.float32),
            jax.ShapeDtypeStruct((2, features), jnp.float32),
            jax.ShapeDtypeStruct(taps.shape, jnp.float32),
        ],
        input_output_aliases={} if prev is None else {14: 0},
        cost_estimate=pl.CostEstimate(
            flops=80 * rows * cols * features,
            transcendentals=0,
            bytes_accessed=12 * rows * cols * features,
        ),
        name="last_stage",
    )(*args)


def shards(
    latents,
    timesteps,
    size_tags,
    w_ada,
    b_ada,
    conv_attn,
    w_qkv,
    w_proj,
    w_fc1,
    b_fc1,
    conv_ffn,
    w_fc2,
    cotangent,
):
    micro_count, _, row_count, side_count, features = latents.shape
    dp, strips = (lax.axis_size("dp"), lax.axis_size("strip"))
    dp_at, strip_at = (lax.axis_index("dp"), lax.axis_index("strip"))
    hidden = conv_ffn.shape[1] * dp
    groups = strips // 4
    group_at, map_at = (strip_at % groups, strip_at // groups)
    score_scale = (features // HEADS) ** (-0.5)
    width = features // groups

    stamps = timesteps[:, 0].astype(jnp.float32)
    all_stamps = [stamps] + [permute_xor(stamps, "dp", k) for k in range(1, dp)]
    conds = [silu_of(embed_times(each, features)) for each in all_stamps]
    ada_rows = features // dp
    ada_wide = w_ada.astype(jnp.float32)
    partial_mods = jnp.dot(
        lax.dynamic_slice_in_dim(jnp.concatenate(conds), dp_at * ada_rows, ada_rows, 1),
        ada_wide,
        precision=lax.Precision.HIGHEST,
    )
    bias_here = lax.dynamic_update_slice_in_dim(
        jnp.zeros((6 * features,), jnp.float32),
        b_ada.astype(jnp.float32),
        dp_at * b_ada.shape[0],
        0,
    )
    partial_mods = (partial_mods + bias_here[None, :]).reshape(dp, micro_count, 6 * features)
    modulation = partial_mods[0]
    for k in range(1, dp):
        modulation = modulation + permute_xor(partial_mods[k], "dp", k)

    small = jnp.concatenate([conv_attn.reshape(-1), conv_ffn.reshape(-1), b_fc1])
    small = gather_small(small)
    n_one, n_two = (conv_attn.size, conv_attn.size + conv_ffn.size)
    conv_one = small[:, :n_one].reshape(dp, 9, -1).transpose(1, 0, 2).reshape(9, features)
    conv_two = small[:, n_one:n_two].reshape(dp, 9, -1).transpose(1, 0, 2).reshape(9, hidden)
    fc1_bias = small[:, n_two:].reshape(1, hidden)
    qkv_pieces = fetch_group(w_qkv, groups)
    proj_pieces = fetch_rows(w_proj)
    fc1_pieces = fetch_rows(w_fc1)
    fc2_pieces = fetch_rows(w_fc2)
    qkv_group = gather_group(qkv_pieces)

    top, end = halo_rows(jnp.moveaxis(latents[:, 0], 1, 0))
    top, end = (top[0], end[0])
    mods = modulation.reshape(micro_count, 6, features)
    micros = range(micro_count)
    places = jnp.stack([strip_at * row_count, map_at, group_at]).astype(jnp.int32)
    scalars = [
        jnp.concatenate(
            [jnp.where(size_tags[at] == 1, side_count, side_count // 2).astype(jnp.int32), places]
        )
        for at in micros
    ]
    kept = [{} for _ in micros]

    for at in micros:
        pieces = before_attention(at, scalars[at], latents, top, end, mods, conv_one)
        kept[at]["u"] = group_exchange(map_exchange(pieces, groups), groups)

    for at in micros:
        keep = kept[at]
        done = attend(scalars[at], keep["u"], qkv_group, score_scale, side_count)
        keep["t"], keep["o"], keep["logs"] = (done[0], done[1 : 1 + groups], done[-1])
        parts = [keep["o"][0]] + [
            permute_xor(keep["o"][k], "strip", k) for k in range(1, groups)
        ]
        keep["o_pieces"] = map_exchange(join_groups(scalars[at], parts, width), groups)

    ready = kept[0]["logs"]
    proj_full = gather_rows(w_proj, after(proj_pieces, ready))
    fc1_full = gather_rows(w_fc1, after(fc1_pieces, ready))
    for at in micros:
        keep = kept[at]
        keep["oc"], keep["attn"], keep["x1"], keep["a2"], keep["f"] = expand(
            at, scalars[at], keep["o_pieces"], latents, mods, proj_full, fc1_full, fc1_bias
        )
        keep["f_halo"] = halo_rows(keep["f"])

    fc2_full = gather_rows(w_fc2, after(fc2_pieces, ready))
    for at in micros:
        keep, grad_type = (kept[at], jnp.bfloat16 if at == micro_count - 1 else jnp.float32)
        prev = None if at == 0 else (term_fc2, term_conv_two, mixed)
        mixed, keep["d_gate2"], keep["d_z"], term_fc2, term_conv_two = ffn_middle(
            at,
            scalars[at],
            keep["f"],
            keep["f_halo"],
            conv_two,
            fc2_full,
            cotangent,
            keep["x1"],
            mods,
            prev,
            grad_type,
        )
        keep["z_halo"] = halo_rows(keep["d_z"])

    for at in micros:
        keep, grad_type = (kept[at], jnp.bfloat16 if at == micro_count - 1 else jnp.float32)
        prev = None if at == 0 else (term_fc1, term_fc1_bias, term_proj)
        done = ffn_back(
            at,
            scalars[at],
            keep["d_z"],
            keep["z_halo"],
            conv_two,
            fc1_full,
            keep["a2"],
            cotangent,
            keep["x1"],
            keep["attn"],
            keep["oc"],
            proj_full,
            mods,
            prev,
            grad_type,
        )
        keep["d_x"], keep["d_mods"], term_fc1, term_fc1_bias, term_proj = done[4:]
        pieces = map_exchange(done[:4], groups)
        if width % 128:
            pieces = group_exchange(pieces, groups)
            pieces = [
                jnp.pad(
                    lax.dynamic_slice_in_dim(piece, group_at * width, width, 1),
                    ((0, 0), (0, -width % 128)),
                )
                for piece in pieces
            ]
        else:
            pieces = group_exchange(pieces, groups)
        keep["d_o"] = pieces

    g_fc2 = scatter_rows(term_fc2)
    g_fc1 = scatter_rows(term_fc1)

    for at in micros:
        keep, grad_type = (kept[at], jnp.bfloat16 if at == micro_count - 1 else jnp.float32)
        done = attend_back(
            scalars[at],
            keep["u"],
            keep["d_o"],
            keep["o"],
            qkv_group,
            keep["t"],
            keep["logs"],
            score_scale,
            side_count,
            None if at == 0 else term_qkv,
            grad_type,
        )
        term_qkv = done[groups]
        parts = [done[0]] + [permute_xor(done[k], "strip", k) for k in range(1, groups)]
        keep["d_u"] = map_exchange(sum_groups(parts), groups)

    g_proj = scatter_rows(term_proj)

    mod_grads = []
    for at in micros:
        keep = kept[at]
        first_row, last_row = edge_rows(scalars[at], keep["d_u"], side_count)
        size = strips
        d_halo = (
            lax.ppermute(last_row, "strip", [(i, i + 1) for i in range(size - 1)]),
            lax.ppermute(first_row, "strip", [(i + 1, i) for i in range(size - 1)]),
        )
        prev = None if at == 0 else (term_conv_one, d_latents)
        d_latents, keep["d_mod1"], term_conv_one = last_stage(
            at,
            scalars[at],
            keep["d_u"],
            d_halo,
            latents,
            top,
            end,
            mods,
            conv_one,
            keep["d_x"],
            prev,
        )
        mod_grads.append(
            jnp.concatenate([keep["d_mod1"], keep["d_mods"], keep["d_gate2"]]).reshape(-1)
        )

    g_qkv = scatter_group(term_qkv, groups, width)
    blocks = dp * strips
    packed = jnp.concatenate(
        [
            term_conv_two.reshape(9, blocks, -1).transpose(1, 0, 2).reshape(blocks, -1),
            term_fc1_bias.reshape(blocks, -1),
            term_conv_one.reshape(9, blocks, -1).transpose(1, 0, 2).reshape(blocks, -1),
        ],
        axis=1,
    )
    packed = scatter_rows(packed, jnp.float32)[0]
    wide, narrow = (hidden // blocks, features // blocks)
    g_conv_two = packed[: 9 * wide].reshape(9, wide)
    g_fc1_bias = packed[9 * wide : 10 * wide]
    g_conv_one = packed[10 * wide :].reshape(9, narrow)

    grad_mod = jnp.stack(mod_grads)
    step = 1
    while step < strips:
        grad_mod = grad_mod + permute_xor(grad_mod, "strip", step)
        step *= 2
    all_mods = jnp.concatenate([grad_mod] + [permute_xor(grad_mod, "dp", k) for k in range(1, dp)])
    block_at = dp_at * strips + strip_at
    conds_here = lax.dynamic_slice_in_dim(
        jnp.concatenate(conds), block_at * narrow, narrow, 1
    )
    g_ada = lax.dot_general(
        conds_here, all_mods, (((0,), (0,)), ((), ())), precision=lax.Precision.HIGHEST
    )
    ada_wide_block = 6 * features // blocks
    g_ada_bias = lax.dynamic_slice_in_dim(
        jnp.sum(all_mods, axis=0), block_at * ada_wide_block, ada_wide_block, 0
    )
    return (
        mixed,
        d_latents,
        g_ada,
        g_ada_bias,
        g_conv_one,
        g_qkv,
        g_proj,
        g_fc1,
        g_fc1_bias,
        g_conv_two,
        g_fc2,
    )


def solution(mesh):
    return jax.shard_map(
        shards,
        mesh=mesh,
        in_specs=(
            P(None, "dp", "strip", None, None),
            P(None, "dp"),
            P(None, "dp"),
            P("dp", None),
            P("dp"),
            P(None, "dp"),
            P("dp", None),
            P("dp", None),
            P("dp", None),
            P("dp"),
            P(None, "dp"),
            P("dp", None),
            P(None, "dp", "strip", None, None),
        ),
        out_specs=(
            P(None, "dp", "strip", None, None),
            P(None, "dp", "strip", None, None),
            P(("dp", "strip"), None),
            P(("dp", "strip")),
            P(None, ("dp", "strip")),
            P(("dp", "strip"), None),
            P(("dp", "strip"), None),
            P(("dp", "strip"), None),
            P(("dp", "strip")),
            P(None, ("dp", "strip")),
            P(("dp", "strip"), None),
        ),
        check_vma=False,
    )
```

```python
import functools
import math

import jax
import jax.numpy as jnp
from jax import lax
from jax.experimental import pallas as pl
from jax.experimental.pallas import tpu as pltpu
from jax.sharding import PartitionSpec as P

HEADS = 12
COVER = pl.CostEstimate(flops=200_000_000_000, transcendentals=0, bytes_accessed=0)
BRIEF = pl.CostEstimate(flops=0, transcendentals=0, bytes_accessed=0)


root_half = 0.7071067811865476
inverse_root_tau = 0.3989422804014327


def permute_xor(x, axis, step):
    size = lax.axis_size(axis)
    return lax.ppermute(x, axis, [(i, i ^ step) for i in range(size)])


def pick(x, at, axis=0):
    return lax.dynamic_index_in_dim(x, at, axis, keepdims=False)


def halo_rows(x):
    size, length = (lax.axis_size("strip"), x.shape[0])
    up = [(i, i + 1) for i in range(size - 1)]
    down = [(i + 1, i) for i in range(size - 1)]
    before = lax.ppermute(x[length - 1 :], "strip", up)
    after = lax.ppermute(x[:1], "strip", down)
    return (before, after)


def place_blocks(blocks, me):
    stacked = jnp.stack(blocks)
    return jnp.stack([pick(stacked, me ^ at) for at in range(len(blocks))])


def gather_butterfly(x):
    step = 1
    while step < lax.axis_size("dp"):
        x = jnp.concatenate([x, permute_xor(x, "dp", step)])
        step *= 2
    return x


def gather_small(x):
    me = lax.axis_index("dp")
    blocks = [x] + [permute_xor(x, "dp", k) for k in range(1, lax.axis_size("dp"))]
    return place_blocks(blocks, me)


def after(x, *done):
    return lax.optimization_barrier((x, done))[0]


HBM = pl.BlockSpec(memory_space=pl.ANY)


def move_all(copies):
    for copy in copies:
        copy.start()
    for copy in copies:
        copy.wait()


def rows_at(start, size):
    return pl.ds(pl.multiple_of(start, 8), size)


def assemble_kernel(at_ref, *refs):
    pieces, whole, sem = (refs[:-2], refs[-2], refs[-1])
    move_all(
        [
            pltpu.make_async_copy(
                piece, whole.at[:, rows_at(at_ref[i], piece.shape[1]), :], sem.at[i]
            )
            for i, piece in enumerate(pieces)
        ]
    )


def assemble(pieces, starts, shape):
    return pl.pallas_call(
        assemble_kernel,
        grid_spec=pltpu.PrefetchScalarGridSpec(
            num_scalar_prefetch=1,
            grid=(1,),
            in_specs=[HBM] * len(pieces),
            out_specs=whole_spec(shape),
            scratch_shapes=[pltpu.SemaphoreType.DMA((len(pieces),))],
        ),
        out_shape=jax.ShapeDtypeStruct(shape, pieces[0].dtype),
        cost_estimate=COVER,
        name="assemble",
    )(jnp.stack(starts).astype(jnp.int32), *pieces)


def pack_layout(proj, fc1, fc2):
    features = proj.shape[1]
    sizes = [proj.shape[0] // 2]
    sizes += [fc1.shape[0] // 2] * (fc1.shape[1] // features) + [fc2.shape[0] // 2]
    starts = [sum(sizes[:i]) for i in range(len(sizes))]
    return sizes, starts


def half_of(refs, row, i, size, features):
    if i == 0:
        return refs[0].at[rows_at(row, size), :]
    if i == len(refs[3]) - 1:
        return refs[2].at[rows_at(row, size), :]
    return refs[1].at[rows_at(row, size), (i - 1) * features : i * features]


def pack_kernel(at_ref, proj, fc1, fc2, out, sem):
    sizes, starts = pack_layout(proj, fc1, fc2)
    copies = []
    for i, (size, start) in enumerate(zip(sizes, starts)):
        source = half_of((proj, fc1, fc2, sizes), at_ref[0] * size, i, size, proj.shape[1])
        copies.append(pltpu.make_async_copy(source, out.at[start : start + size, :], sem.at[i]))
    move_all(copies)


def pack_weights(proj, fc1, fc2):
    core = lax.axis_index("strip") & 1
    sizes, starts = pack_layout(proj, fc1, fc2)
    shape = (starts[-1] + sizes[-1], proj.shape[1])
    return pl.pallas_call(
        pack_kernel,
        grid_spec=pltpu.PrefetchScalarGridSpec(
            num_scalar_prefetch=1,
            grid=(1,),
            in_specs=[HBM] * 3,
            out_specs=whole_spec(shape),
            scratch_shapes=[pltpu.SemaphoreType.DMA((len(sizes),))],
        ),
        out_shape=jax.ShapeDtypeStruct(shape, proj.dtype),
        cost_estimate=BRIEF,
        name="pack_weights",
    )(core[None].astype(jnp.int32), proj, fc1, fc2)


def fetch_relayed(x):
    came, step = ({0: x}, 1)
    while step < lax.axis_size("dp"):
        for k in range(step):
            came[step + k] = permute_xor(came[k], "dp", step)
        step *= 2
    return [came[k] for k in range(1, len(came))]


def unpack_kernel(count, at_ref, *refs):
    own, halves, wholes, sem = (refs[:3], refs[3 : 3 + count], refs[3 + count : 6 + count], refs[-1])
    sizes, starts = pack_layout(*own)
    features = own[0].shape[1]
    copies = []
    for ref, whole in zip(own, wholes):
        target = whole.at[rows_at(at_ref[0] * ref.shape[0], ref.shape[0]), :]
        copies.append(pltpu.make_async_copy(ref, target, sem.at[len(copies)]))
    for k, half in enumerate(halves):
        for i, (size, start) in enumerate(zip(sizes, starts)):
            row = (2 * at_ref[1 + 2 * k] + at_ref[2 + 2 * k]) * size
            target = half_of(wholes + (sizes,), row, i, size, features)
            copies.append(
                pltpu.make_async_copy(
                    half.at[start : start + size, :], target, sem.at[len(copies)]
                )
            )
    move_all(copies)


def unpack_weights(fetched, turn, proj, fc1, fc2):
    size, me = (lax.axis_size("dp"), lax.axis_index("dp"))
    core = lax.axis_index("strip") & 1
    halves, places = ([], [me])
    for k, mine in enumerate(fetched, 1):
        halves += [mine, permute_xor(mine, "strip", 1)]
        places += [me ^ k, core, me ^ k, 1 - core]
    shapes = [(size * w.shape[0], w.shape[1]) for w in (proj, fc1, fc2)]
    copies = 3 + len(halves) * len(pack_layout(proj, fc1, fc2)[0])
    return pl.pallas_call(
        functools.partial(unpack_kernel, len(halves)),
        grid_spec=pltpu.PrefetchScalarGridSpec(
            num_scalar_prefetch=1,
            grid=(1,),
            in_specs=[HBM] * (3 + len(halves)),
            out_specs=[whole_spec(shape) for shape in shapes],
            scratch_shapes=[pltpu.SemaphoreType.DMA((copies,))],
        ),
        out_shape=[jax.ShapeDtypeStruct(shape, proj.dtype) for shape in shapes],
        cost_estimate=BRIEF,
        name="unpack_weights",
    )(after(jnp.stack(places).astype(jnp.int32), turn), proj, fc1, fc2, *halves)


def fetch_group(w, groups):
    rows, cols = w.shape
    width = cols // 3 // groups
    group = lax.axis_index("strip") % groups
    mine = pick(w.reshape(rows, 3, groups, width), group, 2).transpose(1, 0, 2)
    mine = jnp.pad(mine, ((0, 0), (0, 0), (0, -width % 128)))
    return [mine] + [permute_xor(mine, "dp", k) for k in range(1, lax.axis_size("dp"))]


def gather_group(pieces):
    me, rows = (lax.axis_index("dp"), pieces[0].shape[1])
    starts = [(me ^ k) * rows for k in range(len(pieces))]
    return assemble(pieces, starts, (3, len(pieces) * rows, pieces[0].shape[2]))


def exchange_sum(x, axis, me, step, wire, dim=0):
    total = pick(x, me, dim).astype(jnp.float32)
    parts = [
        permute_xor(pick(x, me ^ k, dim).astype(wire), axis, k * step)
        for k in range(1, x.shape[dim])
    ]
    for part in parts:
        total = total + part.astype(jnp.float32)
    return total


def scatter_rows(g, wire=jnp.bfloat16):
    rows, cols = g.shape
    dp, strips = (lax.axis_size("dp"), lax.axis_size("strip"))
    strip = lax.axis_index("strip")
    shaped = g.reshape(dp, strips // 2, 2, rows // dp // strips, cols)
    core = strip & 1
    sent = permute_xor(pick(shaped, 1 - core, 2).astype(wire), "strip", 1)
    kept = pick(shaped, core, 2).astype(jnp.float32) + sent.astype(jnp.float32)
    kept = exchange_sum(kept, "dp", lax.axis_index("dp"), 1, wire)
    return exchange_sum(kept, "strip", strip >> 1, 2, wire)


def group_sums(g, groups, width, wire=jnp.bfloat16):
    rows = g.shape[1]
    dp, strips = (lax.axis_size("dp"), lax.axis_size("strip"))
    kept = g[:, :, :width].reshape(3, dp, strips // groups, groups, rows // dp // strips, width)
    return exchange_sum(kept, "dp", lax.axis_index("dp"), 1, wire, 1)


def group_parts(kept, groups, wire=jnp.bfloat16):
    me = lax.axis_index("strip") // groups
    return [pick(kept, me, 1)] + [
        permute_xor(pick(kept, me ^ k, 1).astype(wire), "strip", k * groups)
        for k in range(1, kept.shape[1])
    ]


def group_columns(parts, groups, wire=jnp.bfloat16):
    kept = parts[0]
    for part in parts[1:]:
        kept = kept + part.astype(jnp.float32)
    group = lax.axis_index("strip") % groups
    blocks = [pick(kept, group, 1)] + [
        permute_xor(pick(kept, group ^ k, 1).astype(wire), "strip", k).astype(jnp.float32)
        for k in range(1, groups)
    ]
    whole = place_blocks(blocks, group)
    return whole.transpose(2, 1, 0, 3).reshape(whole.shape[2], -1)


def lay_rows(out, fc2, fc1, proj, small):
    features = proj.shape[-1]
    parts = [fc2]
    parts += [fc1[:, :, i : i + features] for i in range(0, fc1.shape[-1], features)]
    start = 0
    for part in parts + [proj, small]:
        out[:, start : start + part.shape[1], :] = part
        start += part.shape[1]


def route_kernel(at_ref, fc2, fc1, proj, small, out):
    lay_rows(out, fc2[...], fc1[...], proj[...], small[...])


def by_destination(fc2, fc1, proj, small, rows, dp):
    pairs = small.shape[0] // 2 // dp
    arrays = [
        x.reshape(dp, pairs, 2, -1, x.shape[-1]) for x in (fc2, fc1, proj, small)
    ]
    shapes = [(None, pairs, None) + x.shape[3:] for x in arrays]
    return arrays, shapes


def route_core(arrays, shapes):
    dp, pairs = arrays[0].shape[:2]
    features = arrays[0].shape[-1]
    height = sum(x.shape[3] * x.shape[4] for x in arrays) // features
    core = lax.axis_index("strip") & 1
    return pl.pallas_call(
        route_kernel,
        grid_spec=pltpu.PrefetchScalarGridSpec(
            num_scalar_prefetch=1,
            grid=(dp,),
            in_specs=[
                pl.BlockSpec(shape, lambda j, s: (j, 0, 1 - s[0], 0, 0)) for shape in shapes
            ],
            out_specs=pl.BlockSpec((pairs, height, features), lambda j, s: (j, 0, 0)),
        ),
        out_shape=jax.ShapeDtypeStruct((dp * pairs, height, features), arrays[0].dtype),
        cost_estimate=COVER,
        name="route_core",
    )(core[None].astype(jnp.int32), *arrays)


def core_sum_kernel(at_ref, fc2, fc1, proj, small, came, *refs):
    outs, kept = (refs[:-1], refs[-1])
    lay_rows(kept, fc2[...], fc1[...], proj[...], small[...])
    total = kept[...].astype(jnp.float32) + came[...].astype(jnp.float32)
    for k, out in enumerate(outs):

        @pl.when(pl.program_id(0) == k)
        def _():
            out[...] = total.astype(out.dtype)


def core_sum(arrays, shapes, came, me):
    dp, pairs = arrays[0].shape[:2]
    block = (pairs,) + came.shape[1:]
    core = lax.axis_index("strip") & 1
    return pl.pallas_call(
        core_sum_kernel,
        grid_spec=pltpu.PrefetchScalarGridSpec(
            num_scalar_prefetch=1,
            grid=(dp,),
            in_specs=[
                pl.BlockSpec(shape, lambda j, s: (s[1] ^ j, 0, s[0], 0, 0)) for shape in shapes
            ]
            + [pl.BlockSpec(block, lambda j, s: (s[1] ^ j, 0, 0))],
            out_specs=[whole_spec(block)] * dp,
            scratch_shapes=[pltpu.VMEM(block, came.dtype)],
        ),
        out_shape=[jax.ShapeDtypeStruct(block, came.dtype)] * dp,
        cost_estimate=COVER,
        name="core_sum",
    )(jnp.stack([core, me]).astype(jnp.int32), *arrays, came)


def add_kernel(*refs):
    total = refs[0][...].astype(jnp.float32)
    for ref in refs[1:-1]:
        total = total + ref[...].astype(jnp.float32)
    refs[-1][...] = total.astype(refs[-1].dtype)


def add_up(parts):
    block = (1,) + parts[0].shape[1:]
    spec = pl.BlockSpec(block, lambda j: (j, 0, 0))
    return pl.pallas_call(
        add_kernel,
        grid=parts[0].shape[:1],
        in_specs=[spec] * len(parts),
        out_specs=spec,
        out_shape=jax.ShapeDtypeStruct(parts[0].shape, parts[0].dtype),
        cost_estimate=COVER,
        name="add_up",
    )(*parts)


def map_exchange(maps, groups):
    size = lax.axis_size("strip")
    among = [[m * groups + g for m in range(4)] for g in range(groups)]
    return lax.all_to_all(maps, "strip", 0, 0, axis_index_groups=among, tiled=True)


def group_exchange(x, groups):
    return [x] + [permute_xor(x, "strip", k) for k in range(1, groups)]


def silu_of(values):
    return values / (1.0 + jnp.exp(-values))


def embed_times(stamps, features):
    half_count = features // 2
    frequency = jnp.exp(-math.log(10000.0) * jnp.arange(half_count, dtype=jnp.float32) / half_count)
    angles = stamps[:, None] * frequency[None, :]
    return jnp.concatenate([jnp.cos(angles), jnp.sin(angles)], axis=1)

def normalize(values):
    centre = values - jnp.mean(values, axis=-1, keepdims=True)
    inverse = lax.rsqrt(jnp.mean(centre * centre, axis=-1, keepdims=True) + 1e-06)
    return (centre * inverse, inverse)


def norm_back(normed, inverse, upstream):
    return inverse * (
        upstream
        - jnp.mean(upstream, axis=-1, keepdims=True)
        - normed * jnp.mean(upstream * normed, axis=-1, keepdims=True)
    )


def dot_nn(a, b):
    return lax.dot_general(a, b, (((1,), (0,)), ((), ())), preferred_element_type=jnp.float32)


def dot_nt(a, b):
    return lax.dot_general(a, b, (((1,), (1,)), ((), ())), preferred_element_type=jnp.float32)


def dot_tn(a, b):
    return lax.dot_general(a, b, (((0,), (0,)), ((), ())), preferred_element_type=jnp.float32)


def key_mask(s_ref, groups, tokens, cols):
    block = tokens // groups // 4
    token = lax.broadcasted_iota(jnp.int32, (tokens, 128), 0)
    piece, within = (token // block, token % block)
    strip = (piece % 4) * groups + (s_ref[3] ^ (piece // 4))
    row = strip * (block // (cols // 2)) + within // (cols // 2)
    half = s_ref[0] // 2
    return jnp.where((row < half) & (within % (cols // 2) < half), 0.0, -1e30)


def store_sum(ref, part):
    @pl.when(pl.program_id(0) == 0)
    def _():
        ref[...] = part

    @pl.when(pl.program_id(0) > 0)
    def _():
        ref[...] += part


def attend_kernel(chunk, scale, groups, cols, s_ref, *refs):
    pieces, w_ref, t_ref = (refs[:groups], refs[groups], refs[groups + 1])
    o_refs = refs[groups + 2 : 2 * groups + 2]
    l_ref, u_sc, b_sc, q_sc, k_sc, v_sc, o_sc, l_sc = refs[2 * groups + 2 :]
    tokens = u_sc.shape[0]

    @pl.when(pl.program_id(0) == 0)
    def _():
        size = pieces[0].shape[0]
        for i, piece in enumerate(pieces):
            u_sc[i * size : (i + 1) * size, :] = piece[...]
        b_sc[...] = key_mask(s_ref, groups, tokens, cols)

    u = u_sc[...]
    for part in range(3):
        t_ref[part] = dot_nn(u, w_ref[part]).astype(jnp.bfloat16)
    q, k, v = (t_ref[0].astype(jnp.float32), t_ref[1].astype(jnp.float32), t_ref[2].astype(jnp.float32))
    lane = lax.broadcasted_iota(jnp.int32, (tokens, 128), 1)
    bias = b_sc[...]
    for head in range(2):
        here = (lane < 64) if head == 0 else (lane >= 64)
        spare = lane == (64 if head == 0 else 0)
        q_sc[head] = jnp.where(here, q * scale, jnp.where(spare, 1.0, 0.0)).astype(jnp.bfloat16)
        k_sc[head] = jnp.where(here, k, jnp.where(spare, bias, 0.0)).astype(jnp.bfloat16)
        v_sc[head] = jnp.where(here, v, 0.0).astype(jnp.bfloat16)

    def body(i, carry):
        at = pl.ds(pl.multiple_of(i * chunk, chunk), chunk)
        outs, logs = ([], [])
        for head in range(2):
            s = dot_nt(q_sc[head, at, :], k_sc[head])
            top = jnp.max(s, axis=1, keepdims=True)
            p = jnp.exp(s - top)
            total = jnp.sum(p, axis=1, keepdims=True)
            outs.append(dot_nn(p.astype(jnp.bfloat16), v_sc[head]) * (1.0 / total))
            logs.append(top + jnp.log(total))
        o_sc[at, :] = (outs[0] + outs[1]).astype(jnp.bfloat16)
        l_sc[at, :] = jnp.where(
            lax.broadcasted_iota(jnp.int32, (chunk, 128), 1) < 64, logs[0], logs[1]
        )
        return carry

    lax.fori_loop(0, tokens // chunk, body, 0, unroll=True)
    size = tokens // groups
    for i, o_ref in enumerate(o_refs):
        o_ref[...] = o_sc[i * size : (i + 1) * size, :]
    logs = l_sc[...].T
    l_ref[...] = jnp.concatenate(
        [logs[0:1], logs[64:65], jnp.zeros((6, tokens), jnp.float32)], axis=0
    )[None]


def attend(scalars, pieces, w, score_scale, cols):
    groups = len(pieces)
    features, width = w.shape[1:]
    tokens = groups * pieces[0].shape[0]
    chunk = min(512, tokens)
    piece_spec = pl.BlockSpec(pieces[0].shape, lambda j, s: (0, 0))
    return pl.pallas_call(
        functools.partial(attend_kernel, chunk, score_scale, groups, cols),
        grid_spec=pltpu.PrefetchScalarGridSpec(
            num_scalar_prefetch=1,
            grid=(width // 128,),
            in_specs=[piece_spec] * len(pieces)
            + [pl.BlockSpec((3, features, 128), lambda j, s: (0, 0, j))],
            out_specs=[pl.BlockSpec((3, tokens, 128), lambda j, s: (0, 0, j))]
            + [pl.BlockSpec((tokens // groups, 128), lambda j, s: (0, j))] * groups
            + [pl.BlockSpec((1, 8, tokens), lambda j, s: (j, 0, 0))],
            scratch_shapes=[
                pltpu.VMEM((tokens, features), jnp.bfloat16),
                pltpu.VMEM((tokens, 128), jnp.float32),
            ]
            + [pltpu.VMEM((2, tokens, 128), jnp.bfloat16)] * 3
            + [pltpu.VMEM((tokens, 128), jnp.bfloat16), pltpu.VMEM((tokens, 128), jnp.float32)],
        ),
        out_shape=[jax.ShapeDtypeStruct((3, tokens, width), jnp.bfloat16)]
        + [jax.ShapeDtypeStruct((tokens // groups, width), jnp.bfloat16)] * groups
        + [jax.ShapeDtypeStruct((width // 128, 8, tokens), jnp.float32)],
        cost_estimate=COVER,
        name="attend_forward",
    )(scalars, *pieces, w)


def attend_back_kernel(chunk, scale, groups, cols, first, s_ref, *refs):
    pieces, do_pieces, o_refs = (refs[:groups], refs[groups : 2 * groups], refs[2 * groups : 3 * groups])
    w_ref, t_ref, l_ref = refs[3 * groups : 3 * groups + 3]
    rest = refs[3 * groups + 3 :]
    if not first:
        prev_ref, rest = (rest[0], rest[1:])
    du_refs, g_ref = (rest[:groups], rest[groups])
    u_sc, b_sc, o_sc, din_sc, q_sc, k_sc, do_sc, dq_sc, dt_sc, d_sc = rest[groups + 1 :]
    tokens = u_sc.shape[0]
    size = pieces[0].shape[0]

    @pl.when(pl.program_id(0) == 0)
    def _():
        for i, piece in enumerate(pieces):
            u_sc[i * size : (i + 1) * size, :] = piece[...]
        b_sc[...] = key_mask(s_ref, groups, tokens, cols)

    for i, piece in enumerate(do_pieces):
        din_sc[i * size : (i + 1) * size, :] = piece[...]
    for i, piece in enumerate(o_refs):
        o_sc[i * size : (i + 1) * size, :] = piece[...]
    q, k, do = (t_ref[0].astype(jnp.float32), t_ref[1].astype(jnp.float32), din_sc[...])
    lane = lax.broadcasted_iota(jnp.int32, (tokens, 128), 1)
    bias = b_sc[...]
    do = do.astype(jnp.float32)
    inner = (do * o_sc[...].astype(jnp.float32)).T
    for head in range(2):
        here = (lane < 64) if head == 0 else (lane >= 64)
        spare = lane == (64 if head == 0 else 0)
        q_sc[head] = jnp.where(here, q * scale, jnp.where(spare, 1.0, 0.0)).astype(jnp.bfloat16)
        k_sc[head] = jnp.where(here, k, jnp.where(spare, bias, 0.0)).astype(jnp.bfloat16)
        do_sc[head] = jnp.where(here, do, 0.0).astype(jnp.bfloat16)
        d_sc[head : head + 1, :] = jnp.sum(
            inner[64 * head : 64 * head + 64], axis=0, keepdims=True
        )
    dq_sc[...] = jnp.zeros_like(dq_sc)

    def body(i, carry):
        at = pl.ds(pl.multiple_of(i * chunk, chunk), chunk)
        lanes = lax.broadcasted_iota(jnp.int32, (chunk, 128), 1)
        d_k, d_v, d_q = ([], [], [])
        for head in range(2):
            here = (lanes < 64) if head == 0 else (lanes >= 64)
            s = dot_nt(k_sc[head, at, :], q_sc[head])
            p = jnp.exp(s - l_ref[0, head : head + 1, :])
            d_p = dot_nt(t_ref[2, at, :], do_sc[head])
            d_s = (p * (d_p - d_sc[head : head + 1, :])).astype(jnp.bfloat16)
            d_v.append(dot_nn(p.astype(jnp.bfloat16), do_sc[head]))
            d_k.append(dot_nn(d_s, q_sc[head]))
            keys = jnp.where(here, t_ref[1, at, :].astype(jnp.float32), 0.0).astype(jnp.bfloat16)
            d_q.append(dot_tn(d_s, keys))
        dq_sc[...] += d_q[0] + d_q[1]
        dt_sc[at, 128:256] = jnp.where(lanes < 64, d_k[0], d_k[1]).astype(jnp.bfloat16)
        dt_sc[at, 256:384] = (d_v[0] + d_v[1]).astype(jnp.bfloat16)
        return carry

    lax.fori_loop(0, tokens // chunk, body, 0, unroll=True)
    dt_sc[:, 0:128] = (dq_sc[...] * scale).astype(jnp.bfloat16)
    for i, du_ref in enumerate(du_refs):
        at = slice(i * size, (i + 1) * size)
        part = dot_nt(dt_sc[at, 0:128], w_ref[0])
        part = part + dot_nt(dt_sc[at, 128:256], w_ref[1])
        part = part + dot_nt(dt_sc[at, 256:384], w_ref[2])
        store_sum(du_ref, part)
    grad = dot_tn(u_sc[...], dt_sc[...])
    for at in range(3):
        piece = grad[:, 128 * at : 128 * at + 128]
        if not first:
            piece = piece + prev_ref[at]
        g_ref[at] = piece.astype(g_ref.dtype)


def attend_back(scalars, pieces, d_pieces, outs, w, t, logs, score_scale, cols, prev, grad_type):
    groups = len(outs)
    features, width = w.shape[1:]
    tokens = t.shape[1]
    chunk = min(256, tokens)
    size = pieces[0].shape[0]
    blocks = width // 128
    weight_spec = pl.BlockSpec((3, features, 128), lambda j, s: (0, 0, j))
    offset = 0 if d_pieces[0].shape[1] == width else blocks
    args = list(pieces) + list(d_pieces) + list(outs) + [w, t, logs]
    args += [] if prev is None else [prev]
    return pl.pallas_call(
        functools.partial(attend_back_kernel, chunk, score_scale, groups, cols, prev is None),
        grid_spec=pltpu.PrefetchScalarGridSpec(
            num_scalar_prefetch=1,
            grid=(blocks,),
            in_specs=[pl.BlockSpec((size, features), lambda j, s: (0, 0))] * len(pieces)
            + [pl.BlockSpec((size, 128), lambda j, s: (0, s[3] * offset + j))] * len(d_pieces)
            + [pl.BlockSpec((size, 128), lambda j, s: (0, j))] * groups
            + [
                weight_spec,
                pl.BlockSpec((3, tokens, 128), lambda j, s: (0, 0, j)),
                pl.BlockSpec((1, 8, tokens), lambda j, s: (j, 0, 0)),
            ]
            + ([] if prev is None else [weight_spec]),
            out_specs=[pl.BlockSpec((size, features), lambda j, s: (0, 0))] * groups
            + [weight_spec],
            scratch_shapes=[
                pltpu.VMEM((tokens, features), jnp.bfloat16),
                pltpu.VMEM((tokens, 128), jnp.float32),
                pltpu.VMEM((tokens, 128), jnp.bfloat16),
                pltpu.VMEM((tokens, 128), jnp.bfloat16),
            ]
            + [pltpu.VMEM((2, tokens, 128), jnp.bfloat16)] * 3
            + [
                pltpu.VMEM((tokens, 128), jnp.float32),
                pltpu.VMEM((tokens, 384), jnp.bfloat16),
                pltpu.VMEM((8, tokens), jnp.float32),
            ],
        ),
        out_shape=[jax.ShapeDtypeStruct((size, features), jnp.float32)] * groups
        + [jax.ShapeDtypeStruct(w.shape, grad_type)],
        cost_estimate=COVER,
        name="attend_backward",
    )(scalars, *args)


def shift_cols(x, by, col):
    size = x.shape[0]
    rolled = pltpu.roll(x, (-by) % size, 0)
    return jnp.where(col == (size - 1 if by > 0 else 0), 0.0, rolled)


def wide_taps(c_ref, lanes, cols):
    return [
        jnp.broadcast_to(c_ref[k : k + 1, lanes].astype(jnp.float32), (cols, 128)) for k in range(9)
    ]


def sublane_sum(x):
    return jnp.sum(x.reshape(x.shape[0] // 8, 8, 128), axis=0)


def modulate(x, m_ref, shift_at, col, row, side):
    normed, _ = normalize(x.astype(jnp.float32))
    value = normed * (1.0 + m_ref[shift_at + 1 : shift_at + 2, :]) + m_ref[shift_at : shift_at + 1, :]
    live = (col < side) & (row >= 0) & (row < side)
    return jnp.where(live, value, 0.0).astype(jnp.bfloat16)


def modulated_rows(a_sc, s_ref, x_ref, top_ref, end_ref, m_ref):
    rows, cols, features = x_ref.shape
    side, row_zero = (s_ref[0], s_ref[1])
    col = lax.broadcasted_iota(jnp.int32, (cols, features), 0)
    a_sc[0] = modulate(top_ref[...], m_ref, 0, col, row_zero - 1, side)
    a_sc[rows + 1] = modulate(end_ref[...], m_ref, 0, col, row_zero + rows, side)

    def body(r, carry):
        a_sc[r + 1] = modulate(x_ref[r], m_ref, 0, col, row_zero + r, side)
        return carry

    lax.fori_loop(0, rows, body, 0)


def to_maps(canvas, maps_ref):
    blocks, rows, cols, _ = canvas.shape
    half = cols // 2

    def body(r, carry):
        at = pl.ds(pl.multiple_of(r * half, half), half)
        for m in range(4):
            for b in range(blocks):
                part = canvas[b, 2 * r + m // 2, pl.ds(m % 2, half, stride=2), :]
                maps_ref[m, at, 128 * b : 128 * b + 128] = part.astype(jnp.bfloat16)
        return carry

    lax.fori_loop(0, rows // 2, body, 0)


def from_maps(maps_ref, canvas, row_offset):
    half = canvas.shape[2] // 2
    rows = maps_ref.shape[1] // half * 2

    def body(r, carry):
        at = pl.ds(pl.multiple_of(r * half, half), half)
        for m in range(4):
            for b in range(canvas.shape[0]):
                part = maps_ref[m, at, 128 * b : 128 * b + 128].astype(jnp.float32)
                canvas[b, row_offset + 2 * r + m // 2, pl.ds(m % 2, half, stride=2), :] = part
        return carry

    lax.fori_loop(0, rows // 2, body, 0)


def before_kernel(s_ref, x_ref, top_ref, end_ref, m_ref, c_ref, *refs):
    maps_ref, a_sc, t_sc = refs
    rows, cols, features = x_ref.shape
    modulated_rows(a_sc, s_ref, x_ref, top_ref, end_ref, m_ref)
    col = lax.broadcasted_iota(jnp.int32, (cols, 128), 0)
    for first in range(0, features, 128):
        lanes = slice(first, first + 128)
        taps = wide_taps(c_ref, lanes, cols)

        def body(r, carry):
            x = [a_sc[r + i, :, lanes].astype(jnp.float32) for i in range(3)]
            a = [x[0] * taps[j] + x[1] * taps[3 + j] + x[2] * taps[6 + j] for j in range(3)]
            t_sc[first // 128, r] = a[1] + shift_cols(a[0], -1, col) + shift_cols(a[2], 1, col)
            return carry

        lax.fori_loop(0, rows, body, 0)
    to_maps(t_sc, maps_ref)


def canvas_specs(latents, at):
    rows, cols, features = latents.shape[2:]
    return [
        pl.BlockSpec((None, None, rows, cols, features), lambda j, s: (at, 0, 0, 0, 0)),
        pl.BlockSpec((None, cols, features), lambda j, s: (at, 0, 0)),
        pl.BlockSpec((None, cols, features), lambda j, s: (at, 0, 0)),
        pl.BlockSpec((None, 6, features), lambda j, s: (at, 0, 0)),
    ]


def whole_spec(shape):
    return pl.BlockSpec(shape, lambda j, s: (0,) * len(shape))


def before_attention(at, scalars, latents, top, end, mods, taps):
    rows, cols, features = latents.shape[2:]
    maps = (4, rows * cols // 4, features)
    return pl.pallas_call(
        before_kernel,
        grid_spec=pltpu.PrefetchScalarGridSpec(
            num_scalar_prefetch=1,
            grid=(1,),
            in_specs=canvas_specs(latents, at) + [whole_spec(taps.shape)],
            out_specs=whole_spec(maps),
            scratch_shapes=[
                pltpu.VMEM((rows + 2, cols, features), jnp.bfloat16),
                pltpu.VMEM((features // 128, rows, cols, 128), jnp.float32),
            ],
        ),
        out_shape=jax.ShapeDtypeStruct(maps, jnp.bfloat16),
        cost_estimate=COVER,
        name="before_attention",
    )(scalars, latents, top, end, mods, taps)


def join_kernel(s_ref, mine_ref, other_ref, out_ref):
    width = mine_ref.shape[1]

    def write(low_ref, high_ref):
        out_ref[:, :width] = low_ref[...]
        out_ref[:, width:] = high_ref[...]

    @pl.when(s_ref[3] == 0)
    def _():
        write(mine_ref, other_ref)

    @pl.when(s_ref[3] == 1)
    def _():
        write(other_ref, mine_ref)


def join_groups(scalars, parts, width):
    groups = len(parts)
    tokens = parts[0].shape[0]
    shape = (tokens, groups * width)
    if groups != 2 or parts[0].shape[1] != width:
        whole = place_blocks([part[:, :width] for part in parts], scalars[3])
        whole = whole.transpose(1, 0, 2)
    else:
        whole = pl.pallas_call(
            join_kernel,
            grid_spec=pltpu.PrefetchScalarGridSpec(
                num_scalar_prefetch=1,
                grid=(1,),
                in_specs=[whole_spec(part.shape) for part in parts],
                out_specs=whole_spec(shape),
            ),
            out_shape=jax.ShapeDtypeStruct(shape, parts[0].dtype),
            cost_estimate=BRIEF,
            name="join_groups",
        )(scalars, *parts)
    return whole.reshape(4, tokens // 4, groups * width)


def sum_kernel(count, *refs):
    total = refs[0][...]
    for part in refs[1:count]:
        total = total + part[...]
    refs[count][...] = total.astype(refs[count].dtype)


def sum_groups(parts):
    tokens, features = parts[0].shape
    total = pl.pallas_call(
        functools.partial(sum_kernel, len(parts)),
        out_shape=jax.ShapeDtypeStruct((tokens, features), jnp.bfloat16),
        cost_estimate=BRIEF,
        name="sum_groups",
    )(*parts)
    return total.reshape(4, tokens // 4, features)


def edge_rows(maps, cols):
    size, features = maps.shape[1:]
    first = maps[:2, : cols // 2].reshape(cols, features)
    return first, maps[2:, size - cols // 2 :].reshape(cols, features)


def expand_kernel(s_ref, o_ref, x_ref, m_ref, wp_ref, w_ref, b_ref, *refs):
    oc_ref, at_ref, x1_ref, a2_ref, f_ref, t_sc = refs
    rows, cols, features = x_ref.shape
    side, row_zero = (s_ref[0], s_ref[1])

    @pl.when(pl.program_id(0) == 0)
    def _():
        from_maps(o_ref, t_sc, 0)
        for b in range(features // 128):
            part = t_sc[b].reshape(rows * cols, 128)
            oc_ref[:, 128 * b : 128 * b + 128] = part.astype(jnp.bfloat16)
        at_ref[...] = dot_nn(oc_ref[...], wp_ref[...])

        def body(r, carry):
            here = pl.ds(pl.multiple_of(r * cols, cols), cols)
            x1 = x_ref[r].astype(jnp.float32) + m_ref[2:3, :] * at_ref[here, :]
            x1_ref[here, :] = x1
            normed, _ = normalize(x1)
            a2 = normed * (1.0 + m_ref[4:5, :]) + m_ref[3:4, :]
            a2_ref[here, :] = a2.astype(jnp.bfloat16)
            return carry

        lax.fori_loop(0, rows, body, 0)

    block = f_ref.shape[2]
    f = (dot_nn(a2_ref[...], w_ref[...]) + b_ref[...].astype(jnp.float32)).reshape(rows, cols, block)
    col = lax.broadcasted_iota(jnp.int32, (cols, block), 0)
    for r in range(rows):
        live = (col < side) & (row_zero + r < side)
        f_ref[r] = jnp.where(live, f[r], 0.0).astype(jnp.bfloat16)


def expand(at, scalars, maps, latents, mods, w_proj, w_fc1, bias):
    rows, cols, features = latents.shape[2:]
    hidden = w_fc1.shape[1]
    tokens, block = (rows * cols, 512)
    flat = (tokens, features)
    specs = canvas_specs(latents, at)
    return pl.pallas_call(
        expand_kernel,
        grid_spec=pltpu.PrefetchScalarGridSpec(
            num_scalar_prefetch=1,
            grid=(hidden // block,),
            in_specs=[
                whole_spec(maps.shape),
                specs[0],
                specs[3],
                whole_spec(w_proj.shape),
                pl.BlockSpec((features, block), lambda j, s: (0, j)),
                pl.BlockSpec((1, block), lambda j, s: (0, j)),
            ],
            out_specs=[whole_spec(flat)] * 4
            + [pl.BlockSpec((rows, cols, block), lambda j, s: (0, 0, j))],
            scratch_shapes=[pltpu.VMEM((features // 128, rows, cols, 128), jnp.float32)],
        ),
        out_shape=[
            jax.ShapeDtypeStruct(flat, jnp.bfloat16),
            jax.ShapeDtypeStruct(flat, jnp.float32),
            jax.ShapeDtypeStruct(flat, jnp.float32),
            jax.ShapeDtypeStruct(flat, jnp.bfloat16),
            jax.ShapeDtypeStruct((rows, cols, hidden), jnp.bfloat16),
        ],
        cost_estimate=COVER,
        name="expand",
    )(scalars, maps, latents, mods, w_proj, w_fc1, bias)


def middle_kernel(first, s_ref, f_ref, top_ref, end_ref, c_ref, w_ref, ct_ref, x1_ref, m_ref, *rest):
    if first:
        mixed_ref, dg_ref, dz_ref, g_ref, gc_ref = rest[:5]
    else:
        gp_ref, gcp_ref = rest[:2]
        mixed_ref, dg_ref, dz_ref, g_ref, gc_ref = rest[3:8]
    out_sc, d_sc, x_sc, t_sc, gz_sc, acc_sc = rest[-6:]
    rows, cols, block = f_ref.shape
    features = out_sc.shape[1]
    side, row_zero = (s_ref[0], s_ref[1])

    def upstream(r):
        col = lax.broadcasted_iota(jnp.int32, (cols, features), 0)
        live = (col < side) & (row_zero + r < side)
        return jnp.where(live, ct_ref[r].astype(jnp.float32), 0.0), live

    @pl.when(pl.program_id(0) == 0)
    def _():
        def body(r, carry):
            here = pl.ds(pl.multiple_of(r * cols, cols), cols)
            d_sc[here, :] = (upstream(r)[0] * m_ref[5:6, :]).astype(jnp.bfloat16)
            return carry

        lax.fori_loop(0, rows, body, 0)

    d = d_sc[...]
    t_sc[...] = dot_nt(d, w_ref[...]).reshape(rows, cols, block)
    x_sc[0:1] = top_ref[...]
    x_sc[1 : rows + 1] = f_ref[...]
    x_sc[rows + 1 : rows + 2] = end_ref[...]
    acc_sc[...] = jnp.zeros_like(acc_sc)
    col = lax.broadcasted_iota(jnp.int32, (cols, 128), 0)
    for at in range(block // 128):
        lanes = slice(128 * at, 128 * at + 128)
        taps = wide_taps(c_ref, lanes, cols)

        def body(r, carry):
            x = [x_sc[r + i, :, lanes].astype(jnp.float32) for i in range(3)]
            a = [x[0] * taps[j] + x[1] * taps[3 + j] + x[2] * taps[6 + j] for j in range(3)]
            z = a[1] + shift_cols(a[0], -1, col) + shift_cols(a[2], 1, col)
            half = 0.5 * (1.0 + lax.erf(z * root_half))
            gz_sc[r, :, lanes] = (z * half).astype(jnp.bfloat16)
            slope = half + z * jnp.exp(-0.5 * z * z) * inverse_root_tau
            d_z = (t_sc[r, :, lanes] * slope).astype(jnp.bfloat16)
            dz_ref[r, :, lanes] = d_z
            d_z = d_z.astype(jnp.float32)
            moved = [shift_cols(d_z, 1, col), d_z, shift_cols(d_z, -1, col)]
            for i in range(3):
                for j in range(3):
                    acc_sc[3 * i + j, :, lanes] += sublane_sum(x[i] * moved[j])
            return carry

        lax.fori_loop(0, rows, body, 0, unroll=2)
    gz = gz_sc[...].reshape(rows * cols, block)
    store_sum(out_sc, dot_nn(gz, w_ref[...]))
    grad = dot_tn(gz, d)
    taps_grad = jnp.concatenate(
        [jnp.sum(acc_sc[k], axis=0, keepdims=True) for k in range(9)], axis=0
    )
    if not first:
        grad = grad + gp_ref[...]
        taps_grad = taps_grad + gcp_ref[...]
    g_ref[...] = grad.astype(g_ref.dtype)
    gc_ref[...] = taps_grad

    @pl.when(pl.program_id(0) == pl.num_programs(0) - 1)
    def _():
        def body(r, total):
            here = pl.ds(pl.multiple_of(r * cols, cols), cols)
            value, live = upstream(r)
            out = out_sc[here, :]
            mixed = x1_ref[here, :] + m_ref[5:6, :] * out
            mixed_ref[r] = jnp.where(live, mixed, 0.0).astype(jnp.bfloat16)
            return total + sublane_sum(value * out)

        total = lax.fori_loop(0, rows, body, jnp.zeros((8, features), jnp.float32))
        dg_ref[...] = jnp.sum(total, axis=0, keepdims=True)


def sublane_sum(x):
    return jnp.sum(x.reshape(x.shape[0] // 8, 8, x.shape[1]), axis=0)


def ffn_middle(at, scalars, f, halo, taps, w, cotangent, x1, mods, prev, grad_type):
    rows, cols, hidden = f.shape
    features = w.shape[1]
    block = 512
    wide = lambda j, s: (0, 0, j)
    row_spec = pl.BlockSpec((1, cols, block), wide)
    weight_spec = pl.BlockSpec((block, features), lambda j, s: (j, 0))
    tap_spec = pl.BlockSpec((9, block), lambda j, s: (0, j))
    canvas_spec = pl.BlockSpec((rows, cols, block), wide)
    specs = canvas_specs(cotangent, at)
    args = [scalars, f, halo[0], halo[1], taps, w, cotangent, x1, mods]
    args += [] if prev is None else list(prev)
    return pl.pallas_call(
        functools.partial(middle_kernel, prev is None),
        grid_spec=pltpu.PrefetchScalarGridSpec(
            num_scalar_prefetch=1,
            grid=(hidden // block,),
            in_specs=[canvas_spec, row_spec, row_spec, tap_spec, weight_spec]
            + [specs[0], whole_spec(x1.shape), specs[3]]
            + ([] if prev is None else [weight_spec, tap_spec, pl.BlockSpec(memory_space=pl.ANY)]),
            out_specs=[specs[0], whole_spec((1, features)), canvas_spec, weight_spec, tap_spec],
            scratch_shapes=[
                pltpu.VMEM((rows * cols, features), jnp.float32),
                pltpu.VMEM((rows * cols, features), jnp.bfloat16),
                pltpu.VMEM((rows + 2, cols, block), jnp.bfloat16),
                pltpu.VMEM((rows, cols, block), jnp.float32),
                pltpu.VMEM((rows, cols, block), jnp.bfloat16),
                pltpu.VMEM((9, 8, block), jnp.float32),
            ],
        ),
        out_shape=[
            jax.ShapeDtypeStruct(cotangent.shape, jnp.bfloat16),
            jax.ShapeDtypeStruct((1, features), jnp.float32),
            jax.ShapeDtypeStruct(f.shape, jnp.bfloat16),
            jax.ShapeDtypeStruct((hidden, features), grad_type),
            jax.ShapeDtypeStruct((9, hidden), jnp.float32),
        ],
        input_output_aliases={} if prev is None else {11: 0},
        cost_estimate=COVER,
        name="ffn_middle",
    )(*args)


def ffn_back_kernel(first, s_ref, z_ref, top_ref, end_ref, c_ref, w_ref, a_ref, *rest):
    ct_ref, x1_ref, at_ref, oc_ref, wp_ref, m_ref = rest[:6]
    rest = rest[6:]
    if not first:
        gp_ref, gbp_ref, gpp_ref = rest[:3]
        rest = rest[3:]
    maps_ref, dx_ref, dm_ref, g_ref, gb_ref, gp_out = rest[:6]
    da_sc, x_sc, df_sc, acc_sc, t_sc, dat_sc = rest[6:]
    rows, cols, block = z_ref.shape
    features = da_sc.shape[1]
    x_sc[0:1] = top_ref[...]
    x_sc[1 : rows + 1] = z_ref[...]
    x_sc[rows + 1 : rows + 2] = end_ref[...]
    acc_sc[...] = jnp.zeros_like(acc_sc)
    col = lax.broadcasted_iota(jnp.int32, (cols, 128), 0)
    side, row_zero = (s_ref[0], s_ref[1])
    for at in range(block // 128):
        lanes = slice(128 * at, 128 * at + 128)
        taps = wide_taps(c_ref, lanes, cols)

        def body(r, carry):
            x = [x_sc[r + i, :, lanes].astype(jnp.float32) for i in range(3)]
            b = [x[2] * taps[j] + x[1] * taps[3 + j] + x[0] * taps[6 + j] for j in range(3)]
            d_f = b[1] + shift_cols(b[0], 1, col) + shift_cols(b[2], -1, col)
            live = (col < side) & (row_zero + r < side)
            d_f = jnp.where(live, d_f, 0.0).astype(jnp.bfloat16)
            df_sc[r, :, lanes] = d_f
            acc_sc[:, lanes] += sublane_sum(d_f.astype(jnp.float32))
            return carry

        lax.fori_loop(0, rows, body, 0, unroll=2)
    d_f = df_sc[...].reshape(rows * cols, block)
    store_sum(da_sc, dot_nt(d_f, w_ref[...]))
    grad = dot_tn(a_ref[...], d_f)
    bias_grad = jnp.sum(acc_sc[...], axis=0, keepdims=True)
    if not first:
        grad = grad + gp_ref[...]
        bias_grad = bias_grad + gbp_ref[...]
    g_ref[...] = grad.astype(g_ref.dtype)
    gb_ref[...] = bias_grad

    @pl.when(pl.program_id(0) == pl.num_programs(0) - 1)
    def _():
        wide_col = lax.broadcasted_iota(jnp.int32, (cols, features), 0)

        def body(r, totals):
            here = pl.ds(pl.multiple_of(r * cols, cols), cols)
            d_a = da_sc[here, :]
            normed, inverse = normalize(x1_ref[here, :])
            live = (wide_col < side) & (row_zero + r < side)
            d_x = jnp.where(live, ct_ref[r].astype(jnp.float32), 0.0)
            d_x = d_x + norm_back(normed, inverse, d_a * (1.0 + m_ref[4:5, :]))
            dx_ref[here, :] = d_x
            dat_sc[here, :] = (d_x * m_ref[2:3, :]).astype(jnp.bfloat16)
            return (
                totals[0] + sublane_sum(d_x * at_ref[here, :]),
                totals[1] + sublane_sum(d_a),
                totals[2] + sublane_sum(d_a * normed),
            )

        zero = jnp.zeros((8, features), jnp.float32)
        totals = lax.fori_loop(0, rows, body, (zero, zero, zero))
        for i in range(3):
            dm_ref[i : i + 1, :] = jnp.sum(totals[i], axis=0, keepdims=True)
        proj = dot_tn(oc_ref[...], dat_sc[...])
        if not first:
            proj = proj + gpp_ref[...]
        gp_out[...] = proj.astype(gp_out.dtype)
        d_o = dot_nt(dat_sc[...], wp_ref[...])
        for b in range(features // 128):
            t_sc[b] = d_o[:, 128 * b : 128 * b + 128].reshape(rows, cols, 128)
        to_maps(t_sc, maps_ref)


def ffn_back(
    at, scalars, d_z, halo, taps, w, a, cotangent, x1, attn, oc, w_proj, mods, prev, grad_type
):
    rows, cols, hidden = d_z.shape
    features = a.shape[1]
    block = 512
    wide = lambda j, s: (0, 0, j)
    row_spec = pl.BlockSpec((1, cols, block), wide)
    weight_spec = pl.BlockSpec((features, block), lambda j, s: (0, j))
    bias_spec = pl.BlockSpec((1, block), lambda j, s: (0, j))
    flat_spec = whole_spec((rows * cols, features))
    proj_spec = whole_spec(w_proj.shape)
    maps = (4, rows * cols // 4, features)
    specs = canvas_specs(cotangent, at)
    args = [scalars, d_z, halo[0], halo[1], taps, w, a, cotangent, x1, attn, oc, w_proj, mods]
    args += [] if prev is None else list(prev)
    return pl.pallas_call(
        functools.partial(ffn_back_kernel, prev is None),
        grid_spec=pltpu.PrefetchScalarGridSpec(
            num_scalar_prefetch=1,
            grid=(hidden // block,),
            in_specs=[
                pl.BlockSpec((rows, cols, block), wide),
                row_spec,
                row_spec,
                pl.BlockSpec((9, block), lambda j, s: (0, j)),
                weight_spec,
                flat_spec,
                specs[0],
                flat_spec,
                flat_spec,
                flat_spec,
                proj_spec,
                specs[3],
            ]
            + ([] if prev is None else [weight_spec, bias_spec, proj_spec]),
            out_specs=[whole_spec(maps)]
            + [flat_spec, whole_spec((3, features)), weight_spec, bias_spec, proj_spec],
            scratch_shapes=[
                pltpu.VMEM((rows * cols, features), jnp.float32),
                pltpu.VMEM((rows + 2, cols, block), jnp.bfloat16),
                pltpu.VMEM((rows, cols, block), jnp.bfloat16),
                pltpu.VMEM((8, block), jnp.float32),
                pltpu.VMEM((features // 128, rows, cols, 128), jnp.float32),
                pltpu.VMEM((rows * cols, features), jnp.bfloat16),
            ],
        ),
        out_shape=[jax.ShapeDtypeStruct(maps, jnp.bfloat16)]
        + [
            jax.ShapeDtypeStruct((rows * cols, features), jnp.float32),
            jax.ShapeDtypeStruct((3, features), jnp.float32),
            jax.ShapeDtypeStruct(w.shape, grad_type),
            jax.ShapeDtypeStruct((1, hidden), jnp.float32),
            jax.ShapeDtypeStruct(w_proj.shape, grad_type),
        ],
        cost_estimate=COVER,
        name="ffn_backward",
    )(*args)


def last_kernel(first, s_ref, du_ref, dtop_ref, dend_ref, *rest):
    x_ref, top_ref, end_ref, m_ref, c_ref, dx_ref = rest[:6]
    rest = rest[6:]
    if not first:
        gcp_ref = rest[0]
        rest = rest[2:]
    dl_ref, dm_ref, gc_ref, a_sc, t_sc, d_sc, acc_sc = rest
    rows, cols, features = x_ref.shape
    half = cols // 2
    side, row_zero = (s_ref[0], s_ref[1])
    modulated_rows(a_sc, s_ref, x_ref, top_ref, end_ref, m_ref)
    from_maps(du_ref, t_sc, 1)
    for at, ref in ((0, dtop_ref), (rows + 1, dend_ref)):
        for j in range(2):
            for start in range(0, features, 128):
                lanes = slice(start, start + 128)
                part = ref[j * half : (j + 1) * half, lanes].astype(jnp.float32)
                t_sc[start // 128, at, pl.ds(j, half, stride=2), :] = part
    acc_sc[...] = jnp.zeros_like(acc_sc)
    col = lax.broadcasted_iota(jnp.int32, (cols, 128), 0)
    for start in range(0, features, 128):
        lanes = slice(start, start + 128)
        taps = wide_taps(c_ref, lanes, cols)

        def conv_body(r, carry):
            d = [t_sc[start // 128, r + i] for i in range(3)]
            b = [d[2] * taps[j] + d[1] * taps[3 + j] + d[0] * taps[6 + j] for j in range(3)]
            d_a = b[1] + shift_cols(b[0], 1, col) + shift_cols(b[2], -1, col)
            live = (col < side) & (row_zero + r < side)
            d_sc[r, :, lanes] = jnp.where(live, d_a, 0.0)
            moved = [shift_cols(d[1], 1, col), d[1], shift_cols(d[1], -1, col)]
            for i in range(3):
                x = a_sc[r + i, :, lanes].astype(jnp.float32)
                for j in range(3):
                    acc_sc[3 * i + j, :, lanes] += sublane_sum(x * moved[j])
            return carry

        lax.fori_loop(0, rows, conv_body, 0, unroll=2)
    taps_grad = jnp.concatenate(
        [jnp.sum(acc_sc[k], axis=0, keepdims=True) for k in range(9)], axis=0
    )
    if not first:
        taps_grad = taps_grad + gcp_ref[...]
    gc_ref[...] = taps_grad

    def body(r, totals):
        here = pl.ds(pl.multiple_of(r * cols, cols), cols)
        normed, inverse = normalize(x_ref[r].astype(jnp.float32))
        d_a = d_sc[r]
        dl_ref[r] = dx_ref[here, :] + norm_back(normed, inverse, d_a * (1.0 + m_ref[1:2, :]))
        return (totals[0] + sublane_sum(d_a), totals[1] + sublane_sum(d_a * normed))

    zero = jnp.zeros((8, features), jnp.float32)
    totals = lax.fori_loop(0, rows, body, (zero, zero))
    for i in range(2):
        dm_ref[i : i + 1, :] = jnp.sum(totals[i], axis=0, keepdims=True)


def last_stage(at, scalars, maps, d_halo, latents, top, end, mods, taps, d_x, prev):
    rows, cols, features = latents.shape[2:]
    specs = canvas_specs(latents, at)
    args = [scalars, maps, *d_halo, latents, top, end, mods, taps, d_x]
    args += [] if prev is None else list(prev)
    return pl.pallas_call(
        functools.partial(last_kernel, prev is None),
        grid_spec=pltpu.PrefetchScalarGridSpec(
            num_scalar_prefetch=1,
            grid=(1,),
            in_specs=[whole_spec(maps.shape)]
            + [whole_spec((cols, features))] * 2
            + specs
            + [whole_spec(taps.shape), whole_spec(d_x.shape)]
            + ([] if prev is None else [whole_spec(taps.shape), pl.BlockSpec(memory_space=pl.ANY)]),
            out_specs=[specs[0], whole_spec((2, features)), whole_spec(taps.shape)],
            scratch_shapes=[
                pltpu.VMEM((rows + 2, cols, features), jnp.bfloat16),
                pltpu.VMEM((features // 128, rows + 2, cols, 128), jnp.float32),
                pltpu.VMEM((rows, cols, features), jnp.float32),
                pltpu.VMEM((9, 8, features), jnp.float32),
            ],
        ),
        out_shape=[
            jax.ShapeDtypeStruct(latents.shape, jnp.float32),
            jax.ShapeDtypeStruct((2, features), jnp.float32),
            jax.ShapeDtypeStruct(taps.shape, jnp.float32),
        ],
        input_output_aliases={} if prev is None else {11: 0},
        cost_estimate=COVER,
        name="last_stage",
    )(*args)


def shards(
    latents,
    timesteps,
    size_tags,
    w_ada,
    b_ada,
    conv_attn,
    w_qkv,
    w_proj,
    w_fc1,
    b_fc1,
    conv_ffn,
    w_fc2,
    cotangent,
):
    micro_count, _, row_count, side_count, features = latents.shape
    dp, strips = (lax.axis_size("dp"), lax.axis_size("strip"))
    dp_at, strip_at = (lax.axis_index("dp"), lax.axis_index("strip"))
    hidden = conv_ffn.shape[1] * dp
    groups = strips // 4
    group_at, map_at = (strip_at % groups, strip_at // groups)
    score_scale = (features // HEADS) ** (-0.5)
    width = features // groups

    stamps = timesteps[:, 0].astype(jnp.float32)
    all_stamps = gather_butterfly(stamps[None])
    conds = [silu_of(embed_times(all_stamps[k], features)) for k in range(dp)]
    ada_rows = features // dp
    ada_wide = w_ada.astype(jnp.float32)
    partial_mods = jnp.dot(
        lax.dynamic_slice_in_dim(jnp.concatenate(conds), dp_at * ada_rows, ada_rows, 1),
        ada_wide,
        precision=lax.Precision.HIGHEST,
    )
    bias_here = lax.dynamic_update_slice_in_dim(
        jnp.zeros((6 * features,), jnp.float32),
        b_ada.astype(jnp.float32),
        dp_at * b_ada.shape[0],
        0,
    )
    partial_mods = (partial_mods + bias_here[None, :]).reshape(dp, micro_count, 6 * features)
    count = dp
    while count > 1:
        count //= 2
        partial_mods = partial_mods[:count] + permute_xor(partial_mods[count:], "dp", count)
    modulation = partial_mods[0]

    small = jnp.concatenate([conv_attn.reshape(-1), conv_ffn.reshape(-1), b_fc1])
    small = gather_small(small)
    n_one, n_two = (conv_attn.size, conv_attn.size + conv_ffn.size)
    conv_one = small[:, :n_one].reshape(dp, 9, -1).transpose(1, 0, 2).reshape(9, features)
    conv_two = small[:, n_one:n_two].reshape(dp, 9, -1).transpose(1, 0, 2).reshape(9, hidden)
    fc1_bias = small[:, n_two:].reshape(1, hidden)
    qkv_pieces = fetch_group(w_qkv, groups)
    packed = pack_weights(w_proj, w_fc1, w_fc2)
    fetched = fetch_relayed(after(packed, modulation))

    top, end = halo_rows(jnp.moveaxis(latents[:, 0], 1, 0))
    top, end = (top[0], end[0])
    mods = modulation.reshape(micro_count, 6, features)
    micros = range(micro_count)
    places = jnp.stack([strip_at * row_count, map_at, group_at]).astype(jnp.int32)
    scalars = [
        jnp.concatenate(
            [jnp.where(size_tags[at] == 1, side_count, side_count // 2).astype(jnp.int32), places]
        )
        for at in micros
    ]
    kept = [{} for _ in micros]
    turn = (packed, qkv_pieces[0])

    for at in micros:
        if at == micro_count - 1:
            qkv_group = gather_group(qkv_pieces)
            turn = (turn, qkv_group)
        maps = before_attention(at, after(scalars[at], turn), latents, top, end, mods, conv_one)
        turn = maps
        kept[at]["u"] = map_exchange(maps, groups).reshape(-1, features)

    direct = [k for k in range(1, dp) if k & (k - 1) == 0]
    turn = (turn, [fetched[k - 1] for k in direct])
    for at in micros:
        keep = kept[at]
        u = after(keep["u"], turn if at == 0 else kept[at - 1]["logs"])
        keep["u"] = group_exchange(u, groups)
        done = attend(after(scalars[at], turn), keep["u"], qkv_group, score_scale, side_count)
        keep["t"], keep["o"], keep["logs"] = (done[0], done[1 : 1 + groups], done[-1])
        parts = [keep["o"][0]] + [
            permute_xor(keep["o"][k], "strip", k) for k in range(1, groups)
        ]
        if at == micro_count - 1:
            proj_full, fc1_full, fc2_full = unpack_weights(
                after(fetched, kept[0]["logs"]), keep["logs"], w_proj, w_fc1, w_fc2
            )
        maps = join_groups(scalars[at], parts, width)
        turn = (maps, fetched)
        keep["o_maps"] = map_exchange(maps, groups)

    for at in micros:
        keep = kept[at]
        keep["oc"], keep["attn"], keep["x1"], keep["a2"], keep["f"] = expand(
            at,
            after(scalars[at], turn),
            keep["o_maps"],
            latents,
            mods,
            proj_full,
            fc1_full,
            fc1_bias,
        )
        turn = keep["attn"]
        keep["f_halo"] = halo_rows(keep["f"])

    for at in micros:
        keep, grad_type = (kept[at], jnp.bfloat16 if at == micro_count - 1 else jnp.float32)
        prev = None if at == 0 else (term_fc2, term_conv_two, mixed)
        mixed, keep["d_gate2"], keep["d_z"], term_fc2, term_conv_two = ffn_middle(
            at,
            after(scalars[at], turn),
            keep["f"],
            keep["f_halo"],
            conv_two,
            fc2_full,
            cotangent,
            keep["x1"],
            mods,
            prev,
            grad_type,
        )
        turn = keep["d_gate2"]
        keep["z_halo"] = halo_rows(keep["d_z"])

    for at in micros:
        keep, grad_type = (kept[at], jnp.bfloat16 if at == micro_count - 1 else jnp.float32)
        prev = None if at == 0 else (term_fc1, term_fc1_bias, term_proj)
        done = ffn_back(
            at,
            after(scalars[at], turn),
            keep["d_z"],
            keep["z_halo"],
            conv_two,
            fc1_full,
            keep["a2"],
            cotangent,
            keep["x1"],
            keep["attn"],
            keep["oc"],
            proj_full,
            mods,
            prev,
            grad_type,
        )
        keep["d_x"], keep["d_mods"], term_fc1, term_fc1_bias, term_proj = done[1:]
        turn = keep["d_mods"]
        pieces = group_exchange(map_exchange(done[0], groups).reshape(-1, features), groups)
        if width % 128:
            pieces = [
                jnp.pad(
                    lax.dynamic_slice_in_dim(piece, group_at * width, width, 1),
                    ((0, 0), (0, -width % 128)),
                )
                for piece in pieces
            ]
        keep["d_o"] = pieces

    blocks = dp * strips
    wide, narrow = (hidden // blocks, features // blocks)
    small = jnp.concatenate([term_conv_two, term_fc1_bias]).reshape(10, blocks, wide)
    small = small.transpose(1, 0, 2).reshape(blocks, 10 * wide)
    merged = narrow % 8 == 0
    if merged:
        small_rows = -(-10 * wide // features // 8) * 8
        small = jnp.pad(small, ((0, 0), (0, small_rows * features - 10 * wide)))
        small = small.reshape(blocks, small_rows, features).astype(jnp.bfloat16)
        shares, shapes = by_destination(term_fc2, term_fc1, term_proj, small, narrow, dp)
        send = route_core(shares, shapes)
        came = permute_xor(send, "strip", 1)
        turn = (turn, send)

    for at in micros:
        keep, grad_type = (kept[at], jnp.bfloat16 if at == micro_count - 1 else jnp.float32)
        done = attend_back(
            after(scalars[at], turn),
            keep["u"],
            keep["d_o"],
            keep["o"],
            qkv_group,
            keep["t"],
            keep["logs"],
            score_scale,
            side_count,
            None if at == 0 else term_qkv,
            grad_type,
        )
        term_qkv = done[groups]
        parts = [done[0]] + [permute_xor(done[k], "strip", k) for k in range(1, groups)]
        if at == 0 and merged:
            share = core_sum(shares, shapes, after(came, done[0]), dp_at)
            share = [share[0]] + [permute_xor(share[k], "dp", k) for k in range(1, dp)]
            parts = after(parts, share[0])
        if at == micro_count - 1 and merged:
            ready = (done[0], kept[0]["d_u"])
            share = add_up([after(share[0], ready)] + share[1:])
            parts = after(parts, share)
        maps = sum_groups(parts)
        turn = maps
        keep["d_u"] = map_exchange(maps, groups)

    kept_qkv = group_sums(after(term_qkv, turn), groups, width)
    mod_grads = []
    for at in micros:
        keep = kept[at]
        first_row, last_row = edge_rows(keep["d_u"], side_count)
        size = strips
        d_halo = (
            lax.ppermute(last_row, "strip", [(i, i + 1) for i in range(size - 1)]),
            lax.ppermute(first_row, "strip", [(i + 1, i) for i in range(size - 1)]),
        )
        prev = None if at == 0 else (term_conv_one, d_latents)
        d_latents, keep["d_mod1"], term_conv_one = last_stage(
            at,
            after(scalars[at], turn),
            keep["d_u"],
            d_halo,
            latents,
            top,
            end,
            mods,
            conv_one,
            keep["d_x"],
            prev,
        )
        turn = keep["d_mod1"]
        if at == 0:
            parts_qkv = group_parts(kept_qkv, groups)
        if at == 0 and merged:
            among = [list(range(core, strips, 2)) for core in range(2)]
            share = lax.all_to_all(
                after(share, turn), "strip", 0, 0, axis_index_groups=among, tiled=True
            )
        mod_grads.append(
            jnp.concatenate([keep["d_mod1"], keep["d_mods"], keep["d_gate2"]]).reshape(-1)
        )

    if merged:
        total = jnp.sum(share.astype(jnp.float32), axis=0)
        ratio = hidden // features
        g_fc2 = total[: ratio * narrow]
        g_fc1 = total[ratio * narrow : 2 * ratio * narrow].reshape(ratio, narrow, features)
        g_fc1 = g_fc1.transpose(1, 0, 2).reshape(narrow, hidden)
        g_proj = total[2 * ratio * narrow : (2 * ratio + 1) * narrow]
        small = total[(2 * ratio + 1) * narrow :].reshape(-1)
    else:
        g_fc2 = scatter_rows(term_fc2)
        g_fc1 = scatter_rows(term_fc1)
        g_proj = scatter_rows(term_proj)
        small = scatter_rows(small)[0]
    g_conv_two = small[: 9 * wide].reshape(9, wide)
    g_fc1_bias = small[9 * wide : 10 * wide]
    mod_grads.append(term_conv_one.reshape(-1))

    grad_mod = jnp.concatenate(mod_grads)
    step = 1
    while step < strips:
        grad_mod = grad_mod + permute_xor(grad_mod, "strip", step)
        step *= 2
        if step == 4:
            g_qkv = group_columns(after(parts_qkv, grad_mod), groups)
    all_mods = gather_butterfly(grad_mod[None])
    block_at = dp_at * strips + strip_at
    g_conv_one = jnp.sum(all_mods[:, micro_count * 6 * features :], axis=0).reshape(9, features)
    g_conv_one = lax.dynamic_slice_in_dim(g_conv_one, block_at * narrow, narrow, 1)
    all_mods = all_mods[:, : micro_count * 6 * features].reshape(-1, 6 * features)
    conds_here = lax.dynamic_slice_in_dim(
        jnp.concatenate(conds), block_at * narrow, narrow, 1
    )
    g_ada = lax.dot_general(
        conds_here, all_mods, (((0,), (0,)), ((), ())), precision=lax.Precision.HIGHEST
    )
    ada_wide_block = 6 * features // blocks
    g_ada_bias = lax.dynamic_slice_in_dim(
        jnp.sum(all_mods, axis=0), block_at * ada_wide_block, ada_wide_block, 0
    )
    return (
        mixed,
        d_latents,
        g_ada,
        g_ada_bias,
        g_conv_one,
        g_qkv,
        g_proj,
        g_fc1,
        g_fc1_bias,
        g_conv_two,
        g_fc2,
    )


def solution(mesh):
    return jax.shard_map(
        shards,
        mesh=mesh,
        in_specs=(
            P(None, "dp", "strip", None, None),
            P(None, "dp"),
            P(None, "dp"),
            P("dp", None),
            P("dp"),
            P(None, "dp"),
            P("dp", None),
            P("dp", None),
            P("dp", None),
            P("dp"),
            P(None, "dp"),
            P("dp", None),
            P(None, "dp", "strip", None, None),
        ),
        out_specs=(
            P(None, "dp", "strip", None, None),
            P(None, "dp", "strip", None, None),
            P(("dp", "strip"), None),
            P(("dp", "strip")),
            P(None, ("dp", "strip")),
            P(("dp", "strip"), None),
            P(("dp", "strip"), None),
            P(("dp", "strip"), None),
            P(("dp", "strip")),
            P(None, ("dp", "strip")),
            P(("dp", "strip"), None),
        ),
        check_vma=False,
    )
```

```python
import functools
import math

import jax
import jax.numpy as jnp
from jax import lax
from jax.experimental import pallas as pl
from jax.experimental.pallas import tpu as pltpu
from jax.sharding import PartitionSpec as P

HEADS = 12
COVER = pl.CostEstimate(flops=200_000_000_000, transcendentals=0, bytes_accessed=0)
BRIEF = pl.CostEstimate(flops=0, transcendentals=0, bytes_accessed=0)


root_half = 0.7071067811865476
inverse_root_tau = 0.3989422804014327


def permute_xor(x, axis, step):
    size = lax.axis_size(axis)
    return lax.ppermute(x, axis, [(i, i ^ step) for i in range(size)])


def pick(x, at, axis=0):
    return lax.dynamic_index_in_dim(x, at, axis, keepdims=False)


def halo_rows(first, last):
    size = lax.axis_size("strip")
    up = [(i, i + 1) for i in range(size - 1)]
    down = [(i + 1, i) for i in range(size - 1)]
    return (lax.ppermute(last, "strip", up), lax.ppermute(first, "strip", down))


def place_blocks(blocks, me):
    stacked = jnp.stack(blocks)
    return jnp.stack([pick(stacked, me ^ at) for at in range(len(blocks))])


def gather_butterfly(x):
    step = 1
    while step < lax.axis_size("dp"):
        x = jnp.concatenate([x, permute_xor(x, "dp", step)])
        step *= 2
    return x


def gather_small(x):
    me = lax.axis_index("dp")
    blocks = [x] + [permute_xor(x, "dp", k) for k in range(1, lax.axis_size("dp"))]
    return place_blocks(blocks, me)


def after(x, *done):
    return lax.optimization_barrier((x, done))[0]


HBM = pl.BlockSpec(memory_space=pl.ANY)


def move_all(copies):
    for copy in copies:
        copy.start()
    for copy in copies:
        copy.wait()


def rows_at(start, size):
    return pl.ds(pl.multiple_of(start, 8), size)


def tie(*values):
    return lax.optimization_barrier(values)


def assemble_kernel(at_ref, *refs):
    pieces, whole, sem = (refs[:-2], refs[-2], refs[-1])
    move_all(
        [
            pltpu.make_async_copy(
                piece, whole.at[:, rows_at(at_ref[i], piece.shape[1]), :], sem.at[i]
            )
            for i, piece in enumerate(pieces)
        ]
    )


def assemble(pieces, starts, shape):
    return pl.pallas_call(
        assemble_kernel,
        grid_spec=pltpu.PrefetchScalarGridSpec(
            num_scalar_prefetch=1,
            grid=(1,),
            in_specs=[HBM] * len(pieces),
            out_specs=whole_spec(shape),
            scratch_shapes=[pltpu.SemaphoreType.DMA((len(pieces),))],
        ),
        out_shape=jax.ShapeDtypeStruct(shape, pieces[0].dtype),
        cost_estimate=COVER,
        name="assemble",
    )(jnp.stack(starts).astype(jnp.int32), *pieces)


def pack_layout(proj, fc1, fc2):
    features = proj.shape[1]
    sizes = [proj.shape[0] // 2]
    sizes += [fc1.shape[0] // 2] * (fc1.shape[1] // features) + [fc2.shape[0] // 2]
    starts = [sum(sizes[:i]) for i in range(len(sizes))]
    return sizes, starts


def half_of(refs, row, i, size, features):
    if i == 0:
        return refs[0].at[rows_at(row, size), :]
    if i == len(refs[3]) - 1:
        return refs[2].at[rows_at(row, size), :]
    return refs[1].at[rows_at(row, size), (i - 1) * features : i * features]


def pack_kernel(at_ref, proj, fc1, fc2, out, sem):
    sizes, starts = pack_layout(proj, fc1, fc2)
    copies = []
    for i, (size, start) in enumerate(zip(sizes, starts)):
        source = half_of((proj, fc1, fc2, sizes), at_ref[0] * size, i, size, proj.shape[1])
        copies.append(pltpu.make_async_copy(source, out.at[start : start + size, :], sem.at[i]))
    move_all(copies)


def pack_weights(proj, fc1, fc2):
    core = lax.axis_index("strip") & 1
    sizes, starts = pack_layout(proj, fc1, fc2)
    shape = (starts[-1] + sizes[-1], proj.shape[1])
    return pl.pallas_call(
        pack_kernel,
        grid_spec=pltpu.PrefetchScalarGridSpec(
            num_scalar_prefetch=1,
            grid=(1,),
            in_specs=[HBM] * 3,
            out_specs=whole_spec(shape),
            scratch_shapes=[pltpu.SemaphoreType.DMA((len(sizes),))],
        ),
        out_shape=jax.ShapeDtypeStruct(shape, proj.dtype),
        cost_estimate=BRIEF,
        name="pack_weights",
    )(core[None].astype(jnp.int32), proj, fc1, fc2)


def fetch_relayed(x):
    came, step = ({0: x}, 1)
    while step < lax.axis_size("dp"):
        for k in range(step):
            came[step + k] = permute_xor(came[k], "dp", step)
        step *= 2
    return [came[k] for k in range(1, len(came))]


def unpack_kernel(count, at_ref, *refs):
    own, halves, wholes, sem = (refs[:3], refs[3 : 3 + count], refs[3 + count : 6 + count], refs[-1])
    sizes, starts = pack_layout(*own)
    features = own[0].shape[1]
    copies = []
    for ref, whole in zip(own, wholes):
        target = whole.at[rows_at(at_ref[0] * ref.shape[0], ref.shape[0]), :]
        copies.append(pltpu.make_async_copy(ref, target, sem.at[len(copies)]))
    for k, half in enumerate(halves):
        for i, (size, start) in enumerate(zip(sizes, starts)):
            row = (2 * at_ref[1 + 2 * k] + at_ref[2 + 2 * k]) * size
            target = half_of(wholes + (sizes,), row, i, size, features)
            copies.append(
                pltpu.make_async_copy(
                    half.at[start : start + size, :], target, sem.at[len(copies)]
                )
            )
    move_all(copies)


def unpack_weights(fetched, turn, proj, fc1, fc2):
    size, me = (lax.axis_size("dp"), lax.axis_index("dp"))
    core = lax.axis_index("strip") & 1
    halves, places = ([], [me])
    for k, mine in enumerate(fetched, 1):
        halves += [mine, permute_xor(mine, "strip", 1)]
        places += [me ^ k, core, me ^ k, 1 - core]
    shapes = [(size * w.shape[0], w.shape[1]) for w in (proj, fc1, fc2)]
    copies = 3 + len(halves) * len(pack_layout(proj, fc1, fc2)[0])
    return pl.pallas_call(
        functools.partial(unpack_kernel, len(halves)),
        grid_spec=pltpu.PrefetchScalarGridSpec(
            num_scalar_prefetch=1,
            grid=(1,),
            in_specs=[HBM] * (3 + len(halves)),
            out_specs=[whole_spec(shape) for shape in shapes],
            scratch_shapes=[pltpu.SemaphoreType.DMA((copies,))],
        ),
        out_shape=[jax.ShapeDtypeStruct(shape, proj.dtype) for shape in shapes],
        cost_estimate=BRIEF,
        name="unpack_weights",
    )(after(jnp.stack(places).astype(jnp.int32), turn), proj, fc1, fc2, *halves)


def fetch_group(w, groups, turn):
    rows, cols = w.shape
    width = cols // 3 // groups
    group = lax.axis_index("strip") % groups
    mine = pick(w.reshape(rows, 3, groups, width), group, 2).transpose(1, 0, 2)
    mine, turn = tie(jnp.pad(mine, ((0, 0), (0, 0), (0, -width % 128))), turn)
    pieces = [mine] + [permute_xor(mine, "dp", k) for k in range(1, lax.axis_size("dp"))]
    return pieces, turn


def gather_group(pieces):
    me, rows = (lax.axis_index("dp"), pieces[0].shape[1])
    starts = [(me ^ k) * rows for k in range(len(pieces))]
    return assemble(pieces, starts, (3, len(pieces) * rows, pieces[0].shape[2]))


def exchange_sum(x, axis, me, step, wire, dim=0):
    total = pick(x, me, dim).astype(jnp.float32)
    parts = [
        permute_xor(pick(x, me ^ k, dim).astype(wire), axis, k * step)
        for k in range(1, x.shape[dim])
    ]
    for part in parts:
        total = total + part.astype(jnp.float32)
    return total


def scatter_rows(g, wire=jnp.bfloat16):
    rows, cols = g.shape
    dp, strips = (lax.axis_size("dp"), lax.axis_size("strip"))
    strip = lax.axis_index("strip")
    shaped = g.reshape(dp, strips // 2, 2, rows // dp // strips, cols)
    core = strip & 1
    sent = permute_xor(pick(shaped, 1 - core, 2).astype(wire), "strip", 1)
    kept = pick(shaped, core, 2).astype(jnp.float32) + sent.astype(jnp.float32)
    kept = exchange_sum(kept, "dp", lax.axis_index("dp"), 1, wire)
    return exchange_sum(kept, "strip", strip >> 1, 2, wire)


def group_sums(g, groups, width, wire=jnp.bfloat16):
    rows = g.shape[1]
    dp, strips = (lax.axis_size("dp"), lax.axis_size("strip"))
    kept = g[:, :, :width].reshape(3, dp, strips // groups, groups, rows // dp // strips, width)
    return exchange_sum(kept, "dp", lax.axis_index("dp"), 1, wire, 1)


def group_parts(kept, groups, wire=jnp.bfloat16):
    me = lax.axis_index("strip") // groups
    return [pick(kept, me, 1)] + [
        permute_xor(pick(kept, me ^ k, 1).astype(wire), "strip", k * groups)
        for k in range(1, kept.shape[1])
    ]


def group_columns(parts, groups, wire=jnp.bfloat16):
    kept = parts[0]
    for part in parts[1:]:
        kept = kept + part.astype(jnp.float32)
    group = lax.axis_index("strip") % groups
    blocks = [pick(kept, group, 1)] + [
        permute_xor(pick(kept, group ^ k, 1).astype(wire), "strip", k).astype(jnp.float32)
        for k in range(1, groups)
    ]
    whole = place_blocks(blocks, group)
    return whole.transpose(2, 1, 0, 3).reshape(whole.shape[2], -1)


def lay_rows(out, fc2, fc1, proj, small):
    features = proj.shape[-1]
    parts = [fc2]
    parts += [fc1[:, :, i : i + features] for i in range(0, fc1.shape[-1], features)]
    start = 0
    for part in parts + [proj, small]:
        out[:, start : start + part.shape[1], :] = part
        start += part.shape[1]


def route_kernel(at_ref, fc2, fc1, proj, small, out):
    lay_rows(out, fc2[...], fc1[...], proj[...], small[...])


def by_destination(fc2, fc1, proj, small, rows, dp):
    pairs = small.shape[0] // 2 // dp
    arrays = [
        x.reshape(dp, pairs, 2, -1, x.shape[-1]) for x in (fc2, fc1, proj, small)
    ]
    shapes = [(None, pairs, None) + x.shape[3:] for x in arrays]
    return arrays, shapes


def route_core(arrays, shapes):
    dp, pairs = arrays[0].shape[:2]
    features = arrays[0].shape[-1]
    height = sum(x.shape[3] * x.shape[4] for x in arrays) // features
    core = lax.axis_index("strip") & 1
    return pl.pallas_call(
        route_kernel,
        grid_spec=pltpu.PrefetchScalarGridSpec(
            num_scalar_prefetch=1,
            grid=(dp,),
            in_specs=[
                pl.BlockSpec(shape, lambda j, s: (j, 0, 1 - s[0], 0, 0)) for shape in shapes
            ],
            out_specs=pl.BlockSpec((pairs, height, features), lambda j, s: (j, 0, 0)),
        ),
        out_shape=jax.ShapeDtypeStruct((dp * pairs, height, features), arrays[0].dtype),
        cost_estimate=COVER,
        name="route_core",
    )(core[None].astype(jnp.int32), *arrays)


def core_sum_kernel(at_ref, fc2, fc1, proj, small, came, x_send, x_keep, y_send, y_keep, kept):
    lay_rows(kept, fc2[...], fc1[...], proj[...], small[...])
    total = (kept[...].astype(jnp.float32) + came[...].astype(jnp.float32)).astype(kept.dtype)
    half = total.shape[0] // 2
    for k in range(4):

        @pl.when(pl.program_id(0) == k)
        def _():
            (x_send if k & 1 else x_keep)[k >> 1] = total[:half]
            (y_send if k >> 1 else y_keep)[k & 1] = total[half:]


def core_sum(arrays, shapes, came, me):
    dp, pairs = arrays[0].shape[:2]
    block = (pairs,) + came.shape[1:]
    out = (2, pairs // 2) + came.shape[1:]
    core = lax.axis_index("strip") & 1
    return pl.pallas_call(
        core_sum_kernel,
        grid_spec=pltpu.PrefetchScalarGridSpec(
            num_scalar_prefetch=1,
            grid=(dp,),
            in_specs=[
                pl.BlockSpec(shape, lambda j, s: (s[1] ^ j, 0, s[0], 0, 0)) for shape in shapes
            ]
            + [pl.BlockSpec(block, lambda j, s: (s[1] ^ j, 0, 0))],
            out_specs=[whole_spec(out)] * 4,
            scratch_shapes=[pltpu.VMEM(block, came.dtype)],
        ),
        out_shape=[jax.ShapeDtypeStruct(out, came.dtype)] * 4,
        cost_estimate=COVER,
        name="core_sum",
    )(jnp.stack([core, me]).astype(jnp.int32), *arrays, came)


def turn_kernel(x_keep, x_came, y_keep, y_came, own, x_send, y_send):
    half = own.shape[0] // 2

    def both(keep, came, k):
        return (keep[k].astype(jnp.float32) + came[k].astype(jnp.float32)).astype(own.dtype)

    own[:half] = both(x_keep, x_came, 0)
    own[half:] = both(y_keep, y_came, 0)
    x_send[...] = both(x_keep, x_came, 1)
    y_send[...] = both(y_keep, y_came, 1)


def turn_sums(x_keep, x_came, y_keep, y_came):
    _, half, rows, cols = x_keep.shape
    block = rows // 2
    pair = pl.BlockSpec((2, half, block, cols), lambda j: (0, 0, j, 0))
    one = pl.BlockSpec((half, block, cols), lambda j: (0, j, 0))
    whole = pl.BlockSpec((2 * half, block, cols), lambda j: (0, j, 0))
    shape = (half, rows, cols)
    return pl.pallas_call(
        turn_kernel,
        grid=(rows // block,),
        in_specs=[pair] * 4,
        out_specs=[whole, one, one],
        out_shape=[
            jax.ShapeDtypeStruct((2 * half,) + shape[1:], x_keep.dtype),
            jax.ShapeDtypeStruct(shape, x_keep.dtype),
            jax.ShapeDtypeStruct(shape, x_keep.dtype),
        ],
        cost_estimate=COVER,
        name="turn_sums",
    )(x_keep, x_came, y_keep, y_came)


def add_kernel(at_ref, own, x_came, y_came, *refs):
    outs, kept = (refs[:-1], refs[-1])
    half = own.shape[0] // 2
    for at, came in ((slice(0, half), x_came), (slice(half, None), y_came)):
        total = own[at].astype(jnp.float32) + came[...].astype(jnp.float32)
        kept[at] = total.astype(own.dtype)
    for k, out in enumerate(outs):
        out[...] = kept[at_ref[0] ^ k]


def add_up(own, x_came, y_came, me):
    pairs, rows, cols = own.shape
    return pl.pallas_call(
        add_kernel,
        grid_spec=pltpu.PrefetchScalarGridSpec(
            num_scalar_prefetch=1,
            grid=(1,),
            in_specs=[whole_spec(x.shape) for x in (own, x_came, y_came)],
            out_specs=[whole_spec((rows, cols))] * pairs,
            scratch_shapes=[pltpu.VMEM(own.shape, own.dtype)],
        ),
        out_shape=[jax.ShapeDtypeStruct((rows, cols), own.dtype)] * pairs,
        cost_estimate=BRIEF,
        name="add_up",
    )(me[None].astype(jnp.int32), own, x_came, y_came)


def map_exchange(maps, groups):
    size = lax.axis_size("strip")
    among = [[m * groups + g for m in range(4)] for g in range(groups)]
    return lax.all_to_all(maps, "strip", 0, 0, axis_index_groups=among, tiled=True)


def group_exchange(x, groups):
    return [x] + [permute_xor(x, "strip", k) for k in range(1, groups)]


def silu_of(values):
    return values / (1.0 + jnp.exp(-values))


def embed_times(stamps, features):
    half_count = features // 2
    frequency = jnp.exp(-math.log(10000.0) * jnp.arange(half_count, dtype=jnp.float32) / half_count)
    angles = stamps[:, None] * frequency[None, :]
    return jnp.concatenate([jnp.cos(angles), jnp.sin(angles)], axis=1)

def normalize(values):
    centre = values - jnp.mean(values, axis=-1, keepdims=True)
    inverse = lax.rsqrt(jnp.mean(centre * centre, axis=-1, keepdims=True) + 1e-06)
    return (centre * inverse, inverse)


def norm_back(normed, inverse, upstream):
    return inverse * (
        upstream
        - jnp.mean(upstream, axis=-1, keepdims=True)
        - normed * jnp.mean(upstream * normed, axis=-1, keepdims=True)
    )


def dot_nn(a, b):
    return lax.dot_general(a, b, (((1,), (0,)), ((), ())), preferred_element_type=jnp.float32)


def dot_nt(a, b):
    return lax.dot_general(a, b, (((1,), (1,)), ((), ())), preferred_element_type=jnp.float32)


def dot_tn(a, b):
    return lax.dot_general(a, b, (((0,), (0,)), ((), ())), preferred_element_type=jnp.float32)


def key_mask(s_ref, groups, tokens, cols):
    block = tokens // groups // 4
    token = lax.broadcasted_iota(jnp.int32, (tokens, 128), 0)
    piece, within = (token // block, token % block)
    strip = (piece % 4) * groups + (s_ref[3] ^ (piece // 4))
    row = strip * (block // (cols // 2)) + within // (cols // 2)
    half = s_ref[0] // 2
    return jnp.where((row < half) & (within % (cols // 2) < half), 0.0, -1e30)


def store_sum(ref, part):
    @pl.when(pl.program_id(0) == 0)
    def _():
        ref[...] = part

    @pl.when(pl.program_id(0) > 0)
    def _():
        ref[...] += part


def attend_kernel(chunk, scale, groups, cols, s_ref, *refs):
    pieces, w_ref, t_ref = (refs[:groups], refs[groups], refs[groups + 1])
    o_refs = refs[groups + 2 : 2 * groups + 2]
    l_ref, u_sc, b_sc, q_sc, k_sc, v_sc, o_sc, l_sc = refs[2 * groups + 2 :]
    tokens = u_sc.shape[0]

    @pl.when(pl.program_id(0) == 0)
    def _():
        size = pieces[0].shape[0]
        for i, piece in enumerate(pieces):
            u_sc[i * size : (i + 1) * size, :] = piece[...]
        b_sc[...] = key_mask(s_ref, groups, tokens, cols)

    u = u_sc[...]
    for part in range(3):
        t_ref[part] = dot_nn(u, w_ref[part]).astype(jnp.bfloat16)
    q, k, v = (t_ref[0].astype(jnp.float32), t_ref[1].astype(jnp.float32), t_ref[2].astype(jnp.float32))
    lane = lax.broadcasted_iota(jnp.int32, (tokens, 128), 1)
    bias = b_sc[...]
    for head in range(2):
        here = (lane < 64) if head == 0 else (lane >= 64)
        spare = lane == (64 if head == 0 else 0)
        q_sc[head] = jnp.where(here, q * scale, jnp.where(spare, 1.0, 0.0)).astype(jnp.bfloat16)
        k_sc[head] = jnp.where(here, k, jnp.where(spare, bias, 0.0)).astype(jnp.bfloat16)
        v_sc[head] = jnp.where(here, v, 0.0).astype(jnp.bfloat16)

    def body(i, carry):
        at = pl.ds(pl.multiple_of(i * chunk, chunk), chunk)
        outs, logs = ([], [])
        for head in range(2):
            s = dot_nt(q_sc[head, at, :], k_sc[head])
            top = jnp.max(s, axis=1, keepdims=True)
            p = jnp.exp(s - top)
            total = jnp.sum(p, axis=1, keepdims=True)
            outs.append(dot_nn(p.astype(jnp.bfloat16), v_sc[head]) * (1.0 / total))
            logs.append(top + jnp.log(total))
        o_sc[at, :] = (outs[0] + outs[1]).astype(jnp.bfloat16)
        l_sc[at, :] = jnp.where(
            lax.broadcasted_iota(jnp.int32, (chunk, 128), 1) < 64, logs[0], logs[1]
        )
        return carry

    lax.fori_loop(0, tokens // chunk, body, 0, unroll=True)
    size = tokens // groups
    for i, o_ref in enumerate(o_refs):
        o_ref[...] = o_sc[i * size : (i + 1) * size, :]
    logs = l_sc[...].T
    l_ref[...] = jnp.concatenate(
        [logs[0:1], logs[64:65], jnp.zeros((6, tokens), jnp.float32)], axis=0
    )[None]


def attend(scalars, pieces, w, score_scale, cols):
    groups = len(pieces)
    features, width = w.shape[1:]
    tokens = groups * pieces[0].shape[0]
    chunk = min(512, tokens)
    piece_spec = pl.BlockSpec(pieces[0].shape, lambda j, s: (0, 0))
    return pl.pallas_call(
        functools.partial(attend_kernel, chunk, score_scale, groups, cols),
        grid_spec=pltpu.PrefetchScalarGridSpec(
            num_scalar_prefetch=1,
            grid=(width // 128,),
            in_specs=[piece_spec] * len(pieces)
            + [pl.BlockSpec((3, features, 128), lambda j, s: (0, 0, j))],
            out_specs=[pl.BlockSpec((3, tokens, 128), lambda j, s: (0, 0, j))]
            + [pl.BlockSpec((tokens // groups, 128), lambda j, s: (0, j))] * groups
            + [pl.BlockSpec((1, 8, tokens), lambda j, s: (j, 0, 0))],
            scratch_shapes=[
                pltpu.VMEM((tokens, features), jnp.bfloat16),
                pltpu.VMEM((tokens, 128), jnp.float32),
            ]
            + [pltpu.VMEM((2, tokens, 128), jnp.bfloat16)] * 3
            + [pltpu.VMEM((tokens, 128), jnp.bfloat16), pltpu.VMEM((tokens, 128), jnp.float32)],
        ),
        out_shape=[jax.ShapeDtypeStruct((3, tokens, width), jnp.bfloat16)]
        + [jax.ShapeDtypeStruct((tokens // groups, width), jnp.bfloat16)] * groups
        + [jax.ShapeDtypeStruct((width // 128, 8, tokens), jnp.float32)],
        cost_estimate=COVER,
        name="attend_forward",
    )(scalars, *pieces, w)


def attend_back_kernel(chunk, scale, groups, cols, first, s_ref, *refs):
    pieces, do_pieces, o_refs = (refs[:groups], refs[groups : 2 * groups], refs[2 * groups : 3 * groups])
    w_ref, t_ref, l_ref = refs[3 * groups : 3 * groups + 3]
    rest = refs[3 * groups + 3 :]
    if not first:
        prev_ref, rest = (rest[0], rest[1:])
    du_refs, g_ref = (rest[:groups], rest[groups])
    u_sc, b_sc, o_sc, din_sc, q_sc, k_sc, do_sc, dq_sc, dt_sc, d_sc = rest[groups + 1 :]
    tokens = u_sc.shape[0]
    size = pieces[0].shape[0]

    @pl.when(pl.program_id(0) == 0)
    def _():
        for i, piece in enumerate(pieces):
            u_sc[i * size : (i + 1) * size, :] = piece[...]
        b_sc[...] = key_mask(s_ref, groups, tokens, cols)

    for i, piece in enumerate(do_pieces):
        din_sc[i * size : (i + 1) * size, :] = piece[...]
    for i, piece in enumerate(o_refs):
        o_sc[i * size : (i + 1) * size, :] = piece[...]
    q, k, do = (t_ref[0].astype(jnp.float32), t_ref[1].astype(jnp.float32), din_sc[...])
    lane = lax.broadcasted_iota(jnp.int32, (tokens, 128), 1)
    bias = b_sc[...]
    do = do.astype(jnp.float32)
    inner = (do * o_sc[...].astype(jnp.float32)).T
    for head in range(2):
        here = (lane < 64) if head == 0 else (lane >= 64)
        spare = lane == (64 if head == 0 else 0)
        q_sc[head] = jnp.where(here, q * scale, jnp.where(spare, 1.0, 0.0)).astype(jnp.bfloat16)
        k_sc[head] = jnp.where(here, k, jnp.where(spare, bias, 0.0)).astype(jnp.bfloat16)
        do_sc[head] = jnp.where(here, do, 0.0).astype(jnp.bfloat16)
        d_sc[head : head + 1, :] = jnp.sum(
            inner[64 * head : 64 * head + 64], axis=0, keepdims=True
        )
    dq_sc[...] = jnp.zeros_like(dq_sc)

    def body(i, carry):
        at = pl.ds(pl.multiple_of(i * chunk, chunk), chunk)
        lanes = lax.broadcasted_iota(jnp.int32, (chunk, 128), 1)
        d_k, d_v, d_q = ([], [], [])
        for head in range(2):
            here = (lanes < 64) if head == 0 else (lanes >= 64)
            s = dot_nt(k_sc[head, at, :], q_sc[head])
            p = jnp.exp(s - l_ref[0, head : head + 1, :])
            d_p = dot_nt(t_ref[2, at, :], do_sc[head])
            d_s = (p * (d_p - d_sc[head : head + 1, :])).astype(jnp.bfloat16)
            d_v.append(dot_nn(p.astype(jnp.bfloat16), do_sc[head]))
            d_k.append(dot_nn(d_s, q_sc[head]))
            keys = jnp.where(here, t_ref[1, at, :].astype(jnp.float32), 0.0).astype(jnp.bfloat16)
            d_q.append(dot_tn(d_s, keys))
        dq_sc[...] += d_q[0] + d_q[1]
        dt_sc[at, 128:256] = jnp.where(lanes < 64, d_k[0], d_k[1]).astype(jnp.bfloat16)
        dt_sc[at, 256:384] = (d_v[0] + d_v[1]).astype(jnp.bfloat16)
        return carry

    lax.fori_loop(0, tokens // chunk, body, 0, unroll=True)
    dt_sc[:, 0:128] = (dq_sc[...] * scale).astype(jnp.bfloat16)
    for i, du_ref in enumerate(du_refs):
        at = slice(i * size, (i + 1) * size)
        part = dot_nt(dt_sc[at, 0:128], w_ref[0])
        part = part + dot_nt(dt_sc[at, 128:256], w_ref[1])
        part = part + dot_nt(dt_sc[at, 256:384], w_ref[2])
        store_sum(du_ref, part)
    grad = dot_tn(u_sc[...], dt_sc[...])
    for at in range(3):
        piece = grad[:, 128 * at : 128 * at + 128]
        if not first:
            piece = piece + prev_ref[at]
        g_ref[at] = piece.astype(g_ref.dtype)


def attend_back(scalars, pieces, d_pieces, outs, w, t, logs, score_scale, cols, prev, grad_type):
    groups = len(outs)
    features, width = w.shape[1:]
    tokens = t.shape[1]
    chunk = min(256, tokens)
    size = pieces[0].shape[0]
    blocks = width // 128
    weight_spec = pl.BlockSpec((3, features, 128), lambda j, s: (0, 0, j))
    offset = 0 if d_pieces[0].shape[1] == width else blocks
    args = list(pieces) + list(d_pieces) + list(outs) + [w, t, logs]
    args += [] if prev is None else [prev]
    return pl.pallas_call(
        functools.partial(attend_back_kernel, chunk, score_scale, groups, cols, prev is None),
        grid_spec=pltpu.PrefetchScalarGridSpec(
            num_scalar_prefetch=1,
            grid=(blocks,),
            in_specs=[pl.BlockSpec((size, features), lambda j, s: (0, 0))] * len(pieces)
            + [pl.BlockSpec((size, 128), lambda j, s: (0, s[3] * offset + j))] * len(d_pieces)
            + [pl.BlockSpec((size, 128), lambda j, s: (0, j))] * groups
            + [
                weight_spec,
                pl.BlockSpec((3, tokens, 128), lambda j, s: (0, 0, j)),
                pl.BlockSpec((1, 8, tokens), lambda j, s: (j, 0, 0)),
            ]
            + ([] if prev is None else [weight_spec]),
            out_specs=[pl.BlockSpec((size, features), lambda j, s: (0, 0))] * groups
            + [weight_spec],
            scratch_shapes=[
                pltpu.VMEM((tokens, features), jnp.bfloat16),
                pltpu.VMEM((tokens, 128), jnp.float32),
                pltpu.VMEM((tokens, 128), jnp.bfloat16),
                pltpu.VMEM((tokens, 128), jnp.bfloat16),
            ]
            + [pltpu.VMEM((2, tokens, 128), jnp.bfloat16)] * 3
            + [
                pltpu.VMEM((tokens, 128), jnp.float32),
                pltpu.VMEM((tokens, 384), jnp.bfloat16),
                pltpu.VMEM((8, tokens), jnp.float32),
            ],
        ),
        out_shape=[jax.ShapeDtypeStruct((size, features), jnp.float32)] * groups
        + [jax.ShapeDtypeStruct(w.shape, grad_type)],
        cost_estimate=COVER,
        name="attend_backward",
    )(scalars, *args)


def shift_cols(x, by, col):
    size = x.shape[0]
    rolled = pltpu.roll(x, (-by) % size, 0)
    return jnp.where(col == (size - 1 if by > 0 else 0), 0.0, rolled)


def wide_taps(c_ref, lanes, cols):
    return [
        jnp.broadcast_to(c_ref[k : k + 1, lanes].astype(jnp.float32), (cols, 128)) for k in range(9)
    ]


def sublane_sum(x):
    return jnp.sum(x.reshape(x.shape[0] // 8, 8, 128), axis=0)


def modulate(x, m_ref, shift_at, col, row, side):
    normed, _ = normalize(x.astype(jnp.float32))
    value = normed * (1.0 + m_ref[shift_at + 1 : shift_at + 2, :]) + m_ref[shift_at : shift_at + 1, :]
    live = (col < side) & (row >= 0) & (row < side)
    return jnp.where(live, value, 0.0).astype(jnp.bfloat16)


def modulated_rows(a_sc, s_ref, x_ref, top_ref, end_ref, m_ref):
    rows, cols, features = x_ref.shape
    side, row_zero = (s_ref[0], s_ref[1])
    col = lax.broadcasted_iota(jnp.int32, (cols, features), 0)
    a_sc[0] = modulate(top_ref[...], m_ref, 0, col, row_zero - 1, side)
    a_sc[rows + 1] = modulate(end_ref[...], m_ref, 0, col, row_zero + rows, side)

    def body(r, carry):
        a_sc[r + 1] = modulate(x_ref[r], m_ref, 0, col, row_zero + r, side)
        return carry

    lax.fori_loop(0, rows, body, 0)


def to_maps(canvas, maps_ref):
    blocks, rows, cols, _ = canvas.shape
    half = cols // 2

    def body(r, carry):
        at = pl.ds(pl.multiple_of(r * half, half), half)
        for m in range(4):
            for b in range(blocks):
                part = canvas[b, 2 * r + m // 2, pl.ds(m % 2, half, stride=2), :]
                maps_ref[m, at, 128 * b : 128 * b + 128] = part.astype(jnp.bfloat16)
        return carry

    lax.fori_loop(0, rows // 2, body, 0)


def from_maps(maps_ref, canvas, row_offset):
    half = canvas.shape[2] // 2
    rows = maps_ref.shape[1] // half * 2

    def body(r, carry):
        at = pl.ds(pl.multiple_of(r * half, half), half)
        for m in range(4):
            for b in range(canvas.shape[0]):
                part = maps_ref[m, at, 128 * b : 128 * b + 128].astype(jnp.float32)
                canvas[b, row_offset + 2 * r + m // 2, pl.ds(m % 2, half, stride=2), :] = part
        return carry

    lax.fori_loop(0, rows // 2, body, 0)


def before_kernel(s_ref, x_ref, top_ref, end_ref, m_ref, c_ref, *refs):
    maps_ref, a_sc, t_sc = refs
    rows, cols, features = x_ref.shape
    modulated_rows(a_sc, s_ref, x_ref, top_ref, end_ref, m_ref)
    col = lax.broadcasted_iota(jnp.int32, (cols, 128), 0)
    for first in range(0, features, 128):
        lanes = slice(first, first + 128)
        taps = wide_taps(c_ref, lanes, cols)

        def body(r, carry):
            x = [a_sc[r + i, :, lanes].astype(jnp.float32) for i in range(3)]
            a = [x[0] * taps[j] + x[1] * taps[3 + j] + x[2] * taps[6 + j] for j in range(3)]
            t_sc[first // 128, r] = a[1] + shift_cols(a[0], -1, col) + shift_cols(a[2], 1, col)
            return carry

        lax.fori_loop(0, rows, body, 0)
    to_maps(t_sc, maps_ref)


def canvas_specs(latents, at):
    rows, cols, features = latents.shape[2:]
    return [
        pl.BlockSpec((None, None, rows, cols, features), lambda j, s: (at, 0, 0, 0, 0)),
        pl.BlockSpec((None, cols, features), lambda j, s: (at, 0, 0)),
        pl.BlockSpec((None, cols, features), lambda j, s: (at, 0, 0)),
        pl.BlockSpec((None, 6, features), lambda j, s: (at, 0, 0)),
    ]


def whole_spec(shape):
    return pl.BlockSpec(shape, lambda j, s: (0,) * len(shape))


def before_attention(at, scalars, latents, top, end, mods, taps):
    rows, cols, features = latents.shape[2:]
    maps = (4, rows * cols // 4, features)
    return pl.pallas_call(
        before_kernel,
        grid_spec=pltpu.PrefetchScalarGridSpec(
            num_scalar_prefetch=1,
            grid=(1,),
            in_specs=canvas_specs(latents, at) + [whole_spec(taps.shape)],
            out_specs=whole_spec(maps),
            scratch_shapes=[
                pltpu.VMEM((rows + 2, cols, features), jnp.bfloat16),
                pltpu.VMEM((features // 128, rows, cols, 128), jnp.float32),
            ],
        ),
        out_shape=jax.ShapeDtypeStruct(maps, jnp.bfloat16),
        cost_estimate=COVER,
        name="before_attention",
    )(scalars, latents, top, end, mods, taps)


def join_kernel(s_ref, mine_ref, other_ref, out_ref):
    width = mine_ref.shape[1]

    def write(low_ref, high_ref):
        out_ref[:, :width] = low_ref[...]
        out_ref[:, width:] = high_ref[...]

    @pl.when(s_ref[3] == 0)
    def _():
        write(mine_ref, other_ref)

    @pl.when(s_ref[3] == 1)
    def _():
        write(other_ref, mine_ref)


def join_groups(scalars, parts, width):
    groups = len(parts)
    tokens = parts[0].shape[0]
    shape = (tokens, groups * width)
    if groups != 2 or parts[0].shape[1] != width:
        whole = place_blocks([part[:, :width] for part in parts], scalars[3])
        whole = whole.transpose(1, 0, 2)
    else:
        whole = pl.pallas_call(
            join_kernel,
            grid_spec=pltpu.PrefetchScalarGridSpec(
                num_scalar_prefetch=1,
                grid=(1,),
                in_specs=[whole_spec(part.shape) for part in parts],
                out_specs=whole_spec(shape),
            ),
            out_shape=jax.ShapeDtypeStruct(shape, parts[0].dtype),
            cost_estimate=BRIEF,
            name="join_groups",
        )(scalars, *parts)
    return whole.reshape(4, tokens // 4, groups * width)


def sum_kernel(count, *refs):
    total = refs[0][...]
    for part in refs[1:count]:
        total = total + part[...]
    refs[count][...] = total.astype(refs[count].dtype)


def sum_groups(parts):
    tokens, features = parts[0].shape
    total = pl.pallas_call(
        functools.partial(sum_kernel, len(parts)),
        out_shape=jax.ShapeDtypeStruct((tokens, features), jnp.bfloat16),
        cost_estimate=COVER,
        name="sum_groups",
    )(*parts)
    return total.reshape(4, tokens // 4, features)


def edge_kernel(top_ref, end_ref, first_ref, last_ref):
    half = top_ref.shape[1]
    for j in range(2):
        first_ref[j * half : (j + 1) * half, :] = top_ref[j]
        last_ref[j * half : (j + 1) * half, :] = end_ref[j]


def edge_rows(maps, cols):
    size, features = maps.shape[1:]
    half = cols // 2
    row = (cols, features)
    return pl.pallas_call(
        edge_kernel,
        grid=(1,),
        in_specs=[
            pl.BlockSpec((2, half, features), lambda j: (0, 0, 0)),
            pl.BlockSpec((2, half, features), lambda j: (1, size // half - 1, 0)),
        ],
        out_specs=[pl.BlockSpec(row, lambda j: (0, 0))] * 2,
        out_shape=[jax.ShapeDtypeStruct(row, maps.dtype)] * 2,
        cost_estimate=COVER,
        name="edge_rows",
    )(maps, maps)


def expand_kernel(s_ref, o_ref, x_ref, m_ref, wp_ref, w_ref, b_ref, *refs):
    oc_ref, at_ref, x1_ref, a2_ref, f_ref, first_ref, last_ref, t_sc = refs
    rows, cols, features = x_ref.shape
    side, row_zero = (s_ref[0], s_ref[1])

    @pl.when(pl.program_id(0) == 0)
    def _():
        from_maps(o_ref, t_sc, 0)
        for b in range(features // 128):
            part = t_sc[b].reshape(rows * cols, 128)
            oc_ref[:, 128 * b : 128 * b + 128] = part.astype(jnp.bfloat16)
        at_ref[...] = dot_nn(oc_ref[...], wp_ref[...])

        def body(r, carry):
            here = pl.ds(pl.multiple_of(r * cols, cols), cols)
            x1 = x_ref[r].astype(jnp.float32) + m_ref[2:3, :] * at_ref[here, :]
            x1_ref[here, :] = x1
            normed, _ = normalize(x1)
            a2 = normed * (1.0 + m_ref[4:5, :]) + m_ref[3:4, :]
            a2_ref[here, :] = a2.astype(jnp.bfloat16)
            return carry

        lax.fori_loop(0, rows, body, 0)

    block = f_ref.shape[2]
    f = (dot_nn(a2_ref[...], w_ref[...]) + b_ref[...].astype(jnp.float32)).reshape(rows, cols, block)
    col = lax.broadcasted_iota(jnp.int32, (cols, block), 0)
    for r in range(rows):
        live = (col < side) & (row_zero + r < side)
        f_ref[r] = jnp.where(live, f[r], 0.0).astype(jnp.bfloat16)
    first_ref[...] = f_ref[0:1]
    last_ref[...] = f_ref[rows - 1 : rows]


def expand(at, scalars, maps, latents, mods, w_proj, w_fc1, bias):
    rows, cols, features = latents.shape[2:]
    hidden = w_fc1.shape[1]
    tokens, block = (rows * cols, 512)
    flat = (tokens, features)
    specs = canvas_specs(latents, at)
    return pl.pallas_call(
        expand_kernel,
        grid_spec=pltpu.PrefetchScalarGridSpec(
            num_scalar_prefetch=1,
            grid=(hidden // block,),
            in_specs=[
                whole_spec(maps.shape),
                specs[0],
                specs[3],
                whole_spec(w_proj.shape),
                pl.BlockSpec((features, block), lambda j, s: (0, j)),
                pl.BlockSpec((1, block), lambda j, s: (0, j)),
            ],
            out_specs=[whole_spec(flat)] * 4
            + [pl.BlockSpec((rows, cols, block), lambda j, s: (0, 0, j))]
            + [pl.BlockSpec((1, cols, block), lambda j, s: (0, 0, j))] * 2,
            scratch_shapes=[pltpu.VMEM((features // 128, rows, cols, 128), jnp.float32)],
        ),
        out_shape=[
            jax.ShapeDtypeStruct(flat, jnp.bfloat16),
            jax.ShapeDtypeStruct(flat, jnp.float32),
            jax.ShapeDtypeStruct(flat, jnp.float32),
            jax.ShapeDtypeStruct(flat, jnp.bfloat16),
            jax.ShapeDtypeStruct((rows, cols, hidden), jnp.bfloat16),
        ]
        + [jax.ShapeDtypeStruct((1, cols, hidden), jnp.bfloat16)] * 2,
        cost_estimate=COVER,
        name="expand",
    )(scalars, maps, latents, mods, w_proj, w_fc1, bias)


def middle_kernel(first, s_ref, f_ref, top_ref, end_ref, c_ref, w_ref, ct_ref, x1_ref, m_ref, *rest):
    if first:
        mixed_ref, dg_ref, dz_ref, g_ref, gc_ref, first_ref, last_ref = rest[:7]
    else:
        gp_ref, gcp_ref = rest[:2]
        mixed_ref, dg_ref, dz_ref, g_ref, gc_ref, first_ref, last_ref = rest[3:10]
    out_sc, d_sc, x_sc, t_sc, gz_sc, acc_sc = rest[-6:]
    rows, cols, block = f_ref.shape
    features = out_sc.shape[1]
    side, row_zero = (s_ref[0], s_ref[1])

    def upstream(r):
        col = lax.broadcasted_iota(jnp.int32, (cols, features), 0)
        live = (col < side) & (row_zero + r < side)
        return jnp.where(live, ct_ref[r].astype(jnp.float32), 0.0), live

    @pl.when(pl.program_id(0) == 0)
    def _():
        def body(r, carry):
            here = pl.ds(pl.multiple_of(r * cols, cols), cols)
            d_sc[here, :] = (upstream(r)[0] * m_ref[5:6, :]).astype(jnp.bfloat16)
            return carry

        lax.fori_loop(0, rows, body, 0)

    d = d_sc[...]
    t_sc[...] = dot_nt(d, w_ref[...]).reshape(rows, cols, block)
    x_sc[0:1] = top_ref[...]
    x_sc[1 : rows + 1] = f_ref[...]
    x_sc[rows + 1 : rows + 2] = end_ref[...]
    acc_sc[...] = jnp.zeros_like(acc_sc)
    col = lax.broadcasted_iota(jnp.int32, (cols, 128), 0)
    for at in range(block // 128):
        lanes = slice(128 * at, 128 * at + 128)
        taps = wide_taps(c_ref, lanes, cols)

        def body(r, carry):
            x = [x_sc[r + i, :, lanes].astype(jnp.float32) for i in range(3)]
            a = [x[0] * taps[j] + x[1] * taps[3 + j] + x[2] * taps[6 + j] for j in range(3)]
            z = a[1] + shift_cols(a[0], -1, col) + shift_cols(a[2], 1, col)
            half = 0.5 * (1.0 + lax.erf(z * root_half))
            gz_sc[r, :, lanes] = (z * half).astype(jnp.bfloat16)
            slope = half + z * jnp.exp(-0.5 * z * z) * inverse_root_tau
            d_z = (t_sc[r, :, lanes] * slope).astype(jnp.bfloat16)
            dz_ref[r, :, lanes] = d_z
            d_z = d_z.astype(jnp.float32)
            moved = [shift_cols(d_z, 1, col), d_z, shift_cols(d_z, -1, col)]
            for i in range(3):
                for j in range(3):
                    acc_sc[3 * i + j, :, lanes] += sublane_sum(x[i] * moved[j])
            return carry

        lax.fori_loop(0, rows, body, 0, unroll=2)
    first_ref[...] = dz_ref[0:1]
    last_ref[...] = dz_ref[rows - 1 : rows]
    gz = gz_sc[...].reshape(rows * cols, block)
    store_sum(out_sc, dot_nn(gz, w_ref[...]))
    grad = dot_tn(gz, d)
    taps_grad = jnp.concatenate(
        [jnp.sum(acc_sc[k], axis=0, keepdims=True) for k in range(9)], axis=0
    )
    if not first:
        grad = grad + gp_ref[...]
        taps_grad = taps_grad + gcp_ref[...]
    g_ref[...] = grad.astype(g_ref.dtype)
    gc_ref[...] = taps_grad

    @pl.when(pl.program_id(0) == pl.num_programs(0) - 1)
    def _():
        def body(r, total):
            here = pl.ds(pl.multiple_of(r * cols, cols), cols)
            value, live = upstream(r)
            out = out_sc[here, :]
            mixed = x1_ref[here, :] + m_ref[5:6, :] * out
            mixed_ref[r] = jnp.where(live, mixed, 0.0).astype(jnp.bfloat16)
            return total + sublane_sum(value * out)

        total = lax.fori_loop(0, rows, body, jnp.zeros((8, features), jnp.float32))
        dg_ref[...] = jnp.sum(total, axis=0, keepdims=True)


def sublane_sum(x):
    return jnp.sum(x.reshape(x.shape[0] // 8, 8, x.shape[1]), axis=0)


def ffn_middle(at, scalars, f, halo, taps, w, cotangent, x1, mods, prev, grad_type):
    rows, cols, hidden = f.shape
    features = w.shape[1]
    block = 512
    wide = lambda j, s: (0, 0, j)
    row_spec = pl.BlockSpec((1, cols, block), wide)
    weight_spec = pl.BlockSpec((block, features), lambda j, s: (j, 0))
    tap_spec = pl.BlockSpec((9, block), lambda j, s: (0, j))
    canvas_spec = pl.BlockSpec((rows, cols, block), wide)
    specs = canvas_specs(cotangent, at)
    args = [scalars, f, halo[0], halo[1], taps, w, cotangent, x1, mods]
    args += [] if prev is None else list(prev)
    return pl.pallas_call(
        functools.partial(middle_kernel, prev is None),
        grid_spec=pltpu.PrefetchScalarGridSpec(
            num_scalar_prefetch=1,
            grid=(hidden // block,),
            in_specs=[canvas_spec, row_spec, row_spec, tap_spec, weight_spec]
            + [specs[0], whole_spec(x1.shape), specs[3]]
            + ([] if prev is None else [weight_spec, tap_spec, pl.BlockSpec(memory_space=pl.ANY)]),
            out_specs=[specs[0], whole_spec((1, features)), canvas_spec, weight_spec, tap_spec]
            + [row_spec] * 2,
            scratch_shapes=[
                pltpu.VMEM((rows * cols, features), jnp.float32),
                pltpu.VMEM((rows * cols, features), jnp.bfloat16),
                pltpu.VMEM((rows + 2, cols, block), jnp.bfloat16),
                pltpu.VMEM((rows, cols, block), jnp.float32),
                pltpu.VMEM((rows, cols, block), jnp.bfloat16),
                pltpu.VMEM((9, 8, block), jnp.float32),
            ],
        ),
        out_shape=[
            jax.ShapeDtypeStruct(cotangent.shape, jnp.bfloat16),
            jax.ShapeDtypeStruct((1, features), jnp.float32),
            jax.ShapeDtypeStruct(f.shape, jnp.bfloat16),
            jax.ShapeDtypeStruct((hidden, features), grad_type),
            jax.ShapeDtypeStruct((9, hidden), jnp.float32),
        ]
        + [jax.ShapeDtypeStruct((1, cols, hidden), jnp.bfloat16)] * 2,
        input_output_aliases={} if prev is None else {11: 0},
        cost_estimate=COVER,
        name="ffn_middle",
    )(*args)


def ffn_back_kernel(first, s_ref, z_ref, top_ref, end_ref, c_ref, w_ref, a_ref, *rest):
    ct_ref, x1_ref, at_ref, oc_ref, wp_ref, m_ref = rest[:6]
    rest = rest[6:]
    if not first:
        gp_ref, gbp_ref, gpp_ref = rest[:3]
        rest = rest[3:]
    maps_ref, dx_ref, dm_ref, g_ref, gb_ref, gp_out = rest[:6]
    da_sc, x_sc, df_sc, acc_sc, t_sc, dat_sc = rest[6:]
    rows, cols, block = z_ref.shape
    features = da_sc.shape[1]
    x_sc[0:1] = top_ref[...]
    x_sc[1 : rows + 1] = z_ref[...]
    x_sc[rows + 1 : rows + 2] = end_ref[...]
    acc_sc[...] = jnp.zeros_like(acc_sc)
    col = lax.broadcasted_iota(jnp.int32, (cols, 128), 0)
    side, row_zero = (s_ref[0], s_ref[1])
    for at in range(block // 128):
        lanes = slice(128 * at, 128 * at + 128)
        taps = wide_taps(c_ref, lanes, cols)

        def body(r, carry):
            x = [x_sc[r + i, :, lanes].astype(jnp.float32) for i in range(3)]
            b = [x[2] * taps[j] + x[1] * taps[3 + j] + x[0] * taps[6 + j] for j in range(3)]
            d_f = b[1] + shift_cols(b[0], 1, col) + shift_cols(b[2], -1, col)
            live = (col < side) & (row_zero + r < side)
            d_f = jnp.where(live, d_f, 0.0).astype(jnp.bfloat16)
            df_sc[r, :, lanes] = d_f
            acc_sc[:, lanes] += sublane_sum(d_f.astype(jnp.float32))
            return carry

        lax.fori_loop(0, rows, body, 0, unroll=2)
    d_f = df_sc[...].reshape(rows * cols, block)
    store_sum(da_sc, dot_nt(d_f, w_ref[...]))
    grad = dot_tn(a_ref[...], d_f)
    bias_grad = jnp.sum(acc_sc[...], axis=0, keepdims=True)
    if not first:
        grad = grad + gp_ref[...]
        bias_grad = bias_grad + gbp_ref[...]
    g_ref[...] = grad.astype(g_ref.dtype)
    gb_ref[...] = bias_grad

    @pl.when(pl.program_id(0) == pl.num_programs(0) - 1)
    def _():
        wide_col = lax.broadcasted_iota(jnp.int32, (cols, features), 0)

        def body(r, totals):
            here = pl.ds(pl.multiple_of(r * cols, cols), cols)
            d_a = da_sc[here, :]
            normed, inverse = normalize(x1_ref[here, :])
            live = (wide_col < side) & (row_zero + r < side)
            d_x = jnp.where(live, ct_ref[r].astype(jnp.float32), 0.0)
            d_x = d_x + norm_back(normed, inverse, d_a * (1.0 + m_ref[4:5, :]))
            dx_ref[here, :] = d_x
            dat_sc[here, :] = (d_x * m_ref[2:3, :]).astype(jnp.bfloat16)
            return (
                totals[0] + sublane_sum(d_x * at_ref[here, :]),
                totals[1] + sublane_sum(d_a),
                totals[2] + sublane_sum(d_a * normed),
            )

        zero = jnp.zeros((8, features), jnp.float32)
        totals = lax.fori_loop(0, rows, body, (zero, zero, zero))
        for i in range(3):
            dm_ref[i : i + 1, :] = jnp.sum(totals[i], axis=0, keepdims=True)
        proj = dot_tn(oc_ref[...], dat_sc[...])
        if not first:
            proj = proj + gpp_ref[...]
        gp_out[...] = proj.astype(gp_out.dtype)
        d_o = dot_nt(dat_sc[...], wp_ref[...])
        for b in range(features // 128):
            t_sc[b] = d_o[:, 128 * b : 128 * b + 128].reshape(rows, cols, 128)
        to_maps(t_sc, maps_ref)


def ffn_back(
    at, scalars, d_z, halo, taps, w, a, cotangent, x1, attn, oc, w_proj, mods, prev, grad_type
):
    rows, cols, hidden = d_z.shape
    features = a.shape[1]
    block = 512
    wide = lambda j, s: (0, 0, j)
    row_spec = pl.BlockSpec((1, cols, block), wide)
    weight_spec = pl.BlockSpec((features, block), lambda j, s: (0, j))
    bias_spec = pl.BlockSpec((1, block), lambda j, s: (0, j))
    flat_spec = whole_spec((rows * cols, features))
    proj_spec = whole_spec(w_proj.shape)
    maps = (4, rows * cols // 4, features)
    specs = canvas_specs(cotangent, at)
    args = [scalars, d_z, halo[0], halo[1], taps, w, a, cotangent, x1, attn, oc, w_proj, mods]
    args += [] if prev is None else list(prev)
    return pl.pallas_call(
        functools.partial(ffn_back_kernel, prev is None),
        grid_spec=pltpu.PrefetchScalarGridSpec(
            num_scalar_prefetch=1,
            grid=(hidden // block,),
            in_specs=[
                pl.BlockSpec((rows, cols, block), wide),
                row_spec,
                row_spec,
                pl.BlockSpec((9, block), lambda j, s: (0, j)),
                weight_spec,
                flat_spec,
                specs[0],
                flat_spec,
                flat_spec,
                flat_spec,
                proj_spec,
                specs[3],
            ]
            + ([] if prev is None else [weight_spec, bias_spec, proj_spec]),
            out_specs=[whole_spec(maps)]
            + [flat_spec, whole_spec((3, features)), weight_spec, bias_spec, proj_spec],
            scratch_shapes=[
                pltpu.VMEM((rows * cols, features), jnp.float32),
                pltpu.VMEM((rows + 2, cols, block), jnp.bfloat16),
                pltpu.VMEM((rows, cols, block), jnp.bfloat16),
                pltpu.VMEM((8, block), jnp.float32),
                pltpu.VMEM((features // 128, rows, cols, 128), jnp.float32),
                pltpu.VMEM((rows * cols, features), jnp.bfloat16),
            ],
        ),
        out_shape=[jax.ShapeDtypeStruct(maps, jnp.bfloat16)]
        + [
            jax.ShapeDtypeStruct((rows * cols, features), jnp.float32),
            jax.ShapeDtypeStruct((3, features), jnp.float32),
            jax.ShapeDtypeStruct(w.shape, grad_type),
            jax.ShapeDtypeStruct((1, hidden), jnp.float32),
            jax.ShapeDtypeStruct(w_proj.shape, grad_type),
        ],
        cost_estimate=COVER,
        name="ffn_backward",
    )(*args)


def last_kernel(first, s_ref, du_ref, dtop_ref, dend_ref, *rest):
    x_ref, top_ref, end_ref, m_ref, c_ref, dx_ref = rest[:6]
    rest = rest[6:]
    if not first:
        gcp_ref = rest[0]
        rest = rest[2:]
    dl_ref, dm_ref, gc_ref, a_sc, t_sc, d_sc, acc_sc = rest
    rows, cols, features = x_ref.shape
    half = cols // 2
    side, row_zero = (s_ref[0], s_ref[1])
    modulated_rows(a_sc, s_ref, x_ref, top_ref, end_ref, m_ref)
    from_maps(du_ref, t_sc, 1)
    for at, ref in ((0, dtop_ref), (rows + 1, dend_ref)):
        for j in range(2):
            for start in range(0, features, 128):
                lanes = slice(start, start + 128)
                part = ref[j * half : (j + 1) * half, lanes].astype(jnp.float32)
                t_sc[start // 128, at, pl.ds(j, half, stride=2), :] = part
    acc_sc[...] = jnp.zeros_like(acc_sc)
    col = lax.broadcasted_iota(jnp.int32, (cols, 128), 0)
    for start in range(0, features, 128):
        lanes = slice(start, start + 128)
        taps = wide_taps(c_ref, lanes, cols)

        def conv_body(r, carry):
            d = [t_sc[start // 128, r + i] for i in range(3)]
            b = [d[2] * taps[j] + d[1] * taps[3 + j] + d[0] * taps[6 + j] for j in range(3)]
            d_a = b[1] + shift_cols(b[0], 1, col) + shift_cols(b[2], -1, col)
            live = (col < side) & (row_zero + r < side)
            d_sc[r, :, lanes] = jnp.where(live, d_a, 0.0)
            moved = [shift_cols(d[1], 1, col), d[1], shift_cols(d[1], -1, col)]
            for i in range(3):
                x = a_sc[r + i, :, lanes].astype(jnp.float32)
                for j in range(3):
                    acc_sc[3 * i + j, :, lanes] += sublane_sum(x * moved[j])
            return carry

        lax.fori_loop(0, rows, conv_body, 0, unroll=2)
    taps_grad = jnp.concatenate(
        [jnp.sum(acc_sc[k], axis=0, keepdims=True) for k in range(9)], axis=0
    )
    if not first:
        taps_grad = taps_grad + gcp_ref[...]
    gc_ref[...] = taps_grad

    def body(r, totals):
        here = pl.ds(pl.multiple_of(r * cols, cols), cols)
        normed, inverse = normalize(x_ref[r].astype(jnp.float32))
        d_a = d_sc[r]
        dl_ref[r] = dx_ref[here, :] + norm_back(normed, inverse, d_a * (1.0 + m_ref[1:2, :]))
        return (totals[0] + sublane_sum(d_a), totals[1] + sublane_sum(d_a * normed))

    zero = jnp.zeros((8, features), jnp.float32)
    totals = lax.fori_loop(0, rows, body, (zero, zero))
    for i in range(2):
        dm_ref[i : i + 1, :] = jnp.sum(totals[i], axis=0, keepdims=True)


def last_stage(at, scalars, maps, d_halo, latents, top, end, mods, taps, d_x, prev):
    rows, cols, features = latents.shape[2:]
    specs = canvas_specs(latents, at)
    args = [scalars, maps, *d_halo, latents, top, end, mods, taps, d_x]
    args += [] if prev is None else list(prev)
    return pl.pallas_call(
        functools.partial(last_kernel, prev is None),
        grid_spec=pltpu.PrefetchScalarGridSpec(
            num_scalar_prefetch=1,
            grid=(1,),
            in_specs=[whole_spec(maps.shape)]
            + [whole_spec((cols, features))] * 2
            + specs
            + [whole_spec(taps.shape), whole_spec(d_x.shape)]
            + ([] if prev is None else [whole_spec(taps.shape), pl.BlockSpec(memory_space=pl.ANY)]),
            out_specs=[specs[0], whole_spec((2, features)), whole_spec(taps.shape)],
            scratch_shapes=[
                pltpu.VMEM((rows + 2, cols, features), jnp.bfloat16),
                pltpu.VMEM((features // 128, rows + 2, cols, 128), jnp.float32),
                pltpu.VMEM((rows, cols, features), jnp.float32),
                pltpu.VMEM((9, 8, features), jnp.float32),
            ],
        ),
        out_shape=[
            jax.ShapeDtypeStruct(latents.shape, jnp.float32),
            jax.ShapeDtypeStruct((2, features), jnp.float32),
            jax.ShapeDtypeStruct(taps.shape, jnp.float32),
        ],
        input_output_aliases={} if prev is None else {11: 0},
        cost_estimate=COVER,
        name="last_stage",
    )(*args)


def shards(
    latents,
    timesteps,
    size_tags,
    w_ada,
    b_ada,
    conv_attn,
    w_qkv,
    w_proj,
    w_fc1,
    b_fc1,
    conv_ffn,
    w_fc2,
    cotangent,
):
    micro_count, _, row_count, side_count, features = latents.shape
    dp, strips = (lax.axis_size("dp"), lax.axis_size("strip"))
    dp_at, strip_at = (lax.axis_index("dp"), lax.axis_index("strip"))
    hidden = conv_ffn.shape[1] * dp
    groups = strips // 4
    group_at, map_at = (strip_at % groups, strip_at // groups)
    score_scale = (features // HEADS) ** (-0.5)
    width = features // groups

    stamps = timesteps[:, 0].astype(jnp.float32)
    all_stamps = gather_butterfly(stamps[None])
    conds = [silu_of(embed_times(all_stamps[k], features)) for k in range(dp)]
    ada_rows = features // dp
    ada_wide = w_ada.astype(jnp.float32)
    partial_mods = jnp.dot(
        lax.dynamic_slice_in_dim(jnp.concatenate(conds), dp_at * ada_rows, ada_rows, 1),
        ada_wide,
        precision=lax.Precision.HIGHEST,
    )
    bias_here = lax.dynamic_update_slice_in_dim(
        jnp.zeros((6 * features,), jnp.float32),
        b_ada.astype(jnp.float32),
        dp_at * b_ada.shape[0],
        0,
    )
    partial_mods = (partial_mods + bias_here[None, :]).reshape(dp, micro_count, 6 * features)
    count = dp
    while count > 1:
        count //= 2
        partial_mods = partial_mods[:count] + permute_xor(partial_mods[count:], "dp", count)
    modulation = partial_mods[0]

    small = jnp.concatenate([conv_attn.reshape(-1), conv_ffn.reshape(-1), b_fc1])
    small = gather_small(small)
    n_one, n_two = (conv_attn.size, conv_attn.size + conv_ffn.size)
    conv_one = small[:, :n_one].reshape(dp, 9, -1).transpose(1, 0, 2).reshape(9, features)
    conv_two = small[:, n_one:n_two].reshape(dp, 9, -1).transpose(1, 0, 2).reshape(9, hidden)
    fc1_bias = small[:, n_two:].reshape(1, hidden)
    qkv_pieces, modulation = fetch_group(w_qkv, groups, modulation)
    packed = pack_weights(w_proj, w_fc1, w_fc2)
    packed, modulation = tie(packed, modulation)
    fetched = fetch_relayed(packed)

    top, end = halo_rows(latents[:, 0, 0], latents[:, 0, row_count - 1])
    mods = modulation.reshape(micro_count, 6, features)
    micros = range(micro_count)
    places = jnp.stack([strip_at * row_count, map_at, group_at]).astype(jnp.int32)
    scalars = [
        jnp.concatenate(
            [jnp.where(size_tags[at] == 1, side_count, side_count // 2).astype(jnp.int32), places]
        )
        for at in micros
    ]
    kept = [{} for _ in micros]
    turn = packed

    for at in micros:
        if at == micro_count - 1:
            qkv_group = gather_group(qkv_pieces)
            turn = (turn, qkv_group)
        maps = before_attention(at, after(scalars[at], turn), latents, top, end, mods, conv_one)
        turn = maps
        kept[at]["u"] = map_exchange(maps, groups).reshape(-1, features)

    direct = [fetched[k - 1] for k in range(1, dp) if k & (k - 1) == 0]
    for at in micros:
        keep = kept[at]
        u = after(keep["u"], turn if at == 0 else kept[at - 1]["logs"])
        keep["u"] = group_exchange(u, groups)
        done = attend(after(scalars[at], turn), keep["u"], qkv_group, score_scale, side_count)
        keep["t"], keep["o"], keep["logs"] = (done[0], done[1 : 1 + groups], done[-1])
        parts = [keep["o"][0]] + [
            permute_xor(keep["o"][k], "strip", k) for k in range(1, groups)
        ]
        if at == micro_count - 1:
            for k in range(1, dp):
                if k & (k - 1):
                    fetched[k - 1], keep["logs"] = tie(fetched[k - 1], keep["logs"])
            proj_full, fc1_full, fc2_full = unpack_weights(
                fetched, keep["logs"], w_proj, w_fc1, w_fc2
            )
        maps = join_groups(scalars[at], parts, width)
        turn = (maps, direct)
        keep["o_maps"] = map_exchange(maps, groups)

    for at in micros:
        keep = kept[at]
        keep["oc"], keep["attn"], keep["x1"], keep["a2"], keep["f"], first, last = expand(
            at,
            after(scalars[at], turn),
            keep["o_maps"],
            latents,
            mods,
            proj_full,
            fc1_full,
            fc1_bias,
        )
        turn = keep["attn"]
        keep["f_halo"] = halo_rows(first, last)

    for at in micros:
        keep, grad_type = (kept[at], jnp.bfloat16 if at == micro_count - 1 else jnp.float32)
        prev = None if at == 0 else (term_fc2, term_conv_two, mixed)
        mixed, keep["d_gate2"], keep["d_z"], term_fc2, term_conv_two, first, last = ffn_middle(
            at,
            after(scalars[at], turn),
            keep["f"],
            keep["f_halo"],
            conv_two,
            fc2_full,
            cotangent,
            keep["x1"],
            mods,
            prev,
            grad_type,
        )
        turn = keep["d_gate2"]
        keep["z_halo"] = halo_rows(first, last)

    for at in micros:
        keep, grad_type = (kept[at], jnp.bfloat16 if at == micro_count - 1 else jnp.float32)
        prev = None if at == 0 else (term_fc1, term_fc1_bias, term_proj)
        done = ffn_back(
            at,
            after(scalars[at], turn),
            keep["d_z"],
            keep["z_halo"],
            conv_two,
            fc1_full,
            keep["a2"],
            cotangent,
            keep["x1"],
            keep["attn"],
            keep["oc"],
            proj_full,
            mods,
            prev,
            grad_type,
        )
        keep["d_x"], keep["d_mods"], term_fc1, term_fc1_bias, term_proj = done[1:]
        turn = keep["d_mods"]
        keep["d_o"] = map_exchange(done[0], groups)

    blocks = dp * strips
    wide, narrow = (hidden // blocks, features // blocks)
    small = jnp.concatenate([term_conv_two, term_fc1_bias]).reshape(10, blocks, wide)
    small = small.transpose(1, 0, 2).reshape(blocks, 10 * wide)
    merged = narrow % 8 == 0 and dp == 4
    if merged:
        small_rows = -(-10 * wide // features // 8) * 8
        small = jnp.pad(small, ((0, 0), (0, small_rows * features - 10 * wide)))
        small = small.reshape(blocks, small_rows, features).astype(jnp.bfloat16)
        small, kept[0]["d_o"] = tie(small, kept[0]["d_o"])
        shares, shapes = by_destination(term_fc2, term_fc1, term_proj, small, narrow, dp)
        send = route_core(shares, shapes)
        share = core_sum(shares, shapes, permute_xor(send, "strip", 1), dp_at)
        turn = (turn, share[1])
        came = [permute_xor(share[0], "dp", 1), permute_xor(share[2], "dp", 2)]

    for at in micros:
        keep, grad_type = (kept[at], jnp.bfloat16 if at == micro_count - 1 else jnp.float32)
        if at > 0:
            keep["d_o"], done[0] = tie(keep["d_o"], done[0])
        pieces = group_exchange(keep["d_o"].reshape(-1, features), groups)
        if width % 128:
            pieces = [
                jnp.pad(
                    lax.dynamic_slice_in_dim(piece, group_at * width, width, 1),
                    ((0, 0), (0, -width % 128)),
                )
                for piece in pieces
            ]
        done = attend_back(
            after(scalars[at], turn),
            keep["u"],
            pieces,
            keep["o"],
            qkv_group,
            keep["t"],
            keep["logs"],
            score_scale,
            side_count,
            None if at == 0 else term_qkv,
            grad_type,
        )
        done = list(done)
        term_qkv = done[groups]
        parts = [done[0]] + [permute_xor(done[k], "strip", k) for k in range(1, groups)]
        if at == 0 and merged:
            own, x_send, y_send = turn_sums(after(share[1], done[0]), came[0], share[3], came[1])
            came = [permute_xor(x_send, "dp", 2), permute_xor(y_send, "dp", 1)]
            parts = after(parts, own)
        if at > 0:
            if merged:
                share[1], share[2], kept[0]["d_u"] = tie(share[1], share[2], kept[0]["d_u"])
            kept[0]["edges"] = edge_rows(kept[0]["d_u"], side_count)
            kept[0]["edges"], parts = tie(kept[0]["edges"], parts)
        maps = sum_groups(parts)
        turn = maps
        keep["d_u"] = map_exchange(maps, groups)
        if at == 0 and merged:
            share = list(add_up(after(own, maps), *came, strip_at >> 1))
            turn = (turn, share[0])
            share = [share[0]] + [
                permute_xor(share[k], "strip", 2 * k) for k in range(1, strips // 2)
            ]

    kept_qkv = group_sums(after(term_qkv, turn), groups, width)
    mod_grads = []
    for at in micros:
        keep = kept[at]
        first_row, last_row = (
            keep["edges"] if at == 0 else edge_rows(keep["d_u"], side_count)
        )
        d_halo = halo_rows(first_row, last_row)
        prev = None if at == 0 else (term_conv_one, d_latents)
        d_latents, keep["d_mod1"], term_conv_one = last_stage(
            at,
            after(scalars[at], turn),
            keep["d_u"],
            d_halo,
            latents,
            top,
            end,
            mods,
            conv_one,
            keep["d_x"],
            prev,
        )
        turn = keep["d_mod1"]
        if at == 0:
            parts_qkv = group_parts(kept_qkv, groups)
        mod_grads.append(
            jnp.concatenate([keep["d_mod1"], keep["d_mods"], keep["d_gate2"]]).reshape(-1)
        )

    if merged:
        total = share[0].astype(jnp.float32)
        for part in share[1:]:
            total = total + part.astype(jnp.float32)
        ratio = hidden // features
        g_fc2 = total[: ratio * narrow]
        g_fc1 = total[ratio * narrow : 2 * ratio * narrow].reshape(ratio, narrow, features)
        g_fc1 = g_fc1.transpose(1, 0, 2).reshape(narrow, hidden)
        g_proj = total[2 * ratio * narrow : (2 * ratio + 1) * narrow]
        small = total[(2 * ratio + 1) * narrow :].reshape(-1)
    else:
        g_fc2 = scatter_rows(term_fc2)
        g_fc1 = scatter_rows(term_fc1)
        g_proj = scatter_rows(term_proj)
        small = scatter_rows(small)[0]
    g_conv_two = small[: 9 * wide].reshape(9, wide)
    g_fc1_bias = small[9 * wide : 10 * wide]
    mod_grads.append(term_conv_one.reshape(-1))

    grad_mod, parts_qkv = tie(jnp.concatenate(mod_grads), parts_qkv)
    step = 1
    while step < strips:
        grad_mod = grad_mod + permute_xor(grad_mod, "strip", step)
        step *= 2
        if step == 4:
            g_qkv = group_columns(after(parts_qkv, grad_mod), groups)
    all_mods = gather_butterfly(grad_mod[None])
    block_at = dp_at * strips + strip_at
    g_conv_one = jnp.sum(all_mods[:, micro_count * 6 * features :], axis=0).reshape(9, features)
    g_conv_one = lax.dynamic_slice_in_dim(g_conv_one, block_at * narrow, narrow, 1)
    all_mods = all_mods[:, : micro_count * 6 * features].reshape(-1, 6 * features)
    conds_here = lax.dynamic_slice_in_dim(
        jnp.concatenate(conds), block_at * narrow, narrow, 1
    )
    g_ada = lax.dot_general(
        conds_here, all_mods, (((0,), (0,)), ((), ())), precision=lax.Precision.HIGHEST
    )
    ada_wide_block = 6 * features // blocks
    g_ada_bias = lax.dynamic_slice_in_dim(
        jnp.sum(all_mods, axis=0), block_at * ada_wide_block, ada_wide_block, 0
    )
    return (
        mixed,
        d_latents,
        g_ada,
        g_ada_bias,
        g_conv_one,
        g_qkv,
        g_proj,
        g_fc1,
        g_fc1_bias,
        g_conv_two,
        g_fc2,
    )


def solution(mesh):
    return jax.shard_map(
        shards,
        mesh=mesh,
        in_specs=(
            P(None, "dp", "strip", None, None),
            P(None, "dp"),
            P(None, "dp"),
            P("dp", None),
            P("dp"),
            P(None, "dp"),
            P("dp", None),
            P("dp", None),
            P("dp", None),
            P("dp"),
            P(None, "dp"),
            P("dp", None),
            P(None, "dp", "strip", None, None),
        ),
        out_specs=(
            P(None, "dp", "strip", None, None),
            P(None, "dp", "strip", None, None),
            P(("dp", "strip"), None),
            P(("dp", "strip")),
            P(None, ("dp", "strip")),
            P(("dp", "strip"), None),
            P(("dp", "strip"), None),
            P(("dp", "strip"), None),
            P(("dp", "strip")),
            P(None, ("dp", "strip")),
            P(("dp", "strip"), None),
        ),
        check_vma=False,
    )
```

```python
import functools
import math

import jax
import jax.numpy as jnp
from jax import lax
from jax.experimental import pallas as pl
from jax.experimental.pallas import tpu as pltpu
from jax.sharding import PartitionSpec as P

HEADS = 12
COVER = pl.CostEstimate(flops=200_000_000_000, transcendentals=0, bytes_accessed=0)
BRIEF = pl.CostEstimate(flops=0, transcendentals=0, bytes_accessed=0)


root_half = 0.7071067811865476
inverse_root_tau = 0.3989422804014327


def permute_xor(x, axis, step):
    size = lax.axis_size(axis)
    return lax.ppermute(x, axis, [(i, i ^ step) for i in range(size)])


def pick(x, at, axis=0):
    return lax.dynamic_index_in_dim(x, at, axis, keepdims=False)


def halo_rows(first, last):
    size = lax.axis_size("strip")
    up = [(i, i + 1) for i in range(size - 1)]
    down = [(i + 1, i) for i in range(size - 1)]
    return (lax.ppermute(last, "strip", up), lax.ppermute(first, "strip", down))


def place_blocks(blocks, me):
    stacked = jnp.stack(blocks)
    return jnp.stack([pick(stacked, me ^ at) for at in range(len(blocks))])


def gather_butterfly(x):
    step = 1
    while step < lax.axis_size("dp"):
        x = jnp.concatenate([x, permute_xor(x, "dp", step)])
        step *= 2
    return x


def after(x, *done):
    return lax.optimization_barrier((x, done))[0]


HBM = pl.BlockSpec(memory_space=pl.ANY)


def move_all(copies):
    for copy in copies:
        copy.start()
    for copy in copies:
        copy.wait()


def rows_at(start, size):
    return pl.ds(pl.multiple_of(start, 8), size)


def tie(*values):
    return lax.optimization_barrier(values)


def assemble_kernel(at_ref, *refs):
    pieces, whole, sem = (refs[:-2], refs[-2], refs[-1])
    move_all(
        [
            pltpu.make_async_copy(
                piece, whole.at[:, rows_at(at_ref[i], piece.shape[1]), :], sem.at[i]
            )
            for i, piece in enumerate(pieces)
        ]
    )


def assemble(pieces, starts, shape):
    return pl.pallas_call(
        assemble_kernel,
        grid_spec=pltpu.PrefetchScalarGridSpec(
            num_scalar_prefetch=1,
            grid=(1,),
            in_specs=[HBM] * len(pieces),
            out_specs=whole_spec(shape),
            scratch_shapes=[pltpu.SemaphoreType.DMA((len(pieces),))],
        ),
        out_shape=jax.ShapeDtypeStruct(shape, pieces[0].dtype),
        cost_estimate=COVER,
        name="assemble",
    )(jnp.stack(starts).astype(jnp.int32), *pieces)


def pack_layout(proj, fc1, fc2):
    features = proj.shape[1]
    sizes = [proj.shape[0] // 2]
    sizes += [fc1.shape[0] // 2] * (fc1.shape[1] // features) + [fc2.shape[0] // 2]
    starts = [sum(sizes[:i]) for i in range(len(sizes))]
    return sizes, starts


def half_of(refs, row, i, size, features):
    if i == 0:
        return refs[0].at[rows_at(row, size), :]
    if i == len(refs[3]) - 1:
        return refs[2].at[rows_at(row, size), :]
    return refs[1].at[rows_at(row, size), (i - 1) * features : i * features]


def pack_kernel(at_ref, proj, fc1, fc2, out, sem):
    sizes, starts = pack_layout(proj, fc1, fc2)
    copies = []
    for i, (size, start) in enumerate(zip(sizes, starts)):
        source = half_of((proj, fc1, fc2, sizes), at_ref[0] * size, i, size, proj.shape[1])
        copies.append(pltpu.make_async_copy(source, out.at[start : start + size, :], sem.at[i]))
    move_all(copies)


def pack_weights(proj, fc1, fc2):
    core = lax.axis_index("strip") & 1
    sizes, starts = pack_layout(proj, fc1, fc2)
    shape = (starts[-1] + sizes[-1], proj.shape[1])
    return pl.pallas_call(
        pack_kernel,
        grid_spec=pltpu.PrefetchScalarGridSpec(
            num_scalar_prefetch=1,
            grid=(1,),
            in_specs=[HBM] * 3,
            out_specs=whole_spec(shape),
            scratch_shapes=[pltpu.SemaphoreType.DMA((len(sizes),))],
        ),
        out_shape=jax.ShapeDtypeStruct(shape, proj.dtype),
        cost_estimate=BRIEF,
        name="pack_weights",
    )(core[None].astype(jnp.int32), proj, fc1, fc2)


def fetch_direct(x):
    steps = [k for k in range(1, lax.axis_size("dp")) if k & (k - 1) == 0]
    return {k: permute_xor(x, "dp", k) for k in steps}


def fetch_relayed(came):
    step = 2
    while step < lax.axis_size("dp"):
        for k in range(1, step):
            came[step + k] = permute_xor(came[k], "dp", step)
        step *= 2
    return [came[k] for k in sorted(came)]


def unpack_kernel(count, at_ref, *refs):
    own, halves, wholes, sem = (refs[:3], refs[3 : 3 + count], refs[3 + count : 6 + count], refs[-1])
    sizes, starts = pack_layout(*own)
    features = own[0].shape[1]
    copies = []
    for ref, whole in zip(own, wholes):
        target = whole.at[rows_at(at_ref[0] * ref.shape[0], ref.shape[0]), :]
        copies.append(pltpu.make_async_copy(ref, target, sem.at[len(copies)]))
    for k, half in enumerate(halves):
        for i, (size, start) in enumerate(zip(sizes, starts)):
            row = (2 * at_ref[1 + 2 * k] + at_ref[2 + 2 * k]) * size
            target = half_of(wholes + (sizes,), row, i, size, features)
            copies.append(
                pltpu.make_async_copy(
                    half.at[start : start + size, :], target, sem.at[len(copies)]
                )
            )
    move_all(copies)


def unpack_weights(fetched, turn, proj, fc1, fc2):
    size, me = (lax.axis_size("dp"), lax.axis_index("dp"))
    core = lax.axis_index("strip") & 1
    halves, places = ([], [me])
    for k, mine in enumerate(fetched, 1):
        halves += [mine, permute_xor(mine, "strip", 1)]
        places += [me ^ k, core, me ^ k, 1 - core]
    shapes = [(size * w.shape[0], w.shape[1]) for w in (proj, fc1, fc2)]
    copies = 3 + len(halves) * len(pack_layout(proj, fc1, fc2)[0])
    return pl.pallas_call(
        functools.partial(unpack_kernel, len(halves)),
        grid_spec=pltpu.PrefetchScalarGridSpec(
            num_scalar_prefetch=1,
            grid=(1,),
            in_specs=[HBM] * (3 + len(halves)),
            out_specs=[whole_spec(shape) for shape in shapes],
            scratch_shapes=[pltpu.SemaphoreType.DMA((copies,))],
        ),
        out_shape=[jax.ShapeDtypeStruct(shape, proj.dtype) for shape in shapes],
        cost_estimate=BRIEF,
        name="unpack_weights",
    )(after(jnp.stack(places).astype(jnp.int32), turn), proj, fc1, fc2, *halves)


def fetch_group(w, groups, turn):
    rows, cols = w.shape
    width = cols // 3 // groups
    group = lax.axis_index("strip") % groups
    mine = pick(w.reshape(rows, 3, groups, width), group, 2).transpose(1, 0, 2)
    mine, turn = tie(jnp.pad(mine, ((0, 0), (0, 0), (0, -width % 128))), turn)
    pieces = [mine] + [permute_xor(mine, "dp", k) for k in range(1, lax.axis_size("dp"))]
    return pieces, turn


def gather_group(pieces):
    me, rows = (lax.axis_index("dp"), pieces[0].shape[1])
    starts = [(me ^ k) * rows for k in range(len(pieces))]
    return assemble(pieces, starts, (3, len(pieces) * rows, pieces[0].shape[2]))


def exchange_sum(x, axis, me, step, wire, dim=0):
    total = pick(x, me, dim).astype(jnp.float32)
    parts = [
        permute_xor(pick(x, me ^ k, dim).astype(wire), axis, k * step)
        for k in range(1, x.shape[dim])
    ]
    for part in parts:
        total = total + part.astype(jnp.float32)
    return total


def scatter_rows(g, wire=jnp.bfloat16):
    rows, cols = g.shape
    dp, strips = (lax.axis_size("dp"), lax.axis_size("strip"))
    strip = lax.axis_index("strip")
    shaped = g.reshape(dp, strips // 2, 2, rows // dp // strips, cols)
    core = strip & 1
    sent = permute_xor(pick(shaped, 1 - core, 2).astype(wire), "strip", 1)
    kept = pick(shaped, core, 2).astype(jnp.float32) + sent.astype(jnp.float32)
    kept = exchange_sum(kept, "dp", lax.axis_index("dp"), 1, wire)
    return exchange_sum(kept, "strip", strip >> 1, 2, wire)


def group_sums(g, groups, width, wire=jnp.bfloat16):
    rows = g.shape[1]
    dp, strips = (lax.axis_size("dp"), lax.axis_size("strip"))
    kept = g[:, :, :width].reshape(3, dp, strips // groups, groups, rows // dp // strips, width)
    return exchange_sum(kept, "dp", lax.axis_index("dp"), 1, wire, 1)


def group_parts(kept, groups, wire=jnp.bfloat16):
    me = lax.axis_index("strip") // groups
    return [pick(kept, me, 1)] + [
        permute_xor(pick(kept, me ^ k, 1).astype(wire), "strip", k * groups)
        for k in range(1, kept.shape[1])
    ]


def group_columns(parts, groups, wire=jnp.bfloat16):
    kept = parts[0]
    for part in parts[1:]:
        kept = kept + part.astype(jnp.float32)
    group = lax.axis_index("strip") % groups
    blocks = [pick(kept, group, 1)] + [
        permute_xor(pick(kept, group ^ k, 1).astype(wire), "strip", k).astype(jnp.float32)
        for k in range(1, groups)
    ]
    whole = place_blocks(blocks, group)
    return whole.transpose(2, 1, 0, 3).reshape(whole.shape[2], -1)


def lay_rows(out, fc2, fc1, proj, small):
    features = proj.shape[-1]
    parts = [fc2]
    parts += [fc1[:, :, i : i + features] for i in range(0, fc1.shape[-1], features)]
    start = 0
    for part in parts + [proj, small]:
        out[:, start : start + part.shape[1], :] = part
        start += part.shape[1]


def route_kernel(at_ref, fc2, fc1, proj, small, out):
    lay_rows(out, fc2[...], fc1[...], proj[...], small[...])


def by_destination(fc2, fc1, proj, small, rows, dp):
    pairs = small.shape[0] // 2 // dp
    arrays = [
        x.reshape(dp, pairs, 2, -1, x.shape[-1]) for x in (fc2, fc1, proj, small)
    ]
    shapes = [(None, pairs, None) + x.shape[3:] for x in arrays]
    return arrays, shapes


def route_core(arrays, shapes):
    dp, pairs = arrays[0].shape[:2]
    features = arrays[0].shape[-1]
    height = sum(x.shape[3] * x.shape[4] for x in arrays) // features
    core = lax.axis_index("strip") & 1
    return pl.pallas_call(
        route_kernel,
        grid_spec=pltpu.PrefetchScalarGridSpec(
            num_scalar_prefetch=1,
            grid=(dp,),
            in_specs=[
                pl.BlockSpec(shape, lambda j, s: (j, 0, 1 - s[0], 0, 0)) for shape in shapes
            ],
            out_specs=pl.BlockSpec((pairs, height, features), lambda j, s: (j, 0, 0)),
        ),
        out_shape=jax.ShapeDtypeStruct((dp * pairs, height, features), arrays[0].dtype),
        cost_estimate=COVER,
        name="route_core",
    )(core[None].astype(jnp.int32), *arrays)


def core_sum_kernel(at_ref, fc2, fc1, proj, small, came, x_send, x_keep, y_send, y_keep, kept):
    lay_rows(kept, fc2[...], fc1[...], proj[...], small[...])
    total = (kept[...].astype(jnp.float32) + came[...].astype(jnp.float32)).astype(kept.dtype)
    half = total.shape[0] // 2
    for k in range(4):

        @pl.when(pl.program_id(0) == k)
        def _():
            (x_send if k & 1 else x_keep)[k >> 1] = total[:half]
            (y_send if k >> 1 else y_keep)[k & 1] = total[half:]


def core_sum(arrays, shapes, came, me):
    dp, pairs = arrays[0].shape[:2]
    block = (pairs,) + came.shape[1:]
    out = (2, pairs // 2) + came.shape[1:]
    core = lax.axis_index("strip") & 1
    return pl.pallas_call(
        core_sum_kernel,
        grid_spec=pltpu.PrefetchScalarGridSpec(
            num_scalar_prefetch=1,
            grid=(dp,),
            in_specs=[
                pl.BlockSpec(shape, lambda j, s: (s[1] ^ j, 0, s[0], 0, 0)) for shape in shapes
            ]
            + [pl.BlockSpec(block, lambda j, s: (s[1] ^ j, 0, 0))],
            out_specs=[whole_spec(out)] * 4,
            scratch_shapes=[pltpu.VMEM(block, came.dtype)],
        ),
        out_shape=[jax.ShapeDtypeStruct(out, came.dtype)] * 4,
        cost_estimate=COVER,
        name="core_sum",
    )(jnp.stack([core, me]).astype(jnp.int32), *arrays, came)


def turn_kernel(x_keep, x_came, y_keep, y_came, own, x_send, y_send):
    half = own.shape[0] // 2

    def both(keep, came, k):
        return (keep[k].astype(jnp.float32) + came[k].astype(jnp.float32)).astype(own.dtype)

    own[:half] = both(x_keep, x_came, 0)
    own[half:] = both(y_keep, y_came, 0)
    x_send[...] = both(x_keep, x_came, 1)
    y_send[...] = both(y_keep, y_came, 1)


def turn_sums(x_keep, x_came, y_keep, y_came):
    _, half, rows, cols = x_keep.shape
    block = rows // 2
    pair = pl.BlockSpec((2, half, block, cols), lambda j: (0, 0, j, 0))
    one = pl.BlockSpec((half, block, cols), lambda j: (0, j, 0))
    whole = pl.BlockSpec((2 * half, block, cols), lambda j: (0, j, 0))
    shape = (half, rows, cols)
    return pl.pallas_call(
        turn_kernel,
        grid=(rows // block,),
        in_specs=[pair] * 4,
        out_specs=[whole, one, one],
        out_shape=[
            jax.ShapeDtypeStruct((2 * half,) + shape[1:], x_keep.dtype),
            jax.ShapeDtypeStruct(shape, x_keep.dtype),
            jax.ShapeDtypeStruct(shape, x_keep.dtype),
        ],
        cost_estimate=COVER,
        name="turn_sums",
    )(x_keep, x_came, y_keep, y_came)


def add_kernel(at_ref, own, x_came, y_came, *refs):
    outs, kept = (refs[:-1], refs[-1])
    half = own.shape[0] // 2
    for at, came in ((slice(0, half), x_came), (slice(half, None), y_came)):
        total = own[at].astype(jnp.float32) + came[...].astype(jnp.float32)
        kept[at] = total.astype(own.dtype)
    for k, out in enumerate(outs):
        out[...] = kept[at_ref[0] ^ k]


def add_up(own, x_came, y_came, me):
    pairs, rows, cols = own.shape
    return pl.pallas_call(
        add_kernel,
        grid_spec=pltpu.PrefetchScalarGridSpec(
            num_scalar_prefetch=1,
            grid=(1,),
            in_specs=[whole_spec(x.shape) for x in (own, x_came, y_came)],
            out_specs=[whole_spec((rows, cols))] * pairs,
            scratch_shapes=[pltpu.VMEM(own.shape, own.dtype)],
        ),
        out_shape=[jax.ShapeDtypeStruct((rows, cols), own.dtype)] * pairs,
        cost_estimate=BRIEF,
        name="add_up",
    )(me[None].astype(jnp.int32), own, x_came, y_came)


def map_exchange(maps, groups):
    size = lax.axis_size("strip")
    among = [[m * groups + g for m in range(4)] for g in range(groups)]
    return lax.all_to_all(maps, "strip", 0, 0, axis_index_groups=among, tiled=True)


def group_exchange(x, groups):
    return [x] + [permute_xor(x, "strip", k) for k in range(1, groups)]


def silu_of(values):
    return values / (1.0 + jnp.exp(-values))


def embed_times(stamps, features):
    half_count = features // 2
    frequency = jnp.exp(-math.log(10000.0) * jnp.arange(half_count, dtype=jnp.float32) / half_count)
    angles = stamps[:, None] * frequency[None, :]
    return jnp.concatenate([jnp.cos(angles), jnp.sin(angles)], axis=1)

def normalize(values):
    centre = values - jnp.mean(values, axis=-1, keepdims=True)
    inverse = lax.rsqrt(jnp.mean(centre * centre, axis=-1, keepdims=True) + 1e-06)
    return (centre * inverse, inverse)


def norm_back(normed, inverse, upstream):
    return inverse * (
        upstream
        - jnp.mean(upstream, axis=-1, keepdims=True)
        - normed * jnp.mean(upstream * normed, axis=-1, keepdims=True)
    )


def dot_nn(a, b):
    return lax.dot_general(a, b, (((1,), (0,)), ((), ())), preferred_element_type=jnp.float32)


def dot_nt(a, b):
    return lax.dot_general(a, b, (((1,), (1,)), ((), ())), preferred_element_type=jnp.float32)


def dot_tn(a, b):
    return lax.dot_general(a, b, (((0,), (0,)), ((), ())), preferred_element_type=jnp.float32)


def key_mask(s_ref, groups, tokens, cols):
    block = tokens // groups // 4
    token = lax.broadcasted_iota(jnp.int32, (tokens, 128), 0)
    piece, within = (token // block, token % block)
    strip = (piece % 4) * groups + (s_ref[3] ^ (piece // 4))
    row = strip * (block // (cols // 2)) + within // (cols // 2)
    half = s_ref[0] // 2
    return jnp.where((row < half) & (within % (cols // 2) < half), 0.0, -1e30)


def store_sum(ref, part):
    @pl.when(pl.program_id(0) == 0)
    def _():
        ref[...] = part

    @pl.when(pl.program_id(0) > 0)
    def _():
        ref[...] += part


def attend_kernel(chunk, scale, groups, cols, s_ref, *refs):
    pieces, w_ref, t_ref = (refs[:groups], refs[groups], refs[groups + 1])
    o_refs = refs[groups + 2 : 2 * groups + 2]
    l_ref, u_sc, b_sc, q_sc, k_sc, v_sc, o_sc, l_sc = refs[2 * groups + 2 :]
    tokens = u_sc.shape[0]

    @pl.when(pl.program_id(0) == 0)
    def _():
        size = pieces[0].shape[0]
        for i, piece in enumerate(pieces):
            u_sc[i * size : (i + 1) * size, :] = piece[...]
        b_sc[...] = key_mask(s_ref, groups, tokens, cols)

    u = u_sc[...]
    for part in range(3):
        t_ref[part] = dot_nn(u, w_ref[part]).astype(jnp.bfloat16)
    q, k, v = (t_ref[0].astype(jnp.float32), t_ref[1].astype(jnp.float32), t_ref[2].astype(jnp.float32))
    lane = lax.broadcasted_iota(jnp.int32, (tokens, 128), 1)
    bias = b_sc[...]
    for head in range(2):
        here = (lane < 64) if head == 0 else (lane >= 64)
        spare = lane == (64 if head == 0 else 0)
        q_sc[head] = jnp.where(here, q * scale, jnp.where(spare, 1.0, 0.0)).astype(jnp.bfloat16)
        k_sc[head] = jnp.where(here, k, jnp.where(spare, bias, 0.0)).astype(jnp.bfloat16)
        v_sc[head] = jnp.where(here, v, 0.0).astype(jnp.bfloat16)

    def body(i, carry):
        at = pl.ds(pl.multiple_of(i * chunk, chunk), chunk)
        outs, logs = ([], [])
        for head in range(2):
            s = dot_nt(q_sc[head, at, :], k_sc[head])
            top = jnp.max(s, axis=1, keepdims=True)
            p = jnp.exp(s - top)
            total = jnp.sum(p, axis=1, keepdims=True)
            outs.append(dot_nn(p.astype(jnp.bfloat16), v_sc[head]) * (1.0 / total))
            logs.append(top + jnp.log(total))
        o_sc[at, :] = (outs[0] + outs[1]).astype(jnp.bfloat16)
        l_sc[at, :] = jnp.where(
            lax.broadcasted_iota(jnp.int32, (chunk, 128), 1) < 64, logs[0], logs[1]
        )
        return carry

    lax.fori_loop(0, tokens // chunk, body, 0, unroll=True)
    size = tokens // groups
    for i, o_ref in enumerate(o_refs):
        o_ref[...] = o_sc[i * size : (i + 1) * size, :]
    logs = l_sc[...].T
    l_ref[...] = jnp.concatenate(
        [logs[0:1], logs[64:65], jnp.zeros((6, tokens), jnp.float32)], axis=0
    )[None]


def attend(scalars, pieces, w, score_scale, cols):
    groups = len(pieces)
    features, width = w.shape[1:]
    tokens = groups * pieces[0].shape[0]
    chunk = min(512, tokens)
    piece_spec = pl.BlockSpec(pieces[0].shape, lambda j, s: (0, 0))
    return pl.pallas_call(
        functools.partial(attend_kernel, chunk, score_scale, groups, cols),
        grid_spec=pltpu.PrefetchScalarGridSpec(
            num_scalar_prefetch=1,
            grid=(width // 128,),
            in_specs=[piece_spec] * len(pieces)
            + [pl.BlockSpec((3, features, 128), lambda j, s: (0, 0, j))],
            out_specs=[pl.BlockSpec((3, tokens, 128), lambda j, s: (0, 0, j))]
            + [pl.BlockSpec((tokens // groups, 128), lambda j, s: (0, j))] * groups
            + [pl.BlockSpec((1, 8, tokens), lambda j, s: (j, 0, 0))],
            scratch_shapes=[
                pltpu.VMEM((tokens, features), jnp.bfloat16),
                pltpu.VMEM((tokens, 128), jnp.float32),
            ]
            + [pltpu.VMEM((2, tokens, 128), jnp.bfloat16)] * 3
            + [pltpu.VMEM((tokens, 128), jnp.bfloat16), pltpu.VMEM((tokens, 128), jnp.float32)],
        ),
        out_shape=[jax.ShapeDtypeStruct((3, tokens, width), jnp.bfloat16)]
        + [jax.ShapeDtypeStruct((tokens // groups, width), jnp.bfloat16)] * groups
        + [jax.ShapeDtypeStruct((width // 128, 8, tokens), jnp.float32)],
        cost_estimate=BRIEF,
        name="attend_forward",
    )(scalars, *pieces, w)


def attend_back_kernel(chunk, scale, groups, cols, first, s_ref, *refs):
    pieces, do_pieces, o_refs = (refs[:groups], refs[groups : 2 * groups], refs[2 * groups : 3 * groups])
    w_ref, t_ref, l_ref = refs[3 * groups : 3 * groups + 3]
    rest = refs[3 * groups + 3 :]
    if not first:
        prev_ref, rest = (rest[0], rest[1:])
    du_refs, g_ref = (rest[:groups], rest[groups])
    u_sc, b_sc, o_sc, din_sc, q_sc, k_sc, do_sc, dq_sc, dt_sc, d_sc = rest[groups + 1 :]
    tokens = u_sc.shape[0]
    size = pieces[0].shape[0]

    @pl.when(pl.program_id(0) == 0)
    def _():
        for i, piece in enumerate(pieces):
            u_sc[i * size : (i + 1) * size, :] = piece[...]
        b_sc[...] = key_mask(s_ref, groups, tokens, cols)

    for i, piece in enumerate(do_pieces):
        din_sc[i * size : (i + 1) * size, :] = piece[...]
    for i, piece in enumerate(o_refs):
        o_sc[i * size : (i + 1) * size, :] = piece[...]
    q, k, do = (t_ref[0].astype(jnp.float32), t_ref[1].astype(jnp.float32), din_sc[...])
    lane = lax.broadcasted_iota(jnp.int32, (tokens, 128), 1)
    bias = b_sc[...]
    do = do.astype(jnp.float32)
    inner = (do * o_sc[...].astype(jnp.float32)).T
    for head in range(2):
        here = (lane < 64) if head == 0 else (lane >= 64)
        spare = lane == (64 if head == 0 else 0)
        q_sc[head] = jnp.where(here, q * scale, jnp.where(spare, 1.0, 0.0)).astype(jnp.bfloat16)
        k_sc[head] = jnp.where(here, k, jnp.where(spare, bias, 0.0)).astype(jnp.bfloat16)
        do_sc[head] = jnp.where(here, do, 0.0).astype(jnp.bfloat16)
        d_sc[head : head + 1, :] = jnp.sum(
            inner[64 * head : 64 * head + 64], axis=0, keepdims=True
        )
    dq_sc[...] = jnp.zeros_like(dq_sc)

    def body(i, carry):
        at = pl.ds(pl.multiple_of(i * chunk, chunk), chunk)
        lanes = lax.broadcasted_iota(jnp.int32, (chunk, 128), 1)
        d_k, d_v, d_q = ([], [], [])
        for head in range(2):
            here = (lanes < 64) if head == 0 else (lanes >= 64)
            s = dot_nt(k_sc[head, at, :], q_sc[head])
            p = jnp.exp(s - l_ref[0, head : head + 1, :])
            d_p = dot_nt(t_ref[2, at, :], do_sc[head])
            d_s = (p * (d_p - d_sc[head : head + 1, :])).astype(jnp.bfloat16)
            d_v.append(dot_nn(p.astype(jnp.bfloat16), do_sc[head]))
            d_k.append(dot_nn(d_s, q_sc[head]))
            keys = jnp.where(here, t_ref[1, at, :].astype(jnp.float32), 0.0).astype(jnp.bfloat16)
            d_q.append(dot_tn(d_s, keys))
        dq_sc[...] += d_q[0] + d_q[1]
        dt_sc[at, 128:256] = jnp.where(lanes < 64, d_k[0], d_k[1]).astype(jnp.bfloat16)
        dt_sc[at, 256:384] = (d_v[0] + d_v[1]).astype(jnp.bfloat16)
        return carry

    lax.fori_loop(0, tokens // chunk, body, 0, unroll=True)
    dt_sc[:, 0:128] = (dq_sc[...] * scale).astype(jnp.bfloat16)
    for i, du_ref in enumerate(du_refs):
        at = slice(i * size, (i + 1) * size)
        part = dot_nt(dt_sc[at, 0:128], w_ref[0])
        part = part + dot_nt(dt_sc[at, 128:256], w_ref[1])
        part = part + dot_nt(dt_sc[at, 256:384], w_ref[2])
        store_sum(du_ref, part)
    grad = dot_tn(u_sc[...], dt_sc[...])
    for at in range(3):
        piece = grad[:, 128 * at : 128 * at + 128]
        if not first:
            piece = piece + prev_ref[at]
        g_ref[at] = piece.astype(g_ref.dtype)


def attend_back(scalars, pieces, d_pieces, outs, w, t, logs, score_scale, cols, prev, grad_type):
    groups = len(outs)
    features, width = w.shape[1:]
    tokens = t.shape[1]
    chunk = min(256, tokens)
    size = pieces[0].shape[0]
    blocks = width // 128
    weight_spec = pl.BlockSpec((3, features, 128), lambda j, s: (0, 0, j))
    offset = 0 if d_pieces[0].shape[1] == width else blocks
    args = list(pieces) + list(d_pieces) + list(outs) + [w, t, logs]
    args += [] if prev is None else [prev]
    return pl.pallas_call(
        functools.partial(attend_back_kernel, chunk, score_scale, groups, cols, prev is None),
        grid_spec=pltpu.PrefetchScalarGridSpec(
            num_scalar_prefetch=1,
            grid=(blocks,),
            in_specs=[pl.BlockSpec((size, features), lambda j, s: (0, 0))] * len(pieces)
            + [pl.BlockSpec((size, 128), lambda j, s: (0, s[3] * offset + j))] * len(d_pieces)
            + [pl.BlockSpec((size, 128), lambda j, s: (0, j))] * groups
            + [
                weight_spec,
                pl.BlockSpec((3, tokens, 128), lambda j, s: (0, 0, j)),
                pl.BlockSpec((1, 8, tokens), lambda j, s: (j, 0, 0)),
            ]
            + ([] if prev is None else [weight_spec]),
            out_specs=[pl.BlockSpec((size, features), lambda j, s: (0, 0))] * groups
            + [weight_spec],
            scratch_shapes=[
                pltpu.VMEM((tokens, features), jnp.bfloat16),
                pltpu.VMEM((tokens, 128), jnp.float32),
                pltpu.VMEM((tokens, 128), jnp.bfloat16),
                pltpu.VMEM((tokens, 128), jnp.bfloat16),
            ]
            + [pltpu.VMEM((2, tokens, 128), jnp.bfloat16)] * 3
            + [
                pltpu.VMEM((tokens, 128), jnp.float32),
                pltpu.VMEM((tokens, 384), jnp.bfloat16),
                pltpu.VMEM((8, tokens), jnp.float32),
            ],
        ),
        out_shape=[jax.ShapeDtypeStruct((size, features), jnp.float32)] * groups
        + [jax.ShapeDtypeStruct(w.shape, grad_type)],
        cost_estimate=COVER,
        name="attend_backward",
    )(scalars, *args)


def shift_cols(x, by, col):
    size = x.shape[0]
    rolled = pltpu.roll(x, (-by) % size, 0)
    return jnp.where(col == (size - 1 if by > 0 else 0), 0.0, rolled)


def wide_taps(c_ref, lanes, cols):
    return [
        jnp.broadcast_to(c_ref[k : k + 1, lanes].astype(jnp.float32), (cols, 128)) for k in range(9)
    ]


def sublane_sum(x):
    return jnp.sum(x.reshape(x.shape[0] // 8, 8, 128), axis=0)


def modulate(x, m_ref, shift_at, col, row, side):
    normed, _ = normalize(x.astype(jnp.float32))
    value = normed * (1.0 + m_ref[shift_at + 1 : shift_at + 2, :]) + m_ref[shift_at : shift_at + 1, :]
    live = (col < side) & (row >= 0) & (row < side)
    return jnp.where(live, value, 0.0).astype(jnp.bfloat16)


def modulated_rows(a_sc, s_ref, x_ref, top_ref, end_ref, m_ref):
    rows, cols, features = x_ref.shape
    side, row_zero = (s_ref[0], s_ref[1])
    col = lax.broadcasted_iota(jnp.int32, (cols, features), 0)
    a_sc[0] = modulate(top_ref[...], m_ref, 0, col, row_zero - 1, side)
    a_sc[rows + 1] = modulate(end_ref[...], m_ref, 0, col, row_zero + rows, side)

    def body(r, carry):
        a_sc[r + 1] = modulate(x_ref[r], m_ref, 0, col, row_zero + r, side)
        return carry

    lax.fori_loop(0, rows, body, 0)


def to_maps(canvas, maps_ref):
    blocks, rows, cols, _ = canvas.shape
    half = cols // 2

    def body(r, carry):
        at = pl.ds(pl.multiple_of(r * half, half), half)
        for m in range(4):
            for b in range(blocks):
                part = canvas[b, 2 * r + m // 2, pl.ds(m % 2, half, stride=2), :]
                maps_ref[m, at, 128 * b : 128 * b + 128] = part.astype(jnp.bfloat16)
        return carry

    lax.fori_loop(0, rows // 2, body, 0)


def from_maps(maps_ref, canvas, row_offset):
    half = canvas.shape[2] // 2
    rows = maps_ref.shape[1] // half * 2

    def body(r, carry):
        at = pl.ds(pl.multiple_of(r * half, half), half)
        for m in range(4):
            for b in range(canvas.shape[0]):
                part = maps_ref[m, at, 128 * b : 128 * b + 128].astype(jnp.float32)
                canvas[b, row_offset + 2 * r + m // 2, pl.ds(m % 2, half, stride=2), :] = part
        return carry

    lax.fori_loop(0, rows // 2, body, 0)


def before_kernel(s_ref, x_ref, top_ref, end_ref, m_ref, c_ref, *refs):
    maps_ref, a_sc, t_sc = refs
    rows, cols, features = x_ref.shape
    modulated_rows(a_sc, s_ref, x_ref, top_ref, end_ref, m_ref)
    col = lax.broadcasted_iota(jnp.int32, (cols, 128), 0)
    for first in range(0, features, 128):
        lanes = slice(first, first + 128)
        taps = wide_taps(c_ref, lanes, cols)

        def body(r, carry):
            x = [a_sc[r + i, :, lanes].astype(jnp.float32) for i in range(3)]
            a = [x[0] * taps[j] + x[1] * taps[3 + j] + x[2] * taps[6 + j] for j in range(3)]
            t_sc[first // 128, r] = a[1] + shift_cols(a[0], -1, col) + shift_cols(a[2], 1, col)
            return carry

        lax.fori_loop(0, rows, body, 0)
    to_maps(t_sc, maps_ref)


def canvas_specs(latents, at):
    rows, cols, features = latents.shape[2:]
    return [
        pl.BlockSpec((None, None, rows, cols, features), lambda j, s: (at, 0, 0, 0, 0)),
        pl.BlockSpec((None, cols, features), lambda j, s: (at, 0, 0)),
        pl.BlockSpec((None, cols, features), lambda j, s: (at, 0, 0)),
        pl.BlockSpec((None, 6, features), lambda j, s: (at, 0, 0)),
    ]


def whole_spec(shape):
    return pl.BlockSpec(shape, lambda j, s: (0,) * len(shape))


def before_attention(at, scalars, latents, top, end, mods, taps):
    rows, cols, features = latents.shape[2:]
    maps = (4, rows * cols // 4, features)
    return pl.pallas_call(
        before_kernel,
        grid_spec=pltpu.PrefetchScalarGridSpec(
            num_scalar_prefetch=1,
            grid=(1,),
            in_specs=canvas_specs(latents, at) + [whole_spec(taps.shape)],
            out_specs=whole_spec(maps),
            scratch_shapes=[
                pltpu.VMEM((rows + 2, cols, features), jnp.bfloat16),
                pltpu.VMEM((features // 128, rows, cols, 128), jnp.float32),
            ],
        ),
        out_shape=jax.ShapeDtypeStruct(maps, jnp.bfloat16),
        cost_estimate=COVER,
        name="before_attention",
    )(scalars, latents, top, end, mods, taps)


def join_kernel(s_ref, mine_ref, other_ref, out_ref):
    width = mine_ref.shape[1]

    def write(low_ref, high_ref):
        out_ref[:, :width] = low_ref[...]
        out_ref[:, width:] = high_ref[...]

    @pl.when(s_ref[3] == 0)
    def _():
        write(mine_ref, other_ref)

    @pl.when(s_ref[3] == 1)
    def _():
        write(other_ref, mine_ref)


def join_groups(scalars, parts, width):
    groups = len(parts)
    tokens = parts[0].shape[0]
    shape = (tokens, groups * width)
    if groups != 2 or parts[0].shape[1] != width:
        whole = place_blocks([part[:, :width] for part in parts], scalars[3])
        whole = whole.transpose(1, 0, 2)
    else:
        whole = pl.pallas_call(
            join_kernel,
            grid_spec=pltpu.PrefetchScalarGridSpec(
                num_scalar_prefetch=1,
                grid=(1,),
                in_specs=[whole_spec(part.shape) for part in parts],
                out_specs=whole_spec(shape),
            ),
            out_shape=jax.ShapeDtypeStruct(shape, parts[0].dtype),
            cost_estimate=BRIEF,
            name="join_groups",
        )(scalars, *parts)
    return whole.reshape(4, tokens // 4, groups * width)


def sum_kernel(count, *refs):
    total = refs[0][...]
    for part in refs[1:count]:
        total = total + part[...]
    refs[count][...] = total.astype(refs[count].dtype)


def sum_groups(parts):
    tokens, features = parts[0].shape
    total = pl.pallas_call(
        functools.partial(sum_kernel, len(parts)),
        out_shape=jax.ShapeDtypeStruct((tokens, features), jnp.bfloat16),
        cost_estimate=COVER,
        name="sum_groups",
    )(*parts)
    return total.reshape(4, tokens // 4, features)


def edge_kernel(top_ref, end_ref, first_ref, last_ref):
    half = top_ref.shape[1]
    for j in range(2):
        first_ref[j * half : (j + 1) * half, :] = top_ref[j]
        last_ref[j * half : (j + 1) * half, :] = end_ref[j]


def edge_rows(maps, cols):
    size, features = maps.shape[1:]
    half = cols // 2
    row = (cols, features)
    return pl.pallas_call(
        edge_kernel,
        grid=(1,),
        in_specs=[
            pl.BlockSpec((2, half, features), lambda j: (0, 0, 0)),
            pl.BlockSpec((2, half, features), lambda j: (1, size // half - 1, 0)),
        ],
        out_specs=[pl.BlockSpec(row, lambda j: (0, 0))] * 2,
        out_shape=[jax.ShapeDtypeStruct(row, maps.dtype)] * 2,
        cost_estimate=COVER,
        name="edge_rows",
    )(maps, maps)


def expand_kernel(s_ref, o_ref, x_ref, m_ref, wp_ref, w_ref, b_ref, *refs):
    oc_ref, at_ref, x1_ref, a2_ref, f_ref, first_ref, last_ref, t_sc = refs
    rows, cols, features = x_ref.shape
    side, row_zero = (s_ref[0], s_ref[1])

    @pl.when(pl.program_id(0) == 0)
    def _():
        from_maps(o_ref, t_sc, 0)
        for b in range(features // 128):
            part = t_sc[b].reshape(rows * cols, 128)
            oc_ref[:, 128 * b : 128 * b + 128] = part.astype(jnp.bfloat16)
        at_ref[...] = dot_nn(oc_ref[...], wp_ref[...])

        def body(r, carry):
            here = pl.ds(pl.multiple_of(r * cols, cols), cols)
            x1 = x_ref[r].astype(jnp.float32) + m_ref[2:3, :] * at_ref[here, :]
            x1_ref[here, :] = x1
            normed, _ = normalize(x1)
            a2 = normed * (1.0 + m_ref[4:5, :]) + m_ref[3:4, :]
            a2_ref[here, :] = a2.astype(jnp.bfloat16)
            return carry

        lax.fori_loop(0, rows, body, 0)

    block = f_ref.shape[2]
    f = (dot_nn(a2_ref[...], w_ref[...]) + b_ref[...].astype(jnp.float32)).reshape(rows, cols, block)
    col = lax.broadcasted_iota(jnp.int32, (cols, block), 0)
    for r in range(rows):
        live = (col < side) & (row_zero + r < side)
        f_ref[r] = jnp.where(live, f[r], 0.0).astype(jnp.bfloat16)
    first_ref[...] = f_ref[0:1]
    last_ref[...] = f_ref[rows - 1 : rows]


def expand(at, scalars, maps, latents, mods, w_proj, w_fc1, bias):
    rows, cols, features = latents.shape[2:]
    hidden = w_fc1.shape[1]
    tokens, block = (rows * cols, 512)
    flat = (tokens, features)
    specs = canvas_specs(latents, at)
    return pl.pallas_call(
        expand_kernel,
        grid_spec=pltpu.PrefetchScalarGridSpec(
            num_scalar_prefetch=1,
            grid=(hidden // block,),
            in_specs=[
                whole_spec(maps.shape),
                specs[0],
                specs[3],
                whole_spec(w_proj.shape),
                pl.BlockSpec((features, block), lambda j, s: (0, j)),
                pl.BlockSpec((1, block), lambda j, s: (0, j)),
            ],
            out_specs=[whole_spec(flat)] * 4
            + [pl.BlockSpec((rows, cols, block), lambda j, s: (0, 0, j))]
            + [pl.BlockSpec((1, cols, block), lambda j, s: (0, 0, j))] * 2,
            scratch_shapes=[pltpu.VMEM((features // 128, rows, cols, 128), jnp.float32)],
        ),
        out_shape=[
            jax.ShapeDtypeStruct(flat, jnp.bfloat16),
            jax.ShapeDtypeStruct(flat, jnp.float32),
            jax.ShapeDtypeStruct(flat, jnp.float32),
            jax.ShapeDtypeStruct(flat, jnp.bfloat16),
            jax.ShapeDtypeStruct((rows, cols, hidden), jnp.bfloat16),
        ]
        + [jax.ShapeDtypeStruct((1, cols, hidden), jnp.bfloat16)] * 2,
        cost_estimate=COVER,
        name="expand",
    )(scalars, maps, latents, mods, w_proj, w_fc1, bias)


def middle_kernel(first, s_ref, f_ref, top_ref, end_ref, c_ref, w_ref, ct_ref, x1_ref, m_ref, *rest):
    if first:
        mixed_ref, dg_ref, dz_ref, g_ref, gc_ref, first_ref, last_ref = rest[:7]
    else:
        gp_ref, gcp_ref = rest[:2]
        mixed_ref, dg_ref, dz_ref, g_ref, gc_ref, first_ref, last_ref = rest[3:10]
    gz_sc = rest[-1:]
    out_sc, d_sc, x_sc, t_sc, acc_sc = rest[-6:-1]
    rows, cols, block = f_ref.shape
    features = out_sc.shape[1]
    side, row_zero = (s_ref[0], s_ref[1])

    def upstream(r):
        col = lax.broadcasted_iota(jnp.int32, (cols, features), 0)
        live = (col < side) & (row_zero + r < side)
        return jnp.where(live, ct_ref[r].astype(jnp.float32), 0.0), live

    @pl.when(pl.program_id(0) == 0)
    def _():
        def body(r, carry):
            here = pl.ds(pl.multiple_of(r * cols, cols), cols)
            d_sc[here, :] = (upstream(r)[0] * m_ref[5:6, :]).astype(jnp.bfloat16)
            return carry

        lax.fori_loop(0, rows, body, 0)

    d = d_sc[...]
    x_sc[0:1] = top_ref[...]
    x_sc[1 : rows + 1] = f_ref[...]
    x_sc[rows + 1 : rows + 2] = end_ref[...]
    acc_sc[...] = jnp.zeros_like(acc_sc)
    col = lax.broadcasted_iota(jnp.int32, (cols, 128), 0)
    wide = 256
    count = block // wide
    part, grads = (None, [])

    def start(s):
        t = dot_nt(d, w_ref[s * wide : (s + 1) * wide, :])
        for l in range(wide // 128):
            t_sc[s * (wide // 128) + l] = t[:, 128 * l : 128 * l + 128].reshape(rows, cols, 128)

    start(0)
    for s in range(count):
        if s + 1 < count:
            start(s + 1)
        for l in range(wide // 128):
            at = s * (wide // 128) + l
            lanes = slice(128 * at, 128 * at + 128)
            inner = slice(128 * l, 128 * l + 128)
            taps = wide_taps(c_ref, lanes, cols)

            def body(r, carry):
                x = [x_sc[r + i, :, lanes].astype(jnp.float32) for i in range(3)]
                a = [x[0] * taps[j] + x[1] * taps[3 + j] + x[2] * taps[6 + j] for j in range(3)]
                z = a[1] + shift_cols(a[0], -1, col) + shift_cols(a[2], 1, col)
                half = 0.5 * (1.0 + lax.erf(z * root_half))
                gz_sc[s][r * cols : (r + 1) * cols, inner] = (z * half).astype(jnp.bfloat16)
                slope = half + z * jnp.exp(-0.5 * z * z) * inverse_root_tau
                d_z = (t_sc[at, r] * slope).astype(jnp.bfloat16)
                dz_ref[r, :, lanes] = d_z
                d_z = d_z.astype(jnp.float32)
                moved = [shift_cols(d_z, 1, col), d_z, shift_cols(d_z, -1, col)]
                return [
                    c + sublane_sum(x[k // 3] * moved[k % 3]) for k, c in enumerate(carry)
                ]

            sums = [jnp.zeros((8, 128), jnp.float32)] * 9
            for r in range(rows):
                sums = body(r, sums)
            for k in range(9):
                acc_sc[k, :, lanes] = sums[k]
        gz = gz_sc[s][...]
        here = dot_nn(gz, w_ref[s * wide : (s + 1) * wide, :])
        part = here if part is None else part + here
        grads.append(dot_tn(gz, d))
    first_ref[...] = dz_ref[0:1]
    last_ref[...] = dz_ref[rows - 1 : rows]
    store_sum(out_sc, part)
    grad = jnp.concatenate(grads, axis=0)
    taps_grad = jnp.concatenate(
        [jnp.sum(acc_sc[k], axis=0, keepdims=True) for k in range(9)], axis=0
    )
    if not first:
        grad = grad + gp_ref[...]
        taps_grad = taps_grad + gcp_ref[...]
    g_ref[...] = grad.astype(g_ref.dtype)
    gc_ref[...] = taps_grad

    @pl.when(pl.program_id(0) == pl.num_programs(0) - 1)
    def _():
        def body(r, total):
            here = pl.ds(pl.multiple_of(r * cols, cols), cols)
            value, live = upstream(r)
            out = out_sc[here, :]
            mixed = x1_ref[here, :] + m_ref[5:6, :] * out
            mixed_ref[r] = jnp.where(live, mixed, 0.0).astype(jnp.bfloat16)
            return total + sublane_sum(value * out)

        total = lax.fori_loop(0, rows, body, jnp.zeros((8, features), jnp.float32))
        dg_ref[...] = jnp.sum(total, axis=0, keepdims=True)


def sublane_sum(x):
    return jnp.sum(x.reshape(x.shape[0] // 8, 8, x.shape[1]), axis=0)


def ffn_middle(at, scalars, f, halo, taps, w, cotangent, x1, mods, prev, grad_type):
    rows, cols, hidden = f.shape
    features = w.shape[1]
    block = 256
    wide = lambda j, s: (0, 0, j)
    row_spec = pl.BlockSpec((1, cols, block), wide)
    weight_spec = pl.BlockSpec((block, features), lambda j, s: (j, 0))
    tap_spec = pl.BlockSpec((9, block), lambda j, s: (0, j))
    canvas_spec = pl.BlockSpec((rows, cols, block), wide)
    specs = canvas_specs(cotangent, at)
    args = [scalars, f, halo[0], halo[1], taps, w, cotangent, x1, mods]
    args += [] if prev is None else list(prev)
    return pl.pallas_call(
        functools.partial(middle_kernel, prev is None),
        grid_spec=pltpu.PrefetchScalarGridSpec(
            num_scalar_prefetch=1,
            grid=(hidden // block,),
            in_specs=[canvas_spec, row_spec, row_spec, tap_spec, weight_spec]
            + [specs[0], whole_spec(x1.shape), specs[3]]
            + ([] if prev is None else [weight_spec, tap_spec, pl.BlockSpec(memory_space=pl.ANY)]),
            out_specs=[specs[0], whole_spec((1, features)), canvas_spec, weight_spec, tap_spec]
            + [row_spec] * 2,
            scratch_shapes=[
                pltpu.VMEM((rows * cols, features), jnp.float32),
                pltpu.VMEM((rows * cols, features), jnp.bfloat16),
                pltpu.VMEM((rows + 2, cols, block), jnp.bfloat16),
                pltpu.VMEM((block // 128, rows, cols, 128), jnp.float32),
                pltpu.VMEM((9, 8, block), jnp.float32),
            ]
            + [pltpu.VMEM((rows * cols, 256), jnp.bfloat16)] * 1,
        ),
        out_shape=[
            jax.ShapeDtypeStruct(cotangent.shape, jnp.bfloat16),
            jax.ShapeDtypeStruct((1, features), jnp.float32),
            jax.ShapeDtypeStruct(f.shape, jnp.bfloat16),
            jax.ShapeDtypeStruct((hidden, features), grad_type),
            jax.ShapeDtypeStruct((9, hidden), jnp.float32),
        ]
        + [jax.ShapeDtypeStruct((1, cols, hidden), jnp.bfloat16)] * 2,
        input_output_aliases={} if prev is None else {11: 0},
        cost_estimate=COVER,
        name="ffn_middle",
    )(*args)


def ffn_back_kernel(micro, first, s_ref, z_ref, top_ref, end_ref, c_ref, w_ref, a_ref, *rest):
    far, m_ref = (rest[:5], rest[5])
    near, sem = (rest[-6:-1], rest[-1])
    rest = rest[6:-6]
    ct_ref, x1_ref, at_ref, oc_ref, wp_ref = near
    copies = [
        pltpu.make_async_copy(source.at[micro, 0] if i == 0 else source, target, sem.at[i])
        for i, (source, target) in enumerate(zip(far, near))
    ]

    @pl.when(pl.program_id(0) == 0)
    def _():
        for copy in copies:
            copy.start()

    if not first:
        gp_ref, gbp_ref, gpp_ref = rest[:3]
        rest = rest[3:]
    maps_ref, dx_ref, dm_ref, g_ref, gb_ref, gp_out = rest[:6]
    da_sc, x_sc, df_sc, acc_sc, t_sc, dat_sc = rest[6:]
    rows, cols, block = z_ref.shape
    features = da_sc.shape[1]
    x_sc[0:1] = top_ref[...]
    x_sc[1 : rows + 1] = z_ref[...]
    x_sc[rows + 1 : rows + 2] = end_ref[...]
    acc_sc[...] = jnp.zeros_like(acc_sc)
    col = lax.broadcasted_iota(jnp.int32, (cols, 128), 0)
    side, row_zero = (s_ref[0], s_ref[1])
    for at in range(block // 128):
        lanes = slice(128 * at, 128 * at + 128)
        taps = wide_taps(c_ref, lanes, cols)
        total = jnp.zeros((8, 128), jnp.float32)
        for r in range(rows):
            x = [x_sc[r + i, :, lanes].astype(jnp.float32) for i in range(3)]
            b = [x[2] * taps[j] + x[1] * taps[3 + j] + x[0] * taps[6 + j] for j in range(3)]
            d_f = b[1] + shift_cols(b[0], 1, col) + shift_cols(b[2], -1, col)
            live = (col < side) & (row_zero + r < side)
            d_f = jnp.where(live, d_f, 0.0).astype(jnp.bfloat16)
            df_sc[r, :, lanes] = d_f
            total = total + sublane_sum(d_f.astype(jnp.float32))
        acc_sc[:, lanes] = total
    d_f = df_sc[...].reshape(rows * cols, block)
    store_sum(da_sc, dot_nt(d_f, w_ref[...]))
    grad = dot_tn(a_ref[...], d_f)
    bias_grad = jnp.sum(acc_sc[...], axis=0, keepdims=True)
    if not first:
        grad = grad + gp_ref[...]
        bias_grad = bias_grad + gbp_ref[...]
    g_ref[...] = grad.astype(g_ref.dtype)
    gb_ref[...] = bias_grad

    @pl.when(pl.program_id(0) == pl.num_programs(0) - 1)
    def _():
        for copy in copies:
            copy.wait()
        wide_col = lax.broadcasted_iota(jnp.int32, (cols, features), 0)

        def body(r, totals):
            here = pl.ds(pl.multiple_of(r * cols, cols), cols)
            d_a = da_sc[here, :]
            normed, inverse = normalize(x1_ref[here, :])
            live = (wide_col < side) & (row_zero + r < side)
            d_x = jnp.where(live, ct_ref[r].astype(jnp.float32), 0.0)
            d_x = d_x + norm_back(normed, inverse, d_a * (1.0 + m_ref[4:5, :]))
            dx_ref[here, :] = d_x
            dat_sc[here, :] = (d_x * m_ref[2:3, :]).astype(jnp.bfloat16)
            return (
                totals[0] + sublane_sum(d_x * at_ref[here, :]),
                totals[1] + sublane_sum(d_a),
                totals[2] + sublane_sum(d_a * normed),
            )

        zero = jnp.zeros((8, features), jnp.float32)
        totals = lax.fori_loop(0, rows, body, (zero, zero, zero))
        for i in range(3):
            dm_ref[i : i + 1, :] = jnp.sum(totals[i], axis=0, keepdims=True)
        proj = dot_tn(oc_ref[...], dat_sc[...])
        if not first:
            proj = proj + gpp_ref[...]
        gp_out[...] = proj.astype(gp_out.dtype)
        d_o = dot_nt(dat_sc[...], wp_ref[...])
        for b in range(features // 128):
            t_sc[b] = d_o[:, 128 * b : 128 * b + 128].reshape(rows, cols, 128)
        to_maps(t_sc, maps_ref)


def ffn_back(
    at, scalars, d_z, halo, taps, w, a, cotangent, x1, attn, oc, w_proj, mods, prev, grad_type
):
    rows, cols, hidden = d_z.shape
    features = a.shape[1]
    block = 512
    wide = lambda j, s: (0, 0, j)
    row_spec = pl.BlockSpec((1, cols, block), wide)
    weight_spec = pl.BlockSpec((features, block), lambda j, s: (0, j))
    bias_spec = pl.BlockSpec((1, block), lambda j, s: (0, j))
    flat_spec = whole_spec((rows * cols, features))
    proj_spec = whole_spec(w_proj.shape)
    maps = (4, rows * cols // 4, features)
    specs = canvas_specs(cotangent, at)
    args = [scalars, d_z, halo[0], halo[1], taps, w, a, cotangent, x1, attn, oc, w_proj, mods]
    args += [] if prev is None else list(prev)
    return pl.pallas_call(
        functools.partial(ffn_back_kernel, at, prev is None),
        grid_spec=pltpu.PrefetchScalarGridSpec(
            num_scalar_prefetch=1,
            grid=(hidden // block,),
            in_specs=[
                pl.BlockSpec((rows, cols, block), wide),
                row_spec,
                row_spec,
                pl.BlockSpec((9, block), lambda j, s: (0, j)),
                weight_spec,
                flat_spec,
            ]
            + [HBM] * 5
            + [
                specs[3],
            ]
            + ([] if prev is None else [weight_spec, bias_spec, proj_spec]),
            out_specs=[whole_spec(maps)]
            + [flat_spec, whole_spec((3, features)), weight_spec, bias_spec, proj_spec],
            scratch_shapes=[
                pltpu.VMEM((rows * cols, features), jnp.float32),
                pltpu.VMEM((rows + 2, cols, block), jnp.bfloat16),
                pltpu.VMEM((rows, cols, block), jnp.bfloat16),
                pltpu.VMEM((8, block), jnp.float32),
                pltpu.VMEM((features // 128, rows, cols, 128), jnp.float32),
                pltpu.VMEM((rows * cols, features), jnp.bfloat16),
                pltpu.VMEM((rows, cols, features), cotangent.dtype),
                pltpu.VMEM(x1.shape, x1.dtype),
                pltpu.VMEM(attn.shape, attn.dtype),
                pltpu.VMEM(oc.shape, oc.dtype),
                pltpu.VMEM(w_proj.shape, w_proj.dtype),
                pltpu.SemaphoreType.DMA((5,)),
            ],
        ),
        out_shape=[jax.ShapeDtypeStruct(maps, jnp.bfloat16)]
        + [
            jax.ShapeDtypeStruct((rows * cols, features), jnp.float32),
            jax.ShapeDtypeStruct((3, features), jnp.float32),
            jax.ShapeDtypeStruct(w.shape, grad_type),
            jax.ShapeDtypeStruct((1, hidden), jnp.float32),
            jax.ShapeDtypeStruct(w_proj.shape, grad_type),
        ],
        cost_estimate=COVER,
        name="ffn_backward",
    )(*args)


def last_kernel(first, s_ref, du_ref, dtop_ref, dend_ref, *rest):
    x_ref, top_ref, end_ref, m_ref, c_ref, dx_ref = rest[:6]
    rest = rest[6:]
    if not first:
        gcp_ref = rest[0]
        rest = rest[2:]
    dl_ref, dm_ref, gc_ref, a_sc, t_sc, d_sc, acc_sc = rest
    rows, cols, features = x_ref.shape
    half = cols // 2
    side, row_zero = (s_ref[0], s_ref[1])
    modulated_rows(a_sc, s_ref, x_ref, top_ref, end_ref, m_ref)
    from_maps(du_ref, t_sc, 1)
    for at, ref in ((0, dtop_ref), (rows + 1, dend_ref)):
        for j in range(2):
            for start in range(0, features, 128):
                lanes = slice(start, start + 128)
                part = ref[j * half : (j + 1) * half, lanes].astype(jnp.float32)
                t_sc[start // 128, at, pl.ds(j, half, stride=2), :] = part
    acc_sc[...] = jnp.zeros_like(acc_sc)
    col = lax.broadcasted_iota(jnp.int32, (cols, 128), 0)
    for start in range(0, features, 128):
        lanes = slice(start, start + 128)
        taps = wide_taps(c_ref, lanes, cols)

        def conv_body(r, carry):
            d = [t_sc[start // 128, r + i] for i in range(3)]
            b = [d[2] * taps[j] + d[1] * taps[3 + j] + d[0] * taps[6 + j] for j in range(3)]
            d_a = b[1] + shift_cols(b[0], 1, col) + shift_cols(b[2], -1, col)
            live = (col < side) & (row_zero + r < side)
            d_sc[r, :, lanes] = jnp.where(live, d_a, 0.0)
            moved = [shift_cols(d[1], 1, col), d[1], shift_cols(d[1], -1, col)]
            for i in range(3):
                x = a_sc[r + i, :, lanes].astype(jnp.float32)
                for j in range(3):
                    acc_sc[3 * i + j, :, lanes] += sublane_sum(x * moved[j])
            return carry

        lax.fori_loop(0, rows, conv_body, 0, unroll=2)
    taps_grad = jnp.concatenate(
        [jnp.sum(acc_sc[k], axis=0, keepdims=True) for k in range(9)], axis=0
    )
    if not first:
        taps_grad = taps_grad + gcp_ref[...]
    gc_ref[...] = taps_grad

    def body(r, totals):
        here = pl.ds(pl.multiple_of(r * cols, cols), cols)
        normed, inverse = normalize(x_ref[r].astype(jnp.float32))
        d_a = d_sc[r]
        dl_ref[r] = dx_ref[here, :] + norm_back(normed, inverse, d_a * (1.0 + m_ref[1:2, :]))
        return (totals[0] + sublane_sum(d_a), totals[1] + sublane_sum(d_a * normed))

    zero = jnp.zeros((8, features), jnp.float32)
    totals = lax.fori_loop(0, rows, body, (zero, zero))
    for i in range(2):
        dm_ref[i : i + 1, :] = jnp.sum(totals[i], axis=0, keepdims=True)


def last_stage(at, scalars, maps, d_halo, latents, top, end, mods, taps, d_x, prev):
    rows, cols, features = latents.shape[2:]
    specs = canvas_specs(latents, at)
    args = [scalars, maps, *d_halo, latents, top, end, mods, taps, d_x]
    args += [] if prev is None else list(prev)
    return pl.pallas_call(
        functools.partial(last_kernel, prev is None),
        grid_spec=pltpu.PrefetchScalarGridSpec(
            num_scalar_prefetch=1,
            grid=(1,),
            in_specs=[whole_spec(maps.shape)]
            + [whole_spec((cols, features))] * 2
            + specs
            + [whole_spec(taps.shape), whole_spec(d_x.shape)]
            + ([] if prev is None else [whole_spec(taps.shape), pl.BlockSpec(memory_space=pl.ANY)]),
            out_specs=[specs[0], whole_spec((2, features)), whole_spec(taps.shape)],
            scratch_shapes=[
                pltpu.VMEM((rows + 2, cols, features), jnp.bfloat16),
                pltpu.VMEM((features // 128, rows + 2, cols, 128), jnp.float32),
                pltpu.VMEM((rows, cols, features), jnp.float32),
                pltpu.VMEM((9, 8, features), jnp.float32),
            ],
        ),
        out_shape=[
            jax.ShapeDtypeStruct(latents.shape, jnp.float32),
            jax.ShapeDtypeStruct((2, features), jnp.float32),
            jax.ShapeDtypeStruct(taps.shape, jnp.float32),
        ],
        input_output_aliases={} if prev is None else {11: 0},
        cost_estimate=COVER,
        name="last_stage",
    )(*args)


def shards(
    latents,
    timesteps,
    size_tags,
    w_ada,
    b_ada,
    conv_attn,
    w_qkv,
    w_proj,
    w_fc1,
    b_fc1,
    conv_ffn,
    w_fc2,
    cotangent,
):
    micro_count, _, row_count, side_count, features = latents.shape
    dp, strips = (lax.axis_size("dp"), lax.axis_size("strip"))
    dp_at, strip_at = (lax.axis_index("dp"), lax.axis_index("strip"))
    hidden = conv_ffn.shape[1] * dp
    groups = strips // 4
    group_at, map_at = (strip_at % groups, strip_at // groups)
    score_scale = (features // HEADS) ** (-0.5)
    width = features // groups

    stamps = timesteps[:, 0].astype(jnp.float32)
    small = jnp.concatenate([conv_attn.reshape(-1), conv_ffn.reshape(-1), b_fc1])
    small = gather_butterfly(jnp.concatenate([stamps, small.astype(jnp.float32)])[None])
    all_stamps, small = (small[:, :micro_count], small[:, micro_count:].astype(jnp.bfloat16))
    conds = [silu_of(embed_times(all_stamps[k], features)) for k in range(dp)]
    ada_rows = features // dp
    ada_wide = w_ada.astype(jnp.float32)
    partial_mods = jnp.dot(
        lax.dynamic_slice_in_dim(jnp.concatenate(conds), dp_at * ada_rows, ada_rows, 1),
        ada_wide,
        precision=lax.Precision.HIGHEST,
    )
    bias_here = lax.dynamic_update_slice_in_dim(
        jnp.zeros((6 * features,), jnp.float32),
        b_ada.astype(jnp.float32),
        dp_at * b_ada.shape[0],
        0,
    )
    partial_mods = (partial_mods + bias_here[None, :]).reshape(dp, micro_count, 6 * features)
    count = dp
    while count > 1:
        count //= 2
        partial_mods = partial_mods[:count] + permute_xor(partial_mods[count:], "dp", count)
    modulation = partial_mods[0]

    small = place_blocks([small[k] for k in range(dp)], dp_at)
    n_one, n_two = (conv_attn.size, conv_attn.size + conv_ffn.size)
    conv_one = small[:, :n_one].reshape(dp, 9, -1).transpose(1, 0, 2).reshape(9, features)
    conv_two = small[:, n_one:n_two].reshape(dp, 9, -1).transpose(1, 0, 2).reshape(9, hidden)
    fc1_bias = small[:, n_two:].reshape(1, hidden)
    qkv_pieces, modulation = fetch_group(w_qkv, groups, modulation)
    packed = pack_weights(w_proj, w_fc1, w_fc2)

    top, end = halo_rows(latents[:, 0, 0], latents[:, 0, row_count - 1])
    mods = modulation.reshape(micro_count, 6, features)
    micros = range(micro_count)
    places = jnp.stack([strip_at * row_count, map_at, group_at]).astype(jnp.int32)
    scalars = [
        jnp.concatenate(
            [jnp.where(size_tags[at] == 1, side_count, side_count // 2).astype(jnp.int32), places]
        )
        for at in micros
    ]
    kept = [{} for _ in micros]
    turn = ()

    for at in micros:
        if at == micro_count - 1:
            qkv_group = gather_group(qkv_pieces)
            turn = (turn, qkv_group)
        maps = before_attention(at, after(scalars[at], turn), latents, top, end, mods, conv_one)
        if at == 0:
            packed, maps = tie(packed, maps)
            fetched = fetch_direct(packed)
        turn = maps
        kept[at]["u"] = map_exchange(maps, groups).reshape(-1, features)

    for at in micros:
        keep = kept[at]
        u = after(keep["u"], turn if at == 0 else kept[at - 1]["logs"])
        keep["u"] = group_exchange(u, groups)
        done = attend(after(scalars[at], turn), keep["u"], qkv_group, score_scale, side_count)
        keep["t"], keep["o"], keep["logs"] = (done[0], done[1 : 1 + groups], done[-1])
        parts = [keep["o"][0]] + [
            permute_xor(keep["o"][k], "strip", k) for k in range(1, groups)
        ]
        if at == 0:
            fetched, keep["logs"] = tie(fetched, keep["logs"])
            direct = list(fetched.values())
            fetched = fetch_relayed(fetched)
        if at == micro_count - 1:
            for k in range(1, dp):
                if k & (k - 1):
                    fetched[k - 1], keep["logs"] = tie(fetched[k - 1], keep["logs"])
            proj_full, fc1_full, fc2_full = unpack_weights(
                fetched, keep["logs"], w_proj, w_fc1, w_fc2
            )
        maps = join_groups(scalars[at], parts, width)
        turn = (maps, direct)
        keep["o_maps"] = map_exchange(maps, groups)

    for at in micros:
        keep = kept[at]
        keep["oc"], keep["attn"], keep["x1"], keep["a2"], keep["f"], first, last = expand(
            at,
            after(scalars[at], turn),
            keep["o_maps"],
            latents,
            mods,
            proj_full,
            fc1_full,
            fc1_bias,
        )
        turn = keep["attn"]
        keep["f_halo"] = halo_rows(first, last)

    for at in micros:
        keep, grad_type = (kept[at], jnp.bfloat16)
        prev = None if at == 0 else (term_fc2, term_conv_two, mixed)
        mixed, keep["d_gate2"], keep["d_z"], term_fc2, term_conv_two, first, last = ffn_middle(
            at,
            after(scalars[at], turn),
            keep["f"],
            keep["f_halo"],
            conv_two,
            fc2_full,
            cotangent,
            keep["x1"],
            mods,
            prev,
            grad_type,
        )
        turn = keep["d_gate2"]
        keep["z_halo"] = halo_rows(first, last)

    for at in micros:
        keep, grad_type = (kept[at], jnp.bfloat16)
        prev = None if at == 0 else (term_fc1, term_fc1_bias, term_proj)
        done = ffn_back(
            at,
            after(scalars[at], turn),
            keep["d_z"],
            keep["z_halo"],
            conv_two,
            fc1_full,
            keep["a2"],
            cotangent,
            keep["x1"],
            keep["attn"],
            keep["oc"],
            proj_full,
            mods,
            prev,
            grad_type,
        )
        keep["d_x"], keep["d_mods"], term_fc1, term_fc1_bias, term_proj = done[1:]
        turn = keep["d_mods"]
        keep["d_o"] = map_exchange(done[0], groups)

    blocks = dp * strips
    wide, narrow = (hidden // blocks, features // blocks)
    small = jnp.concatenate([term_conv_two, term_fc1_bias]).reshape(10, blocks, wide)
    small = small.transpose(1, 0, 2).reshape(blocks, 10 * wide)
    merged = narrow % 8 == 0 and dp == 4
    if merged:
        small_rows = -(-10 * wide // features // 8) * 8
        small = jnp.pad(small, ((0, 0), (0, small_rows * features - 10 * wide)))
        small = small.reshape(blocks, small_rows, features).astype(jnp.bfloat16)
        small, kept[0]["d_o"] = tie(small, kept[0]["d_o"])
        shares, shapes = by_destination(term_fc2, term_fc1, term_proj, small, narrow, dp)
        send = route_core(shares, shapes)
        share = core_sum(shares, shapes, permute_xor(send, "strip", 1), dp_at)
        turn = (turn, share[1])
        came = [permute_xor(share[0], "dp", 1), permute_xor(share[2], "dp", 2)]

    for at in micros:
        keep, grad_type = (kept[at], jnp.bfloat16)
        if at > 0:
            keep["d_o"], done[0] = tie(keep["d_o"], done[0])
        pieces = group_exchange(keep["d_o"].reshape(-1, features), groups)
        if width % 128:
            pieces = [
                jnp.pad(
                    lax.dynamic_slice_in_dim(piece, group_at * width, width, 1),
                    ((0, 0), (0, -width % 128)),
                )
                for piece in pieces
            ]
        done = attend_back(
            after(scalars[at], turn),
            keep["u"],
            pieces,
            keep["o"],
            qkv_group,
            keep["t"],
            keep["logs"],
            score_scale,
            side_count,
            None if at == 0 else term_qkv,
            grad_type,
        )
        done = list(done)
        term_qkv = done[groups]
        parts = [done[0]] + [permute_xor(done[k], "strip", k) for k in range(1, groups)]
        if at == 0 and merged:
            own, x_send, y_send = turn_sums(after(share[1], done[0]), came[0], share[3], came[1])
            came = [permute_xor(x_send, "dp", 2), permute_xor(y_send, "dp", 1)]
            parts = after(parts, own)
        if at > 0:
            if merged:
                share[1], share[2], kept[0]["d_u"] = tie(share[1], share[2], kept[0]["d_u"])
            kept[0]["edges"] = edge_rows(kept[0]["d_u"], side_count)
            kept[0]["edges"], parts = tie(kept[0]["edges"], parts)
        maps = sum_groups(parts)
        turn = maps
        keep["d_u"] = map_exchange(maps, groups)
        if at == 0 and merged:
            share = list(add_up(after(own, maps), *came, strip_at >> 1))
            turn = (turn, share[0])
            share = [share[0]] + [
                permute_xor(share[k], "strip", 2 * k) for k in range(1, strips // 2)
            ]

    kept_qkv = group_sums(after(term_qkv, turn), groups, width)
    mod_grads = []
    for at in micros:
        keep = kept[at]
        first_row, last_row = (
            keep["edges"] if at == 0 else edge_rows(keep["d_u"], side_count)
        )
        d_halo = halo_rows(first_row, last_row)
        prev = None if at == 0 else (term_conv_one, d_latents)
        d_latents, keep["d_mod1"], term_conv_one = last_stage(
            at,
            after(scalars[at], turn),
            keep["d_u"],
            d_halo,
            latents,
            top,
            end,
            mods,
            conv_one,
            keep["d_x"],
            prev,
        )
        turn = keep["d_mod1"]
        if at == 0:
            parts_qkv = group_parts(kept_qkv, groups)
        mod_grads.append(
            jnp.concatenate([keep["d_mod1"], keep["d_mods"], keep["d_gate2"]]).reshape(-1)
        )

    if merged:
        total = share[0].astype(jnp.float32)
        for part in share[1:]:
            total = total + part.astype(jnp.float32)
        ratio = hidden // features
        g_fc2 = total[: ratio * narrow]
        g_fc1 = total[ratio * narrow : 2 * ratio * narrow].reshape(ratio, narrow, features)
        g_fc1 = g_fc1.transpose(1, 0, 2).reshape(narrow, hidden)
        g_proj = total[2 * ratio * narrow : (2 * ratio + 1) * narrow]
        small = total[(2 * ratio + 1) * narrow :].reshape(-1)
    else:
        g_fc2 = scatter_rows(term_fc2)
        g_fc1 = scatter_rows(term_fc1)
        g_proj = scatter_rows(term_proj)
        small = scatter_rows(small)[0]
    g_conv_two = small[: 9 * wide].reshape(9, wide)
    g_fc1_bias = small[9 * wide : 10 * wide]
    mod_grads.append(term_conv_one.reshape(-1))

    grad_mod, parts_qkv = tie(jnp.concatenate(mod_grads), parts_qkv)
    step = 1
    while step < strips:
        grad_mod = grad_mod + permute_xor(grad_mod, "strip", step)
        step *= 2
        if step == 4:
            g_qkv = group_columns(after(parts_qkv, grad_mod), groups)
    all_mods = gather_butterfly(grad_mod[None])
    block_at = dp_at * strips + strip_at
    g_conv_one = jnp.sum(all_mods[:, micro_count * 6 * features :], axis=0).reshape(9, features)
    g_conv_one = lax.dynamic_slice_in_dim(g_conv_one, block_at * narrow, narrow, 1)
    all_mods = all_mods[:, : micro_count * 6 * features].reshape(-1, 6 * features)
    conds_here = lax.dynamic_slice_in_dim(
        jnp.concatenate(conds), block_at * narrow, narrow, 1
    )
    g_ada = lax.dot_general(
        conds_here, all_mods, (((0,), (0,)), ((), ())), precision=lax.Precision.HIGHEST
    )
    ada_wide_block = 6 * features // blocks
    g_ada_bias = lax.dynamic_slice_in_dim(
        jnp.sum(all_mods, axis=0), block_at * ada_wide_block, ada_wide_block, 0
    )
    return (
        mixed,
        d_latents,
        g_ada,
        g_ada_bias,
        g_conv_one,
        g_qkv,
        g_proj,
        g_fc1,
        g_fc1_bias,
        g_conv_two,
        g_fc2,
    )


def solution(mesh):
    return jax.shard_map(
        shards,
        mesh=mesh,
        in_specs=(
            P(None, "dp", "strip", None, None),
            P(None, "dp"),
            P(None, "dp"),
            P("dp", None),
            P("dp"),
            P(None, "dp"),
            P("dp", None),
            P("dp", None),
            P("dp", None),
            P("dp"),
            P(None, "dp"),
            P("dp", None),
            P(None, "dp", "strip", None, None),
        ),
        out_specs=(
            P(None, "dp", "strip", None, None),
            P(None, "dp", "strip", None, None),
            P(("dp", "strip"), None),
            P(("dp", "strip")),
            P(None, ("dp", "strip")),
            P(("dp", "strip"), None),
            P(("dp", "strip"), None),
            P(("dp", "strip"), None),
            P(("dp", "strip")),
            P(None, ("dp", "strip")),
            P(("dp", "strip"), None),
        ),
        check_vma=False,
    )
```

```python
import functools
import math

import jax
import jax.numpy as jnp
from jax import lax
from jax.experimental import pallas as pl
from jax.experimental.pallas import tpu as pltpu
from jax.sharding import PartitionSpec as P

HEADS = 12
COVER = pl.CostEstimate(flops=200_000_000_000, transcendentals=0, bytes_accessed=0)
BRIEF = pl.CostEstimate(flops=0, transcendentals=0, bytes_accessed=0)


root_half = 0.7071067811865476
inverse_root_tau = 0.3989422804014327


def permute_xor(x, axis, step):
    size = lax.axis_size(axis)
    return lax.ppermute(x, axis, [(i, i ^ step) for i in range(size)])


def pick(x, at, axis=0):
    return lax.dynamic_index_in_dim(x, at, axis, keepdims=False)


def halo_rows(first, last):
    size = lax.axis_size("strip")
    up = [(i, i + 1) for i in range(size - 1)]
    down = [(i + 1, i) for i in range(size - 1)]
    return (lax.ppermute(last, "strip", up), lax.ppermute(first, "strip", down))


def place_blocks(blocks, me):
    stacked = jnp.stack(blocks)
    return jnp.stack([pick(stacked, me ^ at) for at in range(len(blocks))])


def gather_butterfly(x):
    step = 1
    while step < lax.axis_size("dp"):
        x = jnp.concatenate([x, permute_xor(x, "dp", step)])
        step *= 2
    return x


def after(x, *done):
    return lax.optimization_barrier((x, done))[0]


HBM = pl.BlockSpec(memory_space=pl.ANY)


def move_all(copies):
    for copy in copies:
        copy.start()
    for copy in copies:
        copy.wait()


def rows_at(start, size):
    return pl.ds(pl.multiple_of(start, 8), size)


def tie(*values):
    return lax.optimization_barrier(values)


def assemble_kernel(at_ref, *refs):
    pieces, whole, sem = (refs[:-2], refs[-2], refs[-1])
    move_all(
        [
            pltpu.make_async_copy(
                piece, whole.at[:, rows_at(at_ref[i], piece.shape[1]), :], sem.at[i]
            )
            for i, piece in enumerate(pieces)
        ]
    )


def assemble(pieces, starts, shape):
    return pl.pallas_call(
        assemble_kernel,
        grid_spec=pltpu.PrefetchScalarGridSpec(
            num_scalar_prefetch=1,
            grid=(1,),
            in_specs=[HBM] * len(pieces),
            out_specs=whole_spec(shape),
            scratch_shapes=[pltpu.SemaphoreType.DMA((len(pieces),))],
        ),
        out_shape=jax.ShapeDtypeStruct(shape, pieces[0].dtype),
        cost_estimate=COVER,
        name="assemble",
    )(jnp.stack(starts).astype(jnp.int32), *pieces)


def pack_layout(proj, fc1, fc2):
    features = proj.shape[1]
    sizes = [proj.shape[0] // 2]
    sizes += [fc1.shape[0] // 2] * (fc1.shape[1] // features) + [fc2.shape[0] // 2]
    starts = [sum(sizes[:i]) for i in range(len(sizes))]
    return sizes, starts


def half_of(refs, row, i, size, features):
    if i == 0:
        return refs[0].at[rows_at(row, size), :]
    if i == len(refs[3]) - 1:
        return refs[2].at[rows_at(row, size), :]
    return refs[1].at[rows_at(row, size), (i - 1) * features : i * features]


def pack_kernel(at_ref, proj, fc1, fc2, out, sem):
    sizes, starts = pack_layout(proj, fc1, fc2)
    copies = []
    for i, (size, start) in enumerate(zip(sizes, starts)):
        source = half_of((proj, fc1, fc2, sizes), at_ref[0] * size, i, size, proj.shape[1])
        copies.append(pltpu.make_async_copy(source, out.at[start : start + size, :], sem.at[i]))
    move_all(copies)


def pack_weights(proj, fc1, fc2, turn):
    core = lax.axis_index("strip") & 1
    sizes, starts = pack_layout(proj, fc1, fc2)
    shape = (starts[-1] + sizes[-1], proj.shape[1])
    return pl.pallas_call(
        pack_kernel,
        grid_spec=pltpu.PrefetchScalarGridSpec(
            num_scalar_prefetch=1,
            grid=(1,),
            in_specs=[HBM] * 3,
            out_specs=whole_spec(shape),
            scratch_shapes=[pltpu.SemaphoreType.DMA((len(sizes),))],
        ),
        out_shape=jax.ShapeDtypeStruct(shape, proj.dtype),
        cost_estimate=BRIEF,
        name="pack_weights",
    )(after(core[None].astype(jnp.int32), turn), proj, fc1, fc2)


def fetch_direct(x):
    steps = [k for k in range(1, lax.axis_size("dp")) if k & (k - 1) == 0]
    return {k: permute_xor(x, "dp", k) for k in steps}


def fetch_relayed(came):
    step = 2
    while step < lax.axis_size("dp"):
        for k in range(1, step):
            came[step + k] = permute_xor(came[k], "dp", step)
        step *= 2
    return [came[k] for k in sorted(came)]


def unpack_kernel(count, at_ref, *refs):
    own, halves, wholes, sem = (refs[:3], refs[3 : 3 + count], refs[3 + count : 6 + count], refs[-1])
    sizes, starts = pack_layout(*own)
    features = own[0].shape[1]
    copies = []
    for ref, whole in zip(own, wholes):
        target = whole.at[rows_at(at_ref[0] * ref.shape[0], ref.shape[0]), :]
        copies.append(pltpu.make_async_copy(ref, target, sem.at[len(copies)]))
    for k, half in enumerate(halves):
        for i, (size, start) in enumerate(zip(sizes, starts)):
            row = (2 * at_ref[1 + 2 * k] + at_ref[2 + 2 * k]) * size
            target = half_of(wholes + (sizes,), row, i, size, features)
            copies.append(
                pltpu.make_async_copy(
                    half.at[start : start + size, :], target, sem.at[len(copies)]
                )
            )
    move_all(copies)


def unpack_weights(fetched, turn, proj, fc1, fc2):
    size, me = (lax.axis_size("dp"), lax.axis_index("dp"))
    core = lax.axis_index("strip") & 1
    halves, places = ([], [me])
    for k, mine in enumerate(fetched, 1):
        halves += [mine, permute_xor(mine, "strip", 1)]
        places += [me ^ k, core, me ^ k, 1 - core]
    shapes = [(size * w.shape[0], w.shape[1]) for w in (proj, fc1, fc2)]
    copies = 3 + len(halves) * len(pack_layout(proj, fc1, fc2)[0])
    return pl.pallas_call(
        functools.partial(unpack_kernel, len(halves)),
        grid_spec=pltpu.PrefetchScalarGridSpec(
            num_scalar_prefetch=1,
            grid=(1,),
            in_specs=[HBM] * (3 + len(halves)),
            out_specs=[whole_spec(shape) for shape in shapes],
            scratch_shapes=[pltpu.SemaphoreType.DMA((copies,))],
        ),
        out_shape=[jax.ShapeDtypeStruct(shape, proj.dtype) for shape in shapes],
        cost_estimate=BRIEF,
        name="unpack_weights",
    )(after(jnp.stack(places).astype(jnp.int32), turn), proj, fc1, fc2, *halves)


def fetch_group(w, groups, turn):
    rows, cols = w.shape
    width = cols // 3 // groups
    group = lax.axis_index("strip") % groups
    mine = pick(w.reshape(rows, 3, groups, width), group, 2).transpose(1, 0, 2)
    mine, turn = tie(jnp.pad(mine, ((0, 0), (0, 0), (0, -width % 128))), turn)
    pieces = [mine] + [permute_xor(mine, "dp", k) for k in range(1, lax.axis_size("dp"))]
    return pieces, turn


def gather_group(pieces):
    me, rows = (lax.axis_index("dp"), pieces[0].shape[1])
    starts = [(me ^ k) * rows for k in range(len(pieces))]
    return assemble(pieces, starts, (3, len(pieces) * rows, pieces[0].shape[2]))


def exchange_sum(x, axis, me, step, wire, dim=0):
    total = pick(x, me, dim).astype(jnp.float32)
    parts = [
        permute_xor(pick(x, me ^ k, dim).astype(wire), axis, k * step)
        for k in range(1, x.shape[dim])
    ]
    for part in parts:
        total = total + part.astype(jnp.float32)
    return total


def scatter_rows(g, wire=jnp.bfloat16):
    rows, cols = g.shape
    dp, strips = (lax.axis_size("dp"), lax.axis_size("strip"))
    strip = lax.axis_index("strip")
    shaped = g.reshape(dp, strips // 2, 2, rows // dp // strips, cols)
    core = strip & 1
    sent = permute_xor(pick(shaped, 1 - core, 2).astype(wire), "strip", 1)
    kept = pick(shaped, core, 2).astype(jnp.float32) + sent.astype(jnp.float32)
    kept = exchange_sum(kept, "dp", lax.axis_index("dp"), 1, wire)
    return exchange_sum(kept, "strip", strip >> 1, 2, wire)


def group_sums(g, groups, width, wire=jnp.bfloat16):
    rows = g.shape[1]
    dp, strips = (lax.axis_size("dp"), lax.axis_size("strip"))
    kept = g[:, :, :width].reshape(3, dp, strips // groups, groups, rows // dp // strips, width)
    return exchange_sum(kept, "dp", lax.axis_index("dp"), 1, wire, 1)


def group_parts(kept, groups, wire=jnp.bfloat16):
    me = lax.axis_index("strip") // groups
    return [pick(kept, me, 1)] + [
        permute_xor(pick(kept, me ^ k, 1).astype(wire), "strip", k * groups)
        for k in range(1, kept.shape[1])
    ]


def group_columns(parts, groups, wire=jnp.bfloat16):
    kept = parts[0]
    for part in parts[1:]:
        kept = kept + part.astype(jnp.float32)
    group = lax.axis_index("strip") % groups
    blocks = [pick(kept, group, 1)] + [
        permute_xor(pick(kept, group ^ k, 1).astype(wire), "strip", k).astype(jnp.float32)
        for k in range(1, groups)
    ]
    whole = place_blocks(blocks, group)
    return whole.transpose(2, 1, 0, 3).reshape(whole.shape[2], -1)


def lay_rows(out, fc2, fc1, proj, small):
    features = proj.shape[-1]
    parts = [fc2]
    parts += [fc1[:, :, i : i + features] for i in range(0, fc1.shape[-1], features)]
    start = 0
    for part in parts + [proj, small]:
        out[:, start : start + part.shape[1], :] = part
        start += part.shape[1]


def route_kernel(at_ref, fc2, fc1, proj, small, out):
    lay_rows(out, fc2[...], fc1[...], proj[...], small[...])


def by_destination(fc2, fc1, proj, small, rows, dp):
    pairs = small.shape[0] // 2 // dp
    arrays = [
        x.reshape(dp, pairs, 2, -1, x.shape[-1]) for x in (fc2, fc1, proj, small)
    ]
    shapes = [(None, pairs, None) + x.shape[3:] for x in arrays]
    return arrays, shapes


def route_core(arrays, shapes):
    dp, pairs = arrays[0].shape[:2]
    features = arrays[0].shape[-1]
    height = sum(x.shape[3] * x.shape[4] for x in arrays) // features
    core = lax.axis_index("strip") & 1
    return pl.pallas_call(
        route_kernel,
        grid_spec=pltpu.PrefetchScalarGridSpec(
            num_scalar_prefetch=1,
            grid=(dp,),
            in_specs=[
                pl.BlockSpec(shape, lambda j, s: (j, 0, 1 - s[0], 0, 0)) for shape in shapes
            ],
            out_specs=pl.BlockSpec((pairs, height, features), lambda j, s: (j, 0, 0)),
        ),
        out_shape=jax.ShapeDtypeStruct((dp * pairs, height, features), arrays[0].dtype),
        cost_estimate=COVER,
        name="route_core",
    )(core[None].astype(jnp.int32), *arrays)


def core_sum_kernel(at_ref, fc2, fc1, proj, small, came, x_send, x_keep, y_send, y_keep, kept):
    lay_rows(kept, fc2[...], fc1[...], proj[...], small[...])
    total = (kept[...].astype(jnp.float32) + came[...].astype(jnp.float32)).astype(kept.dtype)
    half = total.shape[0] // 2
    for k in range(4):

        @pl.when(pl.program_id(0) == k)
        def _():
            (x_send if k & 1 else x_keep)[...] = total[:half]
            (y_send if k >> 1 else y_keep)[...] = total[half:]


def core_sum(arrays, shapes, came, me):
    dp, pairs = arrays[0].shape[:2]
    block = (pairs,) + came.shape[1:]
    out = (2, pairs // 2) + came.shape[1:]
    core = lax.axis_index("strip") & 1
    return pl.pallas_call(
        core_sum_kernel,
        grid_spec=pltpu.PrefetchScalarGridSpec(
            num_scalar_prefetch=1,
            grid=(dp,),
            in_specs=[
                pl.BlockSpec(shape, lambda j, s: (s[1] ^ j, 0, s[0], 0, 0)) for shape in shapes
            ]
            + [pl.BlockSpec(block, lambda j, s: (s[1] ^ j, 0, 0))],
            out_specs=[
                pl.BlockSpec((None,) + out[1:], lambda j, s: (j >> 1, 0, 0, 0)),
                pl.BlockSpec((None,) + out[1:], lambda j, s: (j >> 1, 0, 0, 0)),
                pl.BlockSpec((None,) + out[1:], lambda j, s: (jnp.maximum(j - 2, 0), 0, 0, 0)),
                pl.BlockSpec((None,) + out[1:], lambda j, s: (jnp.minimum(j, 1), 0, 0, 0)),
            ],
            scratch_shapes=[pltpu.VMEM(block, came.dtype)],
        ),
        out_shape=[jax.ShapeDtypeStruct(out, came.dtype)] * 4,
        cost_estimate=COVER,
        name="core_sum",
    )(jnp.stack([core, me]).astype(jnp.int32), *arrays, came)


def turn_kernel(x_keep, x_came, y_keep, y_came, own, x_send, y_send):
    half = own.shape[0] // 2

    def both(keep, came, k):
        return (keep[k].astype(jnp.float32) + came[k].astype(jnp.float32)).astype(own.dtype)

    own[:half] = both(x_keep, x_came, 0)
    own[half:] = both(y_keep, y_came, 0)
    x_send[...] = both(x_keep, x_came, 1)
    y_send[...] = both(y_keep, y_came, 1)


def turn_sums(x_keep, x_came, y_keep, y_came):
    _, half, rows, cols = x_keep.shape
    block = rows // 2
    pair = pl.BlockSpec((2, half, block, cols), lambda j: (0, 0, j, 0))
    one = pl.BlockSpec((half, block, cols), lambda j: (0, j, 0))
    whole = pl.BlockSpec((2 * half, block, cols), lambda j: (0, j, 0))
    shape = (half, rows, cols)
    return pl.pallas_call(
        turn_kernel,
        grid=(rows // block,),
        in_specs=[pair] * 4,
        out_specs=[whole, one, one],
        out_shape=[
            jax.ShapeDtypeStruct((2 * half,) + shape[1:], x_keep.dtype),
            jax.ShapeDtypeStruct(shape, x_keep.dtype),
            jax.ShapeDtypeStruct(shape, x_keep.dtype),
        ],
        cost_estimate=COVER,
        name="turn_sums",
    )(x_keep, x_came, y_keep, y_came)


def add_kernel(at_ref, own, x_came, y_came, *refs):
    outs, kept = (refs[:-1], refs[-1])
    half = own.shape[0] // 2
    for at, came in ((slice(0, half), x_came), (slice(half, None), y_came)):
        total = own[at].astype(jnp.float32) + came[...].astype(jnp.float32)
        kept[at] = total.astype(own.dtype)
    for k, out in enumerate(outs):
        out[...] = kept[at_ref[0] ^ k]


def add_up(own, x_came, y_came, me):
    pairs, rows, cols = own.shape
    return pl.pallas_call(
        add_kernel,
        grid_spec=pltpu.PrefetchScalarGridSpec(
            num_scalar_prefetch=1,
            grid=(1,),
            in_specs=[whole_spec(x.shape) for x in (own, x_came, y_came)],
            out_specs=[whole_spec((rows, cols))] * pairs,
            scratch_shapes=[pltpu.VMEM(own.shape, own.dtype)],
        ),
        out_shape=[jax.ShapeDtypeStruct((rows, cols), own.dtype)] * pairs,
        cost_estimate=BRIEF,
        name="add_up",
    )(me[None].astype(jnp.int32), own, x_came, y_came)


def map_exchange(maps, groups):
    size = lax.axis_size("strip")
    among = [[m * groups + g for m in range(4)] for g in range(groups)]
    return lax.all_to_all(maps, "strip", 0, 0, axis_index_groups=among, tiled=True)


def group_exchange(x, groups):
    return [x] + [permute_xor(x, "strip", k) for k in range(1, groups)]


def silu_of(values):
    return values / (1.0 + jnp.exp(-values))


def embed_times(stamps, features):
    half_count = features // 2
    frequency = jnp.exp(-math.log(10000.0) * jnp.arange(half_count, dtype=jnp.float32) / half_count)
    angles = stamps[:, None] * frequency[None, :]
    return jnp.concatenate([jnp.cos(angles), jnp.sin(angles)], axis=1)

def normalize(values):
    centre = values - jnp.mean(values, axis=-1, keepdims=True)
    inverse = lax.rsqrt(jnp.mean(centre * centre, axis=-1, keepdims=True) + 1e-06)
    return (centre * inverse, inverse)


def norm_back(normed, inverse, upstream):
    return inverse * (
        upstream
        - jnp.mean(upstream, axis=-1, keepdims=True)
        - normed * jnp.mean(upstream * normed, axis=-1, keepdims=True)
    )


def dot_nn(a, b):
    return lax.dot_general(a, b, (((1,), (0,)), ((), ())), preferred_element_type=jnp.float32)


def dot_nt(a, b):
    return lax.dot_general(a, b, (((1,), (1,)), ((), ())), preferred_element_type=jnp.float32)


def dot_tn(a, b):
    return lax.dot_general(a, b, (((0,), (0,)), ((), ())), preferred_element_type=jnp.float32)


def key_mask(s_ref, groups, tokens, cols):
    block = tokens // groups // 4
    token = lax.broadcasted_iota(jnp.int32, (tokens, 128), 0)
    piece, within = (token // block, token % block)
    strip = (piece % 4) * groups + (s_ref[3] ^ (piece // 4))
    row = strip * (block // (cols // 2)) + within // (cols // 2)
    half = s_ref[0] // 2
    return jnp.where((row < half) & (within % (cols // 2) < half), 0.0, -1e30)


def store_sum(ref, part):
    @pl.when(pl.program_id(0) == 0)
    def _():
        ref[...] = part

    @pl.when(pl.program_id(0) > 0)
    def _():
        ref[...] += part


def attend_kernel(chunk, scale, groups, cols, s_ref, *refs):
    pieces, w_ref, t_ref = (refs[:groups], refs[groups], refs[groups + 1])
    o_refs = refs[groups + 2 : 2 * groups + 2]
    l_ref, u_sc, b_sc, q_sc, k_sc, v_sc, o_sc, l_sc = refs[2 * groups + 2 :]
    tokens = u_sc.shape[0]

    @pl.when(pl.program_id(0) == 0)
    def _():
        size = pieces[0].shape[0]
        for i, piece in enumerate(pieces):
            u_sc[i * size : (i + 1) * size, :] = piece[...]
        b_sc[...] = key_mask(s_ref, groups, tokens, cols)

    u = u_sc[...]
    for part in range(3):
        t_ref[part] = dot_nn(u, w_ref[part]).astype(jnp.bfloat16)
    q, k, v = (t_ref[0].astype(jnp.float32), t_ref[1].astype(jnp.float32), t_ref[2].astype(jnp.float32))
    lane = lax.broadcasted_iota(jnp.int32, (tokens, 128), 1)
    bias = b_sc[...]
    for head in range(2):
        here = (lane < 64) if head == 0 else (lane >= 64)
        spare = lane == (64 if head == 0 else 0)
        q_sc[head] = jnp.where(here, q * scale, jnp.where(spare, 1.0, 0.0)).astype(jnp.bfloat16)
        k_sc[head] = jnp.where(here, k, jnp.where(spare, bias, 0.0)).astype(jnp.bfloat16)
        v_sc[head] = jnp.where(here, v, 0.0).astype(jnp.bfloat16)

    def body(i, carry):
        at = pl.ds(pl.multiple_of(i * chunk, chunk), chunk)
        outs, logs = ([], [])
        for head in range(2):
            s = dot_nt(q_sc[head, at, :], k_sc[head])
            top = jnp.max(s, axis=1, keepdims=True)
            p = jnp.exp(s - top)
            total = jnp.sum(p, axis=1, keepdims=True)
            outs.append(dot_nn(p.astype(jnp.bfloat16), v_sc[head]) * (1.0 / total))
            logs.append(top + jnp.log(total))
        o_sc[at, :] = (outs[0] + outs[1]).astype(jnp.bfloat16)
        l_sc[at, :] = jnp.where(
            lax.broadcasted_iota(jnp.int32, (chunk, 128), 1) < 64, logs[0], logs[1]
        )
        return carry

    lax.fori_loop(0, tokens // chunk, body, 0, unroll=True)
    size = tokens // groups
    for i, o_ref in enumerate(o_refs):
        o_ref[...] = o_sc[i * size : (i + 1) * size, :]
    logs = l_sc[...].T
    l_ref[...] = jnp.concatenate(
        [logs[0:1], logs[64:65], jnp.zeros((6, tokens), jnp.float32)], axis=0
    )[None]


def attend(scalars, pieces, w, score_scale, cols):
    groups = len(pieces)
    features, width = w.shape[1:]
    tokens = groups * pieces[0].shape[0]
    chunk = min(512, tokens)
    piece_spec = pl.BlockSpec(pieces[0].shape, lambda j, s: (0, 0))
    return pl.pallas_call(
        functools.partial(attend_kernel, chunk, score_scale, groups, cols),
        grid_spec=pltpu.PrefetchScalarGridSpec(
            num_scalar_prefetch=1,
            grid=(width // 128,),
            in_specs=[piece_spec] * len(pieces)
            + [pl.BlockSpec((3, features, 128), lambda j, s: (0, 0, j))],
            out_specs=[pl.BlockSpec((3, tokens, 128), lambda j, s: (0, 0, j))]
            + [pl.BlockSpec((tokens // groups, 128), lambda j, s: (0, j))] * groups
            + [pl.BlockSpec((1, 8, tokens), lambda j, s: (j, 0, 0))],
            scratch_shapes=[
                pltpu.VMEM((tokens, features), jnp.bfloat16),
                pltpu.VMEM((tokens, 128), jnp.float32),
            ]
            + [pltpu.VMEM((2, tokens, 128), jnp.bfloat16)] * 3
            + [pltpu.VMEM((tokens, 128), jnp.bfloat16), pltpu.VMEM((tokens, 128), jnp.float32)],
        ),
        out_shape=[jax.ShapeDtypeStruct((3, tokens, width), jnp.bfloat16)]
        + [jax.ShapeDtypeStruct((tokens // groups, width), jnp.bfloat16)] * groups
        + [jax.ShapeDtypeStruct((width // 128, 8, tokens), jnp.float32)],
        cost_estimate=BRIEF,
        name="attend_forward",
    )(scalars, *pieces, w)


def attend_back_kernel(chunk, scale, groups, cols, first, s_ref, *refs):
    pieces, do_pieces, o_refs = (refs[:groups], refs[groups : 2 * groups], refs[2 * groups : 3 * groups])
    w_ref, t_ref, l_ref = refs[3 * groups : 3 * groups + 3]
    rest = refs[3 * groups + 3 :]
    if not first:
        prev_ref, rest = (rest[0], rest[1:])
    du_refs, g_ref = (rest[:groups], rest[groups])
    u_sc, b_sc, o_sc, din_sc, q_sc, k_sc, do_sc, dq_sc, dt_sc, d_sc = rest[groups + 1 :]
    tokens = u_sc.shape[0]
    size = pieces[0].shape[0]

    @pl.when(pl.program_id(0) == 0)
    def _():
        for i, piece in enumerate(pieces):
            u_sc[i * size : (i + 1) * size, :] = piece[...]
        b_sc[...] = key_mask(s_ref, groups, tokens, cols)

    for i, piece in enumerate(do_pieces):
        din_sc[i * size : (i + 1) * size, :] = piece[...]
    for i, piece in enumerate(o_refs):
        o_sc[i * size : (i + 1) * size, :] = piece[...]
    q, k, do = (t_ref[0].astype(jnp.float32), t_ref[1].astype(jnp.float32), din_sc[...])
    lane = lax.broadcasted_iota(jnp.int32, (tokens, 128), 1)
    bias = b_sc[...]
    do = do.astype(jnp.float32)
    inner = (do * o_sc[...].astype(jnp.float32)).T
    for head in range(2):
        here = (lane < 64) if head == 0 else (lane >= 64)
        spare = lane == (64 if head == 0 else 0)
        q_sc[head] = jnp.where(here, q * scale, jnp.where(spare, 1.0, 0.0)).astype(jnp.bfloat16)
        k_sc[head] = jnp.where(here, k, jnp.where(spare, bias, 0.0)).astype(jnp.bfloat16)
        do_sc[head] = jnp.where(here, do, 0.0).astype(jnp.bfloat16)
        d_sc[head : head + 1, :] = jnp.sum(
            inner[64 * head : 64 * head + 64], axis=0, keepdims=True
        )
    dq_sc[...] = jnp.zeros_like(dq_sc)

    def body(i, carry):
        at = pl.ds(pl.multiple_of(i * chunk, chunk), chunk)
        lanes = lax.broadcasted_iota(jnp.int32, (chunk, 128), 1)
        d_k, d_v, d_q = ([], [], [])
        for head in range(2):
            here = (lanes < 64) if head == 0 else (lanes >= 64)
            s = dot_nt(k_sc[head, at, :], q_sc[head])
            p = jnp.exp(s - l_ref[0, head : head + 1, :])
            d_p = dot_nt(t_ref[2, at, :], do_sc[head])
            d_s = (p * (d_p - d_sc[head : head + 1, :])).astype(jnp.bfloat16)
            d_v.append(dot_nn(p.astype(jnp.bfloat16), do_sc[head]))
            d_k.append(dot_nn(d_s, q_sc[head]))
            keys = jnp.where(here, t_ref[1, at, :].astype(jnp.float32), 0.0).astype(jnp.bfloat16)
            d_q.append(dot_tn(d_s, keys))
        dq_sc[...] += d_q[0] + d_q[1]
        dt_sc[at, 128:256] = jnp.where(lanes < 64, d_k[0], d_k[1]).astype(jnp.bfloat16)
        dt_sc[at, 256:384] = (d_v[0] + d_v[1]).astype(jnp.bfloat16)
        return carry

    lax.fori_loop(0, tokens // chunk, body, 0, unroll=True)
    dt_sc[:, 0:128] = (dq_sc[...] * scale).astype(jnp.bfloat16)
    for i, du_ref in enumerate(du_refs):
        at = slice(i * size, (i + 1) * size)
        part = dot_nt(dt_sc[at, 0:128], w_ref[0])
        part = part + dot_nt(dt_sc[at, 128:256], w_ref[1])
        part = part + dot_nt(dt_sc[at, 256:384], w_ref[2])
        store_sum(du_ref, part)
    grad = dot_tn(u_sc[...], dt_sc[...])
    for at in range(3):
        piece = grad[:, 128 * at : 128 * at + 128]
        if not first:
            piece = piece + prev_ref[at]
        g_ref[at] = piece.astype(g_ref.dtype)


def attend_back(scalars, pieces, d_pieces, outs, w, t, logs, score_scale, cols, prev, grad_type):
    groups = len(outs)
    features, width = w.shape[1:]
    tokens = t.shape[1]
    chunk = min(256, tokens)
    size = pieces[0].shape[0]
    blocks = width // 128
    weight_spec = pl.BlockSpec((3, features, 128), lambda j, s: (0, 0, j))
    offset = 0 if d_pieces[0].shape[1] == width else blocks
    args = list(pieces) + list(d_pieces) + list(outs) + [w, t, logs]
    args += [] if prev is None else [prev]
    return pl.pallas_call(
        functools.partial(attend_back_kernel, chunk, score_scale, groups, cols, prev is None),
        grid_spec=pltpu.PrefetchScalarGridSpec(
            num_scalar_prefetch=1,
            grid=(blocks,),
            in_specs=[pl.BlockSpec((size, features), lambda j, s: (0, 0))] * len(pieces)
            + [pl.BlockSpec((size, 128), lambda j, s: (0, s[3] * offset + j))] * len(d_pieces)
            + [pl.BlockSpec((size, 128), lambda j, s: (0, j))] * groups
            + [
                weight_spec,
                pl.BlockSpec((3, tokens, 128), lambda j, s: (0, 0, j)),
                pl.BlockSpec((1, 8, tokens), lambda j, s: (j, 0, 0)),
            ]
            + ([] if prev is None else [weight_spec]),
            out_specs=[pl.BlockSpec((size, features), lambda j, s: (0, 0))] * groups
            + [weight_spec],
            scratch_shapes=[
                pltpu.VMEM((tokens, features), jnp.bfloat16),
                pltpu.VMEM((tokens, 128), jnp.float32),
                pltpu.VMEM((tokens, 128), jnp.bfloat16),
                pltpu.VMEM((tokens, 128), jnp.bfloat16),
            ]
            + [pltpu.VMEM((2, tokens, 128), jnp.bfloat16)] * 3
            + [
                pltpu.VMEM((tokens, 128), jnp.float32),
                pltpu.VMEM((tokens, 384), jnp.bfloat16),
                pltpu.VMEM((8, tokens), jnp.float32),
            ],
        ),
        out_shape=[jax.ShapeDtypeStruct((size, features), jnp.float32)] * groups
        + [jax.ShapeDtypeStruct(w.shape, grad_type)],
        cost_estimate=COVER,
        name="attend_backward",
    )(scalars, *args)


def shift_cols(x, by, col):
    size = x.shape[0]
    rolled = pltpu.roll(x, (-by) % size, 0)
    return jnp.where(col == (size - 1 if by > 0 else 0), 0.0, rolled)


def wide_taps(c_ref, lanes, cols):
    return [
        jnp.broadcast_to(c_ref[k : k + 1, lanes].astype(jnp.float32), (cols, 128)) for k in range(9)
    ]


def sublane_sum(x):
    return jnp.sum(x.reshape(x.shape[0] // 8, 8, 128), axis=0)


def modulate(x, m_ref, shift_at, col, row, side):
    normed, _ = normalize(x.astype(jnp.float32))
    value = normed * (1.0 + m_ref[shift_at + 1 : shift_at + 2, :]) + m_ref[shift_at : shift_at + 1, :]
    live = (col < side) & (row >= 0) & (row < side)
    return jnp.where(live, value, 0.0).astype(jnp.bfloat16)


def modulated_rows(a_sc, s_ref, x_ref, top_ref, end_ref, m_ref):
    rows, cols, features = x_ref.shape
    side, row_zero = (s_ref[0], s_ref[1])
    col = lax.broadcasted_iota(jnp.int32, (cols, features), 0)
    a_sc[0] = modulate(top_ref[...], m_ref, 0, col, row_zero - 1, side)
    a_sc[rows + 1] = modulate(end_ref[...], m_ref, 0, col, row_zero + rows, side)

    def body(r, carry):
        a_sc[r + 1] = modulate(x_ref[r], m_ref, 0, col, row_zero + r, side)
        return carry

    lax.fori_loop(0, rows, body, 0)


def to_maps(canvas, maps_ref):
    blocks, rows, cols, _ = canvas.shape
    half = cols // 2

    def body(r, carry):
        at = pl.ds(pl.multiple_of(r * half, half), half)
        for m in range(4):
            for b in range(blocks):
                part = canvas[b, 2 * r + m // 2, pl.ds(m % 2, half, stride=2), :]
                maps_ref[m, at, 128 * b : 128 * b + 128] = part.astype(jnp.bfloat16)
        return carry

    lax.fori_loop(0, rows // 2, body, 0)


def from_maps(maps_ref, canvas, row_offset):
    half = canvas.shape[2] // 2
    rows = maps_ref.shape[1] // half * 2

    def body(r, carry):
        at = pl.ds(pl.multiple_of(r * half, half), half)
        for m in range(4):
            for b in range(canvas.shape[0]):
                part = maps_ref[m, at, 128 * b : 128 * b + 128].astype(jnp.float32)
                canvas[b, row_offset + 2 * r + m // 2, pl.ds(m % 2, half, stride=2), :] = part
        return carry

    lax.fori_loop(0, rows // 2, body, 0)


def before_kernel(s_ref, x_ref, top_ref, end_ref, m_ref, c_ref, *refs):
    maps_ref, a_sc, t_sc = refs
    rows, cols, features = x_ref.shape
    modulated_rows(a_sc, s_ref, x_ref, top_ref, end_ref, m_ref)
    col = lax.broadcasted_iota(jnp.int32, (cols, 128), 0)
    for first in range(0, features, 128):
        lanes = slice(first, first + 128)
        taps = wide_taps(c_ref, lanes, cols)

        def body(r, carry):
            x = [a_sc[r + i, :, lanes].astype(jnp.float32) for i in range(3)]
            a = [x[0] * taps[j] + x[1] * taps[3 + j] + x[2] * taps[6 + j] for j in range(3)]
            t_sc[first // 128, r] = a[1] + shift_cols(a[0], -1, col) + shift_cols(a[2], 1, col)
            return carry

        lax.fori_loop(0, rows, body, 0)
    to_maps(t_sc, maps_ref)


def canvas_specs(latents, at):
    rows, cols, features = latents.shape[2:]
    return [
        pl.BlockSpec((None, None, rows, cols, features), lambda j, s: (at, 0, 0, 0, 0)),
        pl.BlockSpec((None, cols, features), lambda j, s: (at, 0, 0)),
        pl.BlockSpec((None, cols, features), lambda j, s: (at, 0, 0)),
        pl.BlockSpec((None, 6, features), lambda j, s: (at, 0, 0)),
    ]


def whole_spec(shape):
    return pl.BlockSpec(shape, lambda j, s: (0,) * len(shape))


def before_attention(at, scalars, latents, top, end, mods, taps):
    rows, cols, features = latents.shape[2:]
    maps = (4, rows * cols // 4, features)
    return pl.pallas_call(
        before_kernel,
        grid_spec=pltpu.PrefetchScalarGridSpec(
            num_scalar_prefetch=1,
            grid=(1,),
            in_specs=canvas_specs(latents, at) + [whole_spec(taps.shape)],
            out_specs=whole_spec(maps),
            scratch_shapes=[
                pltpu.VMEM((rows + 2, cols, features), jnp.bfloat16),
                pltpu.VMEM((features // 128, rows, cols, 128), jnp.float32),
            ],
        ),
        out_shape=jax.ShapeDtypeStruct(maps, jnp.bfloat16),
        cost_estimate=COVER,
        name="before_attention",
    )(scalars, latents, top, end, mods, taps)


def join_kernel(s_ref, mine_ref, other_ref, out_ref):
    width = mine_ref.shape[1]

    def write(low_ref, high_ref):
        out_ref[:, :width] = low_ref[...]
        out_ref[:, width:] = high_ref[...]

    @pl.when(s_ref[3] == 0)
    def _():
        write(mine_ref, other_ref)

    @pl.when(s_ref[3] == 1)
    def _():
        write(other_ref, mine_ref)


def join_groups(scalars, parts, width):
    groups = len(parts)
    tokens = parts[0].shape[0]
    shape = (tokens, groups * width)
    if groups != 2 or parts[0].shape[1] != width:
        whole = place_blocks([part[:, :width] for part in parts], scalars[3])
        whole = whole.transpose(1, 0, 2)
    else:
        whole = pl.pallas_call(
            join_kernel,
            grid_spec=pltpu.PrefetchScalarGridSpec(
                num_scalar_prefetch=1,
                grid=(1,),
                in_specs=[whole_spec(part.shape) for part in parts],
                out_specs=whole_spec(shape),
            ),
            out_shape=jax.ShapeDtypeStruct(shape, parts[0].dtype),
            cost_estimate=BRIEF,
            name="join_groups",
        )(scalars, *parts)
    return whole.reshape(4, tokens // 4, groups * width)


def sum_kernel(count, *refs):
    total = refs[0][...]
    for part in refs[1:count]:
        total = total + part[...]
    refs[count][...] = total.astype(refs[count].dtype)


def sum_groups(parts):
    tokens, features = parts[0].shape
    total = pl.pallas_call(
        functools.partial(sum_kernel, len(parts)),
        out_shape=jax.ShapeDtypeStruct((tokens, features), jnp.bfloat16),
        cost_estimate=COVER,
        name="sum_groups",
    )(*parts)
    return total.reshape(4, tokens // 4, features)


def edge_kernel(top_ref, end_ref, first_ref, last_ref):
    half = top_ref.shape[1]
    for j in range(2):
        first_ref[j * half : (j + 1) * half, :] = top_ref[j]
        last_ref[j * half : (j + 1) * half, :] = end_ref[j]


def edge_rows(maps, cols):
    size, features = maps.shape[1:]
    half = cols // 2
    row = (cols, features)
    return pl.pallas_call(
        edge_kernel,
        grid=(1,),
        in_specs=[
            pl.BlockSpec((2, half, features), lambda j: (0, 0, 0)),
            pl.BlockSpec((2, half, features), lambda j: (1, size // half - 1, 0)),
        ],
        out_specs=[pl.BlockSpec(row, lambda j: (0, 0))] * 2,
        out_shape=[jax.ShapeDtypeStruct(row, maps.dtype)] * 2,
        cost_estimate=COVER,
        name="edge_rows",
    )(maps, maps)


def expand_kernel(s_ref, o_ref, x_ref, m_ref, wp_ref, w_ref, b_ref, *refs):
    oc_ref, at_ref, x1_ref, a2_ref, f_ref, first_ref, last_ref, t_sc = refs
    rows, cols, features = x_ref.shape
    side, row_zero = (s_ref[0], s_ref[1])

    @pl.when(pl.program_id(0) == 0)
    def _():
        from_maps(o_ref, t_sc, 0)
        for b in range(features // 128):
            part = t_sc[b].reshape(rows * cols, 128)
            oc_ref[:, 128 * b : 128 * b + 128] = part.astype(jnp.bfloat16)
        at_ref[...] = dot_nn(oc_ref[...], wp_ref[...])

        def body(r, carry):
            here = pl.ds(pl.multiple_of(r * cols, cols), cols)
            x1 = x_ref[r].astype(jnp.float32) + m_ref[2:3, :] * at_ref[here, :]
            x1_ref[here, :] = x1
            normed, _ = normalize(x1)
            a2 = normed * (1.0 + m_ref[4:5, :]) + m_ref[3:4, :]
            a2_ref[here, :] = a2.astype(jnp.bfloat16)
            return carry

        lax.fori_loop(0, rows, body, 0)

    block = f_ref.shape[2]
    f = (dot_nn(a2_ref[...], w_ref[...]) + b_ref[...].astype(jnp.float32)).reshape(rows, cols, block)
    col = lax.broadcasted_iota(jnp.int32, (cols, block), 0)
    for r in range(rows):
        live = (col < side) & (row_zero + r < side)
        f_ref[r] = jnp.where(live, f[r], 0.0).astype(jnp.bfloat16)
    first_ref[...] = f_ref[0:1]
    last_ref[...] = f_ref[rows - 1 : rows]


def expand(at, scalars, maps, latents, mods, w_proj, w_fc1, bias):
    rows, cols, features = latents.shape[2:]
    hidden = w_fc1.shape[1]
    tokens, block = (rows * cols, 768)
    flat = (tokens, features)
    specs = canvas_specs(latents, at)
    return pl.pallas_call(
        expand_kernel,
        grid_spec=pltpu.PrefetchScalarGridSpec(
            num_scalar_prefetch=1,
            grid=(hidden // block,),
            in_specs=[
                whole_spec(maps.shape),
                specs[0],
                specs[3],
                whole_spec(w_proj.shape),
                pl.BlockSpec((features, block), lambda j, s: (0, j)),
                pl.BlockSpec((1, block), lambda j, s: (0, j)),
            ],
            out_specs=[whole_spec(flat)] * 4
            + [pl.BlockSpec((rows, cols, block), lambda j, s: (0, 0, j))]
            + [pl.BlockSpec((1, cols, block), lambda j, s: (0, 0, j))] * 2,
            scratch_shapes=[pltpu.VMEM((features // 128, rows, cols, 128), jnp.float32)],
        ),
        out_shape=[
            jax.ShapeDtypeStruct(flat, jnp.bfloat16),
            jax.ShapeDtypeStruct(flat, jnp.float32),
            jax.ShapeDtypeStruct(flat, jnp.float32),
            jax.ShapeDtypeStruct(flat, jnp.bfloat16),
            jax.ShapeDtypeStruct((rows, cols, hidden), jnp.bfloat16),
        ]
        + [jax.ShapeDtypeStruct((1, cols, hidden), jnp.bfloat16)] * 2,
        cost_estimate=COVER,
        name="expand",
    )(scalars, maps, latents, mods, w_proj, w_fc1, bias)


def middle_kernel(first, s_ref, f_ref, top_ref, end_ref, c_ref, w_ref, ct_ref, x1_ref, m_ref, *rest):
    if first:
        mixed_ref, dg_ref, dz_ref, g_ref, gc_ref, first_ref, last_ref = rest[:7]
    else:
        gp_ref, gcp_ref = rest[:2]
        mixed_ref, dg_ref, dz_ref, g_ref, gc_ref, first_ref, last_ref = rest[3:10]
    gz_sc = rest[-1:]
    out_sc, d_sc, x_sc, t_sc, acc_sc = rest[-6:-1]
    rows, cols, block = f_ref.shape
    features = out_sc.shape[1]
    side, row_zero = (s_ref[0], s_ref[1])

    def upstream(r):
        col = lax.broadcasted_iota(jnp.int32, (cols, features), 0)
        live = (col < side) & (row_zero + r < side)
        return jnp.where(live, ct_ref[r].astype(jnp.float32), 0.0), live

    @pl.when(pl.program_id(0) == 0)
    def _():
        def body(r, carry):
            here = pl.ds(pl.multiple_of(r * cols, cols), cols)
            d_sc[here, :] = (upstream(r)[0] * m_ref[5:6, :]).astype(jnp.bfloat16)
            return carry

        lax.fori_loop(0, rows, body, 0)

    d = d_sc[...]
    x_sc[0:1] = top_ref[...]
    x_sc[1 : rows + 1] = f_ref[...]
    x_sc[rows + 1 : rows + 2] = end_ref[...]
    acc_sc[...] = jnp.zeros_like(acc_sc)
    col = lax.broadcasted_iota(jnp.int32, (cols, 128), 0)
    wide = 256
    count = block // wide
    part, grads = (None, [])

    def start(s):
        t = dot_nt(d, w_ref[s * wide : (s + 1) * wide, :])
        for l in range(wide // 128):
            t_sc[s * (wide // 128) + l] = t[:, 128 * l : 128 * l + 128].reshape(rows, cols, 128)

    start(0)
    for s in range(count):
        if s + 1 < count:
            start(s + 1)
        for l in range(wide // 128):
            at = s * (wide // 128) + l
            lanes = slice(128 * at, 128 * at + 128)
            inner = slice(128 * l, 128 * l + 128)
            taps = wide_taps(c_ref, lanes, cols)

            def body(r, carry):
                x = [x_sc[r + i, :, lanes].astype(jnp.float32) for i in range(3)]
                a = [x[0] * taps[j] + x[1] * taps[3 + j] + x[2] * taps[6 + j] for j in range(3)]
                z = a[1] + shift_cols(a[0], -1, col) + shift_cols(a[2], 1, col)
                half = 0.5 * (1.0 + lax.erf(z * root_half))
                gz_sc[s][r * cols : (r + 1) * cols, inner] = (z * half).astype(jnp.bfloat16)
                slope = half + z * jnp.exp(-0.5 * z * z) * inverse_root_tau
                d_z = (t_sc[at, r] * slope).astype(jnp.bfloat16)
                dz_ref[r, :, lanes] = d_z
                d_z = d_z.astype(jnp.float32)
                moved = [shift_cols(d_z, 1, col), d_z, shift_cols(d_z, -1, col)]
                return [
                    c + sublane_sum(x[k // 3] * moved[k % 3]) for k, c in enumerate(carry)
                ]

            sums = [jnp.zeros((8, 128), jnp.float32)] * 9
            for r in range(rows):
                sums = body(r, sums)
            for k in range(9):
                acc_sc[k, :, lanes] = sums[k]
        gz = gz_sc[s][...]
        here = dot_nn(gz, w_ref[s * wide : (s + 1) * wide, :])
        part = here if part is None else part + here
        grads.append(dot_tn(gz, d))
    first_ref[...] = dz_ref[0:1]
    last_ref[...] = dz_ref[rows - 1 : rows]
    store_sum(out_sc, part)
    grad = jnp.concatenate(grads, axis=0)
    taps_grad = jnp.concatenate(
        [jnp.sum(acc_sc[k], axis=0, keepdims=True) for k in range(9)], axis=0
    )
    if not first:
        grad = grad + gp_ref[...]
        taps_grad = taps_grad + gcp_ref[...]
    g_ref[...] = grad.astype(g_ref.dtype)
    gc_ref[...] = taps_grad

    @pl.when(pl.program_id(0) == pl.num_programs(0) - 1)
    def _():
        def body(r, total):
            here = pl.ds(pl.multiple_of(r * cols, cols), cols)
            value, live = upstream(r)
            out = out_sc[here, :]
            mixed = x1_ref[here, :] + m_ref[5:6, :] * out
            mixed_ref[r] = jnp.where(live, mixed, 0.0).astype(jnp.bfloat16)
            return total + sublane_sum(value * out)

        total = lax.fori_loop(0, rows, body, jnp.zeros((8, features), jnp.float32))
        dg_ref[...] = jnp.sum(total, axis=0, keepdims=True)


def sublane_sum(x):
    return jnp.sum(x.reshape(x.shape[0] // 8, 8, x.shape[1]), axis=0)


def ffn_middle(at, scalars, f, halo, taps, w, cotangent, x1, mods, prev, grad_type):
    rows, cols, hidden = f.shape
    features = w.shape[1]
    block = 256
    wide = lambda j, s: (0, 0, j)
    row_spec = pl.BlockSpec((1, cols, block), wide)
    weight_spec = pl.BlockSpec((block, features), lambda j, s: (j, 0))
    tap_spec = pl.BlockSpec((9, block), lambda j, s: (0, j))
    canvas_spec = pl.BlockSpec((rows, cols, block), wide)
    specs = canvas_specs(cotangent, at)
    args = [scalars, f, halo[0], halo[1], taps, w, cotangent, x1, mods]
    args += [] if prev is None else list(prev)
    return pl.pallas_call(
        functools.partial(middle_kernel, prev is None),
        grid_spec=pltpu.PrefetchScalarGridSpec(
            num_scalar_prefetch=1,
            grid=(hidden // block,),
            in_specs=[canvas_spec, row_spec, row_spec, tap_spec, weight_spec]
            + [specs[0], whole_spec(x1.shape), specs[3]]
            + ([] if prev is None else [weight_spec, tap_spec, pl.BlockSpec(memory_space=pl.ANY)]),
            out_specs=[specs[0], whole_spec((1, features)), canvas_spec, weight_spec, tap_spec]
            + [row_spec] * 2,
            scratch_shapes=[
                pltpu.VMEM((rows * cols, features), jnp.float32),
                pltpu.VMEM((rows * cols, features), jnp.bfloat16),
                pltpu.VMEM((rows + 2, cols, block), jnp.bfloat16),
                pltpu.VMEM((block // 128, rows, cols, 128), jnp.float32),
                pltpu.VMEM((9, 8, block), jnp.float32),
            ]
            + [pltpu.VMEM((rows * cols, 256), jnp.bfloat16)] * 1,
        ),
        out_shape=[
            jax.ShapeDtypeStruct(cotangent.shape, jnp.bfloat16),
            jax.ShapeDtypeStruct((1, features), jnp.float32),
            jax.ShapeDtypeStruct(f.shape, jnp.bfloat16),
            jax.ShapeDtypeStruct((hidden, features), grad_type),
            jax.ShapeDtypeStruct((9, hidden), jnp.float32),
        ]
        + [jax.ShapeDtypeStruct((1, cols, hidden), jnp.bfloat16)] * 2,
        input_output_aliases={} if prev is None else {11: 0},
        cost_estimate=COVER,
        name="ffn_middle",
    )(*args)


def ffn_back_kernel(micro, first, s_ref, z_ref, top_ref, end_ref, c_ref, w_ref, a_ref, *rest):
    far, m_ref = (rest[:5], rest[5])
    near, sem = (rest[-6:-1], rest[-1])
    rest = rest[6:-6]
    ct_ref, x1_ref, at_ref, oc_ref, wp_ref = near
    copies = [
        pltpu.make_async_copy(source.at[micro, 0] if i == 0 else source, target, sem.at[i])
        for i, (source, target) in enumerate(zip(far, near))
    ]

    @pl.when(pl.program_id(0) == 0)
    def _():
        for copy in copies:
            copy.start()

    if not first:
        gp_ref, gbp_ref, gpp_ref = rest[:3]
        rest = rest[3:]
    maps_ref, dx_ref, dm_ref, g_ref, gb_ref, gp_out = rest[:6]
    da_sc, x_sc, df_sc, acc_sc, t_sc, dat_sc = rest[6:]
    rows, cols, block = z_ref.shape
    features = da_sc.shape[1]
    x_sc[0:1] = top_ref[...]
    x_sc[1 : rows + 1] = z_ref[...]
    x_sc[rows + 1 : rows + 2] = end_ref[...]
    acc_sc[...] = jnp.zeros_like(acc_sc)
    col = lax.broadcasted_iota(jnp.int32, (cols, 128), 0)
    side, row_zero = (s_ref[0], s_ref[1])
    for at in range(block // 128):
        lanes = slice(128 * at, 128 * at + 128)
        taps = wide_taps(c_ref, lanes, cols)
        total = jnp.zeros((8, 128), jnp.float32)
        for r in range(rows):
            x = [x_sc[r + i, :, lanes].astype(jnp.float32) for i in range(3)]
            b = [x[2] * taps[j] + x[1] * taps[3 + j] + x[0] * taps[6 + j] for j in range(3)]
            d_f = b[1] + shift_cols(b[0], 1, col) + shift_cols(b[2], -1, col)
            live = (col < side) & (row_zero + r < side)
            d_f = jnp.where(live, d_f, 0.0).astype(jnp.bfloat16)
            df_sc[r, :, lanes] = d_f
            total = total + sublane_sum(d_f.astype(jnp.float32))
        acc_sc[:, lanes] = total
    d_f = df_sc[...].reshape(rows * cols, block)
    store_sum(da_sc, dot_nt(d_f, w_ref[...]))
    grad = dot_tn(a_ref[...], d_f)
    bias_grad = jnp.sum(acc_sc[...], axis=0, keepdims=True)
    if not first:
        grad = grad + gp_ref[...]
        bias_grad = bias_grad + gbp_ref[...]
    g_ref[...] = grad.astype(g_ref.dtype)
    gb_ref[...] = bias_grad

    @pl.when(pl.program_id(0) == pl.num_programs(0) - 1)
    def _():
        for copy in copies:
            copy.wait()
        wide_col = lax.broadcasted_iota(jnp.int32, (cols, features), 0)

        def body(r, totals):
            here = pl.ds(pl.multiple_of(r * cols, cols), cols)
            d_a = da_sc[here, :]
            normed, inverse = normalize(x1_ref[here, :])
            live = (wide_col < side) & (row_zero + r < side)
            d_x = jnp.where(live, ct_ref[r].astype(jnp.float32), 0.0)
            d_x = d_x + norm_back(normed, inverse, d_a * (1.0 + m_ref[4:5, :]))
            dx_ref[here, :] = d_x
            dat_sc[here, :] = (d_x * m_ref[2:3, :]).astype(jnp.bfloat16)
            return (
                totals[0] + sublane_sum(d_x * at_ref[here, :]),
                totals[1] + sublane_sum(d_a),
                totals[2] + sublane_sum(d_a * normed),
            )

        zero = jnp.zeros((8, features), jnp.float32)
        totals = lax.fori_loop(0, rows, body, (zero, zero, zero))
        for i in range(3):
            dm_ref[i : i + 1, :] = jnp.sum(totals[i], axis=0, keepdims=True)
        proj = dot_tn(oc_ref[...], dat_sc[...])
        if not first:
            proj = proj + gpp_ref[...]
        gp_out[...] = proj.astype(gp_out.dtype)
        d_o = dot_nt(dat_sc[...], wp_ref[...])
        for b in range(features // 128):
            t_sc[b] = d_o[:, 128 * b : 128 * b + 128].reshape(rows, cols, 128)
        to_maps(t_sc, maps_ref)


def ffn_back(
    at, scalars, d_z, halo, taps, w, a, cotangent, x1, attn, oc, w_proj, mods, prev, grad_type
):
    rows, cols, hidden = d_z.shape
    features = a.shape[1]
    block = 512
    wide = lambda j, s: (0, 0, j)
    row_spec = pl.BlockSpec((1, cols, block), wide)
    weight_spec = pl.BlockSpec((features, block), lambda j, s: (0, j))
    bias_spec = pl.BlockSpec((1, block), lambda j, s: (0, j))
    flat_spec = whole_spec((rows * cols, features))
    proj_spec = whole_spec(w_proj.shape)
    maps = (4, rows * cols // 4, features)
    specs = canvas_specs(cotangent, at)
    args = [scalars, d_z, halo[0], halo[1], taps, w, a, cotangent, x1, attn, oc, w_proj, mods]
    args += [] if prev is None else list(prev)
    return pl.pallas_call(
        functools.partial(ffn_back_kernel, at, prev is None),
        grid_spec=pltpu.PrefetchScalarGridSpec(
            num_scalar_prefetch=1,
            grid=(hidden // block,),
            in_specs=[
                pl.BlockSpec((rows, cols, block), wide),
                row_spec,
                row_spec,
                pl.BlockSpec((9, block), lambda j, s: (0, j)),
                weight_spec,
                flat_spec,
            ]
            + [HBM] * 5
            + [
                specs[3],
            ]
            + ([] if prev is None else [weight_spec, bias_spec, proj_spec]),
            out_specs=[whole_spec(maps)]
            + [flat_spec, whole_spec((3, features)), weight_spec, bias_spec, proj_spec],
            scratch_shapes=[
                pltpu.VMEM((rows * cols, features), jnp.float32),
                pltpu.VMEM((rows + 2, cols, block), jnp.bfloat16),
                pltpu.VMEM((rows, cols, block), jnp.bfloat16),
                pltpu.VMEM((8, block), jnp.float32),
                pltpu.VMEM((features // 128, rows, cols, 128), jnp.float32),
                pltpu.VMEM((rows * cols, features), jnp.bfloat16),
                pltpu.VMEM((rows, cols, features), cotangent.dtype),
                pltpu.VMEM(x1.shape, x1.dtype),
                pltpu.VMEM(attn.shape, attn.dtype),
                pltpu.VMEM(oc.shape, oc.dtype),
                pltpu.VMEM(w_proj.shape, w_proj.dtype),
                pltpu.SemaphoreType.DMA((5,)),
            ],
        ),
        out_shape=[jax.ShapeDtypeStruct(maps, jnp.bfloat16)]
        + [
            jax.ShapeDtypeStruct((rows * cols, features), jnp.float32),
            jax.ShapeDtypeStruct((3, features), jnp.float32),
            jax.ShapeDtypeStruct(w.shape, grad_type),
            jax.ShapeDtypeStruct((1, hidden), jnp.float32),
            jax.ShapeDtypeStruct(w_proj.shape, grad_type),
        ],
        cost_estimate=COVER,
        name="ffn_backward",
    )(*args)


def last_kernel(first, s_ref, du_ref, dtop_ref, dend_ref, *rest):
    x_ref, top_ref, end_ref, m_ref, c_ref, dx_ref = rest[:6]
    rest = rest[6:]
    if not first:
        gcp_ref = rest[0]
        rest = rest[2:]
    dl_ref, dm_ref, gc_ref, a_sc, t_sc, d_sc, acc_sc = rest
    rows, cols, features = x_ref.shape
    half = cols // 2
    side, row_zero = (s_ref[0], s_ref[1])
    modulated_rows(a_sc, s_ref, x_ref, top_ref, end_ref, m_ref)
    from_maps(du_ref, t_sc, 1)
    for at, ref in ((0, dtop_ref), (rows + 1, dend_ref)):
        for j in range(2):
            for start in range(0, features, 128):
                lanes = slice(start, start + 128)
                part = ref[j * half : (j + 1) * half, lanes].astype(jnp.float32)
                t_sc[start // 128, at, pl.ds(j, half, stride=2), :] = part
    acc_sc[...] = jnp.zeros_like(acc_sc)
    col = lax.broadcasted_iota(jnp.int32, (cols, 128), 0)
    for start in range(0, features, 128):
        lanes = slice(start, start + 128)
        taps = wide_taps(c_ref, lanes, cols)

        def conv_body(r, carry):
            d = [t_sc[start // 128, r + i] for i in range(3)]
            b = [d[2] * taps[j] + d[1] * taps[3 + j] + d[0] * taps[6 + j] for j in range(3)]
            d_a = b[1] + shift_cols(b[0], 1, col) + shift_cols(b[2], -1, col)
            live = (col < side) & (row_zero + r < side)
            d_sc[r, :, lanes] = jnp.where(live, d_a, 0.0)
            moved = [shift_cols(d[1], 1, col), d[1], shift_cols(d[1], -1, col)]
            for i in range(3):
                x = a_sc[r + i, :, lanes].astype(jnp.float32)
                for j in range(3):
                    acc_sc[3 * i + j, :, lanes] += sublane_sum(x * moved[j])
            return carry

        lax.fori_loop(0, rows, conv_body, 0, unroll=2)
    taps_grad = jnp.concatenate(
        [jnp.sum(acc_sc[k], axis=0, keepdims=True) for k in range(9)], axis=0
    )
    if not first:
        taps_grad = taps_grad + gcp_ref[...]
    gc_ref[...] = taps_grad

    def body(r, totals):
        here = pl.ds(pl.multiple_of(r * cols, cols), cols)
        normed, inverse = normalize(x_ref[r].astype(jnp.float32))
        d_a = d_sc[r]
        dl_ref[r] = dx_ref[here, :] + norm_back(normed, inverse, d_a * (1.0 + m_ref[1:2, :]))
        return (totals[0] + sublane_sum(d_a), totals[1] + sublane_sum(d_a * normed))

    zero = jnp.zeros((8, features), jnp.float32)
    totals = lax.fori_loop(0, rows, body, (zero, zero))
    for i in range(2):
        dm_ref[i : i + 1, :] = jnp.sum(totals[i], axis=0, keepdims=True)


def last_stage(at, scalars, maps, d_halo, latents, top, end, mods, taps, d_x, prev):
    rows, cols, features = latents.shape[2:]
    specs = canvas_specs(latents, at)
    args = [scalars, maps, *d_halo, latents, top, end, mods, taps, d_x]
    args += [] if prev is None else list(prev)
    return pl.pallas_call(
        functools.partial(last_kernel, prev is None),
        grid_spec=pltpu.PrefetchScalarGridSpec(
            num_scalar_prefetch=1,
            grid=(1,),
            in_specs=[whole_spec(maps.shape)]
            + [whole_spec((cols, features))] * 2
            + specs
            + [whole_spec(taps.shape), whole_spec(d_x.shape)]
            + ([] if prev is None else [whole_spec(taps.shape), pl.BlockSpec(memory_space=pl.ANY)]),
            out_specs=[specs[0], whole_spec((2, features)), whole_spec(taps.shape)],
            scratch_shapes=[
                pltpu.VMEM((rows + 2, cols, features), jnp.bfloat16),
                pltpu.VMEM((features // 128, rows + 2, cols, 128), jnp.float32),
                pltpu.VMEM((rows, cols, features), jnp.float32),
                pltpu.VMEM((9, 8, features), jnp.float32),
            ],
        ),
        out_shape=[
            jax.ShapeDtypeStruct(latents.shape, jnp.float32),
            jax.ShapeDtypeStruct((2, features), jnp.float32),
            jax.ShapeDtypeStruct(taps.shape, jnp.float32),
        ],
        input_output_aliases={} if prev is None else {11: 0},
        cost_estimate=COVER,
        name="last_stage",
    )(*args)


def shards(
    latents,
    timesteps,
    size_tags,
    w_ada,
    b_ada,
    conv_attn,
    w_qkv,
    w_proj,
    w_fc1,
    b_fc1,
    conv_ffn,
    w_fc2,
    cotangent,
):
    micro_count, _, row_count, side_count, features = latents.shape
    dp, strips = (lax.axis_size("dp"), lax.axis_size("strip"))
    dp_at, strip_at = (lax.axis_index("dp"), lax.axis_index("strip"))
    hidden = conv_ffn.shape[1] * dp
    groups = strips // 4
    group_at, map_at = (strip_at % groups, strip_at // groups)
    score_scale = (features // HEADS) ** (-0.5)
    width = features // groups

    stamps = timesteps[:, 0].astype(jnp.float32)
    small = jnp.concatenate([conv_attn.reshape(-1), conv_ffn.reshape(-1), b_fc1])
    small = gather_butterfly(jnp.concatenate([stamps, small.astype(jnp.float32)])[None])
    all_stamps, small = (small[:, :micro_count], small[:, micro_count:].astype(jnp.bfloat16))
    conds = [silu_of(embed_times(all_stamps[k], features)) for k in range(dp)]
    ada_rows = features // dp
    ada_wide = w_ada.astype(jnp.float32)
    partial_mods = jnp.dot(
        lax.dynamic_slice_in_dim(jnp.concatenate(conds), dp_at * ada_rows, ada_rows, 1),
        ada_wide,
        precision=lax.Precision.HIGHEST,
    )
    bias_here = lax.dynamic_update_slice_in_dim(
        jnp.zeros((6 * features,), jnp.float32),
        b_ada.astype(jnp.float32),
        dp_at * b_ada.shape[0],
        0,
    )
    partial_mods = (partial_mods + bias_here[None, :]).reshape(dp, micro_count, 6 * features)
    count = dp
    while count > 1:
        count //= 2
        partial_mods = partial_mods[:count] + permute_xor(partial_mods[count:], "dp", count)
    modulation = partial_mods[0]

    small = place_blocks([small[k] for k in range(dp)], dp_at)
    n_one, n_two = (conv_attn.size, conv_attn.size + conv_ffn.size)
    conv_one = small[:, :n_one].reshape(dp, 9, -1).transpose(1, 0, 2).reshape(9, features)
    conv_two = small[:, n_one:n_two].reshape(dp, 9, -1).transpose(1, 0, 2).reshape(9, hidden)
    fc1_bias = small[:, n_two:].reshape(1, hidden)
    qkv_pieces, modulation = fetch_group(w_qkv, groups, modulation)

    top, end = halo_rows(latents[:, 0, 0], latents[:, 0, row_count - 1])
    mods = modulation.reshape(micro_count, 6, features)
    micros = range(micro_count)
    places = jnp.stack([strip_at * row_count, map_at, group_at]).astype(jnp.int32)
    scalars = [
        jnp.concatenate(
            [jnp.where(size_tags[at] == 1, side_count, side_count // 2).astype(jnp.int32), places]
        )
        for at in micros
    ]
    kept = [{} for _ in micros]
    turn = ()

    for at in micros:
        if at == micro_count - 1:
            qkv_group = gather_group(qkv_pieces)
            turn = (turn, qkv_group)
        maps = before_attention(at, after(scalars[at], turn), latents, top, end, mods, conv_one)
        if at == 0:
            fetched = fetch_direct(pack_weights(w_proj, w_fc1, w_fc2, maps))
        turn = maps
        kept[at]["u"] = map_exchange(maps, groups).reshape(-1, features)

    for at in micros:
        keep = kept[at]
        u = after(keep["u"], turn if at == 0 else kept[at - 1]["logs"])
        keep["u"] = group_exchange(u, groups)
        done = attend(after(scalars[at], turn), keep["u"], qkv_group, score_scale, side_count)
        keep["t"], keep["o"], keep["logs"] = (done[0], done[1 : 1 + groups], done[-1])
        parts = [keep["o"][0]] + [
            permute_xor(keep["o"][k], "strip", k) for k in range(1, groups)
        ]
        if at == 0:
            fetched, keep["logs"] = tie(fetched, keep["logs"])
            direct = list(fetched.values())
            fetched = fetch_relayed(fetched)
        if at == micro_count - 1:
            for k in range(1, dp):
                if k & (k - 1):
                    fetched[k - 1], keep["logs"] = tie(fetched[k - 1], keep["logs"])
            proj_full, fc1_full, fc2_full = unpack_weights(
                fetched, keep["logs"], w_proj, w_fc1, w_fc2
            )
        maps = join_groups(scalars[at], parts, width)
        turn = (maps, direct)
        keep["o_maps"] = map_exchange(maps, groups)

    for at in micros:
        keep = kept[at]
        keep["oc"], keep["attn"], keep["x1"], keep["a2"], keep["f"], first, last = expand(
            at,
            after(scalars[at], turn),
            keep["o_maps"],
            latents,
            mods,
            proj_full,
            fc1_full,
            fc1_bias,
        )
        turn = keep["attn"]
        keep["f_halo"] = halo_rows(first, last)

    for at in micros:
        keep, grad_type = (kept[at], jnp.bfloat16)
        prev = None if at == 0 else (term_fc2, term_conv_two, mixed)
        mixed, keep["d_gate2"], keep["d_z"], term_fc2, term_conv_two, first, last = ffn_middle(
            at,
            after(scalars[at], turn),
            keep["f"],
            keep["f_halo"],
            conv_two,
            fc2_full,
            cotangent,
            keep["x1"],
            mods,
            prev,
            grad_type,
        )
        turn = keep["d_gate2"]
        keep["z_halo"] = halo_rows(first, last)

    for at in micros:
        keep, grad_type = (kept[at], jnp.bfloat16)
        prev = None if at == 0 else (term_fc1, term_fc1_bias, term_proj)
        done = ffn_back(
            at,
            after(scalars[at], turn),
            keep["d_z"],
            keep["z_halo"],
            conv_two,
            fc1_full,
            keep["a2"],
            cotangent,
            keep["x1"],
            keep["attn"],
            keep["oc"],
            proj_full,
            mods,
            prev,
            grad_type,
        )
        keep["d_x"], keep["d_mods"], term_fc1, term_fc1_bias, term_proj = done[1:]
        turn = keep["d_mods"]
        keep["d_o"] = map_exchange(done[0], groups)

    blocks = dp * strips
    wide, narrow = (hidden // blocks, features // blocks)
    small = jnp.concatenate([term_conv_two, term_fc1_bias]).reshape(10, blocks, wide)
    small = small.transpose(1, 0, 2).reshape(blocks, 10 * wide)
    merged = narrow % 8 == 0 and dp == 4
    if merged:
        small_rows = -(-10 * wide // features // 8) * 8
        small = jnp.pad(small, ((0, 0), (0, small_rows * features - 10 * wide)))
        small = small.reshape(blocks, small_rows, features).astype(jnp.bfloat16)
        small, kept[0]["d_o"] = tie(small, kept[0]["d_o"])
        shares, shapes = by_destination(term_fc2, term_fc1, term_proj, small, narrow, dp)
        send = route_core(shares, shapes)
        share = core_sum(shares, shapes, permute_xor(send, "strip", 1), dp_at)
        turn = (turn, share[1])
        came = [permute_xor(share[0], "dp", 1), permute_xor(share[2], "dp", 2)]

    for at in micros:
        keep, grad_type = (kept[at], jnp.bfloat16)
        if at > 0:
            keep["d_o"], done[0] = tie(keep["d_o"], done[0])
        pieces = group_exchange(keep["d_o"].reshape(-1, features), groups)
        if width % 128:
            pieces = [
                jnp.pad(
                    lax.dynamic_slice_in_dim(piece, group_at * width, width, 1),
                    ((0, 0), (0, -width % 128)),
                )
                for piece in pieces
            ]
        done = attend_back(
            after(scalars[at], turn),
            keep["u"],
            pieces,
            keep["o"],
            qkv_group,
            keep["t"],
            keep["logs"],
            score_scale,
            side_count,
            None if at == 0 else term_qkv,
            grad_type,
        )
        done = list(done)
        term_qkv = done[groups]
        parts = [done[0]] + [permute_xor(done[k], "strip", k) for k in range(1, groups)]
        if at == 0 and merged:
            own, x_send, y_send = turn_sums(after(share[1], done[0]), came[0], share[3], came[1])
            came = [permute_xor(x_send, "dp", 2), permute_xor(y_send, "dp", 1)]
            parts = after(parts, own)
        if at > 0:
            if merged:
                share[1], share[2], kept[0]["d_u"] = tie(share[1], share[2], kept[0]["d_u"])
            kept[0]["edges"] = edge_rows(kept[0]["d_u"], side_count)
            kept[0]["edges"], parts = tie(kept[0]["edges"], parts)
        maps = sum_groups(parts)
        turn = maps
        keep["d_u"] = map_exchange(maps, groups)
        if at == 0 and merged:
            share = list(add_up(after(own, maps), *came, strip_at >> 1))
            turn = (turn, share[0])
            share = [share[0]] + [
                permute_xor(share[k], "strip", 2 * k) for k in range(1, strips // 2)
            ]

    kept_qkv = group_sums(after(term_qkv, turn), groups, width)
    mod_grads = []
    for at in micros:
        keep = kept[at]
        first_row, last_row = (
            keep["edges"] if at == 0 else edge_rows(keep["d_u"], side_count)
        )
        d_halo = halo_rows(first_row, last_row)
        prev = None if at == 0 else (term_conv_one, d_latents)
        d_latents, keep["d_mod1"], term_conv_one = last_stage(
            at,
            after(scalars[at], turn),
            keep["d_u"],
            d_halo,
            latents,
            top,
            end,
            mods,
            conv_one,
            keep["d_x"],
            prev,
        )
        turn = keep["d_mod1"]
        if at == 0:
            parts_qkv = group_parts(kept_qkv, groups)
        mod_grads.append(
            jnp.concatenate([keep["d_mod1"], keep["d_mods"], keep["d_gate2"]]).reshape(-1)
        )

    if merged:
        total = share[0].astype(jnp.float32)
        for part in share[1:]:
            total = total + part.astype(jnp.float32)
        ratio = hidden // features
        g_fc2 = total[: ratio * narrow]
        g_fc1 = total[ratio * narrow : 2 * ratio * narrow].reshape(ratio, narrow, features)
        g_fc1 = g_fc1.transpose(1, 0, 2).reshape(narrow, hidden)
        g_proj = total[2 * ratio * narrow : (2 * ratio + 1) * narrow]
        small = total[(2 * ratio + 1) * narrow :].reshape(-1)
    else:
        g_fc2 = scatter_rows(term_fc2)
        g_fc1 = scatter_rows(term_fc1)
        g_proj = scatter_rows(term_proj)
        small = scatter_rows(small)[0]
    g_conv_two = small[: 9 * wide].reshape(9, wide)
    g_fc1_bias = small[9 * wide : 10 * wide]
    mod_grads.append(term_conv_one.reshape(-1))

    grad_mod, parts_qkv = tie(jnp.concatenate(mod_grads), parts_qkv)
    step = 1
    while step < strips:
        grad_mod = grad_mod + permute_xor(grad_mod, "strip", step)
        step *= 2
        if step == 4:
            g_qkv = group_columns(after(parts_qkv, grad_mod), groups)
    all_mods = gather_butterfly(grad_mod[None])
    block_at = dp_at * strips + strip_at
    g_conv_one = jnp.sum(all_mods[:, micro_count * 6 * features :], axis=0).reshape(9, features)
    g_conv_one = lax.dynamic_slice_in_dim(g_conv_one, block_at * narrow, narrow, 1)
    all_mods = all_mods[:, : micro_count * 6 * features].reshape(-1, 6 * features)
    conds_here = lax.dynamic_slice_in_dim(
        jnp.concatenate(conds), block_at * narrow, narrow, 1
    )
    g_ada = lax.dot_general(
        conds_here, all_mods, (((0,), (0,)), ((), ())), precision=lax.Precision.HIGHEST
    )
    ada_wide_block = 6 * features // blocks
    g_ada_bias = lax.dynamic_slice_in_dim(
        jnp.sum(all_mods, axis=0), block_at * ada_wide_block, ada_wide_block, 0
    )
    return (
        mixed,
        d_latents,
        g_ada,
        g_ada_bias,
        g_conv_one,
        g_qkv,
        g_proj,
        g_fc1,
        g_fc1_bias,
        g_conv_two,
        g_fc2,
    )


def solution(mesh):
    return jax.shard_map(
        shards,
        mesh=mesh,
        in_specs=(
            P(None, "dp", "strip", None, None),
            P(None, "dp"),
            P(None, "dp"),
            P("dp", None),
            P("dp"),
            P(None, "dp"),
            P("dp", None),
            P("dp", None),
            P("dp", None),
            P("dp"),
            P(None, "dp"),
            P("dp", None),
            P(None, "dp", "strip", None, None),
        ),
        out_specs=(
            P(None, "dp", "strip", None, None),
            P(None, "dp", "strip", None, None),
            P(("dp", "strip"), None),
            P(("dp", "strip")),
            P(None, ("dp", "strip")),
            P(("dp", "strip"), None),
            P(("dp", "strip"), None),
            P(("dp", "strip"), None),
            P(("dp", "strip")),
            P(None, ("dp", "strip")),
            P(("dp", "strip"), None),
        ),
        check_vma=False,
    )
```

```python
import functools
import math

import jax
import jax.numpy as jnp
from jax import lax
from jax.experimental import pallas as pl
from jax.experimental.pallas import tpu as pltpu
from jax.sharding import PartitionSpec as P

HEADS = 12
COVER = pl.CostEstimate(flops=200_000_000_000, transcendentals=0, bytes_accessed=0)
BRIEF = pl.CostEstimate(flops=0, transcendentals=0, bytes_accessed=0)


root_half = 0.7071067811865476
inverse_root_tau = 0.3989422804014327


def permute_xor(x, axis, step):
    size = lax.axis_size(axis)
    return lax.ppermute(x, axis, [(i, i ^ step) for i in range(size)])


def pick(x, at, axis=0):
    return lax.dynamic_index_in_dim(x, at, axis, keepdims=False)


def halo_rows(first, last):
    size = lax.axis_size("strip")
    up = [(i, i + 1) for i in range(size - 1)]
    down = [(i + 1, i) for i in range(size - 1)]
    return (lax.ppermute(last, "strip", up), lax.ppermute(first, "strip", down))


def place_blocks(blocks, me):
    stacked = jnp.stack(blocks)
    return jnp.stack([pick(stacked, me ^ at) for at in range(len(blocks))])


def gather_butterfly(x):
    step = 1
    while step < lax.axis_size("dp"):
        x = jnp.concatenate([x, permute_xor(x, "dp", step)])
        step *= 2
    return x


def after(x, *done):
    return lax.optimization_barrier((x, done))[0]


HBM = pl.BlockSpec(memory_space=pl.ANY)


def move_all(copies):
    for copy in copies:
        copy.start()
    for copy in copies:
        copy.wait()


def rows_at(start, size):
    return pl.ds(pl.multiple_of(start, 8), size)


def tie(*values):
    return lax.optimization_barrier(values)


def assemble_kernel(at_ref, *refs):
    pieces, whole, sem = (refs[:-2], refs[-2], refs[-1])
    move_all(
        [
            pltpu.make_async_copy(
                piece, whole.at[:, rows_at(at_ref[i], piece.shape[1]), :], sem.at[i]
            )
            for i, piece in enumerate(pieces)
        ]
    )


def assemble(pieces, starts, shape):
    return pl.pallas_call(
        assemble_kernel,
        grid_spec=pltpu.PrefetchScalarGridSpec(
            num_scalar_prefetch=1,
            grid=(1,),
            in_specs=[HBM] * len(pieces),
            out_specs=whole_spec(shape),
            scratch_shapes=[pltpu.SemaphoreType.DMA((len(pieces),))],
        ),
        out_shape=jax.ShapeDtypeStruct(shape, pieces[0].dtype),
        cost_estimate=COVER,
        name="assemble",
    )(jnp.stack(starts).astype(jnp.int32), *pieces)


def pack_layout(proj, fc1, fc2):
    features = proj.shape[1]
    sizes = [proj.shape[0] // 2]
    sizes += [fc1.shape[0] // 2] * (fc1.shape[1] // features) + [fc2.shape[0] // 2]
    starts = [sum(sizes[:i]) for i in range(len(sizes))]
    return sizes, starts


def half_of(refs, row, i, size, features):
    if i == 0:
        return refs[0].at[rows_at(row, size), :]
    if i == len(refs[3]) - 1:
        return refs[2].at[rows_at(row, size), :]
    return refs[1].at[rows_at(row, size), (i - 1) * features : i * features]


def pack_kernel(at_ref, proj, fc1, fc2, out, sem):
    sizes, starts = pack_layout(proj, fc1, fc2)
    copies = []
    for i, (size, start) in enumerate(zip(sizes, starts)):
        source = half_of((proj, fc1, fc2, sizes), at_ref[0] * size, i, size, proj.shape[1])
        copies.append(pltpu.make_async_copy(source, out.at[start : start + size, :], sem.at[i]))
    move_all(copies)


def pack_weights(proj, fc1, fc2, turn):
    core = lax.axis_index("strip") & 1
    sizes, starts = pack_layout(proj, fc1, fc2)
    shape = (starts[-1] + sizes[-1], proj.shape[1])
    return pl.pallas_call(
        pack_kernel,
        grid_spec=pltpu.PrefetchScalarGridSpec(
            num_scalar_prefetch=1,
            grid=(1,),
            in_specs=[HBM] * 3,
            out_specs=whole_spec(shape),
            scratch_shapes=[pltpu.SemaphoreType.DMA((len(sizes),))],
        ),
        out_shape=jax.ShapeDtypeStruct(shape, proj.dtype),
        cost_estimate=BRIEF,
        name="pack_weights",
    )(after(core[None].astype(jnp.int32), turn), proj, fc1, fc2)


def fetch_direct(x):
    steps = [k for k in range(1, lax.axis_size("dp")) if k & (k - 1) == 0]
    return {k: permute_xor(x, "dp", k) for k in steps}


def fetch_relayed(came):
    step = 2
    while step < lax.axis_size("dp"):
        for k in range(1, step):
            came[step + k] = permute_xor(came[k], "dp", step)
        step *= 2
    return [came[k] for k in sorted(came)]


def unpack_kernel(count, at_ref, *refs):
    own, halves, wholes, sem = (refs[:3], refs[3 : 3 + count], refs[3 + count : 6 + count], refs[-1])
    sizes, starts = pack_layout(*own)
    features = own[0].shape[1]
    copies = []
    for ref, whole in zip(own, wholes):
        target = whole.at[rows_at(at_ref[0] * ref.shape[0], ref.shape[0]), :]
        copies.append(pltpu.make_async_copy(ref, target, sem.at[len(copies)]))
    for k, half in enumerate(halves):
        for i, (size, start) in enumerate(zip(sizes, starts)):
            row = (2 * at_ref[1 + 2 * k] + at_ref[2 + 2 * k]) * size
            target = half_of(wholes + (sizes,), row, i, size, features)
            copies.append(
                pltpu.make_async_copy(
                    half.at[start : start + size, :], target, sem.at[len(copies)]
                )
            )
    move_all(copies)


def unpack_weights(fetched, turn, proj, fc1, fc2):
    size, me = (lax.axis_size("dp"), lax.axis_index("dp"))
    core = lax.axis_index("strip") & 1
    halves, places = ([], [me])
    for k, mine in enumerate(fetched, 1):
        halves += [mine, permute_xor(mine, "strip", 1)]
        places += [me ^ k, core, me ^ k, 1 - core]
    shapes = [(size * w.shape[0], w.shape[1]) for w in (proj, fc1, fc2)]
    copies = 3 + len(halves) * len(pack_layout(proj, fc1, fc2)[0])
    return pl.pallas_call(
        functools.partial(unpack_kernel, len(halves)),
        grid_spec=pltpu.PrefetchScalarGridSpec(
            num_scalar_prefetch=1,
            grid=(1,),
            in_specs=[HBM] * (3 + len(halves)),
            out_specs=[whole_spec(shape) for shape in shapes],
            scratch_shapes=[pltpu.SemaphoreType.DMA((copies,))],
        ),
        out_shape=[jax.ShapeDtypeStruct(shape, proj.dtype) for shape in shapes],
        cost_estimate=BRIEF,
        name="unpack_weights",
    )(after(jnp.stack(places).astype(jnp.int32), turn), proj, fc1, fc2, *halves)


def fetch_group(w, groups, turn):
    rows, cols = w.shape
    width = cols // 3 // groups
    group = lax.axis_index("strip") % groups
    mine = pick(w.reshape(rows, 3, groups, width), group, 2).transpose(1, 0, 2)
    mine, turn = tie(jnp.pad(mine, ((0, 0), (0, 0), (0, -width % 128))), turn)
    pieces = [mine] + [permute_xor(mine, "dp", k) for k in range(1, lax.axis_size("dp"))]
    return pieces, turn


def gather_group(pieces):
    me, rows = (lax.axis_index("dp"), pieces[0].shape[1])
    starts = [(me ^ k) * rows for k in range(len(pieces))]
    return assemble(pieces, starts, (3, len(pieces) * rows, pieces[0].shape[2]))


def exchange_sum(x, axis, me, step, wire, dim=0):
    total = pick(x, me, dim).astype(jnp.float32)
    parts = [
        permute_xor(pick(x, me ^ k, dim).astype(wire), axis, k * step)
        for k in range(1, x.shape[dim])
    ]
    for part in parts:
        total = total + part.astype(jnp.float32)
    return total


def scatter_rows(g, wire=jnp.bfloat16):
    rows, cols = g.shape
    dp, strips = (lax.axis_size("dp"), lax.axis_size("strip"))
    strip = lax.axis_index("strip")
    shaped = g.reshape(dp, strips // 2, 2, rows // dp // strips, cols)
    core = strip & 1
    sent = permute_xor(pick(shaped, 1 - core, 2).astype(wire), "strip", 1)
    kept = pick(shaped, core, 2).astype(jnp.float32) + sent.astype(jnp.float32)
    kept = exchange_sum(kept, "dp", lax.axis_index("dp"), 1, wire)
    return exchange_sum(kept, "strip", strip >> 1, 2, wire)


def group_sums(g, groups, width, wire=jnp.bfloat16):
    rows = g.shape[1]
    dp, strips = (lax.axis_size("dp"), lax.axis_size("strip"))
    kept = g[:, :, :width].reshape(3, dp, strips // groups, groups, rows // dp // strips, width)
    return exchange_sum(kept, "dp", lax.axis_index("dp"), 1, wire, 1)


def group_parts(kept, groups, wire=jnp.bfloat16):
    me = lax.axis_index("strip") // groups
    return [pick(kept, me, 1)] + [
        permute_xor(pick(kept, me ^ k, 1).astype(wire), "strip", k * groups)
        for k in range(1, kept.shape[1])
    ]


def group_columns(parts, groups, wire=jnp.bfloat16):
    kept = parts[0]
    for part in parts[1:]:
        kept = kept + part.astype(jnp.float32)
    group = lax.axis_index("strip") % groups
    blocks = [pick(kept, group, 1)] + [
        permute_xor(pick(kept, group ^ k, 1).astype(wire), "strip", k).astype(jnp.float32)
        for k in range(1, groups)
    ]
    whole = place_blocks(blocks, group)
    return whole.transpose(2, 1, 0, 3).reshape(whole.shape[2], -1)


def lay_rows(out, fc2, fc1, proj, small):
    features = proj.shape[-1]
    parts = [fc2]
    parts += [fc1[:, :, i : i + features] for i in range(0, fc1.shape[-1], features)]
    start = 0
    for part in parts + [proj, small]:
        out[:, start : start + part.shape[1], :] = part
        start += part.shape[1]


def route_kernel(at_ref, fc2, fc1, proj, small, out):
    lay_rows(out, fc2[...], fc1[...], proj[...], small[...])


def by_destination(fc2, fc1, proj, small, rows, dp):
    pairs = small.shape[0] // 2 // dp
    arrays = [
        x.reshape(dp, pairs, 2, -1, x.shape[-1]) for x in (fc2, fc1, proj, small)
    ]
    shapes = [(None, pairs, None) + x.shape[3:] for x in arrays]
    return arrays, shapes


def route_core(arrays, shapes):
    dp, pairs = arrays[0].shape[:2]
    features = arrays[0].shape[-1]
    height = sum(x.shape[3] * x.shape[4] for x in arrays) // features
    core = lax.axis_index("strip") & 1
    return pl.pallas_call(
        route_kernel,
        grid_spec=pltpu.PrefetchScalarGridSpec(
            num_scalar_prefetch=1,
            grid=(dp,),
            in_specs=[
                pl.BlockSpec(shape, lambda j, s: (j, 0, 1 - s[0], 0, 0)) for shape in shapes
            ],
            out_specs=pl.BlockSpec((pairs, height, features), lambda j, s: (j, 0, 0)),
        ),
        out_shape=jax.ShapeDtypeStruct((dp * pairs, height, features), arrays[0].dtype),
        cost_estimate=COVER,
        name="route_core",
    )(core[None].astype(jnp.int32), *arrays)


def core_sum_kernel(at_ref, fc2, fc1, proj, small, came, x_send, x_keep, y_send, y_keep, kept):
    lay_rows(kept, fc2[...], fc1[...], proj[...], small[...])
    total = (kept[...].astype(jnp.float32) + came[...].astype(jnp.float32)).astype(kept.dtype)
    half = total.shape[0] // 2
    for k in range(4):

        @pl.when(pl.program_id(0) == k)
        def _():
            (x_send if k & 1 else x_keep)[...] = total[:half]
            (y_send if k >> 1 else y_keep)[...] = total[half:]


def core_sum(arrays, shapes, came, me):
    dp, pairs = arrays[0].shape[:2]
    block = (pairs,) + came.shape[1:]
    out = (2, pairs // 2) + came.shape[1:]
    core = lax.axis_index("strip") & 1
    return pl.pallas_call(
        core_sum_kernel,
        grid_spec=pltpu.PrefetchScalarGridSpec(
            num_scalar_prefetch=1,
            grid=(dp,),
            in_specs=[
                pl.BlockSpec(shape, lambda j, s: (s[1] ^ j, 0, s[0], 0, 0)) for shape in shapes
            ]
            + [pl.BlockSpec(block, lambda j, s: (s[1] ^ j, 0, 0))],
            out_specs=[
                pl.BlockSpec((None,) + out[1:], lambda j, s: (j >> 1, 0, 0, 0)),
                pl.BlockSpec((None,) + out[1:], lambda j, s: (j >> 1, 0, 0, 0)),
                pl.BlockSpec((None,) + out[1:], lambda j, s: (jnp.maximum(j - 2, 0), 0, 0, 0)),
                pl.BlockSpec((None,) + out[1:], lambda j, s: (jnp.minimum(j, 1), 0, 0, 0)),
            ],
            scratch_shapes=[pltpu.VMEM(block, came.dtype)],
        ),
        out_shape=[jax.ShapeDtypeStruct(out, came.dtype)] * 4,
        cost_estimate=COVER,
        name="core_sum",
    )(jnp.stack([core, me]).astype(jnp.int32), *arrays, came)


def turn_kernel(x_keep, x_came, y_keep, y_came, own, x_send, y_send):
    half = own.shape[0] // 2

    def both(keep, came, k):
        return (keep[k].astype(jnp.float32) + came[k].astype(jnp.float32)).astype(own.dtype)

    own[:half] = both(x_keep, x_came, 0)
    own[half:] = both(y_keep, y_came, 0)
    x_send[...] = both(x_keep, x_came, 1)
    y_send[...] = both(y_keep, y_came, 1)


def turn_sums(x_keep, x_came, y_keep, y_came):
    _, half, rows, cols = x_keep.shape
    block = rows // 2
    pair = pl.BlockSpec((2, half, block, cols), lambda j: (0, 0, j, 0))
    one = pl.BlockSpec((half, block, cols), lambda j: (0, j, 0))
    whole = pl.BlockSpec((2 * half, block, cols), lambda j: (0, j, 0))
    shape = (half, rows, cols)
    return pl.pallas_call(
        turn_kernel,
        grid=(rows // block,),
        in_specs=[pair] * 4,
        out_specs=[whole, one, one],
        out_shape=[
            jax.ShapeDtypeStruct((2 * half,) + shape[1:], x_keep.dtype),
            jax.ShapeDtypeStruct(shape, x_keep.dtype),
            jax.ShapeDtypeStruct(shape, x_keep.dtype),
        ],
        cost_estimate=COVER,
        name="turn_sums",
    )(x_keep, x_came, y_keep, y_came)


def add_kernel(at_ref, own, x_came, y_came, *refs):
    outs, kept = (refs[:-1], refs[-1])
    half = own.shape[0] // 2
    for at, came in ((slice(0, half), x_came), (slice(half, None), y_came)):
        total = own[at].astype(jnp.float32) + came[...].astype(jnp.float32)
        kept[at] = total.astype(own.dtype)
    for k, out in enumerate(outs):
        out[...] = kept[at_ref[0] ^ k]


def add_up(own, x_came, y_came, me):
    pairs, rows, cols = own.shape
    return pl.pallas_call(
        add_kernel,
        grid_spec=pltpu.PrefetchScalarGridSpec(
            num_scalar_prefetch=1,
            grid=(1,),
            in_specs=[whole_spec(x.shape) for x in (own, x_came, y_came)],
            out_specs=[whole_spec((rows, cols))] * pairs,
            scratch_shapes=[pltpu.VMEM(own.shape, own.dtype)],
        ),
        out_shape=[jax.ShapeDtypeStruct((rows, cols), own.dtype)] * pairs,
        cost_estimate=BRIEF,
        name="add_up",
    )(me[None].astype(jnp.int32), own, x_came, y_came)


def map_exchange(maps, groups):
    size = lax.axis_size("strip")
    among = [[m * groups + g for m in range(4)] for g in range(groups)]
    return lax.all_to_all(maps, "strip", 0, 0, axis_index_groups=among, tiled=True)


def group_exchange(x, groups):
    return [x] + [permute_xor(x, "strip", k) for k in range(1, groups)]


def silu_of(values):
    return values / (1.0 + jnp.exp(-values))


def embed_times(stamps, features):
    half_count = features // 2
    frequency = jnp.exp(-math.log(10000.0) * jnp.arange(half_count, dtype=jnp.float32) / half_count)
    angles = stamps[:, None] * frequency[None, :]
    return jnp.concatenate([jnp.cos(angles), jnp.sin(angles)], axis=1)

def normalize(values):
    centre = values - jnp.mean(values, axis=-1, keepdims=True)
    inverse = lax.rsqrt(jnp.mean(centre * centre, axis=-1, keepdims=True) + 1e-06)
    return (centre * inverse, inverse)


def norm_back(normed, inverse, upstream):
    return inverse * (
        upstream
        - jnp.mean(upstream, axis=-1, keepdims=True)
        - normed * jnp.mean(upstream * normed, axis=-1, keepdims=True)
    )


def dot_nn(a, b):
    return lax.dot_general(a, b, (((1,), (0,)), ((), ())), preferred_element_type=jnp.float32)


def dot_nt(a, b):
    return lax.dot_general(a, b, (((1,), (1,)), ((), ())), preferred_element_type=jnp.float32)


def dot_tn(a, b):
    return lax.dot_general(a, b, (((0,), (0,)), ((), ())), preferred_element_type=jnp.float32)


def key_mask(s_ref, groups, tokens, cols):
    block = tokens // groups // 4
    token = lax.broadcasted_iota(jnp.int32, (tokens, 128), 0)
    piece, within = (token // block, token % block)
    strip = (piece % 4) * groups + (s_ref[3] ^ (piece // 4))
    row = strip * (block // (cols // 2)) + within // (cols // 2)
    half = s_ref[0] // 2
    return jnp.where((row < half) & (within % (cols // 2) < half), 0.0, -1e30)


def store_sum(ref, part):
    @pl.when(pl.program_id(0) == 0)
    def _():
        ref[...] = part

    @pl.when(pl.program_id(0) > 0)
    def _():
        ref[...] += part


def attend_kernel(chunk, scale, groups, cols, s_ref, *refs):
    pieces, w_ref, t_ref = (refs[:groups], refs[groups], refs[groups + 1])
    o_refs = refs[groups + 2 : 2 * groups + 2]
    l_ref, u_sc, b_sc, q_sc, k_sc, v_sc, o_sc, l_sc = refs[2 * groups + 2 :]
    tokens = u_sc.shape[0]

    @pl.when(pl.program_id(0) == 0)
    def _():
        size = pieces[0].shape[0]
        for i, piece in enumerate(pieces):
            u_sc[i * size : (i + 1) * size, :] = piece[...]
        b_sc[...] = key_mask(s_ref, groups, tokens, cols)

    u = u_sc[...]
    for part in range(3):
        t_ref[part] = dot_nn(u, w_ref[part]).astype(jnp.bfloat16)
    q, k, v = (t_ref[0].astype(jnp.float32), t_ref[1].astype(jnp.float32), t_ref[2].astype(jnp.float32))
    lane = lax.broadcasted_iota(jnp.int32, (tokens, 128), 1)
    bias = b_sc[...]
    for head in range(2):
        here = (lane < 64) if head == 0 else (lane >= 64)
        spare = lane == (64 if head == 0 else 0)
        q_sc[head] = jnp.where(here, q * scale, jnp.where(spare, 1.0, 0.0)).astype(jnp.bfloat16)
        k_sc[head] = jnp.where(here, k, jnp.where(spare, bias, 0.0)).astype(jnp.bfloat16)
        v_sc[head] = jnp.where(here, v, 0.0).astype(jnp.bfloat16)

    def body(i, carry):
        at = pl.ds(pl.multiple_of(i * chunk, chunk), chunk)
        outs, logs = ([], [])
        for head in range(2):
            s = dot_nt(q_sc[head, at, :], k_sc[head])
            top = jnp.max(s, axis=1, keepdims=True)
            p = jnp.exp(s - top)
            total = jnp.sum(p, axis=1, keepdims=True)
            outs.append(dot_nn(p.astype(jnp.bfloat16), v_sc[head]) * (1.0 / total))
            logs.append(top + jnp.log(total))
        o_sc[at, :] = (outs[0] + outs[1]).astype(jnp.bfloat16)
        l_sc[at, :] = jnp.where(
            lax.broadcasted_iota(jnp.int32, (chunk, 128), 1) < 64, logs[0], logs[1]
        )
        return carry

    lax.fori_loop(0, tokens // chunk, body, 0, unroll=True)
    size = tokens // groups
    for i, o_ref in enumerate(o_refs):
        o_ref[...] = o_sc[i * size : (i + 1) * size, :]
    logs = l_sc[...].T
    l_ref[...] = jnp.concatenate(
        [logs[0:1], logs[64:65], jnp.zeros((6, tokens), jnp.float32)], axis=0
    )[None]


def attend(scalars, pieces, w, score_scale, cols):
    groups = len(pieces)
    features, width = w.shape[1:]
    tokens = groups * pieces[0].shape[0]
    chunk = min(512, tokens)
    piece_spec = pl.BlockSpec(pieces[0].shape, lambda j, s: (0, 0))
    return pl.pallas_call(
        functools.partial(attend_kernel, chunk, score_scale, groups, cols),
        grid_spec=pltpu.PrefetchScalarGridSpec(
            num_scalar_prefetch=1,
            grid=(width // 128,),
            in_specs=[piece_spec] * len(pieces)
            + [pl.BlockSpec((3, features, 128), lambda j, s: (0, 0, j))],
            out_specs=[pl.BlockSpec((3, tokens, 128), lambda j, s: (0, 0, j))]
            + [pl.BlockSpec((tokens // groups, 128), lambda j, s: (0, j))] * groups
            + [pl.BlockSpec((1, 8, tokens), lambda j, s: (j, 0, 0))],
            scratch_shapes=[
                pltpu.VMEM((tokens, features), jnp.bfloat16),
                pltpu.VMEM((tokens, 128), jnp.float32),
            ]
            + [pltpu.VMEM((2, tokens, 128), jnp.bfloat16)] * 3
            + [pltpu.VMEM((tokens, 128), jnp.bfloat16), pltpu.VMEM((tokens, 128), jnp.float32)],
        ),
        out_shape=[jax.ShapeDtypeStruct((3, tokens, width), jnp.bfloat16)]
        + [jax.ShapeDtypeStruct((tokens // groups, width), jnp.bfloat16)] * groups
        + [jax.ShapeDtypeStruct((width // 128, 8, tokens), jnp.float32)],
        cost_estimate=BRIEF,
        name="attend_forward",
    )(scalars, *pieces, w)


def attend_back_kernel(chunk, scale, groups, cols, first, s_ref, *refs):
    pieces, do_pieces, o_refs = (refs[:groups], refs[groups : 2 * groups], refs[2 * groups : 3 * groups])
    w_ref, t_ref, l_ref = refs[3 * groups : 3 * groups + 3]
    rest = refs[3 * groups + 3 :]
    if not first:
        prev_ref, rest = (rest[0], rest[1:])
    du_refs, g_ref = (rest[:groups], rest[groups])
    u_sc, b_sc, o_sc, din_sc, q_sc, k_sc, do_sc, dq_sc, dt_sc, d_sc = rest[groups + 1 :]
    tokens = u_sc.shape[0]
    size = pieces[0].shape[0]

    @pl.when(pl.program_id(0) == 0)
    def _():
        for i, piece in enumerate(pieces):
            u_sc[i * size : (i + 1) * size, :] = piece[...]
        b_sc[...] = key_mask(s_ref, groups, tokens, cols)

    for i, piece in enumerate(do_pieces):
        din_sc[i * size : (i + 1) * size, :] = piece[...]
    for i, piece in enumerate(o_refs):
        o_sc[i * size : (i + 1) * size, :] = piece[...]
    q, k, do = (t_ref[0].astype(jnp.float32), t_ref[1].astype(jnp.float32), din_sc[...])
    lane = lax.broadcasted_iota(jnp.int32, (tokens, 128), 1)
    bias = b_sc[...]
    do = do.astype(jnp.float32)
    inner = (do * o_sc[...].astype(jnp.float32)).T
    for head in range(2):
        here = (lane < 64) if head == 0 else (lane >= 64)
        spare = lane == (64 if head == 0 else 0)
        q_sc[head] = jnp.where(here, q * scale, jnp.where(spare, 1.0, 0.0)).astype(jnp.bfloat16)
        k_sc[head] = jnp.where(here, k, jnp.where(spare, bias, 0.0)).astype(jnp.bfloat16)
        do_sc[head] = jnp.where(here, do, 0.0).astype(jnp.bfloat16)
        d_sc[head : head + 1, :] = jnp.sum(
            inner[64 * head : 64 * head + 64], axis=0, keepdims=True
        )
    dq_sc[...] = jnp.zeros_like(dq_sc)

    def body(i, carry):
        at = pl.ds(pl.multiple_of(i * chunk, chunk), chunk)
        lanes = lax.broadcasted_iota(jnp.int32, (chunk, 128), 1)
        d_k, d_v, d_q = ([], [], [])
        for head in range(2):
            here = (lanes < 64) if head == 0 else (lanes >= 64)
            s = dot_nt(k_sc[head, at, :], q_sc[head])
            p = jnp.exp(s - l_ref[0, head : head + 1, :])
            d_p = dot_nt(t_ref[2, at, :], do_sc[head])
            d_s = (p * (d_p - d_sc[head : head + 1, :])).astype(jnp.bfloat16)
            d_v.append(dot_nn(p.astype(jnp.bfloat16), do_sc[head]))
            d_k.append(dot_nn(d_s, q_sc[head]))
            keys = jnp.where(here, t_ref[1, at, :].astype(jnp.float32), 0.0).astype(jnp.bfloat16)
            d_q.append(dot_tn(d_s, keys))
        dq_sc[...] += d_q[0] + d_q[1]
        dt_sc[at, 128:256] = jnp.where(lanes < 64, d_k[0], d_k[1]).astype(jnp.bfloat16)
        dt_sc[at, 256:384] = (d_v[0] + d_v[1]).astype(jnp.bfloat16)
        return carry

    lax.fori_loop(0, tokens // chunk, body, 0, unroll=True)
    dt_sc[:, 0:128] = (dq_sc[...] * scale).astype(jnp.bfloat16)
    for i, du_ref in enumerate(du_refs):
        at = slice(i * size, (i + 1) * size)
        part = dot_nt(dt_sc[at, 0:128], w_ref[0])
        part = part + dot_nt(dt_sc[at, 128:256], w_ref[1])
        part = part + dot_nt(dt_sc[at, 256:384], w_ref[2])
        store_sum(du_ref, part)
    grad = dot_tn(u_sc[...], dt_sc[...])
    for at in range(3):
        piece = grad[:, 128 * at : 128 * at + 128]
        if not first:
            piece = piece + prev_ref[at]
        g_ref[at] = piece.astype(g_ref.dtype)


def attend_back(scalars, pieces, d_pieces, outs, w, t, logs, score_scale, cols, prev, grad_type):
    groups = len(outs)
    features, width = w.shape[1:]
    tokens = t.shape[1]
    chunk = min(256, tokens)
    size = pieces[0].shape[0]
    blocks = width // 128
    weight_spec = pl.BlockSpec((3, features, 128), lambda j, s: (0, 0, j))
    offset = 0 if d_pieces[0].shape[1] == width else blocks
    args = list(pieces) + list(d_pieces) + list(outs) + [w, t, logs]
    args += [] if prev is None else [prev]
    return pl.pallas_call(
        functools.partial(attend_back_kernel, chunk, score_scale, groups, cols, prev is None),
        grid_spec=pltpu.PrefetchScalarGridSpec(
            num_scalar_prefetch=1,
            grid=(blocks,),
            in_specs=[pl.BlockSpec((size, features), lambda j, s: (0, 0))] * len(pieces)
            + [pl.BlockSpec((size, 128), lambda j, s: (0, s[3] * offset + j))] * len(d_pieces)
            + [pl.BlockSpec((size, 128), lambda j, s: (0, j))] * groups
            + [
                weight_spec,
                pl.BlockSpec((3, tokens, 128), lambda j, s: (0, 0, j)),
                pl.BlockSpec((1, 8, tokens), lambda j, s: (j, 0, 0)),
            ]
            + ([] if prev is None else [weight_spec]),
            out_specs=[pl.BlockSpec((size, features), lambda j, s: (0, 0))] * groups
            + [weight_spec],
            scratch_shapes=[
                pltpu.VMEM((tokens, features), jnp.bfloat16),
                pltpu.VMEM((tokens, 128), jnp.float32),
                pltpu.VMEM((tokens, 128), jnp.bfloat16),
                pltpu.VMEM((tokens, 128), jnp.bfloat16),
            ]
            + [pltpu.VMEM((2, tokens, 128), jnp.bfloat16)] * 3
            + [
                pltpu.VMEM((tokens, 128), jnp.float32),
                pltpu.VMEM((tokens, 384), jnp.bfloat16),
                pltpu.VMEM((8, tokens), jnp.float32),
            ],
        ),
        out_shape=[jax.ShapeDtypeStruct((size, features), jnp.float32)] * groups
        + [jax.ShapeDtypeStruct(w.shape, grad_type)],
        cost_estimate=COVER,
        name="attend_backward",
    )(scalars, *args)


def shift_cols(x, by, col):
    size = x.shape[0]
    rolled = pltpu.roll(x, (-by) % size, 0)
    return jnp.where(col == (size - 1 if by > 0 else 0), 0.0, rolled)


def wide_taps(c_ref, lanes, cols):
    return [
        jnp.broadcast_to(c_ref[k : k + 1, lanes].astype(jnp.float32), (cols, 128)) for k in range(9)
    ]


def sublane_sum(x):
    return jnp.sum(x.reshape(x.shape[0] // 8, 8, 128), axis=0)


def modulate(x, m_ref, shift_at, col, row, side):
    normed, _ = normalize(x.astype(jnp.float32))
    value = normed * (1.0 + m_ref[shift_at + 1 : shift_at + 2, :]) + m_ref[shift_at : shift_at + 1, :]
    live = (col < side) & (row >= 0) & (row < side)
    return jnp.where(live, value, 0.0).astype(jnp.bfloat16)


def modulated_rows(a_sc, s_ref, x_ref, top_ref, end_ref, m_ref):
    rows, cols, features = x_ref.shape
    side, row_zero = (s_ref[0], s_ref[1])
    col = lax.broadcasted_iota(jnp.int32, (cols, features), 0)
    a_sc[0] = modulate(top_ref[...], m_ref, 0, col, row_zero - 1, side)
    a_sc[rows + 1] = modulate(end_ref[...], m_ref, 0, col, row_zero + rows, side)

    def body(r, carry):
        a_sc[r + 1] = modulate(x_ref[r], m_ref, 0, col, row_zero + r, side)
        return carry

    lax.fori_loop(0, rows, body, 0)


def to_maps(canvas, maps_ref):
    blocks, rows, cols, _ = canvas.shape
    half = cols // 2

    def body(r, carry):
        at = pl.ds(pl.multiple_of(r * half, half), half)
        for m in range(4):
            for b in range(blocks):
                part = canvas[b, 2 * r + m // 2, pl.ds(m % 2, half, stride=2), :]
                maps_ref[m, at, 128 * b : 128 * b + 128] = part.astype(jnp.bfloat16)
        return carry

    lax.fori_loop(0, rows // 2, body, 0)


def from_maps(maps_ref, canvas, row_offset):
    half = canvas.shape[2] // 2
    rows = maps_ref.shape[1] // half * 2

    def body(r, carry):
        at = pl.ds(pl.multiple_of(r * half, half), half)
        for m in range(4):
            for b in range(canvas.shape[0]):
                part = maps_ref[m, at, 128 * b : 128 * b + 128].astype(jnp.float32)
                canvas[b, row_offset + 2 * r + m // 2, pl.ds(m % 2, half, stride=2), :] = part
        return carry

    lax.fori_loop(0, rows // 2, body, 0)


def before_kernel(s_ref, x_ref, top_ref, end_ref, m_ref, c_ref, *refs):
    maps_ref, a_sc, t_sc = refs
    rows, cols, features = x_ref.shape
    modulated_rows(a_sc, s_ref, x_ref, top_ref, end_ref, m_ref)
    col = lax.broadcasted_iota(jnp.int32, (cols, 128), 0)
    for first in range(0, features, 128):
        lanes = slice(first, first + 128)
        taps = wide_taps(c_ref, lanes, cols)

        def body(r, carry):
            x = [a_sc[r + i, :, lanes].astype(jnp.float32) for i in range(3)]
            a = [x[0] * taps[j] + x[1] * taps[3 + j] + x[2] * taps[6 + j] for j in range(3)]
            t_sc[first // 128, r] = a[1] + shift_cols(a[0], -1, col) + shift_cols(a[2], 1, col)
            return carry

        lax.fori_loop(0, rows, body, 0)
    to_maps(t_sc, maps_ref)


def canvas_specs(latents, at):
    rows, cols, features = latents.shape[2:]
    return [
        pl.BlockSpec((None, None, rows, cols, features), lambda j, s: (at, 0, 0, 0, 0)),
        pl.BlockSpec((None, cols, features), lambda j, s: (at, 0, 0)),
        pl.BlockSpec((None, cols, features), lambda j, s: (at, 0, 0)),
        pl.BlockSpec((None, 6, features), lambda j, s: (at, 0, 0)),
    ]


def whole_spec(shape):
    return pl.BlockSpec(shape, lambda j, s: (0,) * len(shape))


def before_attention(at, scalars, latents, top, end, mods, taps):
    rows, cols, features = latents.shape[2:]
    maps = (4, rows * cols // 4, features)
    return pl.pallas_call(
        before_kernel,
        grid_spec=pltpu.PrefetchScalarGridSpec(
            num_scalar_prefetch=1,
            grid=(1,),
            in_specs=canvas_specs(latents, at) + [whole_spec(taps.shape)],
            out_specs=whole_spec(maps),
            scratch_shapes=[
                pltpu.VMEM((rows + 2, cols, features), jnp.bfloat16),
                pltpu.VMEM((features // 128, rows, cols, 128), jnp.float32),
            ],
        ),
        out_shape=jax.ShapeDtypeStruct(maps, jnp.bfloat16),
        cost_estimate=COVER,
        name="before_attention",
    )(scalars, latents, top, end, mods, taps)


def join_kernel(s_ref, mine_ref, other_ref, out_ref):
    width = mine_ref.shape[1]

    def write(low_ref, high_ref):
        out_ref[:, :width] = low_ref[...]
        out_ref[:, width:] = high_ref[...]

    @pl.when(s_ref[3] == 0)
    def _():
        write(mine_ref, other_ref)

    @pl.when(s_ref[3] == 1)
    def _():
        write(other_ref, mine_ref)


def join_groups(scalars, parts, width):
    groups = len(parts)
    tokens = parts[0].shape[0]
    shape = (tokens, groups * width)
    if groups != 2 or parts[0].shape[1] != width:
        whole = place_blocks([part[:, :width] for part in parts], scalars[3])
        whole = whole.transpose(1, 0, 2)
    else:
        whole = pl.pallas_call(
            join_kernel,
            grid_spec=pltpu.PrefetchScalarGridSpec(
                num_scalar_prefetch=1,
                grid=(1,),
                in_specs=[whole_spec(part.shape) for part in parts],
                out_specs=whole_spec(shape),
            ),
            out_shape=jax.ShapeDtypeStruct(shape, parts[0].dtype),
            cost_estimate=COVER,
            name="join_groups",
        )(scalars, *parts)
    return whole.reshape(4, tokens // 4, groups * width)


def sum_kernel(count, *refs):
    total = refs[0][...]
    for part in refs[1:count]:
        total = total + part[...]
    refs[count][...] = total.astype(refs[count].dtype)


def sum_groups(parts):
    tokens, features = parts[0].shape
    total = pl.pallas_call(
        functools.partial(sum_kernel, len(parts)),
        out_shape=jax.ShapeDtypeStruct((tokens, features), jnp.bfloat16),
        cost_estimate=COVER,
        name="sum_groups",
    )(*parts)
    return total.reshape(4, tokens // 4, features)


def edge_kernel(top_ref, end_ref, first_ref, last_ref):
    half = top_ref.shape[1]
    for j in range(2):
        first_ref[j * half : (j + 1) * half, :] = top_ref[j]
        last_ref[j * half : (j + 1) * half, :] = end_ref[j]


def edge_rows(maps, cols):
    size, features = maps.shape[1:]
    half = cols // 2
    row = (cols, features)
    return pl.pallas_call(
        edge_kernel,
        grid=(1,),
        in_specs=[
            pl.BlockSpec((2, half, features), lambda j: (0, 0, 0)),
            pl.BlockSpec((2, half, features), lambda j: (1, size // half - 1, 0)),
        ],
        out_specs=[pl.BlockSpec(row, lambda j: (0, 0))] * 2,
        out_shape=[jax.ShapeDtypeStruct(row, maps.dtype)] * 2,
        cost_estimate=COVER,
        name="edge_rows",
    )(maps, maps)


def expand_kernel(s_ref, o_ref, x_ref, m_ref, wp_ref, w_ref, b_ref, *refs):
    oc_ref, at_ref, x1_ref, a2_ref, f_ref, first_ref, last_ref, t_sc = refs
    rows, cols, features = x_ref.shape
    side, row_zero = (s_ref[0], s_ref[1])

    @pl.when(pl.program_id(0) == 0)
    def _():
        from_maps(o_ref, t_sc, 0)
        for b in range(features // 128):
            part = t_sc[b].reshape(rows * cols, 128)
            oc_ref[:, 128 * b : 128 * b + 128] = part.astype(jnp.bfloat16)
        at_ref[...] = dot_nn(oc_ref[...], wp_ref[...])

        def body(r, carry):
            here = pl.ds(pl.multiple_of(r * cols, cols), cols)
            x1 = x_ref[r].astype(jnp.float32) + m_ref[2:3, :] * at_ref[here, :]
            x1_ref[here, :] = x1
            normed, _ = normalize(x1)
            a2 = normed * (1.0 + m_ref[4:5, :]) + m_ref[3:4, :]
            a2_ref[here, :] = a2.astype(jnp.bfloat16)
            return carry

        lax.fori_loop(0, rows, body, 0)

    block = f_ref.shape[2]
    f = (dot_nn(a2_ref[...], w_ref[...]) + b_ref[...].astype(jnp.float32)).reshape(rows, cols, block)
    col = lax.broadcasted_iota(jnp.int32, (cols, block), 0)
    for r in range(rows):
        live = (col < side) & (row_zero + r < side)
        f_ref[r] = jnp.where(live, f[r], 0.0).astype(jnp.bfloat16)
    first_ref[...] = f_ref[0:1]
    last_ref[...] = f_ref[rows - 1 : rows]


def expand(at, scalars, maps, latents, mods, w_proj, w_fc1, bias):
    rows, cols, features = latents.shape[2:]
    hidden = w_fc1.shape[1]
    tokens, block = (rows * cols, 768)
    flat = (tokens, features)
    specs = canvas_specs(latents, at)
    return pl.pallas_call(
        expand_kernel,
        grid_spec=pltpu.PrefetchScalarGridSpec(
            num_scalar_prefetch=1,
            grid=(hidden // block,),
            in_specs=[
                whole_spec(maps.shape),
                specs[0],
                specs[3],
                whole_spec(w_proj.shape),
                pl.BlockSpec((features, block), lambda j, s: (0, j)),
                pl.BlockSpec((1, block), lambda j, s: (0, j)),
            ],
            out_specs=[whole_spec(flat)] * 4
            + [pl.BlockSpec((rows, cols, block), lambda j, s: (0, 0, j))]
            + [pl.BlockSpec((1, cols, block), lambda j, s: (0, 0, j))] * 2,
            scratch_shapes=[pltpu.VMEM((features // 128, rows, cols, 128), jnp.float32)],
        ),
        out_shape=[
            jax.ShapeDtypeStruct(flat, jnp.bfloat16),
            jax.ShapeDtypeStruct(flat, jnp.float32),
            jax.ShapeDtypeStruct(flat, jnp.float32),
            jax.ShapeDtypeStruct(flat, jnp.bfloat16),
            jax.ShapeDtypeStruct((rows, cols, hidden), jnp.bfloat16),
        ]
        + [jax.ShapeDtypeStruct((1, cols, hidden), jnp.bfloat16)] * 2,
        cost_estimate=COVER,
        name="expand",
    )(scalars, maps, latents, mods, w_proj, w_fc1, bias)


def middle_kernel(first, s_ref, f_ref, top_ref, end_ref, c_ref, w_ref, ct_ref, x1_ref, m_ref, *rest):
    if first:
        mixed_ref, dg_ref, dz_ref, g_ref, gc_ref, first_ref, last_ref = rest[:7]
    else:
        gp_ref, gcp_ref = rest[:2]
        mixed_ref, dg_ref, dz_ref, g_ref, gc_ref, first_ref, last_ref = rest[3:10]
    gz_sc = rest[-1:]
    out_sc, d_sc, x_sc, t_sc, acc_sc = rest[-6:-1]
    rows, cols, block = f_ref.shape
    features = out_sc.shape[1]
    side, row_zero = (s_ref[0], s_ref[1])

    def upstream(r):
        col = lax.broadcasted_iota(jnp.int32, (cols, features), 0)
        live = (col < side) & (row_zero + r < side)
        return jnp.where(live, ct_ref[r].astype(jnp.float32), 0.0), live

    @pl.when(pl.program_id(0) == 0)
    def _():
        def body(r, carry):
            here = pl.ds(pl.multiple_of(r * cols, cols), cols)
            d_sc[here, :] = (upstream(r)[0] * m_ref[5:6, :]).astype(jnp.bfloat16)
            return carry

        lax.fori_loop(0, rows, body, 0)

    d = d_sc[...]
    x_sc[0:1] = top_ref[...]
    x_sc[1 : rows + 1] = f_ref[...]
    x_sc[rows + 1 : rows + 2] = end_ref[...]
    acc_sc[...] = jnp.zeros_like(acc_sc)
    col = lax.broadcasted_iota(jnp.int32, (cols, 128), 0)
    wide = 256
    count = block // wide
    part, grads = (None, [])

    def start(s):
        t = dot_nt(d, w_ref[s * wide : (s + 1) * wide, :])
        for l in range(wide // 128):
            t_sc[s * (wide // 128) + l] = t[:, 128 * l : 128 * l + 128].reshape(rows, cols, 128)

    start(0)
    for s in range(count):
        if s + 1 < count:
            start(s + 1)
        for l in range(wide // 128):
            at = s * (wide // 128) + l
            lanes = slice(128 * at, 128 * at + 128)
            inner = slice(128 * l, 128 * l + 128)
            taps = wide_taps(c_ref, lanes, cols)

            def body(r, carry):
                x = [x_sc[r + i, :, lanes].astype(jnp.float32) for i in range(3)]
                a = [x[0] * taps[j] + x[1] * taps[3 + j] + x[2] * taps[6 + j] for j in range(3)]
                z = a[1] + shift_cols(a[0], -1, col) + shift_cols(a[2], 1, col)
                half = 0.5 * (1.0 + lax.erf(z * root_half))
                gz_sc[s][r * cols : (r + 1) * cols, inner] = (z * half).astype(jnp.bfloat16)
                slope = half + z * jnp.exp(-0.5 * z * z) * inverse_root_tau
                d_z = (t_sc[at, r] * slope).astype(jnp.bfloat16)
                dz_ref[r, :, lanes] = d_z
                d_z = d_z.astype(jnp.float32)
                moved = [shift_cols(d_z, 1, col), d_z, shift_cols(d_z, -1, col)]
                return [
                    c + sublane_sum(x[k // 3] * moved[k % 3]) for k, c in enumerate(carry)
                ]

            sums = [jnp.zeros((8, 128), jnp.float32)] * 9
            for r in range(rows):
                sums = body(r, sums)
            for k in range(9):
                acc_sc[k, :, lanes] = sums[k]
        gz = gz_sc[s][...]
        here = dot_nn(gz, w_ref[s * wide : (s + 1) * wide, :])
        part = here if part is None else part + here
        grads.append(dot_tn(gz, d))
    first_ref[...] = dz_ref[0:1]
    last_ref[...] = dz_ref[rows - 1 : rows]
    store_sum(out_sc, part)
    grad = jnp.concatenate(grads, axis=0)
    taps_grad = jnp.concatenate(
        [jnp.sum(acc_sc[k], axis=0, keepdims=True) for k in range(9)], axis=0
    )
    if not first:
        grad = grad + gp_ref[...]
        taps_grad = taps_grad + gcp_ref[...]
    g_ref[...] = grad.astype(g_ref.dtype)
    gc_ref[...] = taps_grad

    @pl.when(pl.program_id(0) == pl.num_programs(0) - 1)
    def _():
        def body(r, total):
            here = pl.ds(pl.multiple_of(r * cols, cols), cols)
            value, live = upstream(r)
            out = out_sc[here, :]
            mixed = x1_ref[here, :] + m_ref[5:6, :] * out
            mixed_ref[r] = jnp.where(live, mixed, 0.0).astype(jnp.bfloat16)
            return total + sublane_sum(value * out)

        total = lax.fori_loop(0, rows, body, jnp.zeros((8, features), jnp.float32))
        dg_ref[...] = jnp.sum(total, axis=0, keepdims=True)


def sublane_sum(x):
    return jnp.sum(x.reshape(x.shape[0] // 8, 8, x.shape[1]), axis=0)


def ffn_middle(at, scalars, f, halo, taps, w, cotangent, x1, mods, prev, grad_type):
    rows, cols, hidden = f.shape
    features = w.shape[1]
    block = 256
    wide = lambda j, s: (0, 0, j)
    row_spec = pl.BlockSpec((1, cols, block), wide)
    weight_spec = pl.BlockSpec((block, features), lambda j, s: (j, 0))
    tap_spec = pl.BlockSpec((9, block), lambda j, s: (0, j))
    canvas_spec = pl.BlockSpec((rows, cols, block), wide)
    specs = canvas_specs(cotangent, at)
    args = [scalars, f, halo[0], halo[1], taps, w, cotangent, x1, mods]
    args += [] if prev is None else list(prev)
    return pl.pallas_call(
        functools.partial(middle_kernel, prev is None),
        grid_spec=pltpu.PrefetchScalarGridSpec(
            num_scalar_prefetch=1,
            grid=(hidden // block,),
            in_specs=[canvas_spec, row_spec, row_spec, tap_spec, weight_spec]
            + [specs[0], whole_spec(x1.shape), specs[3]]
            + ([] if prev is None else [weight_spec, tap_spec, pl.BlockSpec(memory_space=pl.ANY)]),
            out_specs=[specs[0], whole_spec((1, features)), canvas_spec, weight_spec, tap_spec]
            + [row_spec] * 2,
            scratch_shapes=[
                pltpu.VMEM((rows * cols, features), jnp.float32),
                pltpu.VMEM((rows * cols, features), jnp.bfloat16),
                pltpu.VMEM((rows + 2, cols, block), jnp.bfloat16),
                pltpu.VMEM((block // 128, rows, cols, 128), jnp.float32),
                pltpu.VMEM((9, 8, block), jnp.float32),
            ]
            + [pltpu.VMEM((rows * cols, 256), jnp.bfloat16)] * 1,
        ),
        out_shape=[
            jax.ShapeDtypeStruct(cotangent.shape, jnp.bfloat16),
            jax.ShapeDtypeStruct((1, features), jnp.float32),
            jax.ShapeDtypeStruct(f.shape, jnp.bfloat16),
            jax.ShapeDtypeStruct((hidden, features), grad_type),
            jax.ShapeDtypeStruct((9, hidden), jnp.float32),
        ]
        + [jax.ShapeDtypeStruct((1, cols, hidden), jnp.bfloat16)] * 2,
        input_output_aliases={} if prev is None else {11: 0},
        cost_estimate=COVER,
        name="ffn_middle",
    )(*args)


def ffn_back_kernel(micro, first, s_ref, z_ref, top_ref, end_ref, c_ref, w_ref, a_ref, *rest):
    far, m_ref = (rest[:5], rest[5])
    near, sem = (rest[-6:-1], rest[-1])
    rest = rest[6:-6]
    ct_ref, x1_ref, at_ref, oc_ref, wp_ref = near
    copies = [
        pltpu.make_async_copy(source.at[micro, 0] if i == 0 else source, target, sem.at[i])
        for i, (source, target) in enumerate(zip(far, near))
    ]

    @pl.when(pl.program_id(0) == 0)
    def _():
        for copy in copies:
            copy.start()

    if not first:
        gp_ref, gbp_ref, gpp_ref = rest[:3]
        rest = rest[3:]
    maps_ref, dx_ref, dm_ref, g_ref, gb_ref, gp_out = rest[:6]
    da_sc, x_sc, df_sc, acc_sc, t_sc, dat_sc = rest[6:]
    rows, cols, block = z_ref.shape
    features = da_sc.shape[1]
    x_sc[0:1] = top_ref[...]
    x_sc[1 : rows + 1] = z_ref[...]
    x_sc[rows + 1 : rows + 2] = end_ref[...]
    acc_sc[...] = jnp.zeros_like(acc_sc)
    col = lax.broadcasted_iota(jnp.int32, (cols, 128), 0)
    side, row_zero = (s_ref[0], s_ref[1])
    for at in range(block // 128):
        lanes = slice(128 * at, 128 * at + 128)
        taps = wide_taps(c_ref, lanes, cols)
        total = jnp.zeros((8, 128), jnp.float32)
        for r in range(rows):
            x = [x_sc[r + i, :, lanes].astype(jnp.float32) for i in range(3)]
            b = [x[2] * taps[j] + x[1] * taps[3 + j] + x[0] * taps[6 + j] for j in range(3)]
            d_f = b[1] + shift_cols(b[0], 1, col) + shift_cols(b[2], -1, col)
            live = (col < side) & (row_zero + r < side)
            d_f = jnp.where(live, d_f, 0.0).astype(jnp.bfloat16)
            df_sc[r, :, lanes] = d_f
            total = total + sublane_sum(d_f.astype(jnp.float32))
        acc_sc[:, lanes] = total
    d_f = df_sc[...].reshape(rows * cols, block)
    store_sum(da_sc, dot_nt(d_f, w_ref[...]))
    grad = dot_tn(a_ref[...], d_f)
    bias_grad = jnp.sum(acc_sc[...], axis=0, keepdims=True)
    if not first:
        grad = grad + gp_ref[...]
        bias_grad = bias_grad + gbp_ref[...]
    g_ref[...] = grad.astype(g_ref.dtype)
    gb_ref[...] = bias_grad

    @pl.when(pl.program_id(0) == pl.num_programs(0) - 1)
    def _():
        for copy in copies:
            copy.wait()
        wide_col = lax.broadcasted_iota(jnp.int32, (cols, features), 0)

        def body(r, totals):
            here = pl.ds(pl.multiple_of(r * cols, cols), cols)
            d_a = da_sc[here, :]
            normed, inverse = normalize(x1_ref[here, :])
            live = (wide_col < side) & (row_zero + r < side)
            d_x = jnp.where(live, ct_ref[r].astype(jnp.float32), 0.0)
            d_x = d_x + norm_back(normed, inverse, d_a * (1.0 + m_ref[4:5, :]))
            dx_ref[here, :] = d_x
            dat_sc[here, :] = (d_x * m_ref[2:3, :]).astype(jnp.bfloat16)
            return (
                totals[0] + sublane_sum(d_x * at_ref[here, :]),
                totals[1] + sublane_sum(d_a),
                totals[2] + sublane_sum(d_a * normed),
            )

        zero = jnp.zeros((8, features), jnp.float32)
        totals = lax.fori_loop(0, rows, body, (zero, zero, zero))
        for i in range(3):
            dm_ref[i : i + 1, :] = jnp.sum(totals[i], axis=0, keepdims=True)
        proj = dot_tn(oc_ref[...], dat_sc[...])
        if not first:
            proj = proj + gpp_ref[...]
        gp_out[...] = proj.astype(gp_out.dtype)
        d_o = dot_nt(dat_sc[...], wp_ref[...])
        for b in range(features // 128):
            t_sc[b] = d_o[:, 128 * b : 128 * b + 128].reshape(rows, cols, 128)
        to_maps(t_sc, maps_ref)


def ffn_back(
    at, scalars, d_z, halo, taps, w, a, cotangent, x1, attn, oc, w_proj, mods, prev, grad_type
):
    rows, cols, hidden = d_z.shape
    features = a.shape[1]
    block = 512
    wide = lambda j, s: (0, 0, j)
    row_spec = pl.BlockSpec((1, cols, block), wide)
    weight_spec = pl.BlockSpec((features, block), lambda j, s: (0, j))
    bias_spec = pl.BlockSpec((1, block), lambda j, s: (0, j))
    flat_spec = whole_spec((rows * cols, features))
    proj_spec = whole_spec(w_proj.shape)
    maps = (4, rows * cols // 4, features)
    specs = canvas_specs(cotangent, at)
    args = [scalars, d_z, halo[0], halo[1], taps, w, a, cotangent, x1, attn, oc, w_proj, mods]
    args += [] if prev is None else list(prev)
    return pl.pallas_call(
        functools.partial(ffn_back_kernel, at, prev is None),
        grid_spec=pltpu.PrefetchScalarGridSpec(
            num_scalar_prefetch=1,
            grid=(hidden // block,),
            in_specs=[
                pl.BlockSpec((rows, cols, block), wide),
                row_spec,
                row_spec,
                pl.BlockSpec((9, block), lambda j, s: (0, j)),
                weight_spec,
                flat_spec,
            ]
            + [HBM] * 5
            + [
                specs[3],
            ]
            + ([] if prev is None else [weight_spec, bias_spec, proj_spec]),
            out_specs=[whole_spec(maps)]
            + [flat_spec, whole_spec((3, features)), weight_spec, bias_spec, proj_spec],
            scratch_shapes=[
                pltpu.VMEM((rows * cols, features), jnp.float32),
                pltpu.VMEM((rows + 2, cols, block), jnp.bfloat16),
                pltpu.VMEM((rows, cols, block), jnp.bfloat16),
                pltpu.VMEM((8, block), jnp.float32),
                pltpu.VMEM((features // 128, rows, cols, 128), jnp.float32),
                pltpu.VMEM((rows * cols, features), jnp.bfloat16),
                pltpu.VMEM((rows, cols, features), cotangent.dtype),
                pltpu.VMEM(x1.shape, x1.dtype),
                pltpu.VMEM(attn.shape, attn.dtype),
                pltpu.VMEM(oc.shape, oc.dtype),
                pltpu.VMEM(w_proj.shape, w_proj.dtype),
                pltpu.SemaphoreType.DMA((5,)),
            ],
        ),
        out_shape=[jax.ShapeDtypeStruct(maps, jnp.bfloat16)]
        + [
            jax.ShapeDtypeStruct((rows * cols, features), jnp.float32),
            jax.ShapeDtypeStruct((3, features), jnp.float32),
            jax.ShapeDtypeStruct(w.shape, grad_type),
            jax.ShapeDtypeStruct((1, hidden), jnp.float32),
            jax.ShapeDtypeStruct(w_proj.shape, grad_type),
        ],
        cost_estimate=COVER,
        name="ffn_backward",
    )(*args)


def last_kernel(first, s_ref, du_ref, dtop_ref, dend_ref, *rest):
    x_ref, top_ref, end_ref, m_ref, c_ref, dx_ref = rest[:6]
    rest = rest[6:]
    if not first:
        gcp_ref = rest[0]
        rest = rest[2:]
    dl_ref, dm_ref, gc_ref, a_sc, t_sc, d_sc, acc_sc = rest
    rows, cols, features = x_ref.shape
    half = cols // 2
    side, row_zero = (s_ref[0], s_ref[1])
    modulated_rows(a_sc, s_ref, x_ref, top_ref, end_ref, m_ref)
    from_maps(du_ref, t_sc, 1)
    for at, ref in ((0, dtop_ref), (rows + 1, dend_ref)):
        for j in range(2):
            for start in range(0, features, 128):
                lanes = slice(start, start + 128)
                part = ref[j * half : (j + 1) * half, lanes].astype(jnp.float32)
                t_sc[start // 128, at, pl.ds(j, half, stride=2), :] = part
    acc_sc[...] = jnp.zeros_like(acc_sc)
    col = lax.broadcasted_iota(jnp.int32, (cols, 128), 0)
    for start in range(0, features, 128):
        lanes = slice(start, start + 128)
        taps = wide_taps(c_ref, lanes, cols)

        def conv_body(r, carry):
            d = [t_sc[start // 128, r + i] for i in range(3)]
            b = [d[2] * taps[j] + d[1] * taps[3 + j] + d[0] * taps[6 + j] for j in range(3)]
            d_a = b[1] + shift_cols(b[0], 1, col) + shift_cols(b[2], -1, col)
            live = (col < side) & (row_zero + r < side)
            d_sc[r, :, lanes] = jnp.where(live, d_a, 0.0)
            moved = [shift_cols(d[1], 1, col), d[1], shift_cols(d[1], -1, col)]
            for i in range(3):
                x = a_sc[r + i, :, lanes].astype(jnp.float32)
                for j in range(3):
                    acc_sc[3 * i + j, :, lanes] += sublane_sum(x * moved[j])
            return carry

        lax.fori_loop(0, rows, conv_body, 0, unroll=2)
    taps_grad = jnp.concatenate(
        [jnp.sum(acc_sc[k], axis=0, keepdims=True) for k in range(9)], axis=0
    )
    if not first:
        taps_grad = taps_grad + gcp_ref[...]
    gc_ref[...] = taps_grad

    def body(r, totals):
        here = pl.ds(pl.multiple_of(r * cols, cols), cols)
        normed, inverse = normalize(x_ref[r].astype(jnp.float32))
        d_a = d_sc[r]
        dl_ref[r] = dx_ref[here, :] + norm_back(normed, inverse, d_a * (1.0 + m_ref[1:2, :]))
        return (totals[0] + sublane_sum(d_a), totals[1] + sublane_sum(d_a * normed))

    zero = jnp.zeros((8, features), jnp.float32)
    totals = lax.fori_loop(0, rows, body, (zero, zero))
    for i in range(2):
        dm_ref[i : i + 1, :] = jnp.sum(totals[i], axis=0, keepdims=True)


def last_stage(at, scalars, maps, d_halo, latents, top, end, mods, taps, d_x, prev):
    rows, cols, features = latents.shape[2:]
    specs = canvas_specs(latents, at)
    args = [scalars, maps, *d_halo, latents, top, end, mods, taps, d_x]
    args += [] if prev is None else list(prev)
    return pl.pallas_call(
        functools.partial(last_kernel, prev is None),
        grid_spec=pltpu.PrefetchScalarGridSpec(
            num_scalar_prefetch=1,
            grid=(1,),
            in_specs=[whole_spec(maps.shape)]
            + [whole_spec((cols, features))] * 2
            + specs
            + [whole_spec(taps.shape), whole_spec(d_x.shape)]
            + ([] if prev is None else [whole_spec(taps.shape), pl.BlockSpec(memory_space=pl.ANY)]),
            out_specs=[specs[0], whole_spec((2, features)), whole_spec(taps.shape)],
            scratch_shapes=[
                pltpu.VMEM((rows + 2, cols, features), jnp.bfloat16),
                pltpu.VMEM((features // 128, rows + 2, cols, 128), jnp.float32),
                pltpu.VMEM((rows, cols, features), jnp.float32),
                pltpu.VMEM((9, 8, features), jnp.float32),
            ],
        ),
        out_shape=[
            jax.ShapeDtypeStruct(latents.shape, jnp.float32),
            jax.ShapeDtypeStruct((2, features), jnp.float32),
            jax.ShapeDtypeStruct(taps.shape, jnp.float32),
        ],
        input_output_aliases={} if prev is None else {11: 0},
        cost_estimate=COVER,
        name="last_stage",
    )(*args)


def shards(
    latents,
    timesteps,
    size_tags,
    w_ada,
    b_ada,
    conv_attn,
    w_qkv,
    w_proj,
    w_fc1,
    b_fc1,
    conv_ffn,
    w_fc2,
    cotangent,
):
    micro_count, _, row_count, side_count, features = latents.shape
    dp, strips = (lax.axis_size("dp"), lax.axis_size("strip"))
    dp_at, strip_at = (lax.axis_index("dp"), lax.axis_index("strip"))
    hidden = conv_ffn.shape[1] * dp
    groups = strips // 4
    group_at, map_at = (strip_at % groups, strip_at // groups)
    score_scale = (features // HEADS) ** (-0.5)
    width = features // groups

    stamps = timesteps[:, 0].astype(jnp.float32)
    small = jnp.concatenate([conv_attn.reshape(-1), conv_ffn.reshape(-1), b_fc1])
    small = gather_butterfly(jnp.concatenate([stamps, small.astype(jnp.float32)])[None])
    all_stamps, small = (small[:, :micro_count], small[:, micro_count:].astype(jnp.bfloat16))
    conds = [silu_of(embed_times(all_stamps[k], features)) for k in range(dp)]
    ada_rows = features // dp
    ada_wide = w_ada.astype(jnp.float32)
    partial_mods = jnp.dot(
        lax.dynamic_slice_in_dim(jnp.concatenate(conds), dp_at * ada_rows, ada_rows, 1),
        ada_wide,
        precision=lax.Precision.HIGHEST,
    )
    bias_here = lax.dynamic_update_slice_in_dim(
        jnp.zeros((6 * features,), jnp.float32),
        b_ada.astype(jnp.float32),
        dp_at * b_ada.shape[0],
        0,
    )
    partial_mods = (partial_mods + bias_here[None, :]).reshape(dp, micro_count, 6 * features)
    count = dp
    while count > 1:
        count //= 2
        partial_mods = partial_mods[:count] + permute_xor(partial_mods[count:], "dp", count)
    modulation = partial_mods[0]

    small = place_blocks([small[k] for k in range(dp)], dp_at)
    n_one, n_two = (conv_attn.size, conv_attn.size + conv_ffn.size)
    conv_one = small[:, :n_one].reshape(dp, 9, -1).transpose(1, 0, 2).reshape(9, features)
    conv_two = small[:, n_one:n_two].reshape(dp, 9, -1).transpose(1, 0, 2).reshape(9, hidden)
    fc1_bias = small[:, n_two:].reshape(1, hidden)
    qkv_pieces, modulation = fetch_group(w_qkv, groups, modulation)

    top, end = halo_rows(latents[:, 0, 0], latents[:, 0, row_count - 1])
    mods = modulation.reshape(micro_count, 6, features)
    micros = range(micro_count)
    places = jnp.stack([strip_at * row_count, map_at, group_at]).astype(jnp.int32)
    scalars = [
        jnp.concatenate(
            [jnp.where(size_tags[at] == 1, side_count, side_count // 2).astype(jnp.int32), places]
        )
        for at in micros
    ]
    kept = [{} for _ in micros]
    turn = ()

    for at in micros:
        if at == micro_count - 1:
            qkv_group = gather_group(qkv_pieces)
            turn = (turn, qkv_group)
        maps = before_attention(at, after(scalars[at], turn), latents, top, end, mods, conv_one)
        if at == 0:
            fetched = fetch_direct(pack_weights(w_proj, w_fc1, w_fc2, maps))
        turn = maps
        kept[at]["u"] = map_exchange(maps, groups).reshape(-1, features)

    for at in micros:
        keep = kept[at]
        u = after(keep["u"], turn if at == 0 else kept[at - 1]["logs"])
        keep["u"] = group_exchange(u, groups)
        done = attend(after(scalars[at], turn), keep["u"], qkv_group, score_scale, side_count)
        keep["t"], keep["o"], keep["logs"] = (done[0], done[1 : 1 + groups], done[-1])
        parts = [keep["o"][0]] + [
            permute_xor(keep["o"][k], "strip", k) for k in range(1, groups)
        ]
        if at == 0:
            fetched, keep["logs"] = tie(fetched, keep["logs"])
            direct = list(fetched.values())
            fetched = fetch_relayed(fetched)
        if at == micro_count - 1:
            for k in range(1, dp):
                if k & (k - 1):
                    fetched[k - 1], keep["logs"] = tie(fetched[k - 1], keep["logs"])
            proj_full, fc1_full, fc2_full = unpack_weights(
                fetched, keep["logs"], w_proj, w_fc1, w_fc2
            )
        maps = join_groups(scalars[at], parts, width)
        turn = (maps, direct)
        keep["o_maps"] = map_exchange(maps, groups)

    for at in micros:
        keep = kept[at]
        keep["oc"], keep["attn"], keep["x1"], keep["a2"], keep["f"], first, last = expand(
            at,
            after(scalars[at], turn),
            keep["o_maps"],
            latents,
            mods,
            proj_full,
            fc1_full,
            fc1_bias,
        )
        turn = keep["attn"]
        keep["f_halo"] = halo_rows(first, last)

    for at in micros:
        keep, grad_type = (kept[at], jnp.bfloat16)
        prev = None if at == 0 else (term_fc2, term_conv_two, mixed)
        mixed, keep["d_gate2"], keep["d_z"], term_fc2, term_conv_two, first, last = ffn_middle(
            at,
            after(scalars[at], turn),
            keep["f"],
            keep["f_halo"],
            conv_two,
            fc2_full,
            cotangent,
            keep["x1"],
            mods,
            prev,
            grad_type,
        )
        turn = keep["d_gate2"]
        keep["z_halo"] = halo_rows(first, last)

    for at in micros:
        keep, grad_type = (kept[at], jnp.bfloat16)
        prev = None if at == 0 else (term_fc1, term_fc1_bias, term_proj)
        done = ffn_back(
            at,
            after(scalars[at], turn),
            keep["d_z"],
            keep["z_halo"],
            conv_two,
            fc1_full,
            keep["a2"],
            cotangent,
            keep["x1"],
            keep["attn"],
            keep["oc"],
            proj_full,
            mods,
            prev,
            grad_type,
        )
        keep["d_x"], keep["d_mods"], term_fc1, term_fc1_bias, term_proj = done[1:]
        turn = keep["d_mods"]
        keep["d_o"] = map_exchange(done[0], groups)

    blocks = dp * strips
    wide, narrow = (hidden // blocks, features // blocks)
    small = jnp.concatenate([term_conv_two, term_fc1_bias]).reshape(10, blocks, wide)
    small = small.transpose(1, 0, 2).reshape(blocks, 10 * wide)
    merged = narrow % 8 == 0 and dp == 4
    if merged:
        small_rows = -(-10 * wide // features // 8) * 8
        small = jnp.pad(small, ((0, 0), (0, small_rows * features - 10 * wide)))
        small = small.reshape(blocks, small_rows, features).astype(jnp.bfloat16)
        small, kept[0]["d_o"] = tie(small, kept[0]["d_o"])
        shares, shapes = by_destination(term_fc2, term_fc1, term_proj, small, narrow, dp)
        send = route_core(shares, shapes)
        share = core_sum(shares, shapes, permute_xor(send, "strip", 1), dp_at)
        turn = (turn, share[1])
        came = [permute_xor(share[0], "dp", 1), permute_xor(share[2], "dp", 2)]

    for at in micros:
        keep, grad_type = (kept[at], jnp.bfloat16)
        if at > 0:
            keep["d_o"], done[0] = tie(keep["d_o"], done[0])
        pieces = group_exchange(keep["d_o"].reshape(-1, features), groups)
        if width % 128:
            pieces = [
                jnp.pad(
                    lax.dynamic_slice_in_dim(piece, group_at * width, width, 1),
                    ((0, 0), (0, -width % 128)),
                )
                for piece in pieces
            ]
        done = attend_back(
            after(scalars[at], turn),
            keep["u"],
            pieces,
            keep["o"],
            qkv_group,
            keep["t"],
            keep["logs"],
            score_scale,
            side_count,
            None if at == 0 else term_qkv,
            grad_type,
        )
        done = list(done)
        term_qkv = done[groups]
        parts = [done[0]] + [permute_xor(done[k], "strip", k) for k in range(1, groups)]
        if at == 0 and merged:
            own, x_send, y_send = turn_sums(after(share[1], done[0]), came[0], share[3], came[1])
            came = [permute_xor(x_send, "dp", 2), permute_xor(y_send, "dp", 1)]
            parts = after(parts, own)
        if at > 0:
            if merged:
                share[1], share[2], kept[0]["d_u"] = tie(share[1], share[2], kept[0]["d_u"])
            kept[0]["edges"] = edge_rows(kept[0]["d_u"], side_count)
            kept[0]["edges"], parts = tie(kept[0]["edges"], parts)
        maps = sum_groups(parts)
        turn = maps
        keep["d_u"] = map_exchange(maps, groups)
        if at == 0 and merged:
            share = list(add_up(after(own, maps), *came, strip_at >> 1))
            turn = (turn, share[0])
            share = [share[0]] + [
                permute_xor(share[k], "strip", 2 * k) for k in range(1, strips // 2)
            ]

    kept_qkv = group_sums(after(term_qkv, turn), groups, width)
    mod_grads = []
    for at in micros:
        keep = kept[at]
        first_row, last_row = (
            keep["edges"] if at == 0 else edge_rows(keep["d_u"], side_count)
        )
        d_halo = halo_rows(first_row, last_row)
        prev = None if at == 0 else (term_conv_one, d_latents)
        d_latents, keep["d_mod1"], term_conv_one = last_stage(
            at,
            after(scalars[at], turn),
            keep["d_u"],
            d_halo,
            latents,
            top,
            end,
            mods,
            conv_one,
            keep["d_x"],
            prev,
        )
        turn = keep["d_mod1"]
        if at == 0:
            parts_qkv = group_parts(kept_qkv, groups)
        mod_grads.append(
            jnp.concatenate([keep["d_mod1"], keep["d_mods"], keep["d_gate2"]]).reshape(-1)
        )

    if merged:
        total = share[0].astype(jnp.float32)
        for part in share[1:]:
            total = total + part.astype(jnp.float32)
        ratio = hidden // features
        g_fc2 = total[: ratio * narrow]
        g_fc1 = total[ratio * narrow : 2 * ratio * narrow].reshape(ratio, narrow, features)
        g_fc1 = g_fc1.transpose(1, 0, 2).reshape(narrow, hidden)
        g_proj = total[2 * ratio * narrow : (2 * ratio + 1) * narrow]
        small = total[(2 * ratio + 1) * narrow :].reshape(-1)
    else:
        g_fc2 = scatter_rows(term_fc2)
        g_fc1 = scatter_rows(term_fc1)
        g_proj = scatter_rows(term_proj)
        small = scatter_rows(small)[0]
    g_conv_two = small[: 9 * wide].reshape(9, wide)
    g_fc1_bias = small[9 * wide : 10 * wide]
    mod_grads.append(term_conv_one.reshape(-1))

    grad_mod, parts_qkv = tie(jnp.concatenate(mod_grads), parts_qkv)
    step = 1
    while step < strips:
        grad_mod = grad_mod + permute_xor(grad_mod, "strip", step)
        step *= 2
        if step == 4:
            g_qkv = group_columns(after(parts_qkv, grad_mod), groups)
    all_mods = gather_butterfly(grad_mod[None])
    block_at = dp_at * strips + strip_at
    g_conv_one = jnp.sum(all_mods[:, micro_count * 6 * features :], axis=0).reshape(9, features)
    g_conv_one = lax.dynamic_slice_in_dim(g_conv_one, block_at * narrow, narrow, 1)
    all_mods = all_mods[:, : micro_count * 6 * features].reshape(-1, 6 * features)
    conds_here = lax.dynamic_slice_in_dim(
        jnp.concatenate(conds), block_at * narrow, narrow, 1
    )
    g_ada = lax.dot_general(
        conds_here, all_mods, (((0,), (0,)), ((), ())), precision=lax.Precision.HIGHEST
    )
    ada_wide_block = 6 * features // blocks
    g_ada_bias = lax.dynamic_slice_in_dim(
        jnp.sum(all_mods, axis=0), block_at * ada_wide_block, ada_wide_block, 0
    )
    return (
        mixed,
        d_latents,
        g_ada,
        g_ada_bias,
        g_conv_one,
        g_qkv,
        g_proj,
        g_fc1,
        g_fc1_bias,
        g_conv_two,
        g_fc2,
    )


def solution(mesh):
    return jax.shard_map(
        shards,
        mesh=mesh,
        in_specs=(
            P(None, "dp", "strip", None, None),
            P(None, "dp"),
            P(None, "dp"),
            P("dp", None),
            P("dp"),
            P(None, "dp"),
            P("dp", None),
            P("dp", None),
            P("dp", None),
            P("dp"),
            P(None, "dp"),
            P("dp", None),
            P(None, "dp", "strip", None, None),
        ),
        out_specs=(
            P(None, "dp", "strip", None, None),
            P(None, "dp", "strip", None, None),
            P(("dp", "strip"), None),
            P(("dp", "strip")),
            P(None, ("dp", "strip")),
            P(("dp", "strip"), None),
            P(("dp", "strip"), None),
            P(("dp", "strip"), None),
            P(("dp", "strip")),
            P(None, ("dp", "strip")),
            P(("dp", "strip"), None),
        ),
        check_vma=False,
    )
```
